32 devices in a mesh: dp: 8 (over z, y), mp: 4 (over x, core).
Axes of the slice: x: 2, y: 2, z: 4, core: 2. Of those that a mesh axis runs over, the one named last changes fastest.
Arguments:
- tokens: bfloat16 [2, 16384, 768], P(None, ('dp', 'mp')), may hold values from -6 to 6
- cotangent: bfloat16 [2, 16384, 768], P(None, ('dp', 'mp')), may hold values from -6 to 6
- lengths: int32 [2, 16], P(None, 'dp'), may hold values from 341 to 1024, as said below
- w_query: bfloat16 [768, 768], P('dp', 'mp'), may hold values from -0.3125 to 0.3125
- w_key: bfloat16 [768, 768], P('dp', 'mp'), may hold values from -0.21875 to 0.21875
- w_value: bfloat16 [768, 768], P('dp', 'mp'), may hold values from -0.21875 to 0.21875
- w_out: bfloat16 [768, 768], P(('mp', 'dp')), may hold values from -0.875 to 0.875
- w_up: bfloat16 [768, 3072], P('dp', 'mp'), may hold values from -0.21875 to 0.21875
- w_down: bfloat16 [3072, 768], P(('mp', 'dp')), may hold values from -0.109375 to 0.109375
- b_query: float32 [768], P('mp'), may hold values from -3 to 3
- b_value: float32 [768], P('mp'), may hold values from -0.6 to 0.6
- b_up: float32 [3072], P('mp'), may hold values from -3 to 3
- b_out: float32 [768], replicated, may hold values from -0.6 to 0.6
- b_down: float32 [768], replicated, may hold values from -1.2 to 1.2
- norm1_gain: float32 [768], replicated, may hold values from 0.25 to 1.75
- norm1_shift: float32 [768], replicated, may hold values from -1.2 to 1.2
- norm2_gain: float32 [768], replicated, may hold values from 0.25 to 1.75
- norm2_shift: float32 [768], replicated, may hold values from -1.2 to 1.2
Outputs:
- output: bfloat16 [2, 16384, 768], P(None, ('dp', 'mp'))
- tokens_grad: float32 [2, 16384, 768], P(None, ('dp', 'mp'))
- w_query_grad: float32 [768, 768], P('dp', 'mp')
- w_key_grad: float32 [768, 768], P('dp', 'mp')
- w_value_grad: float32 [768, 768], P('dp', 'mp')
- w_out_grad: float32 [768, 768], P(('mp', 'dp'))
- w_up_grad: float32 [768, 3072], P('dp', 'mp')
- w_down_grad: float32 [3072, 768], P(('mp', 'dp'))
- b_query_grad: float32 [768], P(('mp', 'dp'))
- b_value_grad: float32 [768], P(('mp', 'dp'))
- b_up_grad: float32 [3072], P(('mp', 'dp'))
- b_out_grad: float32 [768], P(('dp', 'mp'))
- b_down_grad: float32 [768], P(('dp', 'mp'))
- norm1_gain_grad: float32 [768], P(('dp', 'mp'))
- norm1_shift_grad: float32 [768], P(('dp', 'mp'))
- norm2_gain_grad: float32 [768], P(('dp', 'mp'))
- norm2_shift_grad: float32 [768], P(('dp', 'mp'))
- rms_values: float32 [3], replicated
The draws below stay inside these ranges and needn't reach their ends.
Inputs may be any that keep to these rules, and one draw needn't show every extreme that they name: The last sequence of every micro-batch has all 1024 positions valid; lengths tend to grow with the sequence's index.
All inputs are finite; a program needn't handle non-finite values.
Results may differ from the reference program's by a relative error of at most 0.019.
Values may be sent and summed in bfloat16 or wider, within the bound.
A program may use at most 192 MiB of HBM per device.

```python
import jax
import jax.numpy as jnp
from jax import lax

D = 768
H = 12
HD = 64
FF = 3072
L = 1024
SEQ_MB = 2
MB = 2
TOK_MB = 16384
NSEQ_MB = 16
N_DP = 8
N_MP = 4


def draw_lengths(key, part):
    index = jnp.arange(NSEQ_MB, dtype=jnp.int32)
    base = L // 3 + L * 8 * index // (15 * max(NSEQ_MB - 1, 1))
    jitter = jax.random.randint(key, (MB, NSEQ_MB), 0, L // 5 + 1, dtype=jnp.int32)
    values = jnp.minimum(base[None, :] + jitter, L)
    values = jnp.where(index[None, :] == NSEQ_MB - 1, L, values)
    return values.astype(jnp.int32)


def draw_tokens(key, part):
    block_index = (jnp.arange(TOK_MB) // (SEQ_MB * L)).astype(jnp.float32)
    fraction = block_index / max(N_DP - 1, 1)
    entries = jnp.clip(jax.random.normal(key, (MB, TOK_MB, D), jnp.float32), -4.0, 4.0)
    ramp = 0.85 * jnp.exp(fraction * 0.5343387)
    return (entries * ramp[None, :, None]).astype(jnp.bfloat16)


def block_scale(own_key, extent, split, smallest, top_value):
    factor_of, own = 1.0, jax.random.fold_in(own_key, 6)
    for dim, blocks in split:
        heights = jnp.exp(jax.random.uniform(jax.random.fold_in(own, dim), (blocks,), jnp.float32, smallest / len(split), top_value / len(split)))
        factor_of = factor_of * jnp.repeat(heights, extent[dim] // blocks).reshape([-1 if axis == dim else 1 for axis in range(len(extent))])
    return factor_of


def gaussian(own_key, extent, scale, bound, shards=(), kind=jnp.bfloat16):
    values = jax.random.normal(own_key, extent, jnp.float32) * scale
    if len(shards) > 0:
        values = block_scale(own_key, extent, shards, -0.22, 0.18) * values
    return jnp.clip(values, min=-bound, max=bound).astype(kind)


def setup_inputs(seed: int = 0) -> dict:
    seeds = jax.random.split(jax.random.key(seed), 19)
    return {
        "tokens": draw_tokens(jax.random.fold_in(seeds[18], 71), 0),
        "cotangent": gaussian(seeds[1], (MB, TOK_MB, D), 1.0, 6.0, ((1, 32),)),
        "lengths": draw_lengths(jax.random.fold_in(seeds[18], 71), 0),
        "w_query": gaussian(seeds[3], (D, D), (D // 2) ** -0.5, 0.3125, ((0, 8), (1, 4))),
        "w_key": gaussian(seeds[4], (D, D), D ** -0.5, 0.21875, ((0, 8), (1, 4))),
        "w_value": gaussian(seeds[5], (D, D), D ** -0.5, 0.21875, ((0, 8), (1, 4))),
        "w_out": gaussian(seeds[6], (D, D), (D // 16) ** -0.5, 0.875, ((0, 32),)),
        "w_up": gaussian(seeds[7], (D, FF), D ** -0.5, 0.21875, ((0, 8), (1, 4))),
        "w_down": gaussian(seeds[8], (FF, D), FF ** -0.5, 0.109375, ((0, 32),)),
        "b_query": gaussian(seeds[9], (D,), 0.5, 3.0, ((0, 4),), jnp.float32),
        "b_value": gaussian(seeds[10], (D,), 0.1, 0.6, ((0, 4),), jnp.float32),
        "b_up": gaussian(seeds[11], (FF,), 0.5, 3.0, ((0, 4),), jnp.float32),
        "b_out": gaussian(seeds[12], (D,), 0.1, 0.6, (), jnp.float32),
        "b_down": gaussian(seeds[13], (D,), 0.2, 1.2, (), jnp.float32),
        "norm1_gain": jnp.clip(1.0 + 0.15 * jax.random.normal(seeds[14], (D,), jnp.float32), 0.25, 1.75),
        "norm1_shift": gaussian(seeds[15], (D,), 0.2, 1.2, (), jnp.float32),
        "norm2_gain": jnp.clip(1.0 + 0.15 * jax.random.normal(seeds[16], (D,), jnp.float32), 0.25, 1.75),
        "norm2_shift": gaussian(seeds[17], (D,), 0.2, 1.2, (), jnp.float32),
    }


epsilon = 1e-05
masked_score = -1e+30

@jax.custom_vjp
def low(v):
    return lax.optimization_barrier(v.astype(jnp.bfloat16)).astype(jnp.float32)

@jax.custom_vjp
def low_back(v):
    return v

def low_keep(v):
    return (low(v), None)

def low_pass(kept, grad):
    return (grad,)

def back_keep(v):
    return (v, None)

def back_low(kept, grad):
    return (low(grad),)
low.defvjp(low_keep, low_pass)
low_back.defvjp(back_keep, back_low)

def matmul(left_side, right_side):
    return jnp.dot(left_side, right_side, precision=lax.Precision.HIGHEST)

def layer_norm(values, norm_gain, norm_shift):
    center = values - lax.optimization_barrier(jnp.mean(values, axis=-1, keepdims=True))
    spread = lax.optimization_barrier(jnp.mean(center * center, axis=-1, keepdims=True))
    return center * lax.rsqrt(spread + epsilon) * norm_gain + norm_shift

def attend(packed):
    queries, keys_all, values_all, length = packed
    scores = jnp.einsum('qhd,khd->hqk', queries, keys_all, precision=lax.Precision.HIGHEST)
    scores = low_back(scores * HD ** (-0.5))
    visible = jnp.arange(L) < length
    scores = jnp.where(visible[None, None, :], scores, masked_score)
    attn_probs = jax.nn.softmax(scores, axis=-1)
    return jnp.einsum('hqk,khd->qhd', low(attn_probs), values_all, precision=lax.Precision.HIGHEST)

def forward(params, hidden_in, seq_lengths):
    w_query, w_key, w_value, w_out, w_up, w_down, b_query, b_value, b_up, b_out, b_down, norm1_gain, norm1_shift, norm2_gain, norm2_shift = params
    row_count = hidden_in.shape[0]
    group_cols = D // N_MP
    group_heads = H // N_MP
    group_units = FF // N_MP
    four_shape = (SEQ_MB, L, group_heads, HD)
    checked = jax.checkpoint(attend)
    attn_total = jnp.zeros((row_count, D), jnp.float32)
    for member in range(N_MP):
        columns = slice(member * group_cols, (member + 1) * group_cols)
        rounded_in = low_back(hidden_in)
        queries = low(low_back(matmul(rounded_in, w_query[:, columns])) + b_query[columns])
        keys_all = low(low_back(matmul(rounded_in, w_key[:, columns])))
        values_all = low(low_back(matmul(rounded_in, w_value[:, columns])) + b_value[columns])
        heads_out = lax.map(checked, (queries.reshape(four_shape), keys_all.reshape(four_shape), values_all.reshape(four_shape), seq_lengths))
        heads_out = low(low_back(heads_out.reshape(row_count, group_cols)))
        attn_total = attn_total + low(matmul(heads_out, w_out[columns, :]))
    attention = low_back(attn_total) + b_out
    first_norm = layer_norm(hidden_in + attention, norm1_gain, norm1_shift)
    first_low = low(first_norm)
    ffn_total = jnp.zeros((row_count, D), jnp.float32)
    for member in range(N_MP):
        units_range = slice(member * group_units, (member + 1) * group_units)
        rounded_norm = low_back(first_low)
        preact = low_back(matmul(rounded_norm, w_up[:, units_range])) + b_up[units_range]
        active = low(jax.nn.gelu(preact, approximate=False))
        ffn_total = ffn_total + low(matmul(active, w_down[units_range, :]))
    ffn_out = low_back(ffn_total) + b_down
    stream = first_norm + ffn_out
    return (layer_norm(stream, norm2_gain, norm2_shift), (attention, ffn_out, stream))

def reference(tokens, cotangent, lengths, w_query, w_key, w_value, w_out, w_up, w_down, b_query, b_value, b_up, b_out, b_down, norm1_gain, norm1_shift, norm2_gain, norm2_shift):
    params = tuple((weight.astype(jnp.float32) for weight in (w_query, w_key, w_value, w_out, w_up, w_down, b_query, b_value, b_up, b_out, b_down, norm1_gain, norm1_shift, norm2_gain, norm2_shift)))
    row_count = SEQ_MB * L
    block_count = MB * N_DP
    inputs = tokens.astype(jnp.float32).reshape(block_count, row_count, D)
    upstream = cotangent.astype(jnp.float32).reshape(block_count, row_count, D)
    seq_table = lengths.reshape(block_count, SEQ_MB)
    positions = jnp.arange(row_count) % L
    owners = jnp.arange(row_count) // L

    def advance(state_now, block_data):
        totals, squares = state_now
        block_in, block_up, block_len = block_data

        def apply_layer(weights, values):
            return forward(weights, values, block_len)
        output, pullback, extras = jax.vjp(apply_layer, params, block_in, has_aux=True)
        weight_grads, input_grad = pullback(block_up)
        totals = jax.tree.map(jnp.add, totals, weight_grads)
        attention, ffn_out, stream = extras
        valid_row = (positions < block_len[owners]).astype(jnp.float32)[:, None]
        fresh = jnp.stack([jnp.sum(valid_row * stream * stream), jnp.sum(valid_row * attention * attention), jnp.sum(valid_row * ffn_out * ffn_out), jnp.sum(valid_row)])
        return ((totals, squares + fresh), (output.astype(jnp.bfloat16), input_grad))
    initial = (jax.tree.map(jnp.zeros_like, params), jnp.zeros((4,), jnp.float32))
    (totals, squares), (outputs, input_grads) = lax.scan(advance, initial, (inputs, upstream, seq_table))
    rms_values = jnp.sqrt(squares[:3] / (squares[3] * D))
    return (outputs.reshape(MB, TOK_MB, D), input_grads.reshape(MB, TOK_MB, D), totals[0], totals[1], totals[2], totals[3], totals[4], totals[5], totals[6], totals[7], totals[8], totals[9], totals[10], totals[11], totals[12], totals[13], totals[14], rms_values)
```

```python
import functools

import jax
import jax.numpy as jnp
from jax import lax
from jax.experimental import pallas as pl
from jax.experimental.pallas import tpu as pltpu
from jax.sharding import PartitionSpec as P

HD = 64
L = 1024
SEQ_MB = 2
MB = 2
GROUPS = 4
GH = 3
GC = GH * HD
PAD = 256

epsilon = 1e-05
masked_score = -1e30
exp2_scale = HD ** (-0.5) * 1.4426950408889634
score_scale = HD ** (-0.5)
BOTH = ("dp", "mp")
NT = (((1,), (1,)), ((), ()))


def product(left_side, right_side):
    return jnp.dot(left_side, right_side, preferred_element_type=jnp.float32)


def contract_rows(left_side, right_side):
    return lax.dot_general(
        left_side, right_side, (((0,), (0,)), ((), ())), preferred_element_type=jnp.float32
    )


def contract_cols(left_side, right_side):
    return lax.dot_general(left_side, right_side, NT, preferred_element_type=jnp.float32)


def layer_norm(values, norm_gain, norm_shift):
    center = values - jnp.mean(values, axis=-1, keepdims=True)
    spread = jnp.mean(center * center, axis=-1, keepdims=True)
    inverse = lax.rsqrt(spread + epsilon)
    scaled = center * inverse
    return (scaled * norm_gain + norm_shift, scaled, inverse)


def norm_back(upstream, scaled, inverse, norm_gain):
    gain_grad = jnp.sum(upstream * scaled, axis=0)
    shift_grad = jnp.sum(upstream, axis=0)
    through = upstream * norm_gain
    result = inverse * (
        through
        - jnp.mean(through, axis=-1, keepdims=True)
        - scaled * jnp.mean(through * scaled, axis=-1, keepdims=True)
    )
    return (result, gain_grad, shift_grad)


def head_keys(keys, bias, h, lane):
    kept = jnp.where((lane >= h * HD) & (lane < (h + 1) * HD), keys, jnp.zeros_like(keys))
    return jnp.where(lane == GC, bias, kept)


def attend_forward_kernel(bias_ref, qkv_ref, out_ref, lse_ref, turned):
    rows = qkv_ref.shape[1]
    chunk = 256
    lane = lax.broadcasted_iota(jnp.int32, (1, PAD), 1)
    keys = qkv_ref[0, :, PAD : 2 * PAD]
    values_t = qkv_ref[0, :, 2 * PAD :].T
    bias = bias_ref[...]
    for h in range(GH):
        own = head_keys(keys, bias, h, lane)
        own_values = values_t[h * HD : (h + 1) * HD, :]
        for at in range(0, rows, chunk):
            queries = qkv_ref[0, at : at + chunk, :PAD]
            scores = contract_cols(own, queries)
            top = jnp.max(scores, axis=0, keepdims=True) * exp2_scale
            raised = jnp.exp2(scores * exp2_scale - top)
            total = jnp.sum(raised, axis=0, keepdims=True)
            mixed = product(own_values, raised.astype(jnp.bfloat16))
            turned[h * HD : (h + 1) * HD, at : at + chunk] = mixed / total
            lse_ref[0, h : h + 1, at : at + chunk] = top + jnp.log2(total)
    turned[GC:, :] = jnp.zeros((PAD - GC, rows), jnp.float32)
    out_ref[0] = turned[...].T.astype(jnp.bfloat16)


def attend_forward(qkv, bias):
    rows = qkv.shape[1]
    return pl.pallas_call(
        attend_forward_kernel,
        grid=(GROUPS,),
        in_specs=[
            pl.BlockSpec((rows, 1), lambda g: (0, 0)),
            pl.BlockSpec((1, rows, 3 * PAD), lambda g: (g, 0, 0)),
        ],
        out_specs=[
            pl.BlockSpec((1, rows, PAD), lambda g: (g, 0, 0)),
            pl.BlockSpec((1, 8, rows), lambda g: (g, 0, 0)),
        ],
        out_shape=[
            jax.ShapeDtypeStruct((GROUPS, rows, PAD), jnp.bfloat16),
            jax.ShapeDtypeStruct((GROUPS, 8, rows), jnp.float32),
        ],
        scratch_shapes=[pltpu.VMEM((PAD, rows), jnp.float32)],
        cost_estimate=pl.CostEstimate(
            flops=45_000_000_000 // 3, bytes_accessed=10_000_000, transcendentals=12_000_000
        ),
    )(bias, qkv)


def attend_backward_kernel(
    bias_ref, qkv_ref, out_ref, lse_ref, grad_ref, joined_ref, sums_ref, probs, slopes, turned
):
    rows = qkv_ref.shape[1]
    chunk = 256
    lane = lax.broadcasted_iota(jnp.int32, (1, PAD), 1)
    keys = qkv_ref[0, :, PAD : 2 * PAD]
    keys_t = keys.T
    values = qkv_ref[0, :, 2 * PAD :]
    bias = bias_ref[...]
    crossed = (grad_ref[0].astype(jnp.float32) * out_ref[0].astype(jnp.float32)).T
    key_grad = jnp.zeros((rows, PAD), jnp.float32)
    value_grad = jnp.zeros((rows, PAD), jnp.float32)
    for h in range(GH):
        head = (lane >= h * HD) & (lane < (h + 1) * HD)
        own = head_keys(keys, bias, h, lane)
        own_values = jnp.where(head, values, jnp.zeros_like(values))
        delta = jnp.sum(crossed[h * HD : (h + 1) * HD, :], axis=0, keepdims=True)
        for at in range(0, rows, chunk):
            queries = qkv_ref[0, at : at + chunk, :PAD]
            grads = grad_ref[0, at : at + chunk, :]
            scores = contract_cols(own, queries)
            attn_probs = jnp.exp2(scores * exp2_scale - lse_ref[0, h : h + 1, at : at + chunk])
            prob_grad = contract_cols(own_values, grads)
            probs[:, at : at + chunk] = attn_probs.astype(jnp.bfloat16)
            slopes[:, at : at + chunk] = (
                attn_probs * (prob_grad - delta[:, at : at + chunk])
            ).astype(jnp.bfloat16)
        own_grads = jnp.where(head, grad_ref[0], jnp.zeros((), jnp.bfloat16))
        own_queries = jnp.where(head, qkv_ref[0, :, :PAD], jnp.zeros((), jnp.bfloat16))
        value_grad = value_grad + product(probs[...], own_grads)
        key_grad = key_grad + product(slopes[...], own_queries)
        turned[h * HD : (h + 1) * HD, :] = product(
            keys_t[h * HD : (h + 1) * HD, :], slopes[...]
        )
    turned[GC:, :] = jnp.zeros((PAD - GC, rows), jnp.float32)
    query_grad = turned[...].T * score_scale
    joined_ref[0, :, :PAD] = query_grad.astype(jnp.bfloat16)
    joined_ref[0, :, PAD : 2 * PAD] = (key_grad * score_scale).astype(jnp.bfloat16)
    joined_ref[0, :, 2 * PAD :] = value_grad.astype(jnp.bfloat16)
    sums_ref[0, 0:1, :] = jnp.sum(query_grad, axis=0, keepdims=True)
    sums_ref[0, 1:2, :] = jnp.sum(value_grad, axis=0, keepdims=True)


def attend_backward(qkv, bias, heads_out, lse, heads_grad):
    rows = qkv.shape[1]
    return pl.pallas_call(
        attend_backward_kernel,
        grid=(GROUPS,),
        in_specs=[
            pl.BlockSpec((rows, 1), lambda g: (0, 0)),
            pl.BlockSpec((1, rows, 3 * PAD), lambda g: (g, 0, 0)),
            pl.BlockSpec((1, rows, PAD), lambda g: (g, 0, 0)),
            pl.BlockSpec((1, 8, rows), lambda g: (g, 0, 0)),
            pl.BlockSpec((1, rows, PAD), lambda g: (g, 0, 0)),
        ],
        out_specs=[
            pl.BlockSpec((1, rows, 3 * PAD), lambda g: (g, 0, 0)),
            pl.BlockSpec((1, 8, PAD), lambda g: (g, 0, 0)),
        ],
        out_shape=[
            jax.ShapeDtypeStruct((GROUPS, rows, 3 * PAD), jnp.bfloat16),
            jax.ShapeDtypeStruct((GROUPS, 8, PAD), jnp.float32),
        ],
        scratch_shapes=[
            pltpu.VMEM((rows, rows), jnp.bfloat16),
            pltpu.VMEM((rows, rows), jnp.bfloat16),
            pltpu.VMEM((PAD, rows), jnp.float32),
        ],
        cost_estimate=pl.CostEstimate(
            flops=30_000_000_000, bytes_accessed=20_000_000, transcendentals=12_000_000
        ),
    )(bias, qkv, heads_out, lse, heads_grad)


def swap_with_partner(values):
    size = lax.axis_size("mp")
    return lax.ppermute(values, "mp", [(i, i ^ 1) for i in range(size)])


def pad_heads(values):
    return jnp.pad(values, [(0, 0)] * (values.ndim - 1) + [(0, PAD - values.shape[-1])])


MESH = pl.DeviceIdType.MESH


def positions():
    mp, dp = lax.axis_index("mp"), lax.axis_index("dp")
    return mp, lax.div(mp, 2), lax.rem(mp, 2), lax.div(dp, 2), lax.rem(dp, 2)


def at_place(x, c, z, y):
    return (2 * z + y, 2 * x + c)


def neighbours(nz):
    mp, x, c, z, y = positions()
    first = at_place(lax.rem(x + c, 2), c, z, lax.rem(y + 1 - c, 2))
    second = at_place(lax.rem(x + 1 - c, 2), c, z, lax.rem(y + c, 2))
    partner = at_place(x, 1 - c, z, y)
    along = [at_place(x, c, lax.rem(z + d, nz), y) for d in range(1, nz)]
    return first, second, partner, along


def meet(devices):
    barrier = pltpu.get_barrier_semaphore()
    for device in devices:
        pl.semaphore_signal(barrier, inc=1, device_id=device, device_id_type=MESH)
    pl.semaphore_wait(barrier, len(devices))


def regions(x, c, y):
    own = (x, y)
    first = (lax.rem(x + c, 2), lax.rem(y + 1 - c, 2))
    second = (lax.rem(x + 1 - c, 2), lax.rem(y + c, 2))
    third = (1 - x, 1 - y)
    return own, first, second, third


def gather_kernel(nz, parts, *refs):
    shards, fulls = refs[:parts], refs[parts : 2 * parts]
    own_sem, z_send, z_recv, send, recv = refs[2 * parts :]
    mp, x, c, z, y = positions()
    first, second, partner, along = neighbours(nz)
    meet([first, second, partner, *along])
    own, got1, got2, got3 = regions(x, c, y)
    other = regions(x, 1 - c, y)

    def remote(src, dst, s, r, device):
        return pltpu.make_async_remote_copy(
            src_ref=src, dst_ref=dst, send_sem=s, recv_sem=r, device_id=device, device_id_type=MESH
        )

    started = []
    locals_ = []
    spread = []
    for p in range(parts):
        keep = pltpu.make_async_copy(shards[p], fulls[p].at[x, c, z, y], own_sem.at[p])
        keep.start()
        locals_.append(keep)
        sends = [
            remote(shards[p], fulls[p].at[x, c, z, y], z_send.at[p, d], z_recv.at[p, d], along[d])
            for d in range(nz - 1)
        ]
        for copy in sends:
            copy.start()
        spread.append(sends)

    def block(p, core, place):
        return fulls[p].at[place[0], core, :, place[1]]

    def push(p, k, core, place, device):
        copy = remote(block(p, core, place), block(p, core, place), send.at[p, k], recv.at[p, k], device)
        copy.start()
        started.append(copy)
        return copy

    def arrived(p, k, core, place):
        here = block(p, core, place)
        remote(here, here, send.at[p, k], recv.at[p, k], first).wait_recv()

    for p in range(parts):
        locals_[p].wait()
        for copy in spread[p]:
            copy.wait_recv()
        push(p, 0, c, own, first)
        push(p, 1, c, own, second)
        push(p, 3, c, own, partner)
    for p in range(parts):
        arrived(p, 0, c, got1)
        push(p, 2, c, got1, second)
        push(p, 4, c, got1, partner)
    for p in range(parts):
        arrived(p, 1, c, got2)
        push(p, 5, c, got2, partner)
        arrived(p, 2, c, got3)
        push(p, 6, c, got3, partner)
    for p in range(parts):
        for k in range(4):
            arrived(p, 3 + k, 1 - c, other[k])
    for sends in spread:
        for copy in sends:
            copy.wait_send()
    for copy in started:
        copy.wait_send()


def gather_all(shards):
    n_dp = lax.axis_size("dp")
    nz, parts = n_dp // 2, len(shards)
    return pl.pallas_call(
        functools.partial(gather_kernel, nz, parts),
        in_specs=[pl.BlockSpec(memory_space=pltpu.VMEM)] * parts,
        out_specs=[pl.BlockSpec(memory_space=pl.ANY)] * parts,
        out_shape=[jax.ShapeDtypeStruct((2, 2, nz, 2, *s.shape), s.dtype) for s in shards],
        scratch_shapes=[
            pltpu.SemaphoreType.DMA((parts,)),
            pltpu.SemaphoreType.DMA((parts, nz - 1)),
            pltpu.SemaphoreType.DMA((parts, nz - 1)),
            pltpu.SemaphoreType.DMA((parts, 7)),
            pltpu.SemaphoreType.DMA((parts, 7)),
        ],
        compiler_params=pltpu.CompilerParams(collective_id=0, has_side_effects=True),
    )(*shards)


def scatter_kernel(nz, parts, *refs):
    partials, results = refs[:parts], refs[parts : 2 * parts]
    at = 2 * parts
    sums, heard1, heard2, heard3, heard4 = (
        refs[at + i * parts : at + (i + 1) * parts] for i in range(5)
    )
    own_sem, send, recv, z_send, z_recv = refs[at + 5 * parts :]
    mp, x, c, z, y = positions()
    first, second, partner, along = neighbours(nz)
    meet([first, second, partner, *along])
    own, got1, got2, got3 = regions(x, c, y)
    started = []

    def remote(src, dst, s, r, device):
        copy = pltpu.make_async_remote_copy(
            src_ref=src, dst_ref=dst, send_sem=s, recv_sem=r, device_id=device, device_id_type=MESH
        )
        copy.start()
        started.append(copy)
        return copy

    def add(p, place, more):
        for i in range(nz):
            here = sums[p].at[place[0], i, place[1]]
            here[...] = (here[...].astype(jnp.float32) + more[i].astype(jnp.float32)).astype(here.dtype)

    kept, core_copies = [], []
    for p in range(parts):
        copies = []
        for k in range(2):
            keep = pltpu.make_async_copy(partials[p].at[k, c], sums[p].at[k], own_sem.at[p, k])
            keep.start()
            copies.append(keep)
        kept.append(copies)
        core_copies.append(
            [
                remote(partials[p].at[k, 1 - c], heard1[p].at[k], send.at[p, k], recv.at[p, k], partner)
                for k in range(2)
            ]
        )
    second_copies = []
    for p in range(parts):
        for copy in kept[p]:
            copy.wait()
        for copy in core_copies[p]:
            copy.wait_recv()
        copies = []
        for k, place in enumerate((got2, got3)):
            add(p, place, heard1[p].at[place[0], :, place[1]])
            copies.append(
                remote(
                    sums[p].at[place[0], :, place[1]],
                    heard2[p].at[k],
                    send.at[p, 2 + k],
                    recv.at[p, 2 + k],
                    second,
                )
            )
        second_copies.append(copies)
        for place in (got1, own):
            add(p, place, heard1[p].at[place[0], :, place[1]])
    first_copies = []
    for p in range(parts):
        second_copies[p][1].wait_recv()
        add(p, got1, heard2[p].at[1])
        first_copies.append(
            remote(sums[p].at[got1[0], :, got1[1]], heard3[p], send.at[p, 4], recv.at[p, 4], first)
        )
        second_copies[p][0].wait_recv()
        add(p, own, heard2[p].at[0])
    last_copies = []
    for p in range(parts):
        first_copies[p].wait_recv()
        add(p, own, heard3[p])
        last_copies.append(
            [
                remote(
                    sums[p].at[x, lax.rem(z + d + 1, nz), y],
                    heard4[p].at[d],
                    z_send.at[p, d],
                    z_recv.at[p, d],
                    along[d],
                )
                for d in range(nz - 1)
            ]
        )
    for p in range(parts):
        for copy in last_copies[p]:
            copy.wait_recv()
        total = sums[p][x, z, y].astype(jnp.float32)
        for d in range(nz - 1):
            total = total + heard4[p][d].astype(jnp.float32)
        results[p][...] = total
    for copy in started:
        copy.wait_send()


def scatter_sums(partials):
    nz, parts = lax.axis_size("dp") // 2, len(partials)
    tails = [p.shape[4:] for p in partials]
    kinds = [p.dtype for p in partials]
    return pl.pallas_call(
        functools.partial(scatter_kernel, nz, parts),
        in_specs=[pl.BlockSpec(memory_space=pl.ANY)] * parts,
        out_specs=[pl.BlockSpec(memory_space=pltpu.VMEM)] * parts,
        out_shape=[jax.ShapeDtypeStruct(t, jnp.float32) for t in tails],
        scratch_shapes=[
            *[pltpu.VMEM((2, nz, 2, *t), k) for t, k in zip(tails, kinds)],
            *[pltpu.VMEM((2, nz, 2, *t), k) for t, k in zip(tails, kinds)],
            *[pltpu.VMEM((2, nz, *t), k) for t, k in zip(tails, kinds)],
            *[pltpu.VMEM((nz, *t), k) for t, k in zip(tails, kinds)],
            *[pltpu.VMEM((nz - 1, *t), k) for t, k in zip(tails, kinds)],
            pltpu.SemaphoreType.DMA((parts, 2)),
            pltpu.SemaphoreType.DMA((parts, 5)),
            pltpu.SemaphoreType.DMA((parts, 5)),
            pltpu.SemaphoreType.DMA((parts, nz - 1)),
            pltpu.SemaphoreType.DMA((parts, nz - 1)),
        ],
        compiler_params=pltpu.CompilerParams(
            collective_id=1, has_side_effects=True, vmem_limit_bytes=60 * 1024 * 1024
        ),
    )(*partials)


def in_place_order(blocks):
    return blocks.reshape(2, 2, blocks.shape[1] // 2, 2, *blocks.shape[2:])


def body(
    tokens,
    cotangent,
    lengths,
    w_query,
    w_key,
    w_value,
    w_out,
    w_up,
    w_down,
    b_query,
    b_value,
    b_up,
    b_out,
    b_down,
    norm1_gain,
    norm1_shift,
    norm2_gain,
    norm2_shift,
):
    half_rows = tokens.shape[1]
    width = tokens.shape[2]
    n_dp, n_mp = lax.axis_size("dp"), lax.axis_size("mp")
    unit_cols = w_up.shape[1]
    mp_index = lax.axis_index("mp")
    half = lax.rem(mp_index, 2)
    seq = lax.div(mp_index, 2)

    def own_of(pair):
        return jnp.where(half == 0, pair[0], pair[1])

    def other_of(pair):
        return jnp.where(half == 0, pair[1], pair[0])

    rows_in = jnp.concatenate([own_of(tokens), swap_with_partner(other_of(tokens))], axis=0)
    rows_cot = jnp.concatenate([own_of(cotangent), swap_with_partner(other_of(cotangent))], axis=0)
    length = lax.dynamic_slice(lengths, (half, seq), (1, 1))[0, 0]
    place = jnp.arange(half_rows, dtype=jnp.int32)
    place = jnp.concatenate([place + half * half_rows, place + (1 - half) * half_rows])
    valid_row = (place < length)[:, None]
    bias = jnp.where(valid_row, 0.0, masked_score).astype(jnp.bfloat16)
    valid_row = valid_row.astype(jnp.float32)

    biases = jnp.pad(jnp.concatenate([b_query, b_value, b_up]), (0, 896)).reshape(16, 128)
    qkv_shard = jnp.concatenate([w_query, w_key, w_value], axis=1)
    gathered = gather_all([qkv_shard, w_out, w_up, w_down, biases])
    full_qkv, full_out, full_up, full_down, full_bias = (
        g.reshape(n_mp, n_dp, *g.shape[4:]) for g in gathered
    )
    full_qkv = full_qkv.reshape(n_mp, width, 3, GC)
    w_joined = pad_heads(full_qkv).reshape(n_mp, width, 3 * PAD)
    full_out = full_out.reshape(n_mp, GC, width)
    out_pad = jnp.pad(full_out, ((0, 0), (0, PAD - GC), (0, 0))).reshape(n_mp * PAD, width)
    full_up = full_up.reshape(n_mp, width, unit_cols).transpose(1, 0, 2).reshape(width, n_mp * unit_cols)
    full_down = full_down.reshape(n_mp * unit_cols, width)
    full_bias = full_bias[:, 0].reshape(n_mp, -1)
    bias_q, bias_v, bias_up = full_bias[:, :GC], full_bias[:, GC:2*GC], full_bias[:, 2*GC:2*GC+unit_cols]
    mark = jnp.zeros((n_mp, PAD - GC), jnp.float32).at[:, 0].set(1.0)
    joined_bias = jnp.concatenate(
        [bias_q, mark, jnp.zeros((n_mp, PAD), jnp.float32), pad_heads(bias_v)], axis=1
    )

    qkv = lax.dot_general(
        jnp.broadcast_to(rows_in[None], (n_mp, *rows_in.shape)),
        w_joined,
        (((2,), (1,)), ((0,), (0,))),
        preferred_element_type=jnp.float32,
    )
    qkv = (qkv + joined_bias[:, None, :]).astype(jnp.bfloat16)
    heads_out, lse = attend_forward(qkv, bias)
    heads_flat = heads_out.transpose(1, 0, 2).reshape(2 * half_rows, n_mp * PAD)
    attention = product(heads_flat, out_pad) + b_out
    first_norm, first_scaled, first_inverse = layer_norm(
        rows_in.astype(jnp.float32) + attention, norm1_gain, norm1_shift
    )
    first_low = first_norm.astype(jnp.bfloat16)
    preact = product(first_low, full_up) + bias_up.reshape(-1)
    cumulative = 0.5 * (1.0 + lax.erf(preact * 0.7071067811865476))
    active = (preact * cumulative).astype(jnp.bfloat16)
    slope = cumulative + preact * (jnp.exp(-0.5 * preact * preact) * 0.3989422804014327)
    ffn_out = product(active, full_down) + b_down
    stream = first_norm + ffn_out
    final_norm, final_scaled, final_inverse = layer_norm(stream, norm2_gain, norm2_shift)
    output = final_norm.astype(jnp.bfloat16)
    squares = jnp.stack(
        [
            jnp.sum(valid_row * stream * stream),
            jnp.sum(valid_row * attention * attention),
            jnp.sum(valid_row * ffn_out * ffn_out),
            jnp.sum(valid_row),
        ]
    )

    stream_grad, gain2_grad, shift2_grad = norm_back(
        rows_cot.astype(jnp.float32), final_scaled, final_inverse, norm2_gain
    )
    down_bias_grad = jnp.sum(stream_grad, axis=0)
    ffn_grad_low = stream_grad.astype(jnp.bfloat16)
    active_grad = contract_cols(ffn_grad_low, full_down)
    down_wgrad = contract_rows(active, ffn_grad_low)
    preact_grad = active_grad * slope
    up_bias_grad = jnp.sum(preact_grad, axis=0)
    preact_low = preact_grad.astype(jnp.bfloat16)
    up_wgrad = contract_rows(first_low, preact_low)
    first_grad = stream_grad + contract_cols(preact_low, full_up)
    attn_grad, gain1_grad, shift1_grad = norm_back(
        first_grad, first_scaled, first_inverse, norm1_gain
    )
    out_bias_grad = jnp.sum(attn_grad, axis=0)
    attn_grad_low = attn_grad.astype(jnp.bfloat16)
    out_wgrad = contract_rows(heads_flat, attn_grad_low)
    heads_grad = contract_cols(attn_grad_low, out_pad).astype(jnp.bfloat16)
    heads_grad = heads_grad.reshape(2 * half_rows, n_mp, PAD).transpose(1, 0, 2)
    joined, sums = attend_backward(qkv, bias, heads_out, lse, heads_grad)
    joined_wgrad = lax.dot_general(
        jnp.broadcast_to(rows_in[None], (n_mp, *rows_in.shape)),
        joined,
        (((1,), (1,)), ((0,), (0,))),
        preferred_element_type=jnp.float32,
    )
    tokens_grad = attn_grad + jnp.sum(
        lax.dot_general(
            joined, w_joined, (((2,), (2,)), ((0,), (0,))), preferred_element_type=jnp.float32
        ),
        axis=0,
    )

    low = jnp.bfloat16
    joined_blocks = (
        joined_wgrad.astype(low)
        .reshape(n_mp, n_dp, width // n_dp, 3, PAD)[..., :GC]
        .reshape(n_mp, n_dp, width // n_dp, 3 * GC)
    )
    out_blocks = (
        out_wgrad.astype(low)
        .reshape(n_mp, PAD, width)[:, :GC]
        .reshape(n_mp, n_dp, GC // n_dp, width)
    )
    up_blocks = up_wgrad.astype(low).reshape(n_dp, width // n_dp, n_mp, unit_cols).transpose(2, 0, 1, 3)
    down_blocks = down_wgrad.astype(low).reshape(n_mp, n_dp, unit_cols // n_dp, width)

    def by_mp(vector):
        return vector.reshape(n_mp, n_dp, -1)

    def by_dp(vector):
        return vector.reshape(n_dp, n_mp, -1).transpose(1, 0, 2)

    vectors = [by_mp(sums[:, 0, :GC]), by_mp(sums[:, 1, :GC]), by_mp(up_bias_grad)]
    vectors += [
        by_dp(v)
        for v in (out_bias_grad, down_bias_grad, gain1_grad, shift1_grad, gain2_grad, shift2_grad)
    ]
    vectors.append(jnp.broadcast_to(squares, (n_mp, n_dp, 4)))
    ends = [v.shape[-1] for v in vectors]
    vectors = jnp.concatenate(vectors, axis=-1)
    vectors = jnp.pad(vectors, ((0, 0), (0, 0), (0, 1024 - vectors.shape[-1])))
    vectors = vectors.reshape(n_mp, n_dp, 8, 128)
    own_down, own_up, own_out, own_joined, own_vector = scatter_sums(
        [
            in_place_order(b)
            for b in (down_blocks, up_blocks, out_blocks, joined_blocks, vectors)
        ]
    )
    own_vector = own_vector.reshape(-1)
    own_vectors, start = [], 0
    for size in ends:
        own_vectors.append(own_vector[start : start + size])
        start += size
    totals = own_vectors.pop()
    rms_values = jnp.sqrt(totals[:3] / (totals[3] * width))

    def back_home(rows):
        mine, sent = rows[:half_rows], swap_with_partner(rows[half_rows:])
        return jnp.where(half == 0, jnp.stack([mine, sent]), jnp.stack([sent, mine]))

    return (
        back_home(output),
        back_home(tokens_grad),
        own_joined[:, :GC],
        own_joined[:, GC : 2 * GC],
        own_joined[:, 2 * GC :],
        own_out,
        own_up,
        own_down,
        *own_vectors,
        rms_values,
    )


def solution(mesh):
    rows = P(None, BOTH, None)
    split, rows_split = P("dp", "mp"), P(("mp", "dp"), None)
    return jax.shard_map(
        body,
        mesh=mesh,
        in_specs=(
            rows,
            rows,
            P(None, "dp"),
            split,
            split,
            split,
            rows_split,
            split,
            rows_split,
            P("mp"),
            P("mp"),
            P("mp"),
            *([P()] * 6),
        ),
        out_specs=(
            rows,
            rows,
            split,
            split,
            split,
            rows_split,
            split,
            rows_split,
            *([P(("mp", "dp"))] * 3),
            *([P(BOTH)] * 6),
            P(),
        ),
        check_vma=False,
    )
```

```python
import functools

import jax
import jax.numpy as jnp
from jax import lax
from jax.experimental import pallas as pl
from jax.experimental.pallas import tpu as pltpu
from jax.sharding import PartitionSpec as P

HD = 64
L = 1024
SEQ_MB = 2
MB = 2
GROUPS = 4
GH = 3
GC = GH * HD
PAD = 256

epsilon = 1e-05
masked_score = -1e30
exp2_scale = HD ** (-0.5) * 1.4426950408889634
score_scale = HD ** (-0.5)
BOTH = ("dp", "mp")
NT = (((1,), (1,)), ((), ()))


def product(left_side, right_side):
    return jnp.dot(left_side, right_side, preferred_element_type=jnp.float32)


def contract_rows(left_side, right_side):
    return lax.dot_general(
        left_side, right_side, (((0,), (0,)), ((), ())), preferred_element_type=jnp.float32
    )


def contract_cols(left_side, right_side):
    return lax.dot_general(left_side, right_side, NT, preferred_element_type=jnp.float32)


def layer_norm(values, norm_gain, norm_shift):
    center = values - jnp.mean(values, axis=-1, keepdims=True)
    spread = jnp.mean(center * center, axis=-1, keepdims=True)
    inverse = lax.rsqrt(spread + epsilon)
    scaled = center * inverse
    return (scaled * norm_gain + norm_shift, scaled, inverse)


def norm_back(upstream, scaled, inverse, norm_gain):
    gain_grad = jnp.sum(upstream * scaled, axis=0)
    shift_grad = jnp.sum(upstream, axis=0)
    through = upstream * norm_gain
    result = inverse * (
        through
        - jnp.mean(through, axis=-1, keepdims=True)
        - scaled * jnp.mean(through * scaled, axis=-1, keepdims=True)
    )
    return (result, gain_grad, shift_grad)


def head_keys(keys, bias, h, lane):
    kept = jnp.where((lane >= h * HD) & (lane < (h + 1) * HD), keys, jnp.zeros_like(keys))
    return jnp.where(lane == GC, bias, kept)


def attend_forward_kernel(bias_ref, qkv_ref, out_ref, lse_ref, turned):
    rows = qkv_ref.shape[1]
    chunk = 256
    lane = lax.broadcasted_iota(jnp.int32, (1, PAD), 1)
    keys = qkv_ref[0, :, PAD : 2 * PAD]
    values_t = qkv_ref[0, :, 2 * PAD :].T
    bias = bias_ref[...]
    for h in range(GH):
        own = head_keys(keys, bias, h, lane)
        own_values = values_t[h * HD : (h + 1) * HD, :]
        for at in range(0, rows, chunk):
            queries = qkv_ref[0, at : at + chunk, :PAD]
            scores = contract_cols(own, queries)
            top = jnp.max(scores, axis=0, keepdims=True) * exp2_scale
            raised = jnp.exp2(scores * exp2_scale - top)
            total = jnp.sum(raised, axis=0, keepdims=True)
            mixed = product(own_values, raised.astype(jnp.bfloat16))
            turned[h * HD : (h + 1) * HD, at : at + chunk] = mixed / total
            lse_ref[0, h : h + 1, at : at + chunk] = top + jnp.log2(total)
    turned[GC:, :] = jnp.zeros((PAD - GC, rows), jnp.float32)
    out_ref[0] = turned[...].T.astype(jnp.bfloat16)


def attend_forward(qkv, bias):
    rows = qkv.shape[1]
    return pl.pallas_call(
        attend_forward_kernel,
        grid=(GROUPS,),
        in_specs=[
            pl.BlockSpec((rows, 1), lambda g: (0, 0)),
            pl.BlockSpec((1, rows, 3 * PAD), lambda g: (g, 0, 0)),
        ],
        out_specs=[
            pl.BlockSpec((1, rows, PAD), lambda g: (g, 0, 0)),
            pl.BlockSpec((1, 8, rows), lambda g: (g, 0, 0)),
        ],
        out_shape=[
            jax.ShapeDtypeStruct((GROUPS, rows, PAD), jnp.bfloat16),
            jax.ShapeDtypeStruct((GROUPS, 8, rows), jnp.float32),
        ],
        scratch_shapes=[pltpu.VMEM((PAD, rows), jnp.float32)],
        cost_estimate=pl.CostEstimate(
            flops=45_000_000_000 // 3, bytes_accessed=10_000_000, transcendentals=12_000_000
        ),
    )(bias, qkv)


def attend_backward_kernel(
    bias_ref, qkv_ref, out_ref, lse_ref, grad_ref, joined_ref, sums_ref, probs, slopes, turned
):
    rows = qkv_ref.shape[1]
    chunk = 256
    lane = lax.broadcasted_iota(jnp.int32, (1, PAD), 1)
    keys = qkv_ref[0, :, PAD : 2 * PAD]
    keys_t = keys.T
    values = qkv_ref[0, :, 2 * PAD :]
    bias = bias_ref[...]
    crossed = (grad_ref[0].astype(jnp.float32) * out_ref[0].astype(jnp.float32)).T
    key_grad = jnp.zeros((rows, PAD), jnp.float32)
    value_grad = jnp.zeros((rows, PAD), jnp.float32)
    for h in range(GH):
        head = (lane >= h * HD) & (lane < (h + 1) * HD)
        own = head_keys(keys, bias, h, lane)
        own_values = jnp.where(head, values, jnp.zeros_like(values))
        delta = jnp.sum(crossed[h * HD : (h + 1) * HD, :], axis=0, keepdims=True)
        for at in range(0, rows, chunk):
            queries = qkv_ref[0, at : at + chunk, :PAD]
            grads = grad_ref[0, at : at + chunk, :]
            scores = contract_cols(own, queries)
            attn_probs = jnp.exp2(scores * exp2_scale - lse_ref[0, h : h + 1, at : at + chunk])
            prob_grad = contract_cols(own_values, grads)
            probs[:, at : at + chunk] = attn_probs.astype(jnp.bfloat16)
            slopes[:, at : at + chunk] = (
                attn_probs * (prob_grad - delta[:, at : at + chunk])
            ).astype(jnp.bfloat16)
        own_grads = jnp.where(head, grad_ref[0], jnp.zeros((), jnp.bfloat16))
        own_queries = jnp.where(head, qkv_ref[0, :, :PAD], jnp.zeros((), jnp.bfloat16))
        value_grad = value_grad + product(probs[...], own_grads)
        key_grad = key_grad + product(slopes[...], own_queries)
        turned[h * HD : (h + 1) * HD, :] = product(
            keys_t[h * HD : (h + 1) * HD, :], slopes[...]
        )
    turned[GC:, :] = jnp.zeros((PAD - GC, rows), jnp.float32)
    query_grad = turned[...].T * score_scale
    joined_ref[0, :, :PAD] = query_grad.astype(jnp.bfloat16)
    joined_ref[0, :, PAD : 2 * PAD] = (key_grad * score_scale).astype(jnp.bfloat16)
    joined_ref[0, :, 2 * PAD :] = value_grad.astype(jnp.bfloat16)
    sums_ref[0, 0:1, :] = jnp.sum(query_grad, axis=0, keepdims=True)
    sums_ref[0, 1:2, :] = jnp.sum(value_grad, axis=0, keepdims=True)


def attend_backward(qkv, bias, heads_out, lse, heads_grad):
    rows = qkv.shape[1]
    return pl.pallas_call(
        attend_backward_kernel,
        grid=(GROUPS,),
        in_specs=[
            pl.BlockSpec((rows, 1), lambda g: (0, 0)),
            pl.BlockSpec((1, rows, 3 * PAD), lambda g: (g, 0, 0)),
            pl.BlockSpec((1, rows, PAD), lambda g: (g, 0, 0)),
            pl.BlockSpec((1, 8, rows), lambda g: (g, 0, 0)),
            pl.BlockSpec((1, rows, PAD), lambda g: (g, 0, 0)),
        ],
        out_specs=[
            pl.BlockSpec((1, rows, 3 * PAD), lambda g: (g, 0, 0)),
            pl.BlockSpec((1, 8, PAD), lambda g: (g, 0, 0)),
        ],
        out_shape=[
            jax.ShapeDtypeStruct((GROUPS, rows, 3 * PAD), jnp.bfloat16),
            jax.ShapeDtypeStruct((GROUPS, 8, PAD), jnp.float32),
        ],
        scratch_shapes=[
            pltpu.VMEM((rows, rows), jnp.bfloat16),
            pltpu.VMEM((rows, rows), jnp.bfloat16),
            pltpu.VMEM((PAD, rows), jnp.float32),
        ],
        cost_estimate=pl.CostEstimate(
            flops=30_000_000_000, bytes_accessed=20_000_000, transcendentals=12_000_000
        ),
    )(bias, qkv, heads_out, lse, heads_grad)


def swap_with_partner(values):
    size = lax.axis_size("mp")
    return lax.ppermute(values, "mp", [(i, i ^ 1) for i in range(size)])


def pad_heads(values):
    return jnp.pad(values, [(0, 0)] * (values.ndim - 1) + [(0, PAD - values.shape[-1])])


MESH = pl.DeviceIdType.MESH


def positions():
    mp, dp = lax.axis_index("mp"), lax.axis_index("dp")
    return mp, lax.div(mp, 2), lax.rem(mp, 2), lax.div(dp, 2), lax.rem(dp, 2)


def at_place(x, c, z, y):
    return (2 * z + y, 2 * x + c)


def neighbours(nz):
    mp, x, c, z, y = positions()
    first = at_place(lax.rem(x + c, 2), c, z, lax.rem(y + 1 - c, 2))
    second = at_place(lax.rem(x + 1 - c, 2), c, z, lax.rem(y + c, 2))
    partner = at_place(x, 1 - c, z, y)
    along = [at_place(x, c, lax.rem(z + d, nz), y) for d in range(1, nz)]
    return first, second, partner, along


def meet(devices):
    barrier = pltpu.get_barrier_semaphore()
    for device in devices:
        pl.semaphore_signal(barrier, inc=1, device_id=device, device_id_type=MESH)
    pl.semaphore_wait(barrier, len(devices))


def regions(x, c, y):
    own = (x, y)
    first = (lax.rem(x + c, 2), lax.rem(y + 1 - c, 2))
    second = (lax.rem(x + 1 - c, 2), lax.rem(y + c, 2))
    third = (1 - x, 1 - y)
    return own, first, second, third


def gather_kernel(nz, parts, *refs):
    shards, fulls = refs[:parts], refs[parts : 2 * parts]
    own_sem, z_send, z_recv, send, recv = refs[2 * parts :]
    mp, x, c, z, y = positions()
    first, second, partner, along = neighbours(nz)
    meet([first, second, partner, *along])
    own, got1, got2, got3 = regions(x, c, y)
    other = regions(x, 1 - c, y)

    def remote(src, dst, s, r, device):
        return pltpu.make_async_remote_copy(
            src_ref=src, dst_ref=dst, send_sem=s, recv_sem=r, device_id=device, device_id_type=MESH
        )

    started = []
    locals_ = []
    spread = []
    for p in range(parts):
        keep = pltpu.make_async_copy(shards[p], fulls[p].at[x, c, z, y], own_sem.at[p])
        keep.start()
        locals_.append(keep)
        sends = [
            remote(shards[p], fulls[p].at[x, c, z, y], z_send.at[p, d], z_recv.at[p, d], along[d])
            for d in range(nz - 1)
        ]
        for copy in sends:
            copy.start()
        spread.append(sends)

    def block(p, core, place):
        return fulls[p].at[place[0], core, :, place[1]]

    def push(p, k, core, place, device):
        copy = remote(block(p, core, place), block(p, core, place), send.at[p, k], recv.at[p, k], device)
        copy.start()
        started.append(copy)
        return copy

    def arrived(p, k, core, place):
        here = block(p, core, place)
        remote(here, here, send.at[p, k], recv.at[p, k], first).wait_recv()

    for p in range(parts):
        locals_[p].wait()
        for copy in spread[p]:
            copy.wait_recv()
        push(p, 0, c, own, first)
        push(p, 1, c, own, second)
        push(p, 3, c, own, partner)
    for p in range(parts):
        arrived(p, 0, c, got1)
        push(p, 2, c, got1, second)
        push(p, 4, c, got1, partner)
    for p in range(parts):
        arrived(p, 1, c, got2)
        push(p, 5, c, got2, partner)
        arrived(p, 2, c, got3)
        push(p, 6, c, got3, partner)
    for p in range(parts):
        for k in range(4):
            arrived(p, 3 + k, 1 - c, other[k])
    for sends in spread:
        for copy in sends:
            copy.wait_send()
    for copy in started:
        copy.wait_send()


def gather_all(shards):
    n_dp = lax.axis_size("dp")
    nz, parts = n_dp // 2, len(shards)
    return pl.pallas_call(
        functools.partial(gather_kernel, nz, parts),
        in_specs=[pl.BlockSpec(memory_space=pltpu.VMEM)] * parts,
        out_specs=[pl.BlockSpec(memory_space=pl.ANY)] * parts,
        out_shape=[jax.ShapeDtypeStruct((2, 2, nz, 2, *s.shape), s.dtype) for s in shards],
        scratch_shapes=[
            pltpu.SemaphoreType.DMA((parts,)),
            pltpu.SemaphoreType.DMA((parts, nz - 1)),
            pltpu.SemaphoreType.DMA((parts, nz - 1)),
            pltpu.SemaphoreType.DMA((parts, 7)),
            pltpu.SemaphoreType.DMA((parts, 7)),
        ],
        compiler_params=pltpu.CompilerParams(collective_id=0, has_side_effects=True),
    )(*shards)


def scatter_kernel(nz, parts, *refs):
    partials, results = refs[:parts], refs[parts : 2 * parts]
    at = 2 * parts
    sums, heard1, heard2, heard3, heard4 = (
        refs[at + i * parts : at + (i + 1) * parts] for i in range(5)
    )
    own_sem, send, recv, z_send, z_recv = refs[at + 5 * parts :]
    mp, x, c, z, y = positions()
    first, second, partner, along = neighbours(nz)
    meet([first, second, partner, *along])
    own, got1, got2, got3 = regions(x, c, y)
    started = []

    def remote(src, dst, s, r, device):
        copy = pltpu.make_async_remote_copy(
            src_ref=src, dst_ref=dst, send_sem=s, recv_sem=r, device_id=device, device_id_type=MESH
        )
        copy.start()
        started.append(copy)
        return copy

    def add(p, place, more):
        for i in range(nz):
            here = sums[p].at[place[0], i, place[1]]
            here[...] = (here[...].astype(jnp.float32) + more[i].astype(jnp.float32)).astype(here.dtype)

    kept, core_copies = [], []
    for p in range(parts):
        copies = []
        for k in range(2):
            keep = pltpu.make_async_copy(partials[p].at[k, c], sums[p].at[k], own_sem.at[p, k])
            keep.start()
            copies.append(keep)
        kept.append(copies)
        core_copies.append(
            [
                remote(partials[p].at[k, 1 - c], heard1[p].at[k], send.at[p, k], recv.at[p, k], partner)
                for k in range(2)
            ]
        )
    second_copies = []
    for p in range(parts):
        for copy in kept[p]:
            copy.wait()
        for copy in core_copies[p]:
            copy.wait_recv()
        copies = []
        for k, place in enumerate((got2, got3)):
            add(p, place, heard1[p].at[place[0], :, place[1]])
            copies.append(
                remote(
                    sums[p].at[place[0], :, place[1]],
                    heard2[p].at[k],
                    send.at[p, 2 + k],
                    recv.at[p, 2 + k],
                    second,
                )
            )
        second_copies.append(copies)
        for place in (got1, own):
            add(p, place, heard1[p].at[place[0], :, place[1]])
    first_copies = []
    for p in range(parts):
        second_copies[p][1].wait_recv()
        add(p, got1, heard2[p].at[1])
        first_copies.append(
            remote(sums[p].at[got1[0], :, got1[1]], heard3[p], send.at[p, 4], recv.at[p, 4], first)
        )
        second_copies[p][0].wait_recv()
        add(p, own, heard2[p].at[0])
    last_copies = []
    for p in range(parts):
        first_copies[p].wait_recv()
        add(p, own, heard3[p])
        last_copies.append(
            [
                remote(
                    sums[p].at[x, lax.rem(z + d + 1, nz), y],
                    heard4[p].at[d],
                    z_send.at[p, d],
                    z_recv.at[p, d],
                    along[d],
                )
                for d in range(nz - 1)
            ]
        )
    for p in range(parts):
        for copy in last_copies[p]:
            copy.wait_recv()
        total = sums[p][x, z, y].astype(jnp.float32)
        for d in range(nz - 1):
            total = total + heard4[p][d].astype(jnp.float32)
        results[p][...] = total
    for copy in started:
        copy.wait_send()


def scatter_sums(partials):
    nz, parts = lax.axis_size("dp") // 2, len(partials)
    tails = [p.shape[4:] for p in partials]
    kinds = [p.dtype for p in partials]
    return pl.pallas_call(
        functools.partial(scatter_kernel, nz, parts),
        in_specs=[pl.BlockSpec(memory_space=pl.ANY)] * parts,
        out_specs=[pl.BlockSpec(memory_space=pltpu.VMEM)] * parts,
        out_shape=[jax.ShapeDtypeStruct(t, jnp.float32) for t in tails],
        scratch_shapes=[
            *[pltpu.VMEM((2, nz, 2, *t), k) for t, k in zip(tails, kinds)],
            *[pltpu.VMEM((2, nz, 2, *t), k) for t, k in zip(tails, kinds)],
            *[pltpu.VMEM((2, nz, *t), k) for t, k in zip(tails, kinds)],
            *[pltpu.VMEM((nz, *t), k) for t, k in zip(tails, kinds)],
            *[pltpu.VMEM((nz - 1, *t), k) for t, k in zip(tails, kinds)],
            pltpu.SemaphoreType.DMA((parts, 2)),
            pltpu.SemaphoreType.DMA((parts, 5)),
            pltpu.SemaphoreType.DMA((parts, 5)),
            pltpu.SemaphoreType.DMA((parts, nz - 1)),
            pltpu.SemaphoreType.DMA((parts, nz - 1)),
        ],
        compiler_params=pltpu.CompilerParams(
            collective_id=1, has_side_effects=True, vmem_limit_bytes=60 * 1024 * 1024
        ),
    )(*partials)


def in_place_order(blocks):
    return blocks.reshape(2, 2, blocks.shape[1] // 2, 2, *blocks.shape[2:])


def body_any(
    tokens,
    cotangent,
    lengths,
    w_query,
    w_key,
    w_value,
    w_out,
    w_up,
    w_down,
    b_query,
    b_value,
    b_up,
    b_out,
    b_down,
    norm1_gain,
    norm1_shift,
    norm2_gain,
    norm2_shift,
):
    half_rows = tokens.shape[1]
    width = tokens.shape[2]
    n_dp, n_mp = lax.axis_size("dp"), lax.axis_size("mp")
    unit_cols = w_up.shape[1]
    mp_index = lax.axis_index("mp")
    half = lax.rem(mp_index, 2)
    seq = lax.div(mp_index, 2)

    def own_of(pair):
        return jnp.where(half == 0, pair[0], pair[1])

    def other_of(pair):
        return jnp.where(half == 0, pair[1], pair[0])

    rows_in = jnp.concatenate([own_of(tokens), swap_with_partner(other_of(tokens))], axis=0)
    rows_cot = jnp.concatenate([own_of(cotangent), swap_with_partner(other_of(cotangent))], axis=0)
    length = lax.dynamic_slice(lengths, (half, seq), (1, 1))[0, 0]
    place = jnp.arange(half_rows, dtype=jnp.int32)
    place = jnp.concatenate([place + half * half_rows, place + (1 - half) * half_rows])
    valid_row = (place < length)[:, None]
    bias = jnp.where(valid_row, 0.0, masked_score).astype(jnp.bfloat16)
    valid_row = valid_row.astype(jnp.float32)

    biases = jnp.pad(jnp.concatenate([b_query, b_value, b_up]), (0, 896)).reshape(16, 128)
    qkv_shard = jnp.concatenate([w_query, w_key, w_value], axis=1)
    gathered = gather_all([qkv_shard, w_out, w_up, w_down, biases])
    full_qkv, full_out, full_up, full_down, full_bias = (
        g.reshape(n_mp, n_dp, *g.shape[4:]) for g in gathered
    )
    full_qkv = full_qkv.reshape(n_mp, width, 3, GC)
    w_joined = pad_heads(full_qkv).reshape(n_mp, width, 3 * PAD)
    full_out = full_out.reshape(n_mp, GC, width)
    out_pad = jnp.pad(full_out, ((0, 0), (0, PAD - GC), (0, 0))).reshape(n_mp * PAD, width)
    full_up = full_up.reshape(n_mp, width, unit_cols).transpose(1, 0, 2).reshape(width, n_mp * unit_cols)
    full_down = full_down.reshape(n_mp * unit_cols, width)
    full_bias = full_bias[:, 0].reshape(n_mp, -1)
    bias_q, bias_v, bias_up = full_bias[:, :GC], full_bias[:, GC:2*GC], full_bias[:, 2*GC:2*GC+unit_cols]
    mark = jnp.zeros((n_mp, PAD - GC), jnp.float32).at[:, 0].set(1.0)
    joined_bias = jnp.concatenate(
        [bias_q, mark, jnp.zeros((n_mp, PAD), jnp.float32), pad_heads(bias_v)], axis=1
    )

    qkv = lax.dot_general(
        jnp.broadcast_to(rows_in[None], (n_mp, *rows_in.shape)),
        w_joined,
        (((2,), (1,)), ((0,), (0,))),
        preferred_element_type=jnp.float32,
    )
    qkv = (qkv + joined_bias[:, None, :]).astype(jnp.bfloat16)
    heads_out, lse = attend_forward(qkv, bias)
    heads_flat = heads_out.transpose(1, 0, 2).reshape(2 * half_rows, n_mp * PAD)
    attention = product(heads_flat, out_pad) + b_out
    first_norm, first_scaled, first_inverse = layer_norm(
        rows_in.astype(jnp.float32) + attention, norm1_gain, norm1_shift
    )
    first_low = first_norm.astype(jnp.bfloat16)
    preact = product(first_low, full_up) + bias_up.reshape(-1)
    cumulative = 0.5 * (1.0 + lax.erf(preact * 0.7071067811865476))
    active = (preact * cumulative).astype(jnp.bfloat16)
    slope = cumulative + preact * (jnp.exp(-0.5 * preact * preact) * 0.3989422804014327)
    ffn_out = product(active, full_down) + b_down
    stream = first_norm + ffn_out
    final_norm, final_scaled, final_inverse = layer_norm(stream, norm2_gain, norm2_shift)
    output = final_norm.astype(jnp.bfloat16)
    squares = jnp.stack(
        [
            jnp.sum(valid_row * stream * stream),
            jnp.sum(valid_row * attention * attention),
            jnp.sum(valid_row * ffn_out * ffn_out),
            jnp.sum(valid_row),
        ]
    )

    stream_grad, gain2_grad, shift2_grad = norm_back(
        rows_cot.astype(jnp.float32), final_scaled, final_inverse, norm2_gain
    )
    down_bias_grad = jnp.sum(stream_grad, axis=0)
    ffn_grad_low = stream_grad.astype(jnp.bfloat16)
    active_grad = contract_cols(ffn_grad_low, full_down)
    down_wgrad = contract_rows(active, ffn_grad_low)
    preact_grad = active_grad * slope
    up_bias_grad = jnp.sum(preact_grad, axis=0)
    preact_low = preact_grad.astype(jnp.bfloat16)
    up_wgrad = contract_rows(first_low, preact_low)
    first_grad = stream_grad + contract_cols(preact_low, full_up)
    attn_grad, gain1_grad, shift1_grad = norm_back(
        first_grad, first_scaled, first_inverse, norm1_gain
    )
    out_bias_grad = jnp.sum(attn_grad, axis=0)
    attn_grad_low = attn_grad.astype(jnp.bfloat16)
    out_wgrad = contract_rows(heads_flat, attn_grad_low)
    heads_grad = contract_cols(attn_grad_low, out_pad).astype(jnp.bfloat16)
    heads_grad = heads_grad.reshape(2 * half_rows, n_mp, PAD).transpose(1, 0, 2)
    joined, sums = attend_backward(qkv, bias, heads_out, lse, heads_grad)
    joined_wgrad = lax.dot_general(
        jnp.broadcast_to(rows_in[None], (n_mp, *rows_in.shape)),
        joined,
        (((1,), (1,)), ((0,), (0,))),
        preferred_element_type=jnp.float32,
    )
    tokens_grad = attn_grad + jnp.sum(
        lax.dot_general(
            joined, w_joined, (((2,), (2,)), ((0,), (0,))), preferred_element_type=jnp.float32
        ),
        axis=0,
    )

    low = jnp.bfloat16
    joined_blocks = (
        joined_wgrad.astype(low)
        .reshape(n_mp, n_dp, width // n_dp, 3, PAD)[..., :GC]
        .reshape(n_mp, n_dp, width // n_dp, 3 * GC)
    )
    out_blocks = (
        out_wgrad.astype(low)
        .reshape(n_mp, PAD, width)[:, :GC]
        .reshape(n_mp, n_dp, GC // n_dp, width)
    )
    up_blocks = up_wgrad.astype(low).reshape(n_dp, width // n_dp, n_mp, unit_cols).transpose(2, 0, 1, 3)
    down_blocks = down_wgrad.astype(low).reshape(n_mp, n_dp, unit_cols // n_dp, width)

    def by_mp(vector):
        return vector.reshape(n_mp, n_dp, -1)

    def by_dp(vector):
        return vector.reshape(n_dp, n_mp, -1).transpose(1, 0, 2)

    vectors = [by_mp(sums[:, 0, :GC]), by_mp(sums[:, 1, :GC]), by_mp(up_bias_grad)]
    vectors += [
        by_dp(v)
        for v in (out_bias_grad, down_bias_grad, gain1_grad, shift1_grad, gain2_grad, shift2_grad)
    ]
    vectors.append(jnp.broadcast_to(squares, (n_mp, n_dp, 4)))
    ends = [v.shape[-1] for v in vectors]
    vectors = jnp.concatenate(vectors, axis=-1)
    vectors = jnp.pad(vectors, ((0, 0), (0, 0), (0, 1024 - vectors.shape[-1])))
    vectors = vectors.reshape(n_mp, n_dp, 8, 128)
    own_down, own_up, own_out, own_joined, own_vector = scatter_sums(
        [
            in_place_order(b)
            for b in (down_blocks, up_blocks, out_blocks, joined_blocks, vectors)
        ]
    )
    own_vector = own_vector.reshape(-1)
    own_vectors, start = [], 0
    for size in ends:
        own_vectors.append(own_vector[start : start + size])
        start += size
    totals = own_vectors.pop()
    rms_values = jnp.sqrt(totals[:3] / (totals[3] * width))

    def back_home(rows):
        mine, sent = rows[:half_rows], swap_with_partner(rows[half_rows:])
        return jnp.where(half == 0, jnp.stack([mine, sent]), jnp.stack([sent, mine]))

    return (
        back_home(output),
        back_home(tokens_grad),
        own_joined[:, :GC],
        own_joined[:, GC : 2 * GC],
        own_joined[:, 2 * GC :],
        own_out,
        own_up,
        own_down,
        *own_vectors,
        rms_values,
    )


PARTS = 4


def remote_copy(src, dst, s, r, device):
    return pltpu.make_async_remote_copy(
        src_ref=src, dst_ref=dst, send_sem=s, recv_sem=r, device_id=device, device_id_type=MESH
    )


def forward_kernel(
    nz,
    lengths,
    tokens,
    cotangent,
    shard_q,
    shard_o,
    shard_u,
    shard_d,
    bias_shard,
    full_q,
    full_o,
    full_u,
    full_d,
    bias_full,
    rows_got,
    cot_got,
    qkv_out,
    heads_out,
    lse_out,
    rows,
    w_got,
    w_pad,
    qkv,
    values_t,
    turned,
    heads,
    own_sem,
    z_send,
    z_recv,
    relay_send,
    send,
    recv,
    swap_send,
    swap_recv,
    bias_send,
    bias_recv,
    out_sem,
):
    shards = (shard_q, shard_o, shard_u, shard_d)
    fulls = (full_q, full_o, full_u, full_d)
    half_rows = tokens.shape[1]
    length = 2 * half_rows
    mp, x, c, z, y = positions()
    half = c
    seq = x
    first, second, partner, along = neighbours(nz)
    across = at_place(1 - x, c, z, y)
    slanted = at_place(1 - x, 1 - c, z, y)
    own, got1, got2, got3 = regions(x, c, y)
    other = regions(x, 1 - c, y)
    meet([first, second, partner, slanted, *along])

    def block(p, core, place, d):
        return fulls[p].at[place[0], core, lax.rem(z + nz - d, nz), place[1]]

    places = (own, own, got1, own, got1, got2, got3)
    targets = (first, second, second, partner, partner, partner, partner)
    landing = (got1, got2, got3, *other)
    cores = (c, c, c, 1 - c, 1 - c, 1 - c, 1 - c)

    def outgoing(p, k, d):
        here = block(p, c, places[k], d)
        return remote_copy(here, here, send.at[p, k, d], recv.at[p, k, d], targets[k])

    def incoming(p, k, d):
        here = block(p, cores[k], landing[k], d)
        return remote_copy(here, here, send.at[p, k, d], recv.at[p, k, d], targets[k])

    at_low = 1 - lax.div(z + nz - 1, nz)
    near, far = 1 + 2 * at_low, 3 - 2 * at_low

    def z_copy(p, d):
        return remote_copy(
            shards[p], fulls[p].at[x, c, z, y], z_send.at[p, d - 1], z_recv.at[p, d - 1], along[d - 1]
        )

    def z_each(p, act):
        act(z_copy(p, 2))
        pl.when(z != nz - 1)(lambda: act(z_copy(p, 1)))
        pl.when(z != 0)(lambda: act(z_copy(p, 3)))

    def z_start(p):
        z_each(p, lambda copy: copy.start())

    def z_relay(p, low):
        here = block(p, c, own, 2)
        d = 1 if low else 3
        return remote_copy(here, here, relay_send.at[p], z_recv.at[p, d - 1], at_place(x, c, z + d - 2, y))

    def spread(p, d):
        if not (isinstance(d, int) and d == 0):
            here = block(p, c, own, d)
            remote_copy(here, here, z_send.at[p, d - 1], z_recv.at[p, d - 1], first).wait_recv()
        if isinstance(d, int) and d == 2:
            pl.when(z == 1)(lambda: z_relay(p, True).start())
            pl.when(z == 2)(lambda: z_relay(p, False).start())
        for k in (0, 1, 3):
            outgoing(p, k, d).start()

    def forward1(p):
        for d in range(nz):
            incoming(p, 0, d).wait_recv()
            outgoing(p, 2, d).start()
            outgoing(p, 4, d).start()

    def forward2(p):
        for d in range(nz):
            incoming(p, 1, d).wait_recv()
            outgoing(p, 5, d).start()

    def forward3(p):
        for d in range(nz):
            incoming(p, 2, d).wait_recv()
            outgoing(p, 6, d).start()

    def take(p, k):
        for d in range(nz):
            incoming(p, k, d).wait_recv()

    keep = [
        pltpu.make_async_copy(shards[p], fulls[p].at[x, c, z, y], own_sem.at[p]) for p in range(PARTS)
    ]
    keep_rows = pltpu.make_async_copy(tokens.at[half], rows.at[pl.ds(0, half_rows)], own_sem.at[PARTS])
    swap_rows = remote_copy(
        tokens.at[1 - half], rows.at[pl.ds(half_rows, half_rows)], swap_send.at[0], swap_recv.at[0], partner
    )
    swap_cot = remote_copy(cotangent.at[1 - half], cot_got, swap_send.at[1], swap_recv.at[1], partner)
    bias_copies = [
        remote_copy(bias_shard, bias_full.at[mp], bias_send.at[k], bias_recv.at[k], device)
        for k, device in enumerate((partner, across, slanted))
    ]
    z_start(0)
    keep[0].start()
    for copy in bias_copies:
        copy.start()
    swap_rows.start()
    keep_rows.start()
    for p in range(1, PARTS):
        keep[p].start()
    keep[0].wait()
    spread(0, 0)
    for p in range(1, PARTS):
        z_start(p)
    w_pad[...] = jnp.zeros_like(w_pad)
    turned[...] = jnp.zeros_like(turned)
    bias_full[mp] = bias_shard[...]
    for d in (2, near, far):
        spread(0, d)
    for copy in keep[1:]:
        copy.wait()
    forward1(0)
    for p in range(1, PARTS):
        spread(p, 0)
    forward2(0)
    swap_cot.start()
    keep_rows.wait()
    swap_rows.wait_recv()
    rows_out = pltpu.make_async_copy(rows.at[pl.ds(half_rows, half_rows)], rows_got, out_sem.at[2])
    rows_out.start()
    for copy in bias_copies:
        copy.wait_recv()

    hooks = {
        0: [lambda: [spread(1, d) for d in (2, near, far)]],
        1: [lambda: forward3(0)],
        2: [lambda: [spread(2, d) for d in (2, near)]],
        3: [lambda: spread(2, far), lambda: forward1(1)],
        4: [lambda: forward2(1), lambda: forward3(1)],
        5: [lambda: [spread(3, d) for d in (2, near)]],
        6: [lambda: spread(3, far)],
        7: [lambda: forward1(2)],
        8: [lambda: forward2(2)],
        10: [lambda: forward1(3)],
        11: [lambda: forward2(3)],
    }
    seq_length = lengths[half, seq]
    row = lax.broadcasted_iota(jnp.int32, (length, 1), 0)
    place = jnp.where(row < half_rows, row + half * half_rows, row - half * half_rows)
    bias = jnp.where(place < seq_length, 0.0, masked_score).astype(jnp.bfloat16)
    lane = lax.broadcasted_iota(jnp.int32, (1, PAD), 1)
    chunk = 256

    def heads_copy(gx, gc):
        return pltpu.make_async_copy(heads, heads_out.at[2 * gx + gc], out_sem.at[0])

    def qkv_copy(gx, gc):
        return pltpu.make_async_copy(qkv, qkv_out.at[2 * gx + gc], out_sem.at[1])

    def group_step(r, carry):
        gx, gc = lax.rem(x + lax.div(r, 2), 2), lax.rem(c + lax.rem(r, 2), 2)
        group = 2 * gx + gc

        @pl.when(r == 1)
        def _():
            for d in range(nz):
                incoming(0, 3, d).wait_recv()
            for d in range(nz):
                here = block(0, 1 - c, own, d)
                remote_copy(here, here, send.at[0, 5 - c, d], recv.at[0, 5 - c, d], first).wait_recv()

        @pl.when(r == 3)
        def _():
            for d in range(nz):
                here = block(0, 1 - c, own, d)
                remote_copy(here, here, send.at[0, 4 + c, d], recv.at[0, 4 + c, d], first).wait_recv()
            take(0, 6)

        load = pltpu.make_async_copy(full_q.at[gx, gc], w_got, own_sem.at[PARTS + 1])
        load.start()
        load.wait()

        @pl.when(r > 0)
        def _():
            qkv_copy(gx, gc).wait()

        w_flat = w_got[...].reshape(-1, 3 * GC)
        for k in range(3):
            w_pad[:, k * PAD : k * PAD + GC] = w_flat[:, k * GC : (k + 1) * GC]
        joined_bias = bias_full[group, 0:1, :]
        for at in range(0, length, 512):
            qkv[at : at + 512, :] = (product(rows[at : at + 512, :], w_pad[...]) + joined_bias).astype(
                jnp.bfloat16
            )
        qkv_copy(gx, gc).start()
        values_t[...] = qkv[:, 2 * PAD :].T

        def head_step(h, carry):
            for k, todo in hooks.items():
                if todo:

                    @pl.when(r * GH + h == k)
                    def _():
                        for task in todo:
                            task()

            start = h * HD
            keys = qkv[:, PAD : 2 * PAD]
            kept = jnp.where((lane >= start) & (lane < start + HD), keys, jnp.zeros_like(keys))
            own_keys = jnp.where(lane == GC, bias, kept)
            own_values = values_t[pl.ds(pl.multiple_of(start, HD), HD), :]
            for at in range(0, length, chunk):
                scores = contract_cols(own_keys, qkv[at : at + chunk, :PAD])
                top = jnp.max(scores, axis=0, keepdims=True) * exp2_scale
                raised = jnp.exp2(scores * exp2_scale - top)
                total = jnp.sum(raised, axis=0, keepdims=True)
                mixed = product(own_values, raised.astype(jnp.bfloat16))
                turned[pl.ds(pl.multiple_of(start, HD), HD), at : at + chunk] = mixed / total
                lse_out[group, pl.ds(h, 1), at : at + chunk] = top + jnp.log2(total)
            return carry

        lax.fori_loop(0, GH, head_step, 0)

        @pl.when(r > 0)
        def _():
            heads_copy(gx, gc).wait()

        heads[...] = turned[...].T.astype(jnp.bfloat16)
        heads_copy(gx, gc).start()
        return carry

    lax.fori_loop(0, GROUPS, group_step, 0)
    forward3(2)
    forward3(3)
    for p in range(1, PARTS):
        for k in range(3, 7):
            take(p, k)
    heads_copy(x, c).wait()
    qkv_copy(x, c).wait()
    rows_out.wait()
    swap_cot.wait_recv()
    swap_cot.wait_send()
    swap_rows.wait_send()
    for copy in bias_copies:
        copy.wait_send()
    for p in range(PARTS):
        z_each(p, lambda copy: copy.wait_send())
        pl.when(z == 1)(lambda: z_relay(p, True).wait_send())
        pl.when(z == 2)(lambda: z_relay(p, False).wait_send())
        for k in range(7):
            for d in range(nz):
                outgoing(p, k, d).wait_send()


def forward_attention(lengths, tokens, cotangent, shards, bias_shard):
    nz = lax.axis_size("dp") // 2
    half_rows, width = tokens.shape[1:]
    rows = 2 * half_rows
    low = jnp.bfloat16
    anywhere, vmem = pl.BlockSpec(memory_space=pl.ANY), pl.BlockSpec(memory_space=pltpu.VMEM)
    dma = pltpu.SemaphoreType.DMA
    return pl.pallas_call(
        functools.partial(forward_kernel, nz),
        in_specs=[pl.BlockSpec(memory_space=pltpu.SMEM), anywhere, anywhere, *[vmem] * 5],
        out_specs=[*[anywhere] * PARTS, vmem, *[anywhere] * 4, vmem],
        out_shape=[
            *[jax.ShapeDtypeStruct((2, 2, nz, 2, *s.shape), s.dtype) for s in shards],
            jax.ShapeDtypeStruct((GROUPS, *bias_shard.shape), jnp.float32),
            jax.ShapeDtypeStruct((half_rows, width), low),
            jax.ShapeDtypeStruct((half_rows, width), low),
            jax.ShapeDtypeStruct((GROUPS, rows, 3 * PAD), low),
            jax.ShapeDtypeStruct((GROUPS, rows, PAD), low),
            jax.ShapeDtypeStruct((GROUPS, 8, rows), jnp.float32),
        ],
        scratch_shapes=[
            pltpu.VMEM((rows, width), low),
            pltpu.VMEM((nz, 2, *shards[0].shape), low),
            pltpu.VMEM((width, 3 * PAD), low),
            pltpu.VMEM((rows, 3 * PAD), low),
            pltpu.VMEM((PAD, rows), low),
            pltpu.VMEM((PAD, rows), jnp.float32),
            pltpu.VMEM((rows, PAD), low),
            dma((PARTS + 2,)),
            dma((PARTS, nz - 1)),
            dma((PARTS, nz - 1)),
            dma((PARTS,)),
            dma((PARTS, 7, nz)),
            dma((PARTS, 7, nz)),
            dma((2,)),
            dma((2,)),
            dma((3,)),
            dma((3,)),
            dma((3,)),
        ],
        compiler_params=pltpu.CompilerParams(
            collective_id=2, has_side_effects=True, vmem_limit_bytes=60 * 1024 * 1024
        ),
    )(lengths, tokens, cotangent, *shards, bias_shard)


def body_fused(
    tokens,
    cotangent,
    lengths,
    w_query,
    w_key,
    w_value,
    w_out,
    w_up,
    w_down,
    b_query,
    b_value,
    b_up,
    b_out,
    b_down,
    norm1_gain,
    norm1_shift,
    norm2_gain,
    norm2_shift,
):
    half_rows = tokens.shape[1]
    width = tokens.shape[2]
    n_dp, n_mp = lax.axis_size("dp"), lax.axis_size("mp")
    unit_cols = w_up.shape[1]
    mp_index = lax.axis_index("mp")
    half = lax.rem(mp_index, 2)
    seq = lax.div(mp_index, 2)

    def own_of(pair):
        return jnp.where(half == 0, pair[0], pair[1])

    def other_of(pair):
        return jnp.where(half == 0, pair[1], pair[0])

    length = lax.dynamic_slice(lengths, (half, seq), (1, 1))[0, 0]
    place = jnp.arange(half_rows, dtype=jnp.int32)
    place = jnp.concatenate([place + half * half_rows, place + (1 - half) * half_rows])
    valid_row = (place < length)[:, None]
    bias = jnp.where(valid_row, 0.0, masked_score).astype(jnp.bfloat16)
    valid_row = valid_row.astype(jnp.float32)

    mark = jnp.zeros((PAD - GC,), jnp.float32).at[0].set(1.0)
    bias_rows = jnp.concatenate(
        [b_query, mark, jnp.zeros((PAD,), jnp.float32), b_value, jnp.zeros((PAD - GC,), jnp.float32), b_up]
    ).reshape(2, width)
    bias_rows = jnp.pad(bias_rows, ((0, 6), (0, 0)))
    qkv_shard = jnp.concatenate([w_query, w_key, w_value], axis=1)
    gathered = forward_attention(
        lengths, tokens, cotangent, (qkv_shard, w_out, w_up, w_down), bias_rows
    )
    full_qkv, full_out, full_up, full_down = (
        g.reshape(n_mp, n_dp * g.shape[4], g.shape[5]) for g in gathered[:4]
    )
    full_bias, rows_got, cot_got, qkv, heads_out, lse = gathered[4:]
    rows_in = jnp.concatenate([own_of(tokens), rows_got], axis=0)
    rows_cot = jnp.concatenate([own_of(cotangent), cot_got], axis=0)
    w_joined = pad_heads(full_qkv.reshape(n_mp, width, 3, GC)).reshape(n_mp, width, 3 * PAD)
    out_pad = jnp.pad(full_out, ((0, 0), (0, PAD - GC), (0, 0))).reshape(n_mp * PAD, width)
    full_up = full_up.transpose(1, 0, 2).reshape(width, n_mp * unit_cols)
    full_down = full_down.reshape(n_mp * unit_cols, width)
    bias_up = full_bias[:, 1]
    heads_flat = heads_out.transpose(1, 0, 2).reshape(2 * half_rows, n_mp * PAD)
    attention = product(heads_flat, out_pad) + b_out
    first_norm, first_scaled, first_inverse = layer_norm(
        rows_in.astype(jnp.float32) + attention, norm1_gain, norm1_shift
    )
    first_low = first_norm.astype(jnp.bfloat16)
    preact = product(first_low, full_up) + bias_up.reshape(-1)
    cumulative = 0.5 * (1.0 + lax.erf(preact * 0.7071067811865476))
    active = (preact * cumulative).astype(jnp.bfloat16)
    slope = cumulative + preact * (jnp.exp(-0.5 * preact * preact) * 0.3989422804014327)
    ffn_out = product(active, full_down) + b_down
    stream = first_norm + ffn_out
    final_norm, final_scaled, final_inverse = layer_norm(stream, norm2_gain, norm2_shift)
    output = final_norm.astype(jnp.bfloat16)
    squares = jnp.stack(
        [
            jnp.sum(valid_row * stream * stream),
            jnp.sum(valid_row * attention * attention),
            jnp.sum(valid_row * ffn_out * ffn_out),
            jnp.sum(valid_row),
        ]
    )

    stream_grad, gain2_grad, shift2_grad = norm_back(
        rows_cot.astype(jnp.float32), final_scaled, final_inverse, norm2_gain
    )
    down_bias_grad = jnp.sum(stream_grad, axis=0)
    ffn_grad_low = stream_grad.astype(jnp.bfloat16)
    active_grad = contract_cols(ffn_grad_low, full_down)
    down_wgrad = contract_rows(active, ffn_grad_low)
    preact_grad = active_grad * slope
    up_bias_grad = jnp.sum(preact_grad, axis=0)
    preact_low = preact_grad.astype(jnp.bfloat16)
    up_wgrad = contract_rows(first_low, preact_low)
    first_grad = stream_grad + contract_cols(preact_low, full_up)
    attn_grad, gain1_grad, shift1_grad = norm_back(
        first_grad, first_scaled, first_inverse, norm1_gain
    )
    out_bias_grad = jnp.sum(attn_grad, axis=0)
    attn_grad_low = attn_grad.astype(jnp.bfloat16)
    out_wgrad = contract_rows(heads_flat, attn_grad_low)
    heads_grad = contract_cols(attn_grad_low, out_pad).astype(jnp.bfloat16)
    heads_grad = heads_grad.reshape(2 * half_rows, n_mp, PAD).transpose(1, 0, 2)
    joined, sums = attend_backward(qkv, bias, heads_out, lse, heads_grad)
    joined_wgrad = lax.dot_general(
        jnp.broadcast_to(rows_in[None], (n_mp, *rows_in.shape)),
        joined,
        (((1,), (1,)), ((0,), (0,))),
        preferred_element_type=jnp.float32,
    )
    tokens_grad = attn_grad + jnp.sum(
        lax.dot_general(
            joined, w_joined, (((2,), (2,)), ((0,), (0,))), preferred_element_type=jnp.float32
        ),
        axis=0,
    )

    low = jnp.bfloat16
    joined_blocks = (
        joined_wgrad.astype(low)
        .reshape(n_mp, n_dp, width // n_dp, 3, PAD)[..., :GC]
        .reshape(n_mp, n_dp, width // n_dp, 3 * GC)
    )
    out_blocks = (
        out_wgrad.astype(low)
        .reshape(n_mp, PAD, width)[:, :GC]
        .reshape(n_mp, n_dp, GC // n_dp, width)
    )
    up_blocks = up_wgrad.astype(low).reshape(n_dp, width // n_dp, n_mp, unit_cols).transpose(2, 0, 1, 3)
    down_blocks = down_wgrad.astype(low).reshape(n_mp, n_dp, unit_cols // n_dp, width)

    def by_mp(vector):
        return vector.reshape(n_mp, n_dp, -1)

    def by_dp(vector):
        return vector.reshape(n_dp, n_mp, -1).transpose(1, 0, 2)

    vectors = [by_mp(sums[:, 0, :GC]), by_mp(sums[:, 1, :GC]), by_mp(up_bias_grad)]
    vectors += [
        by_dp(v)
        for v in (out_bias_grad, down_bias_grad, gain1_grad, shift1_grad, gain2_grad, shift2_grad)
    ]
    vectors.append(jnp.broadcast_to(squares, (n_mp, n_dp, 4)))
    ends = [v.shape[-1] for v in vectors]
    vectors = jnp.concatenate(vectors, axis=-1)
    vectors = jnp.pad(vectors, ((0, 0), (0, 0), (0, 1024 - vectors.shape[-1])))
    vectors = vectors.reshape(n_mp, n_dp, 8, 128)
    own_down, own_up, own_out, own_joined, own_vector = scatter_sums(
        [
            in_place_order(b)
            for b in (down_blocks, up_blocks, out_blocks, joined_blocks, vectors)
        ]
    )
    own_vector = own_vector.reshape(-1)
    own_vectors, start = [], 0
    for size in ends:
        own_vectors.append(own_vector[start : start + size])
        start += size
    totals = own_vectors.pop()
    rms_values = jnp.sqrt(totals[:3] / (totals[3] * width))

    def back_home(rows):
        mine, sent = rows[:half_rows], swap_with_partner(rows[half_rows:])
        return jnp.where(half == 0, jnp.stack([mine, sent]), jnp.stack([sent, mine]))

    return (
        back_home(output),
        back_home(tokens_grad),
        own_joined[:, :GC],
        own_joined[:, GC : 2 * GC],
        own_joined[:, 2 * GC :],
        own_out,
        own_up,
        own_down,
        *own_vectors,
        rms_values,
    )


def solution(mesh):
    rows = P(None, BOTH, None)
    split, rows_split = P("dp", "mp"), P(("mp", "dp"), None)
    aligned = mesh.shape["dp"] == 8 and mesh.shape["mp"] == 4
    return jax.shard_map(
        body_fused if aligned else body_any,
        mesh=mesh,
        in_specs=(
            rows,
            rows,
            P(None, "dp"),
            split,
            split,
            split,
            rows_split,
            split,
            rows_split,
            P("mp"),
            P("mp"),
            P("mp"),
            *([P()] * 6),
        ),
        out_specs=(
            rows,
            rows,
            split,
            split,
            split,
            rows_split,
            split,
            rows_split,
            *([P(("mp", "dp"))] * 3),
            *([P(BOTH)] * 6),
            P(),
        ),
        check_vma=False,
    )
```

```python
import functools

import jax
import jax.numpy as jnp
from jax import lax
from jax.experimental import pallas as pl
from jax.experimental.pallas import tpu as pltpu
from jax.sharding import PartitionSpec as P

HD = 64
L = 1024
SEQ_MB = 2
MB = 2
GROUPS = 4
GH = 3
GC = GH * HD
PAD = 256

epsilon = 1e-05
masked_score = -1e30
exp2_scale = HD ** (-0.5) * 1.4426950408889634
score_scale = HD ** (-0.5)
BOTH = ("dp", "mp")
NT = (((1,), (1,)), ((), ()))


def product(left_side, right_side):
    return jnp.dot(left_side, right_side, preferred_element_type=jnp.float32)


def contract_rows(left_side, right_side):
    return lax.dot_general(
        left_side, right_side, (((0,), (0,)), ((), ())), preferred_element_type=jnp.float32
    )


def contract_cols(left_side, right_side):
    return lax.dot_general(left_side, right_side, NT, preferred_element_type=jnp.float32)


def layer_norm(values, norm_gain, norm_shift):
    center = values - jnp.mean(values, axis=-1, keepdims=True)
    spread = jnp.mean(center * center, axis=-1, keepdims=True)
    inverse = lax.rsqrt(spread + epsilon)
    scaled = center * inverse
    return (scaled * norm_gain + norm_shift, scaled, inverse)


def norm_back(upstream, scaled, inverse, norm_gain):
    gain_grad = jnp.sum(upstream * scaled, axis=0)
    shift_grad = jnp.sum(upstream, axis=0)
    through = upstream * norm_gain
    result = inverse * (
        through
        - jnp.mean(through, axis=-1, keepdims=True)
        - scaled * jnp.mean(through * scaled, axis=-1, keepdims=True)
    )
    return (result, gain_grad, shift_grad)


def head_keys(keys, bias, h, lane):
    kept = jnp.where((lane >= h * HD) & (lane < (h + 1) * HD), keys, jnp.zeros_like(keys))
    return jnp.where(lane == GC, bias, kept)


def attend_forward_kernel(bias_ref, qkv_ref, out_ref, lse_ref, turned):
    rows = qkv_ref.shape[1]
    chunk = 256
    lane = lax.broadcasted_iota(jnp.int32, (1, PAD), 1)
    keys = qkv_ref[0, :, PAD : 2 * PAD]
    values_t = qkv_ref[0, :, 2 * PAD :].T
    bias = bias_ref[...]
    for h in range(GH):
        own = head_keys(keys, bias, h, lane)
        own_values = values_t[h * HD : (h + 1) * HD, :]
        for at in range(0, rows, chunk):
            queries = qkv_ref[0, at : at + chunk, :PAD]
            scores = contract_cols(own, queries)
            top = jnp.max(scores, axis=0, keepdims=True) * exp2_scale
            raised = jnp.exp2(scores * exp2_scale - top)
            total = jnp.sum(raised, axis=0, keepdims=True)
            mixed = product(own_values, raised.astype(jnp.bfloat16))
            turned[h * HD : (h + 1) * HD, at : at + chunk] = mixed / total
            lse_ref[0, h : h + 1, at : at + chunk] = top + jnp.log2(total)
    turned[GC:, :] = jnp.zeros((PAD - GC, rows), jnp.float32)
    out_ref[0] = turned[...].T.astype(jnp.bfloat16)


def attend_forward(qkv, bias):
    rows = qkv.shape[1]
    return pl.pallas_call(
        attend_forward_kernel,
        grid=(GROUPS,),
        in_specs=[
            pl.BlockSpec((rows, 1), lambda g: (0, 0)),
            pl.BlockSpec((1, rows, 3 * PAD), lambda g: (g, 0, 0)),
        ],
        out_specs=[
            pl.BlockSpec((1, rows, PAD), lambda g: (g, 0, 0)),
            pl.BlockSpec((1, 8, rows), lambda g: (g, 0, 0)),
        ],
        out_shape=[
            jax.ShapeDtypeStruct((GROUPS, rows, PAD), jnp.bfloat16),
            jax.ShapeDtypeStruct((GROUPS, 8, rows), jnp.float32),
        ],
        scratch_shapes=[pltpu.VMEM((PAD, rows), jnp.float32)],
        cost_estimate=pl.CostEstimate(
            flops=45_000_000_000 // 3, bytes_accessed=10_000_000, transcendentals=12_000_000
        ),
    )(bias, qkv)


def attend_backward_kernel(
    bias_ref, qkv_ref, out_ref, lse_ref, grad_ref, joined_ref, sums_ref, probs, slopes, turned
):
    rows = qkv_ref.shape[1]
    chunk = 256
    lane = lax.broadcasted_iota(jnp.int32, (1, PAD), 1)
    keys = qkv_ref[0, :, PAD : 2 * PAD]
    keys_t = keys.T
    values = qkv_ref[0, :, 2 * PAD :]
    bias = bias_ref[...]
    crossed = (grad_ref[0].astype(jnp.float32) * out_ref[0].astype(jnp.float32)).T
    key_grad = jnp.zeros((rows, PAD), jnp.float32)
    value_grad = jnp.zeros((rows, PAD), jnp.float32)
    for h in range(GH):
        head = (lane >= h * HD) & (lane < (h + 1) * HD)
        own = head_keys(keys, bias, h, lane)
        own_values = jnp.where(head, values, jnp.zeros_like(values))
        delta = jnp.sum(crossed[h * HD : (h + 1) * HD, :], axis=0, keepdims=True)
        for at in range(0, rows, chunk):
            queries = qkv_ref[0, at : at + chunk, :PAD]
            grads = grad_ref[0, at : at + chunk, :]
            scores = contract_cols(own, queries)
            attn_probs = jnp.exp2(scores * exp2_scale - lse_ref[0, h : h + 1, at : at + chunk])
            prob_grad = contract_cols(own_values, grads)
            probs[:, at : at + chunk] = attn_probs.astype(jnp.bfloat16)
            slopes[:, at : at + chunk] = (
                attn_probs * (prob_grad - delta[:, at : at + chunk])
            ).astype(jnp.bfloat16)
        own_grads = jnp.where(head, grad_ref[0], jnp.zeros((), jnp.bfloat16))
        own_queries = jnp.where(head, qkv_ref[0, :, :PAD], jnp.zeros((), jnp.bfloat16))
        value_grad = value_grad + product(probs[...], own_grads)
        key_grad = key_grad + product(slopes[...], own_queries)
        turned[h * HD : (h + 1) * HD, :] = product(
            keys_t[h * HD : (h + 1) * HD, :], slopes[...]
        )
    turned[GC:, :] = jnp.zeros((PAD - GC, rows), jnp.float32)
    query_grad = turned[...].T * score_scale
    joined_ref[0, :, :PAD] = query_grad.astype(jnp.bfloat16)
    joined_ref[0, :, PAD : 2 * PAD] = (key_grad * score_scale).astype(jnp.bfloat16)
    joined_ref[0, :, 2 * PAD :] = value_grad.astype(jnp.bfloat16)
    sums_ref[0, 0:1, :] = jnp.sum(query_grad, axis=0, keepdims=True)
    sums_ref[0, 1:2, :] = jnp.sum(value_grad, axis=0, keepdims=True)


def attend_backward(qkv, bias, heads_out, lse, heads_grad):
    rows = qkv.shape[1]
    return pl.pallas_call(
        attend_backward_kernel,
        grid=(GROUPS,),
        in_specs=[
            pl.BlockSpec((rows, 1), lambda g: (0, 0)),
            pl.BlockSpec((1, rows, 3 * PAD), lambda g: (g, 0, 0)),
            pl.BlockSpec((1, rows, PAD), lambda g: (g, 0, 0)),
            pl.BlockSpec((1, 8, rows), lambda g: (g, 0, 0)),
            pl.BlockSpec((1, rows, PAD), lambda g: (g, 0, 0)),
        ],
        out_specs=[
            pl.BlockSpec((1, rows, 3 * PAD), lambda g: (g, 0, 0)),
            pl.BlockSpec((1, 8, PAD), lambda g: (g, 0, 0)),
        ],
        out_shape=[
            jax.ShapeDtypeStruct((GROUPS, rows, 3 * PAD), jnp.bfloat16),
            jax.ShapeDtypeStruct((GROUPS, 8, PAD), jnp.float32),
        ],
        scratch_shapes=[
            pltpu.VMEM((rows, rows), jnp.bfloat16),
            pltpu.VMEM((rows, rows), jnp.bfloat16),
            pltpu.VMEM((PAD, rows), jnp.float32),
        ],
        cost_estimate=pl.CostEstimate(
            flops=30_000_000_000, bytes_accessed=20_000_000, transcendentals=12_000_000
        ),
    )(bias, qkv, heads_out, lse, heads_grad)


def swap_with_partner(values):
    size = lax.axis_size("mp")
    return lax.ppermute(values, "mp", [(i, i ^ 1) for i in range(size)])


def pad_heads(values):
    return jnp.pad(values, [(0, 0)] * (values.ndim - 1) + [(0, PAD - values.shape[-1])])


MESH = pl.DeviceIdType.MESH


def positions():
    mp, dp = lax.axis_index("mp"), lax.axis_index("dp")
    return mp, lax.div(mp, 2), lax.rem(mp, 2), lax.div(dp, 2), lax.rem(dp, 2)


def at_place(x, c, z, y):
    return (2 * z + y, 2 * x + c)


def neighbours(nz):
    mp, x, c, z, y = positions()
    first = at_place(lax.rem(x + c, 2), c, z, lax.rem(y + 1 - c, 2))
    second = at_place(lax.rem(x + 1 - c, 2), c, z, lax.rem(y + c, 2))
    partner = at_place(x, 1 - c, z, y)
    along = [at_place(x, c, lax.rem(z + d, nz), y) for d in range(1, nz)]
    return first, second, partner, along


def meet(devices):
    barrier = pltpu.get_barrier_semaphore()
    for device in devices:
        pl.semaphore_signal(barrier, inc=1, device_id=device, device_id_type=MESH)
    pl.semaphore_wait(barrier, len(devices))


def regions(x, c, y):
    own = (x, y)
    first = (lax.rem(x + c, 2), lax.rem(y + 1 - c, 2))
    second = (lax.rem(x + 1 - c, 2), lax.rem(y + c, 2))
    third = (1 - x, 1 - y)
    return own, first, second, third


def gather_kernel(nz, parts, *refs):
    shards, fulls = refs[:parts], refs[parts : 2 * parts]
    own_sem, z_send, z_recv, send, recv = refs[2 * parts :]
    mp, x, c, z, y = positions()
    first, second, partner, along = neighbours(nz)
    meet([first, second, partner, *along])
    own, got1, got2, got3 = regions(x, c, y)
    other = regions(x, 1 - c, y)

    def remote(src, dst, s, r, device):
        return pltpu.make_async_remote_copy(
            src_ref=src, dst_ref=dst, send_sem=s, recv_sem=r, device_id=device, device_id_type=MESH
        )

    started = []
    locals_ = []
    spread = []
    for p in range(parts):
        keep = pltpu.make_async_copy(shards[p], fulls[p].at[x, c, z, y], own_sem.at[p])
        keep.start()
        locals_.append(keep)
        sends = [
            remote(shards[p], fulls[p].at[x, c, z, y], z_send.at[p, d], z_recv.at[p, d], along[d])
            for d in range(nz - 1)
        ]
        for copy in sends:
            copy.start()
        spread.append(sends)

    def block(p, core, place):
        return fulls[p].at[place[0], core, :, place[1]]

    def push(p, k, core, place, device):
        copy = remote(block(p, core, place), block(p, core, place), send.at[p, k], recv.at[p, k], device)
        copy.start()
        started.append(copy)
        return copy

    def arrived(p, k, core, place):
        here = block(p, core, place)
        remote(here, here, send.at[p, k], recv.at[p, k], first).wait_recv()

    for p in range(parts):
        locals_[p].wait()
        for copy in spread[p]:
            copy.wait_recv()
        push(p, 0, c, own, first)
        push(p, 1, c, own, second)
        push(p, 3, c, own, partner)
    for p in range(parts):
        arrived(p, 0, c, got1)
        push(p, 2, c, got1, second)
        push(p, 4, c, got1, partner)
    for p in range(parts):
        arrived(p, 1, c, got2)
        push(p, 5, c, got2, partner)
        arrived(p, 2, c, got3)
        push(p, 6, c, got3, partner)
    for p in range(parts):
        for k in range(4):
            arrived(p, 3 + k, 1 - c, other[k])
    for sends in spread:
        for copy in sends:
            copy.wait_send()
    for copy in started:
        copy.wait_send()


def gather_all(shards):
    n_dp = lax.axis_size("dp")
    nz, parts = n_dp // 2, len(shards)
    return pl.pallas_call(
        functools.partial(gather_kernel, nz, parts),
        in_specs=[pl.BlockSpec(memory_space=pltpu.VMEM)] * parts,
        out_specs=[pl.BlockSpec(memory_space=pl.ANY)] * parts,
        out_shape=[jax.ShapeDtypeStruct((2, 2, nz, 2, *s.shape), s.dtype) for s in shards],
        scratch_shapes=[
            pltpu.SemaphoreType.DMA((parts,)),
            pltpu.SemaphoreType.DMA((parts, nz - 1)),
            pltpu.SemaphoreType.DMA((parts, nz - 1)),
            pltpu.SemaphoreType.DMA((parts, 7)),
            pltpu.SemaphoreType.DMA((parts, 7)),
        ],
        compiler_params=pltpu.CompilerParams(collective_id=0, has_side_effects=True),
    )(*shards)


def scatter_kernel(nz, parts, side, *refs):
    partials, results = refs[:parts], refs[parts : 2 * parts]
    at = 2 * parts
    sums, heard1, heard2, heard3, heard4 = (
        refs[at + i * parts : at + (i + 1) * parts] for i in range(5)
    )
    own_sem, send, recv, z_send, z_recv = refs[at + 5 * parts :]
    mp, x, c, z, y = positions()
    first, second, partner, along = neighbours(nz)
    meet([first, second, partner, *along])
    own, got1, got2, got3 = regions(x, c, y)
    started = []

    def remote(src, dst, s, r, device):
        copy = pltpu.make_async_remote_copy(
            src_ref=src, dst_ref=dst, send_sem=s, recv_sem=r, device_id=device, device_id_type=MESH
        )
        copy.start()
        started.append(copy)
        return copy

    def add(p, place, more):
        for i in range(nz):
            here = sums[p].at[place[0], i, place[1]]
            here[...] = (here[...].astype(jnp.float32) + more[i].astype(jnp.float32)).astype(here.dtype)

    def cut(p, k, core):
        if p not in side:
            return partials[p].at[k, core]
        size = partials[p].shape[3] // 4
        return partials[p].at[:, :, :, pl.ds(pl.multiple_of((2 * k + core) * size, size), size)]

    kept, core_copies = [], []
    for p in range(parts):
        copies = []
        for k in range(2):
            keep = pltpu.make_async_copy(cut(p, k, c), sums[p].at[k], own_sem.at[p, k])
            keep.start()
            copies.append(keep)
        kept.append(copies)
        core_copies.append(
            [
                remote(cut(p, k, 1 - c), heard1[p].at[k], send.at[p, k], recv.at[p, k], partner)
                for k in range(2)
            ]
        )
    second_copies = []
    for p in range(parts):
        for copy in kept[p]:
            copy.wait()
        for copy in core_copies[p]:
            copy.wait_recv()
        copies = []
        for k, place in enumerate((got2, got3)):
            add(p, place, heard1[p].at[place[0], :, place[1]])
            copies.append(
                remote(
                    sums[p].at[place[0], :, place[1]],
                    heard2[p].at[k],
                    send.at[p, 2 + k],
                    recv.at[p, 2 + k],
                    second,
                )
            )
        second_copies.append(copies)
        for place in (got1, own):
            add(p, place, heard1[p].at[place[0], :, place[1]])
    first_copies = []
    for p in range(parts):
        second_copies[p][1].wait_recv()
        add(p, got1, heard2[p].at[1])
        first_copies.append(
            remote(sums[p].at[got1[0], :, got1[1]], heard3[p], send.at[p, 4], recv.at[p, 4], first)
        )
        second_copies[p][0].wait_recv()
        add(p, own, heard2[p].at[0])
    last_copies = []
    for p in range(parts):
        first_copies[p].wait_recv()
        add(p, own, heard3[p])
        last_copies.append(
            [
                remote(
                    sums[p].at[x, lax.rem(z + d + 1, nz), y],
                    heard4[p].at[d],
                    z_send.at[p, d],
                    z_recv.at[p, d],
                    along[d],
                )
                for d in range(nz - 1)
            ]
        )
    for p in range(parts):
        for copy in last_copies[p]:
            copy.wait_recv()
        total = sums[p][x, z, y].astype(jnp.float32)
        for d in range(nz - 1):
            total = total + heard4[p][d].astype(jnp.float32)
        results[p][...] = total
    for copy in started:
        copy.wait_send()


def scatter_sums(partials, side=()):
    nz, parts = lax.axis_size("dp") // 2, len(partials)
    tails = [
        (p.shape[2], p.shape[3] // 4) if i in side else p.shape[4:] for i, p in enumerate(partials)
    ]
    kinds = [p.dtype for p in partials]
    return pl.pallas_call(
        functools.partial(scatter_kernel, nz, parts, side),
        in_specs=[pl.BlockSpec(memory_space=pl.ANY)] * parts,
        out_specs=[pl.BlockSpec(memory_space=pltpu.VMEM)] * parts,
        out_shape=[jax.ShapeDtypeStruct(t, jnp.float32) for t in tails],
        scratch_shapes=[
            *[pltpu.VMEM((2, nz, 2, *t), k) for t, k in zip(tails, kinds)],
            *[pltpu.VMEM((2, nz, 2, *t), k) for t, k in zip(tails, kinds)],
            *[pltpu.VMEM((2, nz, *t), k) for t, k in zip(tails, kinds)],
            *[pltpu.VMEM((nz, *t), k) for t, k in zip(tails, kinds)],
            *[pltpu.VMEM((nz - 1, *t), k) for t, k in zip(tails, kinds)],
            pltpu.SemaphoreType.DMA((parts, 2)),
            pltpu.SemaphoreType.DMA((parts, 5)),
            pltpu.SemaphoreType.DMA((parts, 5)),
            pltpu.SemaphoreType.DMA((parts, nz - 1)),
            pltpu.SemaphoreType.DMA((parts, nz - 1)),
        ],
        compiler_params=pltpu.CompilerParams(
            collective_id=1, has_side_effects=True, vmem_limit_bytes=60 * 1024 * 1024
        ),
    )(*partials)


def in_place_order(blocks):
    return blocks.reshape(2, 2, blocks.shape[1] // 2, 2, *blocks.shape[2:])


def body_any(
    tokens,
    cotangent,
    lengths,
    w_query,
    w_key,
    w_value,
    w_out,
    w_up,
    w_down,
    b_query,
    b_value,
    b_up,
    b_out,
    b_down,
    norm1_gain,
    norm1_shift,
    norm2_gain,
    norm2_shift,
):
    half_rows = tokens.shape[1]
    width = tokens.shape[2]
    n_dp, n_mp = lax.axis_size("dp"), lax.axis_size("mp")
    unit_cols = w_up.shape[1]
    mp_index = lax.axis_index("mp")
    half = lax.rem(mp_index, 2)
    seq = lax.div(mp_index, 2)

    def own_of(pair):
        return jnp.where(half == 0, pair[0], pair[1])

    def other_of(pair):
        return jnp.where(half == 0, pair[1], pair[0])

    rows_in = jnp.concatenate([own_of(tokens), swap_with_partner(other_of(tokens))], axis=0)
    rows_cot = jnp.concatenate([own_of(cotangent), swap_with_partner(other_of(cotangent))], axis=0)
    length = lax.dynamic_slice(lengths, (half, seq), (1, 1))[0, 0]
    place = jnp.arange(half_rows, dtype=jnp.int32)
    place = jnp.concatenate([place + half * half_rows, place + (1 - half) * half_rows])
    valid_row = (place < length)[:, None]
    bias = jnp.where(valid_row, 0.0, masked_score).astype(jnp.bfloat16)
    valid_row = valid_row.astype(jnp.float32)

    biases = jnp.pad(jnp.concatenate([b_query, b_value, b_up]), (0, 896)).reshape(16, 128)
    qkv_shard = jnp.concatenate([w_query, w_key, w_value], axis=1)
    gathered = gather_all([qkv_shard, w_out, w_up, w_down, biases])
    full_qkv, full_out, full_up, full_down, full_bias = (
        g.reshape(n_mp, n_dp, *g.shape[4:]) for g in gathered
    )
    full_qkv = full_qkv.reshape(n_mp, width, 3, GC)
    w_joined = pad_heads(full_qkv).reshape(n_mp, width, 3 * PAD)
    full_out = full_out.reshape(n_mp, GC, width)
    out_pad = jnp.pad(full_out, ((0, 0), (0, PAD - GC), (0, 0))).reshape(n_mp * PAD, width)
    full_up = full_up.reshape(n_mp, width, unit_cols).transpose(1, 0, 2).reshape(width, n_mp * unit_cols)
    full_down = full_down.reshape(n_mp * unit_cols, width)
    full_bias = full_bias[:, 0].reshape(n_mp, -1)
    bias_q, bias_v, bias_up = full_bias[:, :GC], full_bias[:, GC:2*GC], full_bias[:, 2*GC:2*GC+unit_cols]
    mark = jnp.zeros((n_mp, PAD - GC), jnp.float32).at[:, 0].set(1.0)
    joined_bias = jnp.concatenate(
        [bias_q, mark, jnp.zeros((n_mp, PAD), jnp.float32), pad_heads(bias_v)], axis=1
    )

    qkv = lax.dot_general(
        jnp.broadcast_to(rows_in[None], (n_mp, *rows_in.shape)),
        w_joined,
        (((2,), (1,)), ((0,), (0,))),
        preferred_element_type=jnp.float32,
    )
    qkv = (qkv + joined_bias[:, None, :]).astype(jnp.bfloat16)
    heads_out, lse = attend_forward(qkv, bias)
    heads_flat = heads_out.transpose(1, 0, 2).reshape(2 * half_rows, n_mp * PAD)
    attention = product(heads_flat, out_pad) + b_out
    first_norm, first_scaled, first_inverse = layer_norm(
        rows_in.astype(jnp.float32) + attention, norm1_gain, norm1_shift
    )
    first_low = first_norm.astype(jnp.bfloat16)
    preact = product(first_low, full_up) + bias_up.reshape(-1)
    cumulative = 0.5 * (1.0 + lax.erf(preact * 0.7071067811865476))
    active = (preact * cumulative).astype(jnp.bfloat16)
    slope = cumulative + preact * (jnp.exp(-0.5 * preact * preact) * 0.3989422804014327)
    ffn_out = product(active, full_down) + b_down
    stream = first_norm + ffn_out
    final_norm, final_scaled, final_inverse = layer_norm(stream, norm2_gain, norm2_shift)
    output = final_norm.astype(jnp.bfloat16)
    squares = jnp.stack(
        [
            jnp.sum(valid_row * stream * stream),
            jnp.sum(valid_row * attention * attention),
            jnp.sum(valid_row * ffn_out * ffn_out),
            jnp.sum(valid_row),
        ]
    )

    stream_grad, gain2_grad, shift2_grad = norm_back(
        rows_cot.astype(jnp.float32), final_scaled, final_inverse, norm2_gain
    )
    down_bias_grad = jnp.sum(stream_grad, axis=0)
    ffn_grad_low = stream_grad.astype(jnp.bfloat16)
    active_grad = contract_cols(ffn_grad_low, full_down)
    down_wgrad = contract_rows(active, ffn_grad_low)
    preact_grad = active_grad * slope
    up_bias_grad = jnp.sum(preact_grad, axis=0)
    preact_low = preact_grad.astype(jnp.bfloat16)
    up_wgrad = contract_rows(first_low, preact_low)
    first_grad = stream_grad + contract_cols(preact_low, full_up)
    attn_grad, gain1_grad, shift1_grad = norm_back(
        first_grad, first_scaled, first_inverse, norm1_gain
    )
    out_bias_grad = jnp.sum(attn_grad, axis=0)
    attn_grad_low = attn_grad.astype(jnp.bfloat16)
    out_wgrad = contract_rows(heads_flat, attn_grad_low)
    heads_grad = contract_cols(attn_grad_low, out_pad).astype(jnp.bfloat16)
    heads_grad = heads_grad.reshape(2 * half_rows, n_mp, PAD).transpose(1, 0, 2)
    joined, sums = attend_backward(qkv, bias, heads_out, lse, heads_grad)
    joined_wgrad = lax.dot_general(
        jnp.broadcast_to(rows_in[None], (n_mp, *rows_in.shape)),
        joined,
        (((1,), (1,)), ((0,), (0,))),
        preferred_element_type=jnp.float32,
    )
    tokens_grad = attn_grad + jnp.sum(
        lax.dot_general(
            joined, w_joined, (((2,), (2,)), ((0,), (0,))), preferred_element_type=jnp.float32
        ),
        axis=0,
    )

    low = jnp.bfloat16
    joined_blocks = (
        joined_wgrad.astype(low)
        .reshape(n_mp, n_dp, width // n_dp, 3, PAD)[..., :GC]
        .reshape(n_mp, n_dp, width // n_dp, 3 * GC)
    )
    out_blocks = (
        out_wgrad.astype(low)
        .reshape(n_mp, PAD, width)[:, :GC]
        .reshape(n_mp, n_dp, GC // n_dp, width)
    )
    up_blocks = up_wgrad.astype(low).reshape(n_dp, width // n_dp, n_mp, unit_cols).transpose(2, 0, 1, 3)
    down_blocks = down_wgrad.astype(low).reshape(n_mp, n_dp, unit_cols // n_dp, width)

    def by_mp(vector):
        return vector.reshape(n_mp, n_dp, -1)

    def by_dp(vector):
        return vector.reshape(n_dp, n_mp, -1).transpose(1, 0, 2)

    vectors = [by_mp(sums[:, 0, :GC]), by_mp(sums[:, 1, :GC]), by_mp(up_bias_grad)]
    vectors += [
        by_dp(v)
        for v in (out_bias_grad, down_bias_grad, gain1_grad, shift1_grad, gain2_grad, shift2_grad)
    ]
    vectors.append(jnp.broadcast_to(squares, (n_mp, n_dp, 4)))
    ends = [v.shape[-1] for v in vectors]
    vectors = jnp.concatenate(vectors, axis=-1)
    vectors = jnp.pad(vectors, ((0, 0), (0, 0), (0, 1024 - vectors.shape[-1])))
    vectors = vectors.reshape(n_mp, n_dp, 8, 128)
    own_down, own_up, own_out, own_joined, own_vector = scatter_sums(
        [
            in_place_order(b)
            for b in (down_blocks, up_blocks, out_blocks, joined_blocks, vectors)
        ]
    )
    own_vector = own_vector.reshape(-1)
    own_vectors, start = [], 0
    for size in ends:
        own_vectors.append(own_vector[start : start + size])
        start += size
    totals = own_vectors.pop()
    rms_values = jnp.sqrt(totals[:3] / (totals[3] * width))

    def back_home(rows):
        mine, sent = rows[:half_rows], swap_with_partner(rows[half_rows:])
        return jnp.where(half == 0, jnp.stack([mine, sent]), jnp.stack([sent, mine]))

    return (
        back_home(output),
        back_home(tokens_grad),
        own_joined[:, :GC],
        own_joined[:, GC : 2 * GC],
        own_joined[:, 2 * GC :],
        own_out,
        own_up,
        own_down,
        *own_vectors,
        rms_values,
    )


PARTS = 4


def remote_copy(src, dst, s, r, device):
    return pltpu.make_async_remote_copy(
        src_ref=src, dst_ref=dst, send_sem=s, recv_sem=r, device_id=device, device_id_type=MESH
    )


def forward_kernel(
    nz,
    lengths,
    tokens,
    cotangent,
    shard_q,
    shard_o,
    shard_u,
    shard_d,
    bias_shard,
    full_q,
    full_o,
    full_u,
    full_d,
    bias_full,
    rows_out,
    cot_out,
    w_out,
    qkv_out,
    heads_out,
    lse_out,
    rows,
    cots,
    w_got,
    w_pad,
    qkv,
    values_t,
    turned,
    heads,
    own_sem,
    z_send,
    z_recv,
    relay_send,
    send,
    recv,
    swap_send,
    swap_recv,
    bias_send,
    bias_recv,
    out_sem,
):
    shards = (shard_q, shard_o, shard_u, shard_d)
    fulls = (full_q, full_o, full_u, full_d)
    half_rows = tokens.shape[1]
    length = 2 * half_rows
    mp, x, c, z, y = positions()
    half = c
    seq = x
    first, second, partner, along = neighbours(nz)
    across = at_place(1 - x, c, z, y)
    slanted = at_place(1 - x, 1 - c, z, y)
    own, got1, got2, got3 = regions(x, c, y)
    other = regions(x, 1 - c, y)
    meet([first, second, partner, slanted, *along])

    def block(p, core, place, d):
        return fulls[p].at[place[0], core, lax.rem(z + nz - d, nz), place[1]]

    places = (own, own, got1, own, got1, got2, got3)
    targets = (first, second, second, partner, partner, partner, partner)
    landing = (got1, got2, got3, *other)
    cores = (c, c, c, 1 - c, 1 - c, 1 - c, 1 - c)

    def outgoing(p, k, d):
        here = block(p, c, places[k], d)
        return remote_copy(here, here, send.at[p, k, d], recv.at[p, k, d], targets[k])

    def incoming(p, k, d):
        here = block(p, cores[k], landing[k], d)
        return remote_copy(here, here, send.at[p, k, d], recv.at[p, k, d], targets[k])

    at_low = 1 - lax.div(z + nz - 1, nz)
    near, far = 1 + 2 * at_low, 3 - 2 * at_low

    def z_copy(p, d):
        return remote_copy(
            shards[p], fulls[p].at[x, c, z, y], z_send.at[p, d - 1], z_recv.at[p, d - 1], along[d - 1]
        )

    def z_each(p, act):
        act(z_copy(p, 2))
        pl.when(z != nz - 1)(lambda: act(z_copy(p, 1)))
        pl.when(z != 0)(lambda: act(z_copy(p, 3)))

    def z_start(p):
        z_each(p, lambda copy: copy.start())

    def z_relay(p, low):
        here = block(p, c, own, 2)
        d = 1 if low else 3
        return remote_copy(here, here, relay_send.at[p], z_recv.at[p, d - 1], at_place(x, c, z + d - 2, y))

    def spread(p, d):
        if not (isinstance(d, int) and d == 0):
            here = block(p, c, own, d)
            remote_copy(here, here, z_send.at[p, d - 1], z_recv.at[p, d - 1], first).wait_recv()
        if isinstance(d, int) and d == 2:
            pl.when(z == 1)(lambda: z_relay(p, True).start())
            pl.when(z == 2)(lambda: z_relay(p, False).start())
        for k in (0, 1, 3):
            outgoing(p, k, d).start()

    def forward1(p):
        for d in range(nz):
            incoming(p, 0, d).wait_recv()
            outgoing(p, 2, d).start()
            outgoing(p, 4, d).start()

    def forward2(p):
        for d in range(nz):
            incoming(p, 1, d).wait_recv()
            outgoing(p, 5, d).start()

    def forward3(p):
        for d in range(nz):
            incoming(p, 2, d).wait_recv()
            outgoing(p, 6, d).start()

    def take(p, k):
        for d in range(nz):
            incoming(p, k, d).wait_recv()

    keep = [
        pltpu.make_async_copy(shards[p], fulls[p].at[x, c, z, y], own_sem.at[p]) for p in range(PARTS)
    ]
    keep_rows = pltpu.make_async_copy(tokens.at[half], rows.at[pl.ds(0, half_rows)], own_sem.at[PARTS])
    keep_cots = pltpu.make_async_copy(cotangent.at[half], cots.at[pl.ds(0, half_rows)], own_sem.at[PARTS + 2])
    swap_rows = remote_copy(
        tokens.at[1 - half], rows.at[pl.ds(half_rows, half_rows)], swap_send.at[0], swap_recv.at[0], partner
    )
    swap_cot = remote_copy(
        cotangent.at[1 - half], cots.at[pl.ds(half_rows, half_rows)], swap_send.at[1], swap_recv.at[1], partner
    )
    bias_copies = [
        remote_copy(bias_shard, bias_full.at[mp], bias_send.at[k], bias_recv.at[k], device)
        for k, device in enumerate((partner, across, slanted))
    ]
    z_start(0)
    keep[0].start()
    for copy in bias_copies:
        copy.start()
    swap_rows.start()
    keep_rows.start()
    for p in range(1, PARTS):
        keep[p].start()
    keep[0].wait()
    spread(0, 0)
    for p in range(1, PARTS):
        z_start(p)
    w_pad[...] = jnp.zeros_like(w_pad)
    turned[...] = jnp.zeros_like(turned)
    bias_full[mp] = bias_shard[...]
    for d in (2, near, far):
        spread(0, d)
    for copy in keep[1:]:
        copy.wait()
    forward1(0)
    for p in range(1, PARTS):
        spread(p, 0)
    forward2(0)
    swap_cot.start()
    keep_cots.start()
    keep_rows.wait()
    swap_rows.wait_recv()
    rows_copy = pltpu.make_async_copy(rows, rows_out, out_sem.at[2])
    rows_copy.start()
    cots_copy = pltpu.make_async_copy(cots, cot_out, out_sem.at[4])
    for copy in bias_copies:
        copy.wait_recv()

    hooks = {
        0: [lambda: [spread(1, d) for d in (2, near, far)]],
        1: [lambda: forward3(0)],
        2: [lambda: [spread(2, d) for d in (2, near)]],
        3: [lambda: spread(2, far), lambda: forward1(1)],
        4: [lambda: forward2(1), lambda: forward3(1)],
        5: [lambda: [spread(3, d) for d in (2, near)]],
        6: [lambda: spread(3, far)],
        7: [lambda: forward1(2)],
        8: [lambda: forward2(2)],
        10: [lambda: forward1(3)],
        11: [lambda: forward2(3)],
    }
    seq_length = lengths[half, seq]
    row = lax.broadcasted_iota(jnp.int32, (length, 1), 0)
    place = jnp.where(row < half_rows, row + half * half_rows, row - half * half_rows)
    bias = jnp.where(place < seq_length, 0.0, masked_score).astype(jnp.bfloat16)
    lane = lax.broadcasted_iota(jnp.int32, (1, PAD), 1)
    chunk = 256

    def heads_copy(gx, gc):
        columns = pl.ds(pl.multiple_of((2 * gx + gc) * PAD, PAD), PAD)
        return pltpu.make_async_copy(heads, heads_out.at[:, columns], out_sem.at[0])

    def qkv_copy(gx, gc):
        return pltpu.make_async_copy(qkv, qkv_out.at[2 * gx + gc], out_sem.at[1])

    def w_copy(gx, gc):
        return pltpu.make_async_copy(w_pad, w_out.at[2 * gx + gc], out_sem.at[3])

    def group_step(r, carry):
        gx, gc = lax.rem(x + lax.div(r, 2), 2), lax.rem(c + lax.rem(r, 2), 2)
        group = 2 * gx + gc

        @pl.when(r == 1)
        def _():
            for d in range(nz):
                incoming(0, 3, d).wait_recv()
            for d in range(nz):
                here = block(0, 1 - c, own, d)
                remote_copy(here, here, send.at[0, 5 - c, d], recv.at[0, 5 - c, d], first).wait_recv()

        @pl.when(r == 3)
        def _():
            for d in range(nz):
                here = block(0, 1 - c, own, d)
                remote_copy(here, here, send.at[0, 4 + c, d], recv.at[0, 4 + c, d], first).wait_recv()
            take(0, 6)

        load = pltpu.make_async_copy(full_q.at[gx, gc], w_got, own_sem.at[PARTS + 1])
        load.start()
        load.wait()

        @pl.when(r > 0)
        def _():
            qkv_copy(gx, gc).wait()
            w_copy(gx, gc).wait()

        w_flat = w_got[...].reshape(-1, 3 * GC)
        for k in range(3):
            w_pad[:, k * PAD : k * PAD + GC] = w_flat[:, k * GC : (k + 1) * GC]
        w_copy(gx, gc).start()
        joined_bias = bias_full[group, 0:1, :]
        for at in range(0, length, 512):
            qkv[at : at + 512, :] = (product(rows[at : at + 512, :], w_pad[...]) + joined_bias).astype(
                jnp.bfloat16
            )
        qkv_copy(gx, gc).start()
        values_t[...] = qkv[:, 2 * PAD :].T

        def head_step(h, carry):
            for k, todo in hooks.items():
                if todo:

                    @pl.when(r * GH + h == k)
                    def _():
                        for task in todo:
                            task()

            start = h * HD
            keys = qkv[:, PAD : 2 * PAD]
            kept = jnp.where((lane >= start) & (lane < start + HD), keys, jnp.zeros_like(keys))
            own_keys = jnp.where(lane == GC, bias, kept)
            own_values = values_t[pl.ds(pl.multiple_of(start, HD), HD), :]
            for at in range(0, length, chunk):
                scores = contract_cols(own_keys, qkv[at : at + chunk, :PAD])
                top = jnp.max(scores, axis=0, keepdims=True) * exp2_scale
                raised = jnp.exp2(scores * exp2_scale - top)
                total = jnp.sum(raised, axis=0, keepdims=True)
                mixed = product(own_values, raised.astype(jnp.bfloat16))
                turned[pl.ds(pl.multiple_of(start, HD), HD), at : at + chunk] = mixed / total
                lse_out[group, pl.ds(h, 1), at : at + chunk] = top + jnp.log2(total)
            return carry

        lax.fori_loop(0, GH, head_step, 0)

        @pl.when(r > 0)
        def _():
            heads_copy(gx, gc).wait()

        heads[...] = turned[...].T.astype(jnp.bfloat16)
        heads_copy(gx, gc).start()
        return carry

    lax.fori_loop(0, GROUPS, group_step, 0)
    keep_cots.wait()
    swap_cot.wait_recv()
    cots_copy.start()
    forward3(2)
    forward3(3)
    for p in range(1, PARTS):
        for k in range(3, 7):
            take(p, k)
    heads_copy(x, c).wait()
    qkv_copy(x, c).wait()
    w_copy(x, c).wait()
    rows_copy.wait()
    cots_copy.wait()
    swap_cot.wait_send()
    swap_rows.wait_send()
    for copy in bias_copies:
        copy.wait_send()
    for p in range(PARTS):
        z_each(p, lambda copy: copy.wait_send())
        pl.when(z == 1)(lambda: z_relay(p, True).wait_send())
        pl.when(z == 2)(lambda: z_relay(p, False).wait_send())
        for k in range(7):
            for d in range(nz):
                outgoing(p, k, d).wait_send()


def forward_attention(lengths, tokens, cotangent, shards, bias_shard):
    nz = lax.axis_size("dp") // 2
    half_rows, width = tokens.shape[1:]
    rows = 2 * half_rows
    low = jnp.bfloat16
    anywhere, vmem = pl.BlockSpec(memory_space=pl.ANY), pl.BlockSpec(memory_space=pltpu.VMEM)
    dma = pltpu.SemaphoreType.DMA
    return pl.pallas_call(
        functools.partial(forward_kernel, nz),
        in_specs=[pl.BlockSpec(memory_space=pltpu.SMEM), anywhere, anywhere, *[vmem] * 5],
        out_specs=[*[anywhere] * PARTS, vmem, *[anywhere] * 5, vmem],
        out_shape=[
            *[jax.ShapeDtypeStruct((2, 2, nz, 2, *s.shape), s.dtype) for s in shards],
            jax.ShapeDtypeStruct((GROUPS, *bias_shard.shape), jnp.float32),
            jax.ShapeDtypeStruct((rows, width), low),
            jax.ShapeDtypeStruct((rows, width), low),
            jax.ShapeDtypeStruct((GROUPS, width, 3 * PAD), low),
            jax.ShapeDtypeStruct((GROUPS, rows, 3 * PAD), low),
            jax.ShapeDtypeStruct((rows, GROUPS * PAD), low),
            jax.ShapeDtypeStruct((GROUPS, 8, rows), jnp.float32),
        ],
        scratch_shapes=[
            pltpu.VMEM((rows, width), low),
            pltpu.VMEM((rows, width), low),
            pltpu.VMEM((nz, 2, *shards[0].shape), low),
            pltpu.VMEM((width, 3 * PAD), low),
            pltpu.VMEM((rows, 3 * PAD), low),
            pltpu.VMEM((PAD, rows), low),
            pltpu.VMEM((PAD, rows), jnp.float32),
            pltpu.VMEM((rows, PAD), low),
            dma((PARTS + 3,)),
            dma((PARTS, nz - 1)),
            dma((PARTS, nz - 1)),
            dma((PARTS,)),
            dma((PARTS, 7, nz)),
            dma((PARTS, 7, nz)),
            dma((2,)),
            dma((2,)),
            dma((3,)),
            dma((3,)),
            dma((5,)),
        ],
        compiler_params=pltpu.CompilerParams(
            collective_id=2, has_side_effects=True, vmem_limit_bytes=60 * 1024 * 1024
        ),
    )(lengths, tokens, cotangent, *shards, bias_shard)


def place_of(info_ref, row, half_rows):
    half = info_ref[1]
    return jnp.where(row < half_rows, row + half * half_rows, row - half * half_rows)


def dense_kernel(
    info_ref,
    heads_ref,
    rows_ref,
    cot_ref,
    out_w,
    up_w,
    down_w,
    vec_ref,
    bias_ref,
    output_ref,
    first_ref,
    active_ref,
    ffn_low_ref,
    preact_low_ref,
    attn_ref,
    attn_low_ref,
    heads_grad_ref,
    sums_ref,
    slope,
):
    t = pl.program_id(0)
    low = jnp.bfloat16
    tile, width = rows_ref.shape
    units = up_w.shape[2]
    b_out, b_down, gain1, shift1, gain2, shift2 = (vec_ref[k : k + 1, :] for k in range(6))

    @pl.when(t == 0)
    def _():
        sums_ref[...] = jnp.zeros_like(sums_ref)

    def count(k, values):
        sums_ref[k : k + 1, :] += jnp.sum(values, axis=0, keepdims=True)

    attention = product(heads_ref[...], out_w[...]) + b_out
    first_norm, first_scaled, first_inverse = layer_norm(
        rows_ref[...].astype(jnp.float32) + attention, gain1, shift1
    )
    first_low = first_norm.astype(low)
    first_ref[...] = first_low
    ffn_out = jnp.broadcast_to(b_down, (tile, width))
    for g in range(GROUPS):
        preact = product(first_low, up_w[g]) + bias_ref[g, 1:2, :]
        cumulative = 0.5 * (1.0 + lax.erf(preact * 0.7071067811865476))
        active = (preact * cumulative).astype(low)
        active_ref[:, g * units : (g + 1) * units] = active
        slope[:, g * units : (g + 1) * units] = cumulative + preact * (
            jnp.exp(-0.5 * preact * preact) * 0.3989422804014327
        )
        ffn_out = ffn_out + product(active, down_w[g])
    stream = first_norm + ffn_out
    row = lax.broadcasted_iota(jnp.int32, (tile, 1), 0) + t * tile
    valid = (place_of(info_ref, row, pl.num_programs(0) * tile // 2) < info_ref[0]).astype(jnp.float32)
    count(6, valid * stream * stream)
    count(7, valid * attention * attention)
    count(8, valid * ffn_out * ffn_out)
    final_norm, final_scaled, final_inverse = layer_norm(stream, gain2, shift2)
    output_ref[...] = final_norm.astype(low)

    def norm_step(k, upstream, scaled, inverse, gain):
        count(k, upstream * scaled)
        count(k + 1, upstream)
        through = upstream * gain
        return inverse * (
            through
            - jnp.mean(through, axis=-1, keepdims=True)
            - scaled * jnp.mean(through * scaled, axis=-1, keepdims=True)
        )

    stream_grad = norm_step(4, cot_ref[...].astype(jnp.float32), final_scaled, final_inverse, gain2)
    count(1, stream_grad)
    ffn_grad_low = stream_grad.astype(low)
    ffn_low_ref[...] = ffn_grad_low
    first_grad = stream_grad
    for g in range(GROUPS):
        preact_grad = contract_cols(ffn_grad_low, down_w[g]) * slope[:, g * units : (g + 1) * units]
        count(12 + g, preact_grad)
        preact_low = preact_grad.astype(low)
        preact_low_ref[:, g * units : (g + 1) * units] = preact_low
        first_grad = first_grad + contract_cols(preact_low, up_w[g])
    attn_grad = norm_step(2, first_grad, first_scaled, first_inverse, gain1)
    count(0, attn_grad)
    attn_ref[...] = attn_grad
    attn_grad_low = attn_grad.astype(low)
    attn_low_ref[...] = attn_grad_low
    heads_grad_ref[...] = contract_cols(attn_grad_low, out_w[...]).astype(low)


def dense(info, heads, rows, cots, out_w, up_w, down_w, vecs, biases):
    count, width = rows.shape
    tile = 256
    units = up_w.shape[2]
    low = jnp.bfloat16

    def whole(shape):
        return pl.BlockSpec(shape, lambda t: (0,) * len(shape))

    def tiled(columns):
        return pl.BlockSpec((tile, columns), lambda t: (t, 0))

    outs = [
        (width, low),
        (width, low),
        (GROUPS * units, low),
        (width, low),
        (GROUPS * units, low),
        (width, jnp.float32),
        (width, low),
        (GROUPS * PAD, low),
    ]
    return pl.pallas_call(
        dense_kernel,
        grid=(count // tile,),
        in_specs=[
            pl.BlockSpec(memory_space=pltpu.SMEM),
            tiled(GROUPS * PAD),
            tiled(width),
            tiled(width),
            whole(out_w.shape),
            whole(up_w.shape),
            whole(down_w.shape),
            whole(vecs.shape),
            whole(biases.shape),
        ],
        out_specs=[*[tiled(columns) for columns, _ in outs], whole((16, width))],
        out_shape=[
            *[jax.ShapeDtypeStruct((count, columns), kind) for columns, kind in outs],
            jax.ShapeDtypeStruct((16, width), jnp.float32),
        ],
        scratch_shapes=[pltpu.VMEM((tile, GROUPS * units), jnp.float32)],
        cost_estimate=pl.CostEstimate(
            flops=22_600_000_000, bytes_accessed=40_000_000, transcendentals=7_000_000
        ),
    )(info, heads, rows, cots, out_w, up_w, down_w, vecs, biases)


def attend_back_kernel(
    info_ref,
    rows_ref,
    w_ref,
    attn_ref,
    qkv_ref,
    out_ref,
    lse_ref,
    grad_ref,
    wgrad_ref,
    tokens_ref,
    sums_ref,
    probs,
    slopes,
    turned,
    rows_t,
    joined,
):
    g = pl.program_id(0)
    low = jnp.bfloat16
    rows = qkv_ref.shape[1]
    width = rows_ref.shape[1]
    chunk = 256

    @pl.when(g == 0)
    def _():
        rows_t[...] = rows_ref[...].T
        tokens_ref[...] = attn_ref[...]

    row = lax.broadcasted_iota(jnp.int32, (rows, 1), 0)
    bias = jnp.where(place_of(info_ref, row, rows // 2) < info_ref[0], 0.0, masked_score).astype(low)
    lane = lax.broadcasted_iota(jnp.int32, (1, PAD), 1)
    keys = qkv_ref[0, :, PAD : 2 * PAD]
    keys_t = keys.T
    values = qkv_ref[0, :, 2 * PAD :]
    crossed = (grad_ref[...].astype(jnp.float32) * out_ref[...].astype(jnp.float32)).T
    key_grad = jnp.zeros((rows, PAD), jnp.float32)
    value_grad = jnp.zeros((rows, PAD), jnp.float32)
    for h in range(GH):
        head = (lane >= h * HD) & (lane < (h + 1) * HD)
        own = head_keys(keys, bias, h, lane)
        own_values = jnp.where(head, values, jnp.zeros_like(values))
        delta = jnp.sum(crossed[h * HD : (h + 1) * HD, :], axis=0, keepdims=True)
        for at in range(0, rows, chunk):
            queries = qkv_ref[0, at : at + chunk, :PAD]
            grads = grad_ref[at : at + chunk, :]
            scores = contract_cols(own, queries)
            attn_probs = jnp.exp2(scores * exp2_scale - lse_ref[0, h : h + 1, at : at + chunk])
            prob_grad = contract_cols(own_values, grads)
            probs[:, at : at + chunk] = attn_probs.astype(low)
            slopes[:, at : at + chunk] = (
                attn_probs * (prob_grad - delta[:, at : at + chunk])
            ).astype(low)
        own_grads = jnp.where(head, grad_ref[...], jnp.zeros((), low))
        own_queries = jnp.where(head, qkv_ref[0, :, :PAD], jnp.zeros((), low))
        value_grad = value_grad + product(probs[...], own_grads)
        key_grad = key_grad + product(slopes[...], own_queries)
        turned[h * HD : (h + 1) * HD, :] = product(keys_t[h * HD : (h + 1) * HD, :], slopes[...])
    turned[GC:, :] = jnp.zeros((PAD - GC, rows), jnp.float32)
    query_grad = turned[...].T * score_scale
    joined[:, :PAD] = query_grad.astype(low)
    joined[:, PAD : 2 * PAD] = (key_grad * score_scale).astype(low)
    joined[:, 2 * PAD :] = value_grad.astype(low)
    sums_ref[0, 0:1, :] = jnp.sum(query_grad, axis=0, keepdims=True)
    sums_ref[0, 1:2, :] = jnp.sum(value_grad, axis=0, keepdims=True)
    for at in range(0, width, chunk):
        part = product(rows_t[at : at + chunk, :], joined[...]).astype(low)
        for k in range(3):
            wgrad_ref[0, at : at + chunk, k * GC : (k + 1) * GC] = part[:, k * PAD : k * PAD + GC]
    for at in range(0, rows, chunk):
        tokens_ref[at : at + chunk, :] += contract_cols(joined[at : at + chunk, :], w_ref[0])


def attend_back(info, rows_in, w_joined, attn_grad, qkv, heads, lse, heads_grad):
    rows, width = rows_in.shape
    low = jnp.bfloat16

    def whole(shape):
        return pl.BlockSpec(shape, lambda g: (0,) * len(shape))

    def one(*shape):
        return pl.BlockSpec((1, *shape), lambda g: (g, 0, 0))

    beside = pl.BlockSpec((rows, PAD), lambda g: (0, g))
    return pl.pallas_call(
        attend_back_kernel,
        grid=(GROUPS,),
        in_specs=[
            pl.BlockSpec(memory_space=pltpu.SMEM),
            whole((rows, width)),
            one(width, 3 * PAD),
            whole((rows, width)),
            one(rows, 3 * PAD),
            beside,
            one(8, rows),
            beside,
        ],
        out_specs=[one(width, 3 * GC), whole((rows, width)), one(8, PAD)],
        out_shape=[
            jax.ShapeDtypeStruct((GROUPS, width, 3 * GC), low),
            jax.ShapeDtypeStruct((rows, width), jnp.float32),
            jax.ShapeDtypeStruct((GROUPS, 8, PAD), jnp.float32),
        ],
        scratch_shapes=[
            pltpu.VMEM((rows, rows), low),
            pltpu.VMEM((rows, rows), low),
            pltpu.VMEM((PAD, rows), jnp.float32),
            pltpu.VMEM((width, rows), low),
            pltpu.VMEM((rows, 3 * PAD), low),
        ],
        cost_estimate=pl.CostEstimate(
            flops=40_000_000_000, bytes_accessed=30_000_000, transcendentals=12_000_000
        ),
    )(info, rows_in, w_joined, attn_grad, qkv, heads, lse, heads_grad)


def body_fused(
    tokens,
    cotangent,
    lengths,
    w_query,
    w_key,
    w_value,
    w_out,
    w_up,
    w_down,
    b_query,
    b_value,
    b_up,
    b_out,
    b_down,
    norm1_gain,
    norm1_shift,
    norm2_gain,
    norm2_shift,
):
    half_rows = tokens.shape[1]
    width = tokens.shape[2]
    n_dp, n_mp = lax.axis_size("dp"), lax.axis_size("mp")
    unit_cols = w_up.shape[1]
    mp_index = lax.axis_index("mp")
    half = lax.rem(mp_index, 2)
    seq = lax.div(mp_index, 2)

    length = lax.dynamic_slice(lengths, (half, seq), (1, 1))[0, 0]
    info = jnp.stack([length, half])
    mark = jnp.zeros((PAD - GC,), jnp.float32).at[0].set(1.0)
    bias_rows = jnp.concatenate(
        [b_query, mark, jnp.zeros((PAD,), jnp.float32), b_value, jnp.zeros((PAD - GC,), jnp.float32), b_up]
    ).reshape(2, width)
    bias_rows = jnp.pad(bias_rows, ((0, 6), (0, 0)))
    qkv_shard = jnp.concatenate([w_query, w_key, w_value], axis=1)
    gathered = forward_attention(
        lengths, tokens, cotangent, (qkv_shard, w_out, w_up, w_down), bias_rows
    )
    full_out, full_up, full_down = (
        g.reshape(n_mp, n_dp * g.shape[4], g.shape[5]) for g in gathered[1:4]
    )
    full_bias, rows_in, rows_cot, w_joined, qkv, heads, lse = gathered[4:]
    out_pad = jnp.pad(full_out, ((0, 0), (0, PAD - GC), (0, 0))).reshape(n_mp * PAD, width)
    vecs = jnp.stack([b_out, b_down, norm1_gain, norm1_shift, norm2_gain, norm2_shift, b_out, b_out])
    (
        output,
        first_low,
        active,
        ffn_grad_low,
        preact_low,
        attn_grad,
        attn_grad_low,
        heads_grad,
        dense_sums,
    ) = dense(info, heads, rows_in, rows_cot, out_pad, full_up, full_down, vecs, full_bias)
    down_wgrad = contract_rows(active, ffn_grad_low)
    up_wgrad = contract_rows(first_low, preact_low)
    out_wgrad = contract_rows(heads, attn_grad_low)
    joined_wgrad, tokens_grad, sums = attend_back(
        info, rows_in, w_joined, attn_grad, qkv, heads, lse, heads_grad
    )
    squares = jnp.append(jnp.sum(dense_sums[6:9], axis=1), length.astype(jnp.float32))

    low = jnp.bfloat16
    joined_blocks = joined_wgrad.reshape(n_mp, n_dp, width // n_dp, 3 * GC)
    out_blocks = (
        out_wgrad.astype(low)
        .reshape(n_mp, PAD, width)[:, :GC]
        .reshape(n_mp, n_dp, GC // n_dp, width)
    )
    up_blocks = up_wgrad.astype(low).reshape(n_dp // 2, 2, width // n_dp, n_mp * unit_cols)
    down_blocks = down_wgrad.astype(low).reshape(n_mp, n_dp, unit_cols // n_dp, width)

    def by_mp(vector):
        return vector.reshape(n_mp, n_dp, -1)

    def by_dp(vector):
        return vector.reshape(n_dp, n_mp, -1).transpose(1, 0, 2)

    vectors = [by_mp(sums[:, 0, :GC]), by_mp(sums[:, 1, :GC]), by_mp(dense_sums[12:])]
    vectors += [by_dp(dense_sums[k]) for k in (0, 1, 2, 3, 4, 5)]
    vectors.append(jnp.broadcast_to(squares, (n_mp, n_dp, 4)))
    ends = [v.shape[-1] for v in vectors]
    vectors = jnp.concatenate(vectors, axis=-1)
    vectors = jnp.pad(vectors, ((0, 0), (0, 0), (0, 1024 - vectors.shape[-1])))
    vectors = vectors.reshape(n_mp, n_dp, 8, 128)
    own_down, own_up, own_out, own_joined, own_vector = scatter_sums(
        [
            in_place_order(down_blocks),
            up_blocks,
            in_place_order(out_blocks),
            in_place_order(joined_blocks),
            in_place_order(vectors),
        ],
        side=(1,),
    )
    own_vector = own_vector.reshape(-1)
    own_vectors, start = [], 0
    for size in ends:
        own_vectors.append(own_vector[start : start + size])
        start += size
    totals = own_vectors.pop()
    rms_values = jnp.sqrt(totals[:3] / (totals[3] * width))

    def back_home(rows):
        mine, sent = rows[:half_rows], swap_with_partner(rows[half_rows:])
        return jnp.where(half == 0, jnp.stack([mine, sent]), jnp.stack([sent, mine]))

    return (
        back_home(output),
        back_home(tokens_grad),
        own_joined[:, :GC],
        own_joined[:, GC : 2 * GC],
        own_joined[:, 2 * GC :],
        own_out,
        own_up,
        own_down,
        *own_vectors,
        rms_values,
    )


def solution(mesh):
    rows = P(None, BOTH, None)
    split, rows_split = P("dp", "mp"), P(("mp", "dp"), None)
    aligned = mesh.shape["dp"] == 8 and mesh.shape["mp"] == 4
    return jax.shard_map(
        body_fused if aligned else body_any,
        mesh=mesh,
        in_specs=(
            rows,
            rows,
            P(None, "dp"),
            split,
            split,
            split,
            rows_split,
            split,
            rows_split,
            P("mp"),
            P("mp"),
            P("mp"),
            *([P()] * 6),
        ),
        out_specs=(
            rows,
            rows,
            split,
            split,
            split,
            rows_split,
            split,
            rows_split,
            *([P(("mp", "dp"))] * 3),
            *([P(BOTH)] * 6),
            P(),
        ),
        check_vma=False,
    )
```

```python
import functools

import jax
import jax.numpy as jnp
from jax import lax
from jax.experimental import pallas as pl
from jax.experimental.pallas import tpu as pltpu
from jax.sharding import PartitionSpec as P

HD = 64
L = 1024
SEQ_MB = 2
MB = 2
GROUPS = 4
GH = 3
GC = GH * HD
PAD = 256

epsilon = 1e-05
masked_score = -1e30
exp2_scale = HD ** (-0.5) * 1.4426950408889634
score_scale = HD ** (-0.5)
BOTH = ("dp", "mp")
NT = (((1,), (1,)), ((), ()))


def product(left_side, right_side):
    return jnp.dot(left_side, right_side, preferred_element_type=jnp.float32)


def contract_rows(left_side, right_side):
    return lax.dot_general(
        left_side, right_side, (((0,), (0,)), ((), ())), preferred_element_type=jnp.float32
    )


def contract_cols(left_side, right_side):
    return lax.dot_general(left_side, right_side, NT, preferred_element_type=jnp.float32)


def layer_norm(values, norm_gain, norm_shift):
    center = values - jnp.mean(values, axis=-1, keepdims=True)
    spread = jnp.mean(center * center, axis=-1, keepdims=True)
    inverse = lax.rsqrt(spread + epsilon)
    scaled = center * inverse
    return (scaled * norm_gain + norm_shift, scaled, inverse)


def norm_back(upstream, scaled, inverse, norm_gain):
    gain_grad = jnp.sum(upstream * scaled, axis=0)
    shift_grad = jnp.sum(upstream, axis=0)
    through = upstream * norm_gain
    result = inverse * (
        through
        - jnp.mean(through, axis=-1, keepdims=True)
        - scaled * jnp.mean(through * scaled, axis=-1, keepdims=True)
    )
    return (result, gain_grad, shift_grad)


def head_keys(keys, bias, h, lane):
    kept = jnp.where((lane >= h * HD) & (lane < (h + 1) * HD), keys, jnp.zeros_like(keys))
    return jnp.where(lane == GC, bias, kept)


def attend_forward_kernel(bias_ref, qkv_ref, out_ref, lse_ref, turned):
    rows = qkv_ref.shape[1]
    chunk = 256
    lane = lax.broadcasted_iota(jnp.int32, (1, PAD), 1)
    keys = qkv_ref[0, :, PAD : 2 * PAD]
    values_t = qkv_ref[0, :, 2 * PAD :].T
    bias = bias_ref[...]
    for h in range(GH):
        own = head_keys(keys, bias, h, lane)
        own_values = values_t[h * HD : (h + 1) * HD, :]
        for at in range(0, rows, chunk):
            queries = qkv_ref[0, at : at + chunk, :PAD]
            scores = contract_cols(own, queries)
            top = jnp.max(scores, axis=0, keepdims=True) * exp2_scale
            raised = jnp.exp2(scores * exp2_scale - top)
            total = jnp.sum(raised, axis=0, keepdims=True)
            mixed = product(own_values, raised.astype(jnp.bfloat16))
            turned[h * HD : (h + 1) * HD, at : at + chunk] = mixed / total
            lse_ref[0, h : h + 1, at : at + chunk] = top + jnp.log2(total)
    turned[GC:, :] = jnp.zeros((PAD - GC, rows), jnp.float32)
    out_ref[0] = turned[...].T.astype(jnp.bfloat16)


def attend_forward(qkv, bias):
    rows = qkv.shape[1]
    return pl.pallas_call(
        attend_forward_kernel,
        grid=(GROUPS,),
        in_specs=[
            pl.BlockSpec((rows, 1), lambda g: (0, 0)),
            pl.BlockSpec((1, rows, 3 * PAD), lambda g: (g, 0, 0)),
        ],
        out_specs=[
            pl.BlockSpec((1, rows, PAD), lambda g: (g, 0, 0)),
            pl.BlockSpec((1, 8, rows), lambda g: (g, 0, 0)),
        ],
        out_shape=[
            jax.ShapeDtypeStruct((GROUPS, rows, PAD), jnp.bfloat16),
            jax.ShapeDtypeStruct((GROUPS, 8, rows), jnp.float32),
        ],
        scratch_shapes=[pltpu.VMEM((PAD, rows), jnp.float32)],
        cost_estimate=pl.CostEstimate(
            flops=45_000_000_000 // 3, bytes_accessed=10_000_000, transcendentals=12_000_000
        ),
    )(bias, qkv)


def attend_backward_kernel(
    bias_ref, qkv_ref, out_ref, lse_ref, grad_ref, joined_ref, sums_ref, probs, slopes, turned
):
    rows = qkv_ref.shape[1]
    chunk = 256
    lane = lax.broadcasted_iota(jnp.int32, (1, PAD), 1)
    keys = qkv_ref[0, :, PAD : 2 * PAD]
    keys_t = keys.T
    values = qkv_ref[0, :, 2 * PAD :]
    bias = bias_ref[...]
    crossed = (grad_ref[0].astype(jnp.float32) * out_ref[0].astype(jnp.float32)).T
    key_grad = jnp.zeros((rows, PAD), jnp.float32)
    value_grad = jnp.zeros((rows, PAD), jnp.float32)
    for h in range(GH):
        head = (lane >= h * HD) & (lane < (h + 1) * HD)
        own = head_keys(keys, bias, h, lane)
        own_values = jnp.where(head, values, jnp.zeros_like(values))
        delta = jnp.sum(crossed[h * HD : (h + 1) * HD, :], axis=0, keepdims=True)
        for at in range(0, rows, chunk):
            queries = qkv_ref[0, at : at + chunk, :PAD]
            grads = grad_ref[0, at : at + chunk, :]
            scores = contract_cols(own, queries)
            attn_probs = jnp.exp2(scores * exp2_scale - lse_ref[0, h : h + 1, at : at + chunk])
            prob_grad = contract_cols(own_values, grads)
            probs[:, at : at + chunk] = attn_probs.astype(jnp.bfloat16)
            slopes[:, at : at + chunk] = (
                attn_probs * (prob_grad - delta[:, at : at + chunk])
            ).astype(jnp.bfloat16)
        own_grads = jnp.where(head, grad_ref[0], jnp.zeros((), jnp.bfloat16))
        own_queries = jnp.where(head, qkv_ref[0, :, :PAD], jnp.zeros((), jnp.bfloat16))
        value_grad = value_grad + product(probs[...], own_grads)
        key_grad = key_grad + product(slopes[...], own_queries)
        turned[h * HD : (h + 1) * HD, :] = product(
            keys_t[h * HD : (h + 1) * HD, :], slopes[...]
        )
    turned[GC:, :] = jnp.zeros((PAD - GC, rows), jnp.float32)
    query_grad = turned[...].T * score_scale
    joined_ref[0, :, :PAD] = query_grad.astype(jnp.bfloat16)
    joined_ref[0, :, PAD : 2 * PAD] = (key_grad * score_scale).astype(jnp.bfloat16)
    joined_ref[0, :, 2 * PAD :] = value_grad.astype(jnp.bfloat16)
    sums_ref[0, 0:1, :] = jnp.sum(query_grad, axis=0, keepdims=True)
    sums_ref[0, 1:2, :] = jnp.sum(value_grad, axis=0, keepdims=True)


def attend_backward(qkv, bias, heads_out, lse, heads_grad):
    rows = qkv.shape[1]
    return pl.pallas_call(
        attend_backward_kernel,
        grid=(GROUPS,),
        in_specs=[
            pl.BlockSpec((rows, 1), lambda g: (0, 0)),
            pl.BlockSpec((1, rows, 3 * PAD), lambda g: (g, 0, 0)),
            pl.BlockSpec((1, rows, PAD), lambda g: (g, 0, 0)),
            pl.BlockSpec((1, 8, rows), lambda g: (g, 0, 0)),
            pl.BlockSpec((1, rows, PAD), lambda g: (g, 0, 0)),
        ],
        out_specs=[
            pl.BlockSpec((1, rows, 3 * PAD), lambda g: (g, 0, 0)),
            pl.BlockSpec((1, 8, PAD), lambda g: (g, 0, 0)),
        ],
        out_shape=[
            jax.ShapeDtypeStruct((GROUPS, rows, 3 * PAD), jnp.bfloat16),
            jax.ShapeDtypeStruct((GROUPS, 8, PAD), jnp.float32),
        ],
        scratch_shapes=[
            pltpu.VMEM((rows, rows), jnp.bfloat16),
            pltpu.VMEM((rows, rows), jnp.bfloat16),
            pltpu.VMEM((PAD, rows), jnp.float32),
        ],
        cost_estimate=pl.CostEstimate(
            flops=30_000_000_000, bytes_accessed=20_000_000, transcendentals=12_000_000
        ),
    )(bias, qkv, heads_out, lse, heads_grad)


def swap_with_partner(values):
    size = lax.axis_size("mp")
    return lax.ppermute(values, "mp", [(i, i ^ 1) for i in range(size)])


def pad_heads(values):
    return jnp.pad(values, [(0, 0)] * (values.ndim - 1) + [(0, PAD - values.shape[-1])])


MESH = pl.DeviceIdType.MESH


def positions():
    mp, dp = lax.axis_index("mp"), lax.axis_index("dp")
    return mp, lax.div(mp, 2), lax.rem(mp, 2), lax.div(dp, 2), lax.rem(dp, 2)


def at_place(x, c, z, y):
    return (2 * z + y, 2 * x + c)


def neighbours(nz):
    mp, x, c, z, y = positions()
    first = at_place(lax.rem(x + c, 2), c, z, lax.rem(y + 1 - c, 2))
    second = at_place(lax.rem(x + 1 - c, 2), c, z, lax.rem(y + c, 2))
    partner = at_place(x, 1 - c, z, y)
    along = [at_place(x, c, lax.rem(z + d, nz), y) for d in range(1, nz)]
    return first, second, partner, along


def meet(devices):
    barrier = pltpu.get_barrier_semaphore()
    for device in devices:
        pl.semaphore_signal(barrier, inc=1, device_id=device, device_id_type=MESH)
    pl.semaphore_wait(barrier, len(devices))


def regions(x, c, y):
    own = (x, y)
    first = (lax.rem(x + c, 2), lax.rem(y + 1 - c, 2))
    second = (lax.rem(x + 1 - c, 2), lax.rem(y + c, 2))
    third = (1 - x, 1 - y)
    return own, first, second, third


def gather_kernel(nz, parts, *refs):
    shards, fulls = refs[:parts], refs[parts : 2 * parts]
    own_sem, z_send, z_recv, send, recv = refs[2 * parts :]
    mp, x, c, z, y = positions()
    first, second, partner, along = neighbours(nz)
    meet([first, second, partner, *along])
    own, got1, got2, got3 = regions(x, c, y)
    other = regions(x, 1 - c, y)

    def remote(src, dst, s, r, device):
        return pltpu.make_async_remote_copy(
            src_ref=src, dst_ref=dst, send_sem=s, recv_sem=r, device_id=device, device_id_type=MESH
        )

    started = []
    locals_ = []
    spread = []
    for p in range(parts):
        keep = pltpu.make_async_copy(shards[p], fulls[p].at[x, c, z, y], own_sem.at[p])
        keep.start()
        locals_.append(keep)
        sends = [
            remote(shards[p], fulls[p].at[x, c, z, y], z_send.at[p, d], z_recv.at[p, d], along[d])
            for d in range(nz - 1)
        ]
        for copy in sends:
            copy.start()
        spread.append(sends)

    def block(p, core, place):
        return fulls[p].at[place[0], core, :, place[1]]

    def push(p, k, core, place, device):
        copy = remote(block(p, core, place), block(p, core, place), send.at[p, k], recv.at[p, k], device)
        copy.start()
        started.append(copy)
        return copy

    def arrived(p, k, core, place):
        here = block(p, core, place)
        remote(here, here, send.at[p, k], recv.at[p, k], first).wait_recv()

    for p in range(parts):
        locals_[p].wait()
        for copy in spread[p]:
            copy.wait_recv()
        push(p, 0, c, own, first)
        push(p, 1, c, own, second)
        push(p, 3, c, own, partner)
    for p in range(parts):
        arrived(p, 0, c, got1)
        push(p, 2, c, got1, second)
        push(p, 4, c, got1, partner)
    for p in range(parts):
        arrived(p, 1, c, got2)
        push(p, 5, c, got2, partner)
        arrived(p, 2, c, got3)
        push(p, 6, c, got3, partner)
    for p in range(parts):
        for k in range(4):
            arrived(p, 3 + k, 1 - c, other[k])
    for sends in spread:
        for copy in sends:
            copy.wait_send()
    for copy in started:
        copy.wait_send()


def gather_all(shards):
    n_dp = lax.axis_size("dp")
    nz, parts = n_dp // 2, len(shards)
    return pl.pallas_call(
        functools.partial(gather_kernel, nz, parts),
        in_specs=[pl.BlockSpec(memory_space=pltpu.VMEM)] * parts,
        out_specs=[pl.BlockSpec(memory_space=pl.ANY)] * parts,
        out_shape=[jax.ShapeDtypeStruct((2, 2, nz, 2, *s.shape), s.dtype) for s in shards],
        scratch_shapes=[
            pltpu.SemaphoreType.DMA((parts,)),
            pltpu.SemaphoreType.DMA((parts, nz - 1)),
            pltpu.SemaphoreType.DMA((parts, nz - 1)),
            pltpu.SemaphoreType.DMA((parts, 7)),
            pltpu.SemaphoreType.DMA((parts, 7)),
        ],
        compiler_params=pltpu.CompilerParams(collective_id=0, has_side_effects=True),
    )(*shards)


def scatter_kernel(nz, parts, side, *refs):
    partials, results = refs[:parts], refs[parts : 2 * parts]
    at = 2 * parts
    sums, heard1, heard2, heard3, heard4 = (
        refs[at + i * parts : at + (i + 1) * parts] for i in range(5)
    )
    own_sem, send, recv, z_send, z_recv = refs[at + 5 * parts :]
    mp, x, c, z, y = positions()
    first, second, partner, along = neighbours(nz)
    meet([first, second, partner, *along])
    own, got1, got2, got3 = regions(x, c, y)
    started = []

    def remote(src, dst, s, r, device):
        copy = pltpu.make_async_remote_copy(
            src_ref=src, dst_ref=dst, send_sem=s, recv_sem=r, device_id=device, device_id_type=MESH
        )
        copy.start()
        started.append(copy)
        return copy

    def add(p, place, more):
        for i in range(nz):
            here = sums[p].at[place[0], i, place[1]]
            here[...] = (here[...].astype(jnp.float32) + more[i].astype(jnp.float32)).astype(here.dtype)

    def cut(p, k, core):
        if p not in side:
            return partials[p].at[k, core]
        size = partials[p].shape[3] // 4
        return partials[p].at[:, :, :, pl.ds(pl.multiple_of((2 * k + core) * size, size), size)]

    kept, core_copies = [], []
    for p in range(parts):
        copies = []
        for k in range(2):
            keep = pltpu.make_async_copy(cut(p, k, c), sums[p].at[k], own_sem.at[p, k])
            keep.start()
            copies.append(keep)
        kept.append(copies)
        core_copies.append(
            [
                remote(cut(p, k, 1 - c), heard1[p].at[k], send.at[p, k], recv.at[p, k], partner)
                for k in range(2)
            ]
        )
    second_copies = []
    for p in range(parts):
        for copy in kept[p]:
            copy.wait()
        for copy in core_copies[p]:
            copy.wait_recv()
        copies = []
        for k, place in enumerate((got2, got3)):
            add(p, place, heard1[p].at[place[0], :, place[1]])
            copies.append(
                remote(
                    sums[p].at[place[0], :, place[1]],
                    heard2[p].at[k],
                    send.at[p, 2 + k],
                    recv.at[p, 2 + k],
                    second,
                )
            )
        second_copies.append(copies)
        for place in (got1, own):
            add(p, place, heard1[p].at[place[0], :, place[1]])
    first_copies = []
    for p in range(parts):
        second_copies[p][1].wait_recv()
        add(p, got1, heard2[p].at[1])
        first_copies.append(
            remote(sums[p].at[got1[0], :, got1[1]], heard3[p], send.at[p, 4], recv.at[p, 4], first)
        )
        second_copies[p][0].wait_recv()
        add(p, own, heard2[p].at[0])
    last_copies = []
    for p in range(parts):
        first_copies[p].wait_recv()
        add(p, own, heard3[p])
        last_copies.append(
            [
                remote(
                    sums[p].at[x, lax.rem(z + d + 1, nz), y],
                    heard4[p].at[d],
                    z_send.at[p, d],
                    z_recv.at[p, d],
                    along[d],
                )
                for d in range(nz - 1)
            ]
        )
    for p in range(parts):
        for copy in last_copies[p]:
            copy.wait_recv()
        total = sums[p][x, z, y].astype(jnp.float32)
        for d in range(nz - 1):
            total = total + heard4[p][d].astype(jnp.float32)
        results[p][...] = total
    for copy in started:
        copy.wait_send()


def scatter_sums(partials, side=()):
    nz, parts = lax.axis_size("dp") // 2, len(partials)
    tails = [
        (p.shape[2], p.shape[3] // 4) if i in side else p.shape[4:] for i, p in enumerate(partials)
    ]
    kinds = [p.dtype for p in partials]
    return pl.pallas_call(
        functools.partial(scatter_kernel, nz, parts, side),
        in_specs=[pl.BlockSpec(memory_space=pl.ANY)] * parts,
        out_specs=[pl.BlockSpec(memory_space=pltpu.VMEM)] * parts,
        out_shape=[jax.ShapeDtypeStruct(t, jnp.float32) for t in tails],
        scratch_shapes=[
            *[pltpu.VMEM((2, nz, 2, *t), k) for t, k in zip(tails, kinds)],
            *[pltpu.VMEM((2, nz, 2, *t), k) for t, k in zip(tails, kinds)],
            *[pltpu.VMEM((2, nz, *t), k) for t, k in zip(tails, kinds)],
            *[pltpu.VMEM((nz, *t), k) for t, k in zip(tails, kinds)],
            *[pltpu.VMEM((nz - 1, *t), k) for t, k in zip(tails, kinds)],
            pltpu.SemaphoreType.DMA((parts, 2)),
            pltpu.SemaphoreType.DMA((parts, 5)),
            pltpu.SemaphoreType.DMA((parts, 5)),
            pltpu.SemaphoreType.DMA((parts, nz - 1)),
            pltpu.SemaphoreType.DMA((parts, nz - 1)),
        ],
        compiler_params=pltpu.CompilerParams(
            collective_id=1, has_side_effects=True, vmem_limit_bytes=60 * 1024 * 1024
        ),
    )(*partials)


def in_place_order(blocks):
    return blocks.reshape(2, 2, blocks.shape[1] // 2, 2, *blocks.shape[2:])


def body_any(
    tokens,
    cotangent,
    lengths,
    w_query,
    w_key,
    w_value,
    w_out,
    w_up,
    w_down,
    b_query,
    b_value,
    b_up,
    b_out,
    b_down,
    norm1_gain,
    norm1_shift,
    norm2_gain,
    norm2_shift,
):
    half_rows = tokens.shape[1]
    width = tokens.shape[2]
    n_dp, n_mp = lax.axis_size("dp"), lax.axis_size("mp")
    unit_cols = w_up.shape[1]
    mp_index = lax.axis_index("mp")
    half = lax.rem(mp_index, 2)
    seq = lax.div(mp_index, 2)

    def own_of(pair):
        return jnp.where(half == 0, pair[0], pair[1])

    def other_of(pair):
        return jnp.where(half == 0, pair[1], pair[0])

    rows_in = jnp.concatenate([own_of(tokens), swap_with_partner(other_of(tokens))], axis=0)
    rows_cot = jnp.concatenate([own_of(cotangent), swap_with_partner(other_of(cotangent))], axis=0)
    length = lax.dynamic_slice(lengths, (half, seq), (1, 1))[0, 0]
    place = jnp.arange(half_rows, dtype=jnp.int32)
    place = jnp.concatenate([place + half * half_rows, place + (1 - half) * half_rows])
    valid_row = (place < length)[:, None]
    bias = jnp.where(valid_row, 0.0, masked_score).astype(jnp.bfloat16)
    valid_row = valid_row.astype(jnp.float32)

    biases = jnp.pad(jnp.concatenate([b_query, b_value, b_up]), (0, 896)).reshape(16, 128)
    qkv_shard = jnp.concatenate([w_query, w_key, w_value], axis=1)
    gathered = gather_all([qkv_shard, w_out, w_up, w_down, biases])
    full_qkv, full_out, full_up, full_down, full_bias = (
        g.reshape(n_mp, n_dp, *g.shape[4:]) for g in gathered
    )
    full_qkv = full_qkv.reshape(n_mp, width, 3, GC)
    w_joined = pad_heads(full_qkv).reshape(n_mp, width, 3 * PAD)
    full_out = full_out.reshape(n_mp, GC, width)
    out_pad = jnp.pad(full_out, ((0, 0), (0, PAD - GC), (0, 0))).reshape(n_mp * PAD, width)
    full_up = full_up.reshape(n_mp, width, unit_cols).transpose(1, 0, 2).reshape(width, n_mp * unit_cols)
    full_down = full_down.reshape(n_mp * unit_cols, width)
    full_bias = full_bias[:, 0].reshape(n_mp, -1)
    bias_q, bias_v, bias_up = full_bias[:, :GC], full_bias[:, GC:2*GC], full_bias[:, 2*GC:2*GC+unit_cols]
    mark = jnp.zeros((n_mp, PAD - GC), jnp.float32).at[:, 0].set(1.0)
    joined_bias = jnp.concatenate(
        [bias_q, mark, jnp.zeros((n_mp, PAD), jnp.float32), pad_heads(bias_v)], axis=1
    )

    qkv = lax.dot_general(
        jnp.broadcast_to(rows_in[None], (n_mp, *rows_in.shape)),
        w_joined,
        (((2,), (1,)), ((0,), (0,))),
        preferred_element_type=jnp.float32,
    )
    qkv = (qkv + joined_bias[:, None, :]).astype(jnp.bfloat16)
    heads_out, lse = attend_forward(qkv, bias)
    heads_flat = heads_out.transpose(1, 0, 2).reshape(2 * half_rows, n_mp * PAD)
    attention = product(heads_flat, out_pad) + b_out
    first_norm, first_scaled, first_inverse = layer_norm(
        rows_in.astype(jnp.float32) + attention, norm1_gain, norm1_shift
    )
    first_low = first_norm.astype(jnp.bfloat16)
    preact = product(first_low, full_up) + bias_up.reshape(-1)
    cumulative = 0.5 * (1.0 + lax.erf(preact * 0.7071067811865476))
    active = (preact * cumulative).astype(jnp.bfloat16)
    slope = cumulative + preact * (jnp.exp(-0.5 * preact * preact) * 0.3989422804014327)
    ffn_out = product(active, full_down) + b_down
    stream = first_norm + ffn_out
    final_norm, final_scaled, final_inverse = layer_norm(stream, norm2_gain, norm2_shift)
    output = final_norm.astype(jnp.bfloat16)
    squares = jnp.stack(
        [
            jnp.sum(valid_row * stream * stream),
            jnp.sum(valid_row * attention * attention),
            jnp.sum(valid_row * ffn_out * ffn_out),
            jnp.sum(valid_row),
        ]
    )

    stream_grad, gain2_grad, shift2_grad = norm_back(
        rows_cot.astype(jnp.float32), final_scaled, final_inverse, norm2_gain
    )
    down_bias_grad = jnp.sum(stream_grad, axis=0)
    ffn_grad_low = stream_grad.astype(jnp.bfloat16)
    active_grad = contract_cols(ffn_grad_low, full_down)
    down_wgrad = contract_rows(active, ffn_grad_low)
    preact_grad = active_grad * slope
    up_bias_grad = jnp.sum(preact_grad, axis=0)
    preact_low = preact_grad.astype(jnp.bfloat16)
    up_wgrad = contract_rows(first_low, preact_low)
    first_grad = stream_grad + contract_cols(preact_low, full_up)
    attn_grad, gain1_grad, shift1_grad = norm_back(
        first_grad, first_scaled, first_inverse, norm1_gain
    )
    out_bias_grad = jnp.sum(attn_grad, axis=0)
    attn_grad_low = attn_grad.astype(jnp.bfloat16)
    out_wgrad = contract_rows(heads_flat, attn_grad_low)
    heads_grad = contract_cols(attn_grad_low, out_pad).astype(jnp.bfloat16)
    heads_grad = heads_grad.reshape(2 * half_rows, n_mp, PAD).transpose(1, 0, 2)
    joined, sums = attend_backward(qkv, bias, heads_out, lse, heads_grad)
    joined_wgrad = lax.dot_general(
        jnp.broadcast_to(rows_in[None], (n_mp, *rows_in.shape)),
        joined,
        (((1,), (1,)), ((0,), (0,))),
        preferred_element_type=jnp.float32,
    )
    tokens_grad = attn_grad + jnp.sum(
        lax.dot_general(
            joined, w_joined, (((2,), (2,)), ((0,), (0,))), preferred_element_type=jnp.float32
        ),
        axis=0,
    )

    low = jnp.bfloat16
    joined_blocks = (
        joined_wgrad.astype(low)
        .reshape(n_mp, n_dp, width // n_dp, 3, PAD)[..., :GC]
        .reshape(n_mp, n_dp, width // n_dp, 3 * GC)
    )
    out_blocks = (
        out_wgrad.astype(low)
        .reshape(n_mp, PAD, width)[:, :GC]
        .reshape(n_mp, n_dp, GC // n_dp, width)
    )
    up_blocks = up_wgrad.astype(low).reshape(n_dp, width // n_dp, n_mp, unit_cols).transpose(2, 0, 1, 3)
    down_blocks = down_wgrad.astype(low).reshape(n_mp, n_dp, unit_cols // n_dp, width)

    def by_mp(vector):
        return vector.reshape(n_mp, n_dp, -1)

    def by_dp(vector):
        return vector.reshape(n_dp, n_mp, -1).transpose(1, 0, 2)

    vectors = [by_mp(sums[:, 0, :GC]), by_mp(sums[:, 1, :GC]), by_mp(up_bias_grad)]
    vectors += [
        by_dp(v)
        for v in (out_bias_grad, down_bias_grad, gain1_grad, shift1_grad, gain2_grad, shift2_grad)
    ]
    vectors.append(jnp.broadcast_to(squares, (n_mp, n_dp, 4)))
    ends = [v.shape[-1] for v in vectors]
    vectors = jnp.concatenate(vectors, axis=-1)
    vectors = jnp.pad(vectors, ((0, 0), (0, 0), (0, 1024 - vectors.shape[-1])))
    vectors = vectors.reshape(n_mp, n_dp, 8, 128)
    own_down, own_up, own_out, own_joined, own_vector = scatter_sums(
        [
            in_place_order(b)
            for b in (down_blocks, up_blocks, out_blocks, joined_blocks, vectors)
        ]
    )
    own_vector = own_vector.reshape(-1)
    own_vectors, start = [], 0
    for size in ends:
        own_vectors.append(own_vector[start : start + size])
        start += size
    totals = own_vectors.pop()
    rms_values = jnp.sqrt(totals[:3] / (totals[3] * width))

    def back_home(rows):
        mine, sent = rows[:half_rows], swap_with_partner(rows[half_rows:])
        return jnp.where(half == 0, jnp.stack([mine, sent]), jnp.stack([sent, mine]))

    return (
        back_home(output),
        back_home(tokens_grad),
        own_joined[:, :GC],
        own_joined[:, GC : 2 * GC],
        own_joined[:, 2 * GC :],
        own_out,
        own_up,
        own_down,
        *own_vectors,
        rms_values,
    )


PARTS = 4


def remote_copy(src, dst, s, r, device):
    return pltpu.make_async_remote_copy(
        src_ref=src, dst_ref=dst, send_sem=s, recv_sem=r, device_id=device, device_id_type=MESH
    )


def forward_kernel(
    nz,
    lengths,
    tokens,
    cotangent,
    shard_q,
    shard_o,
    shard_u,
    shard_d,
    bias_shard,
    full_q,
    full_o,
    full_u,
    full_d,
    bias_full,
    rows_out,
    cot_out,
    w_out,
    qkv_out,
    heads_out,
    lse_out,
    rows,
    cots,
    w_got,
    w_pad,
    qkv,
    values_t,
    turned,
    heads,
    own_sem,
    z_send,
    z_recv,
    relay_send,
    send,
    recv,
    swap_send,
    swap_recv,
    bias_send,
    bias_recv,
    out_sem,
):
    shards = (shard_q, shard_o, shard_u, shard_d)
    fulls = (full_q, full_o, full_u, full_d)
    half_rows = tokens.shape[1]
    length = 2 * half_rows
    mp, x, c, z, y = positions()
    half = c
    seq = x
    first, second, partner, along = neighbours(nz)
    across = at_place(1 - x, c, z, y)
    slanted = at_place(1 - x, 1 - c, z, y)
    own, got1, got2, got3 = regions(x, c, y)
    other = regions(x, 1 - c, y)
    meet([first, second, partner, slanted, *along])

    def block(p, core, place, d):
        return fulls[p].at[place[0], core, lax.rem(z + nz - d, nz), place[1]]

    places = (own, own, got1, own, got1, got2, got3)
    targets = (first, second, second, partner, partner, partner, partner)
    landing = (got1, got2, got3, *other)
    cores = (c, c, c, 1 - c, 1 - c, 1 - c, 1 - c)

    def outgoing(p, k, d):
        here = block(p, c, places[k], d)
        return remote_copy(here, here, send.at[p, k, d], recv.at[p, k, d], targets[k])

    def incoming(p, k, d):
        here = block(p, cores[k], landing[k], d)
        return remote_copy(here, here, send.at[p, k, d], recv.at[p, k, d], targets[k])

    at_low = 1 - lax.div(z + nz - 1, nz)
    near, far = 1 + 2 * at_low, 3 - 2 * at_low

    def z_copy(p, d):
        return remote_copy(
            shards[p], fulls[p].at[x, c, z, y], z_send.at[p, d - 1], z_recv.at[p, d - 1], along[d - 1]
        )

    def z_each(p, act):
        act(z_copy(p, 2))
        pl.when(z != nz - 1)(lambda: act(z_copy(p, 1)))
        pl.when(z != 0)(lambda: act(z_copy(p, 3)))

    def z_start(p):
        z_each(p, lambda copy: copy.start())

    def z_relay(p, low):
        here = block(p, c, own, 2)
        d = 1 if low else 3
        return remote_copy(here, here, relay_send.at[p], z_recv.at[p, d - 1], at_place(x, c, z + d - 2, y))

    def spread(p, d):
        if not (isinstance(d, int) and d == 0):
            here = block(p, c, own, d)
            remote_copy(here, here, z_send.at[p, d - 1], z_recv.at[p, d - 1], first).wait_recv()
        if isinstance(d, int) and d == 2:
            pl.when(z == 1)(lambda: z_relay(p, True).start())
            pl.when(z == 2)(lambda: z_relay(p, False).start())
        for k in (0, 1, 3):
            outgoing(p, k, d).start()

    def forward1(p):
        for d in range(nz):
            incoming(p, 0, d).wait_recv()
            outgoing(p, 2, d).start()
            outgoing(p, 4, d).start()

    def forward2(p):
        for d in range(nz):
            incoming(p, 1, d).wait_recv()
            outgoing(p, 5, d).start()

    def forward3(p):
        for d in range(nz):
            incoming(p, 2, d).wait_recv()
            outgoing(p, 6, d).start()

    def take(p, k):
        for d in range(nz):
            incoming(p, k, d).wait_recv()

    keep = [
        pltpu.make_async_copy(shards[p], fulls[p].at[x, c, z, y], own_sem.at[p]) for p in range(PARTS)
    ]
    keep_rows = pltpu.make_async_copy(tokens.at[half], rows.at[pl.ds(0, half_rows)], own_sem.at[PARTS])
    keep_cots = pltpu.make_async_copy(cotangent.at[half], cots.at[pl.ds(0, half_rows)], own_sem.at[PARTS + 2])
    swap_rows = remote_copy(
        tokens.at[1 - half], rows.at[pl.ds(half_rows, half_rows)], swap_send.at[0], swap_recv.at[0], partner
    )
    swap_cot = remote_copy(
        cotangent.at[1 - half], cots.at[pl.ds(half_rows, half_rows)], swap_send.at[1], swap_recv.at[1], partner
    )
    bias_copies = [
        remote_copy(bias_shard, bias_full.at[mp], bias_send.at[k], bias_recv.at[k], device)
        for k, device in enumerate((partner, across, slanted))
    ]
    z_start(0)
    keep[0].start()
    for copy in bias_copies:
        copy.start()
    swap_rows.start()
    keep_rows.start()
    for p in range(1, PARTS):
        keep[p].start()
    keep[0].wait()
    spread(0, 0)
    for p in range(1, PARTS):
        z_start(p)
    w_pad[...] = jnp.zeros_like(w_pad)
    turned[...] = jnp.zeros_like(turned)
    bias_full[mp] = bias_shard[...]
    for d in (2, near, far):
        spread(0, d)
    for copy in keep[1:]:
        copy.wait()
    forward1(0)
    for p in range(1, PARTS):
        spread(p, 0)
    forward2(0)
    swap_cot.start()
    keep_cots.start()
    keep_rows.wait()
    swap_rows.wait_recv()
    rows_copy = pltpu.make_async_copy(rows, rows_out, out_sem.at[2])
    rows_copy.start()
    cots_copy = pltpu.make_async_copy(cots, cot_out, out_sem.at[4])
    for copy in bias_copies:
        copy.wait_recv()

    hooks = {
        0: [lambda: [spread(1, d) for d in (2, near, far)]],
        1: [lambda: forward3(0)],
        2: [lambda: [spread(2, d) for d in (2, near)]],
        3: [lambda: spread(2, far), lambda: forward1(1)],
        4: [lambda: forward2(1), lambda: forward3(1)],
        5: [lambda: [spread(3, d) for d in (2, near)]],
        6: [lambda: spread(3, far)],
        7: [lambda: forward1(2)],
        8: [lambda: forward2(2)],
        10: [lambda: forward1(3)],
        11: [lambda: forward2(3)],
    }
    seq_length = lengths[half, seq]
    row = lax.broadcasted_iota(jnp.int32, (length, 1), 0)
    place = jnp.where(row < half_rows, row + half * half_rows, row - half * half_rows)
    bias = jnp.where(place < seq_length, 0.0, masked_score).astype(jnp.bfloat16)
    lane = lax.broadcasted_iota(jnp.int32, (1, PAD), 1)
    chunk = 256

    def heads_copy(gx, gc):
        columns = pl.ds(pl.multiple_of((2 * gx + gc) * PAD, PAD), PAD)
        return pltpu.make_async_copy(heads, heads_out.at[:, columns], out_sem.at[0])

    def qkv_copy(gx, gc):
        return pltpu.make_async_copy(qkv, qkv_out.at[2 * gx + gc], out_sem.at[1])

    def w_copy(gx, gc):
        return pltpu.make_async_copy(w_pad, w_out.at[2 * gx + gc], out_sem.at[3])

    def group_step(r, carry):
        gx, gc = lax.rem(x + lax.div(r, 2), 2), lax.rem(c + lax.rem(r, 2), 2)
        group = 2 * gx + gc

        @pl.when(r == 1)
        def _():
            for d in range(nz):
                incoming(0, 3, d).wait_recv()
            for d in range(nz):
                here = block(0, 1 - c, own, d)
                remote_copy(here, here, send.at[0, 5 - c, d], recv.at[0, 5 - c, d], first).wait_recv()

        @pl.when(r == 3)
        def _():
            for d in range(nz):
                here = block(0, 1 - c, own, d)
                remote_copy(here, here, send.at[0, 4 + c, d], recv.at[0, 4 + c, d], first).wait_recv()
            take(0, 6)

        load = pltpu.make_async_copy(full_q.at[gx, gc], w_got, own_sem.at[PARTS + 1])
        load.start()
        load.wait()

        @pl.when(r > 0)
        def _():
            qkv_copy(gx, gc).wait()
            w_copy(gx, gc).wait()

        w_flat = w_got[...].reshape(-1, 3 * GC)
        for k in range(3):
            w_pad[:, k * PAD : k * PAD + GC] = w_flat[:, k * GC : (k + 1) * GC]
        w_copy(gx, gc).start()
        joined_bias = bias_full[group, 0:1, :]
        for at in range(0, length, 512):
            qkv[at : at + 512, :] = (product(rows[at : at + 512, :], w_pad[...]) + joined_bias).astype(
                jnp.bfloat16
            )
        qkv_copy(gx, gc).start()
        values_t[...] = qkv[:, 2 * PAD :].T

        def head_step(h, carry):
            for k, todo in hooks.items():
                if todo:

                    @pl.when(r * GH + h == k)
                    def _():
                        for task in todo:
                            task()

            start = h * HD
            keys = qkv[:, PAD : 2 * PAD]
            kept = jnp.where((lane >= start) & (lane < start + HD), keys, jnp.zeros_like(keys))
            own_keys = jnp.where(lane == GC, bias, kept)
            own_values = values_t[pl.ds(pl.multiple_of(start, HD), HD), :]
            for at in range(0, length, chunk):
                scores = contract_cols(own_keys, qkv[at : at + chunk, :PAD])
                top = jnp.max(scores, axis=0, keepdims=True) * exp2_scale
                raised = jnp.exp2(scores * exp2_scale - top)
                total = jnp.sum(raised, axis=0, keepdims=True)
                mixed = product(own_values, raised.astype(jnp.bfloat16))
                turned[pl.ds(pl.multiple_of(start, HD), HD), at : at + chunk] = mixed / total
                lse_out[group, pl.ds(h, 1), at : at + chunk] = top + jnp.log2(total)
            return carry

        lax.fori_loop(0, GH, head_step, 0)

        @pl.when(r > 0)
        def _():
            heads_copy(gx, gc).wait()

        heads[...] = turned[...].T.astype(jnp.bfloat16)
        heads_copy(gx, gc).start()
        return carry

    lax.fori_loop(0, GROUPS, group_step, 0)
    keep_cots.wait()
    swap_cot.wait_recv()
    cots_copy.start()
    forward3(2)
    forward3(3)
    for p in range(1, PARTS):
        for k in range(3, 7):
            take(p, k)
    heads_copy(x, c).wait()
    qkv_copy(x, c).wait()
    w_copy(x, c).wait()
    rows_copy.wait()
    cots_copy.wait()
    swap_cot.wait_send()
    swap_rows.wait_send()
    for copy in bias_copies:
        copy.wait_send()
    for p in range(PARTS):
        z_each(p, lambda copy: copy.wait_send())
        pl.when(z == 1)(lambda: z_relay(p, True).wait_send())
        pl.when(z == 2)(lambda: z_relay(p, False).wait_send())
        for k in range(7):
            for d in range(nz):
                outgoing(p, k, d).wait_send()


def forward_attention(lengths, tokens, cotangent, shards, bias_shard):
    nz = lax.axis_size("dp") // 2
    half_rows, width = tokens.shape[1:]
    rows = 2 * half_rows
    low = jnp.bfloat16
    anywhere, vmem = pl.BlockSpec(memory_space=pl.ANY), pl.BlockSpec(memory_space=pltpu.VMEM)
    dma = pltpu.SemaphoreType.DMA
    return pl.pallas_call(
        functools.partial(forward_kernel, nz),
        in_specs=[pl.BlockSpec(memory_space=pltpu.SMEM), anywhere, anywhere, *[vmem] * 5],
        out_specs=[*[anywhere] * PARTS, vmem, *[anywhere] * 5, vmem],
        out_shape=[
            *[jax.ShapeDtypeStruct((2, 2, nz, 2, *s.shape), s.dtype) for s in shards],
            jax.ShapeDtypeStruct((GROUPS, *bias_shard.shape), jnp.float32),
            jax.ShapeDtypeStruct((rows, width), low),
            jax.ShapeDtypeStruct((rows, width), low),
            jax.ShapeDtypeStruct((GROUPS, width, 3 * PAD), low),
            jax.ShapeDtypeStruct((GROUPS, rows, 3 * PAD), low),
            jax.ShapeDtypeStruct((rows, GROUPS * PAD), low),
            jax.ShapeDtypeStruct((GROUPS, 8, rows), jnp.float32),
        ],
        scratch_shapes=[
            pltpu.VMEM((rows, width), low),
            pltpu.VMEM((rows, width), low),
            pltpu.VMEM((nz, 2, *shards[0].shape), low),
            pltpu.VMEM((width, 3 * PAD), low),
            pltpu.VMEM((rows, 3 * PAD), low),
            pltpu.VMEM((PAD, rows), low),
            pltpu.VMEM((PAD, rows), jnp.float32),
            pltpu.VMEM((rows, PAD), low),
            dma((PARTS + 3,)),
            dma((PARTS, nz - 1)),
            dma((PARTS, nz - 1)),
            dma((PARTS,)),
            dma((PARTS, 7, nz)),
            dma((PARTS, 7, nz)),
            dma((2,)),
            dma((2,)),
            dma((3,)),
            dma((3,)),
            dma((5,)),
        ],
        compiler_params=pltpu.CompilerParams(
            collective_id=2, has_side_effects=True, vmem_limit_bytes=60 * 1024 * 1024
        ),
    )(lengths, tokens, cotangent, *shards, bias_shard)


def place_of(info_ref, row, half_rows):
    half = info_ref[1]
    return jnp.where(row < half_rows, row + half * half_rows, row - half * half_rows)


def dense_kernel(
    info_ref,
    heads_ref,
    rows_ref,
    cot_ref,
    out_w,
    up_w,
    down_w,
    vec_ref,
    bias_ref,
    output_ref,
    first_ref,
    active_ref,
    ffn_low_ref,
    preact_low_ref,
    attn_ref,
    attn_low_ref,
    heads_grad_ref,
    sums_ref,
    slope,
):
    t = pl.program_id(0)
    low = jnp.bfloat16
    tile, width = rows_ref.shape
    units = up_w.shape[2]
    b_out, b_down, gain1, shift1, gain2, shift2 = (vec_ref[k : k + 1, :] for k in range(6))

    @pl.when(t == 0)
    def _():
        sums_ref[...] = jnp.zeros_like(sums_ref)

    def count(k, values):
        sums_ref[k : k + 1, :] += jnp.sum(values, axis=0, keepdims=True)

    attention = product(heads_ref[...], out_w[...]) + b_out
    first_norm, first_scaled, first_inverse = layer_norm(
        rows_ref[...].astype(jnp.float32) + attention, gain1, shift1
    )
    first_low = first_norm.astype(low)
    first_ref[...] = first_low
    ffn_out = jnp.broadcast_to(b_down, (tile, width))
    for g in range(GROUPS):
        preact = product(first_low, up_w[g]) + bias_ref[g, 1:2, :]
        cumulative = 0.5 * (1.0 + lax.erf(preact * 0.7071067811865476))
        active = (preact * cumulative).astype(low)
        active_ref[:, g * units : (g + 1) * units] = active
        slope[:, g * units : (g + 1) * units] = cumulative + preact * (
            jnp.exp(-0.5 * preact * preact) * 0.3989422804014327
        )
        ffn_out = ffn_out + product(active, down_w[g])
    stream = first_norm + ffn_out
    row = lax.broadcasted_iota(jnp.int32, (tile, 1), 0) + t * tile
    valid = (place_of(info_ref, row, pl.num_programs(0) * tile // 2) < info_ref[0]).astype(jnp.float32)
    count(6, valid * stream * stream)
    count(7, valid * attention * attention)
    count(8, valid * ffn_out * ffn_out)
    count(9, jnp.broadcast_to(valid, (tile, width)))
    final_norm, final_scaled, final_inverse = layer_norm(stream, gain2, shift2)
    output_ref[...] = final_norm.astype(low)

    def norm_step(k, upstream, scaled, inverse, gain):
        count(k, upstream * scaled)
        count(k + 1, upstream)
        through = upstream * gain
        return inverse * (
            through
            - jnp.mean(through, axis=-1, keepdims=True)
            - scaled * jnp.mean(through * scaled, axis=-1, keepdims=True)
        )

    stream_grad = norm_step(4, cot_ref[...].astype(jnp.float32), final_scaled, final_inverse, gain2)
    count(1, stream_grad)
    ffn_grad_low = stream_grad.astype(low)
    ffn_low_ref[...] = ffn_grad_low
    first_grad = stream_grad
    for g in range(GROUPS):
        preact_grad = contract_cols(ffn_grad_low, down_w[g]) * slope[:, g * units : (g + 1) * units]
        count(12 + g, preact_grad)
        preact_low = preact_grad.astype(low)
        preact_low_ref[:, g * units : (g + 1) * units] = preact_low
        first_grad = first_grad + contract_cols(preact_low, up_w[g])
    attn_grad = norm_step(2, first_grad, first_scaled, first_inverse, gain1)
    count(0, attn_grad)
    attn_ref[...] = attn_grad
    attn_grad_low = attn_grad.astype(low)
    attn_low_ref[...] = attn_grad_low
    heads_grad_ref[...] = contract_cols(attn_grad_low, out_w[...]).astype(low)


def dense(info, heads, rows, cots, out_w, up_w, down_w, vecs, biases):
    count, width = rows.shape
    tile = 256
    units = up_w.shape[2]
    low = jnp.bfloat16

    def whole(shape):
        return pl.BlockSpec(shape, lambda t: (0,) * len(shape))

    def tiled(columns):
        return pl.BlockSpec((tile, columns), lambda t: (t, 0))

    outs = [
        (width, low),
        (width, low),
        (GROUPS * units, low),
        (width, low),
        (GROUPS * units, low),
        (width, jnp.float32),
        (width, low),
        (GROUPS * PAD, low),
    ]
    return pl.pallas_call(
        dense_kernel,
        grid=(count // tile,),
        in_specs=[
            pl.BlockSpec(memory_space=pltpu.SMEM),
            tiled(GROUPS * PAD),
            tiled(width),
            tiled(width),
            whole(out_w.shape),
            whole(up_w.shape),
            whole(down_w.shape),
            whole(vecs.shape),
            whole(biases.shape),
        ],
        out_specs=[*[tiled(columns) for columns, _ in outs], whole((16, width))],
        out_shape=[
            *[jax.ShapeDtypeStruct((count, columns), kind) for columns, kind in outs],
            jax.ShapeDtypeStruct((16, width), jnp.float32),
        ],
        scratch_shapes=[pltpu.VMEM((tile, GROUPS * units), jnp.float32)],
        cost_estimate=pl.CostEstimate(
            flops=22_600_000_000, bytes_accessed=40_000_000, transcendentals=7_000_000
        ),
    )(info, heads, rows, cots, out_w, up_w, down_w, vecs, biases)


BIG = 4


def backward_kernel(
    nz,
    info,
    lse_ref,
    dense_sums,
    rows_in,
    w_joined,
    attn_grad,
    qkv,
    heads,
    heads_grad,
    active,
    ffn_low,
    first_low,
    preact_low,
    attn_low,
    down_out,
    up_out,
    out_out,
    query_out,
    key_out,
    value_out,
    dense_total,
    head_total,
    tokens_out,
    *refs,
):
    parts, heard1, heard2, heard3, heard4 = (refs[BIG * i : BIG * (i + 1)] for i in range(5))
    (
        dense_kept,
        head_kept,
        dense_heard,
        head_heard,
        acc,
        slots,
        right,
        left_t,
        joined,
        heads_in,
        grad_in,
        w_in,
        tokens,
        probs,
        slopes,
        turned,
        crossed,
        keys_t,
        key_acc,
        value_acc,
        send,
        recv,
        z_send,
        z_recv,
        v_send,
        v_recv,
        swap_sem,
        load_sem,
        slot_sem,
        heads_sem,
        grad_sem,
    ) = refs[5 * BIG :]
    low = jnp.bfloat16
    rows, width = tokens.shape
    half_rows = rows // 2
    chunk, span = 256, 384
    mp, x, c, z, y = positions()
    first, second, partner, along = neighbours(nz)
    own, got1, got2, got3 = regions(x, c, y)

    def group_of(r):
        return lax.rem(x + 1 + lax.rem(r, 2), 2), lax.rem(c + 1 + lax.div(r, 2), 2)

    def index_of(r):
        gx, gc = group_of(r)
        return 2 * gx + gc

    def columns(r, size):
        return pl.ds(pl.multiple_of(index_of(r) * size, size), size)

    def load(src, dst, k):
        return pltpu.make_async_copy(src, dst, load_sem.at[k])

    def slot_load(src, s):
        return pltpu.make_async_copy(src, slots.at[s], slot_sem.at[s])

    def active_load(r):
        return slot_load(active.at[:, columns(r, width)], lax.rem(r, 2))

    def preact_load(r):
        return slot_load(preact_low.at[:, columns(r, width)], lax.rem(r, 2))

    def qkv_load(r):
        return slot_load(qkv.at[index_of(r)], lax.rem(r, 2))

    def heads_load(r):
        s = lax.rem(r, 2)
        return pltpu.make_async_copy(heads.at[:, columns(r, PAD)], heads_in.at[s], heads_sem.at[s])

    def grad_load(r):
        s = lax.rem(r, 2)
        return pltpu.make_async_copy(heads_grad.at[:, columns(r, PAD)], grad_in.at[s], grad_sem.at[s])

    def w_load(r):
        return load(w_joined.at[index_of(r)], w_in, 3)

    ffn_load, attn_low_load = load(ffn_low, right, 0), load(attn_low, right, 0)
    first_load, rows_load = load(first_low, joined, 1), load(rows_in, joined, 1)
    tokens_load = load(attn_grad, tokens, 2)

    def core_copy(p, r):
        gx, gc = group_of(r)
        return remote_copy(parts[p].at[gx, gc], heard1[p].at[r], send.at[p, r], recv.at[p, r], partner)

    def second_copy(p, k):
        place = (got2, got3)[k]
        return remote_copy(
            parts[p].at[place[0], c, :, place[1]], heard2[p].at[k], send.at[p, 2 + k], recv.at[p, 2 + k], second
        )

    def first_copy(p):
        return remote_copy(
            parts[p].at[got1[0], c, :, got1[1]], heard3[p], send.at[p, 4], recv.at[p, 4], first
        )

    def z_copy(p, d):
        return remote_copy(
            parts[p].at[x, c, lax.rem(z + d + 1, nz), y],
            heard4[p].at[d],
            z_send.at[p, d],
            z_recv.at[p, d],
            along[d],
        )

    def add(p, place, more):
        for i in range(nz):
            here = parts[p].at[place[0], c, i, place[1]]
            here[...] = (here[...].astype(jnp.float32) + more[i].astype(jnp.float32)).astype(low)

    def take_second(p, k):
        second_copy(p, k).wait_recv()
        add(p, got1 if k else own, heard2[p].at[k])

    def pass_first(p):
        take_second(p, 1)
        first_copy(p).start()

    def take_first(p):
        first_copy(p).wait_recv()
        add(p, own, heard3[p])
        for d in range(nz - 1):
            z_copy(p, d).start()

    def take_z(p):
        total = parts[p][x, c, z, y].astype(jnp.float32)
        for d in range(nz - 1):
            z_copy(p, d).wait_recv()
            total = total + heard4[p][d].astype(jnp.float32)
        if p < BIG - 1:
            (down_out, up_out, out_out)[p][...] = total
        else:
            for k, result in enumerate((query_out, key_out, value_out)):
                result[...] = total[:, k * GC : (k + 1) * GC]

    kept, heard_sums = (dense_kept, head_kept), (dense_heard, head_heard)

    def sums_copy(v, k):
        device = (first, second)[k - 1] if 0 < k < 3 else along[k - 3] if k else partner
        return remote_copy(
            kept[v].at[min(k, 3)], heard_sums[v].at[k], v_send.at[v, k], v_recv.at[v, k], device
        )

    def sums_step(v, k):
        sums_copy(v, k).wait_recv()
        kept[v][k + 1] = kept[v][k] + heard_sums[v][k]
        for later in (k + 1,) if k < 2 else range(3, nz + 2):
            sums_copy(v, later).start()

    def sums_last(v):
        total = kept[v][3]
        for k in range(3, nz + 2):
            sums_copy(v, k).wait_recv()
            total = total + heard_sums[v][k]
        (dense_total, head_total)[v][...] = total

    def finish(p, r):
        gx, gc = group_of(r)
        deep, wide = parts[p].shape[4:]
        pieces = [(0, 0, wide)] if p < BIG - 1 else [(k * GC, k * PAD, GC) for k in range(3)]

        def put(more):
            for i in range(nz):
                for at, source, size in pieces:
                    value = acc[2 * deep * i : 2 * deep * (i + 1), source : source + size].reshape(2, deep, size)
                    if more is not None:
                        value = value + more[i, :, :, at : at + size].astype(jnp.float32)
                    parts[p][gx, gc, i, :, :, at : at + size] = value.astype(low)

        @pl.when(r < 2)
        def _():
            put(None)
            core_copy(p, r).start()

        @pl.when(r >= 2)
        def _():
            core_copy(p, r - 2).wait_recv()
            put(heard1[p].at[r - 2])

        @pl.when(r == 2)
        def _():
            second_copy(p, 1).start()
            pl.when(c == 0)(lambda: second_copy(p, 0).start())

        @pl.when(r == 3)
        def _():
            pl.when(c == 1)(lambda: second_copy(p, 0).start())

    ffn_load.start()
    active_load(0).start()
    heads_load(0).start()
    first_load.start()
    w_load(0).start()
    tokens_load.start()
    meet([first, second, partner, *along])
    dense_kept[0] = dense_sums[...]
    ffn_load.wait()

    def down_step(r, carry):
        active_load(r).wait()
        pl.when(r < 3)(lambda: active_load(r + 1).start())
        pl.when(r == 3)(lambda: preact_load(0).start())
        s = lax.rem(r, 2)
        for at in range(0, width, span):
            acc[at : at + span, :] = product(slots[s, :, at : at + span].T, right[...])
        finish(0, r)
        return carry

    lax.fori_loop(0, GROUPS, down_step, 0)
    sums_copy(0, 0).start()
    attn_low_load.start()
    first_load.wait()
    left_t[...] = joined[...].T
    rows_load.start()

    def up_step(r, carry):
        preact_load(r).wait()
        pl.when(r < 3)(lambda: preact_load(r + 1).start())
        pl.when(r == 3)(lambda: qkv_load(0).start())
        s = lax.rem(r, 2)
        for at in range(0, width, span):
            acc[at : at + span, :] = product(left_t[at : at + span, :], slots[s])
        finish(1, r)
        return carry

    lax.fori_loop(0, GROUPS, up_step, 0)
    sums_step(0, 0)
    attn_low_load.wait()

    def out_step(r, carry):
        heads_load(r).wait()
        heads_load(lax.rem(r + 1, GROUPS)).start()
        acc[:PAD, :] = product(heads_in[lax.rem(r, 2)].T, right[...])
        finish(2, r)
        return carry

    lax.fori_loop(0, GROUPS, out_step, 0)
    grad_load(0).start()
    rows_load.wait()
    left_t[...] = joined[...].T
    tokens_load.wait()

    hooks = {
        0: lambda: sums_step(0, 1),
        1: lambda: (pass_first(0), take_second(0, 0)),
        2: lambda: sums_step(0, 2),
        4: lambda: take_first(0),
        5: lambda: (pass_first(1), take_second(1, 0)),
        6: lambda: (pass_first(2), take_second(2, 0)),
        8: lambda: take_first(1),
        9: lambda: (take_first(2), sums_last(0)),
        10: lambda: take_z(0),
        11: lambda: pl.when(c == 1)(lambda: pass_first(3)),
    }
    row = lax.broadcasted_iota(jnp.int32, (rows, 1), 0)
    bias = jnp.where(place_of(info, row, half_rows) < info[0], 0.0, masked_score).astype(low)
    lane = lax.broadcasted_iota(jnp.int32, (1, PAD), 1)
    turned[...] = jnp.zeros_like(turned)

    def group_step(r, carry):
        s = lax.rem(r, 2)
        group = index_of(r)
        for copy in (qkv_load, heads_load, grad_load):
            copy(r).wait()

        @pl.when(r < 3)
        def _():
            for copy in (qkv_load, heads_load, grad_load):
                copy(r + 1).start()

        crossed[...] = (grad_in[s].astype(jnp.float32) * heads_in[s].astype(jnp.float32)).T
        keys_t[...] = slots[s, :, PAD : 2 * PAD].T
        key_acc[...] = jnp.zeros_like(key_acc)
        value_acc[...] = jnp.zeros_like(value_acc)

        def head_step(h, carry):
            for k, todo in hooks.items():
                pl.when(r * GH + h == k)(todo_of(todo))
            start = pl.multiple_of(h * HD, HD)
            head = (lane >= start) & (lane < start + HD)
            keys = slots[s, :, PAD : 2 * PAD]
            own_keys = jnp.where(lane == GC, bias, jnp.where(head, keys, jnp.zeros_like(keys)))
            own_values = jnp.where(head, slots[s, :, 2 * PAD :], jnp.zeros((), low))
            delta = jnp.sum(crossed[pl.ds(start, HD), :], axis=0, keepdims=True)
            for at in range(0, rows, chunk):
                scores = contract_cols(own_keys, slots[s, at : at + chunk, :PAD])
                attn_probs = jnp.exp2(scores * exp2_scale - lse_ref[group, pl.ds(h, 1), at : at + chunk])
                prob_grad = contract_cols(own_values, grad_in[s, at : at + chunk, :])
                probs[:, at : at + chunk] = attn_probs.astype(low)
                slopes[:, at : at + chunk] = (
                    attn_probs * (prob_grad - delta[:, at : at + chunk])
                ).astype(low)
            own_grads = jnp.where(head, grad_in[s], jnp.zeros((), low))
            own_queries = jnp.where(head, slots[s, :, :PAD], jnp.zeros((), low))
            value_acc[...] += product(probs[...], own_grads)
            key_acc[...] += product(slopes[...], own_queries)
            turned[pl.ds(start, HD), :] = product(keys_t[pl.ds(start, HD), :], slopes[...])
            return carry

        lax.fori_loop(0, GH, head_step, 0)
        query_grad = turned[...].T * score_scale
        joined[:, :PAD] = query_grad.astype(low)
        joined[:, PAD : 2 * PAD] = (key_acc[...] * score_scale).astype(low)
        joined[:, 2 * PAD :] = value_acc[...].astype(low)
        head_kept[0, pl.ds(group, 1), :] = jnp.sum(query_grad, axis=0, keepdims=True)
        head_kept[0, pl.ds(group + GROUPS, 1), :] = jnp.sum(value_acc[...], axis=0, keepdims=True)
        for at in range(0, width, span):
            acc[at : at + span, :] = product(left_t[at : at + span, :], joined[...])
        finish(3, r)
        w_load(r).wait()
        for at in range(0, rows, chunk):
            tokens[at : at + chunk, :] += contract_cols(joined[at : at + chunk, :], w_in[...])
        pl.when(r < 3)(lambda: w_load(r + 1).start())
        return carry

    lax.fori_loop(0, GROUPS, group_step, 0)
    sums_copy(1, 0).start()
    pl.when(c == 0)(lambda: pass_first(3))
    swap = remote_copy(
        tokens.at[pl.ds(half_rows, half_rows)], tokens_out.at[c], swap_sem.at[0], swap_sem.at[1], partner
    )
    keep = pltpu.make_async_copy(tokens.at[pl.ds(0, half_rows)], tokens_out.at[c], load_sem.at[4])
    swap.start()
    keep.start()
    sums_step(1, 0)
    take_second(3, 0)
    sums_step(1, 1)
    take_z(1)
    take_first(3)
    sums_step(1, 2)
    take_z(2)
    take_z(3)
    sums_last(1)
    keep.wait()
    swap.wait()
    for p in range(BIG):
        for r in range(2):
            core_copy(p, r).wait_send()
            second_copy(p, r).wait_send()
        first_copy(p).wait_send()
        for d in range(nz - 1):
            z_copy(p, d).wait_send()
    for v in range(2):
        for k in range(nz + 2):
            sums_copy(v, k).wait_send()


def todo_of(todo):
    def run():
        todo()

    return run


def backward(info, lse, dense_sums, *operands):
    rows_in, w_joined = operands[:2]
    nz = lax.axis_size("dp") // 2
    rows, width = rows_in.shape
    low, wide = jnp.bfloat16, jnp.float32
    deep = width // (2 * nz)
    tails = [(deep, width), (deep, width), (GC // (2 * nz), width), (deep, 3 * GC)]
    results = [*tails[:3], *[(deep, GC)] * 3]
    sums = [dense_sums.shape, (2 * GROUPS, PAD)]
    anywhere, vmem = pl.BlockSpec(memory_space=pl.ANY), pl.BlockSpec(memory_space=pltpu.VMEM)
    dma = pltpu.SemaphoreType.DMA
    return pl.pallas_call(
        functools.partial(backward_kernel, nz),
        in_specs=[pl.BlockSpec(memory_space=pltpu.SMEM), vmem, vmem, *[anywhere] * len(operands)],
        out_specs=[*[vmem] * 8, anywhere],
        out_shape=[
            *[jax.ShapeDtypeStruct(shape, wide) for shape in (*results, *sums)],
            jax.ShapeDtypeStruct((MB, rows // 2, width), wide),
        ],
        scratch_shapes=[
            *[pltpu.VMEM((2, 2, nz, 2, *t), low) for t in tails],
            *[pltpu.VMEM((2, nz, 2, *t), low) for t in tails],
            *[pltpu.VMEM((2, nz, *t), low) for t in tails],
            *[pltpu.VMEM((nz, *t), low) for t in tails],
            *[pltpu.VMEM((nz - 1, *t), low) for t in tails],
            *[pltpu.VMEM((4, *shape), wide) for shape in sums],
            *[pltpu.VMEM((nz + 2, *shape), wide) for shape in sums],
            pltpu.VMEM((width, 3 * PAD), wide),
            pltpu.VMEM((2, rows, width), low),
            pltpu.VMEM((rows, width), low),
            pltpu.VMEM((width, rows), low),
            pltpu.VMEM((rows, 3 * PAD), low),
            pltpu.VMEM((2, rows, PAD), low),
            pltpu.VMEM((2, rows, PAD), low),
            pltpu.VMEM((width, 3 * PAD), low),
            pltpu.VMEM((rows, width), wide),
            pltpu.VMEM((rows, rows), low),
            pltpu.VMEM((rows, rows), low),
            pltpu.VMEM((PAD, rows), wide),
            pltpu.VMEM((PAD, rows), wide),
            pltpu.VMEM((PAD, rows), low),
            pltpu.VMEM((rows, PAD), wide),
            pltpu.VMEM((rows, PAD), wide),
            dma((BIG, 5)),
            dma((BIG, 5)),
            dma((BIG, nz - 1)),
            dma((BIG, nz - 1)),
            dma((2, nz + 2)),
            dma((2, nz + 2)),
            dma((2,)),
            dma((5,)),
            dma((2,)),
            dma((2,)),
            dma((2,)),
        ],
        compiler_params=pltpu.CompilerParams(
            collective_id=1, has_side_effects=True, vmem_limit_bytes=63 * 1024 * 1024
        ),
    )(info, lse, dense_sums, *operands)


def body_fused(
    tokens,
    cotangent,
    lengths,
    w_query,
    w_key,
    w_value,
    w_out,
    w_up,
    w_down,
    b_query,
    b_value,
    b_up,
    b_out,
    b_down,
    norm1_gain,
    norm1_shift,
    norm2_gain,
    norm2_shift,
):
    half_rows = tokens.shape[1]
    width = tokens.shape[2]
    n_dp, n_mp = lax.axis_size("dp"), lax.axis_size("mp")
    unit_cols = w_up.shape[1]
    mp_index = lax.axis_index("mp")
    half = lax.rem(mp_index, 2)
    seq = lax.div(mp_index, 2)

    length = lax.dynamic_slice(lengths, (half, seq), (1, 1))[0, 0]
    info = jnp.stack([length, half])
    mark = jnp.zeros((PAD - GC,), jnp.float32).at[0].set(1.0)
    bias_rows = jnp.concatenate(
        [b_query, mark, jnp.zeros((PAD,), jnp.float32), b_value, jnp.zeros((PAD - GC,), jnp.float32), b_up]
    ).reshape(2, width)
    bias_rows = jnp.pad(bias_rows, ((0, 6), (0, 0)))
    qkv_shard = jnp.concatenate([w_query, w_key, w_value], axis=1)
    gathered = forward_attention(
        lengths, tokens, cotangent, (qkv_shard, w_out, w_up, w_down), bias_rows
    )
    full_out, full_up, full_down = (
        g.reshape(n_mp, n_dp * g.shape[4], g.shape[5]) for g in gathered[1:4]
    )
    full_bias, rows_in, rows_cot, w_joined, qkv, heads, lse = gathered[4:]
    out_pad = jnp.pad(full_out, ((0, 0), (0, PAD - GC), (0, 0))).reshape(n_mp * PAD, width)
    vecs = jnp.stack([b_out, b_down, norm1_gain, norm1_shift, norm2_gain, norm2_shift, b_out, b_out])
    (
        output,
        first_low,
        active,
        ffn_grad_low,
        preact_low,
        attn_grad,
        attn_grad_low,
        heads_grad,
        dense_sums,
    ) = dense(info, heads, rows_in, rows_cot, out_pad, full_up, full_down, vecs, full_bias)
    *matrix_grads, dense_total, head_total, tokens_grad = backward(
        info,
        lse,
        dense_sums,
        rows_in,
        w_joined,
        attn_grad,
        qkv,
        heads,
        heads_grad,
        active,
        ffn_grad_low,
        first_low,
        preact_low,
        attn_grad_low,
    )
    own_down, own_up, own_out, own_query, own_key, own_value = matrix_grads
    dp_index = lax.axis_index("dp")

    def piece(values, row, index, size):
        return lax.dynamic_slice(values, (row, index * size), (1, size))[0]

    share = width // (n_dp * n_mp)
    bias_grads = [piece(head_total, at + mp_index, dp_index, share) for at in (0, GROUPS)]
    bias_grads.append(piece(dense_total, 12 + mp_index, dp_index, unit_cols // n_dp))
    vector_grads = lax.dynamic_slice(dense_total, (0, (dp_index * n_mp + mp_index) * share), (6, share))
    squares = jnp.sum(dense_total[6:9], axis=1)
    rms_values = jnp.sqrt(squares / (dense_total[9, 0] * width))

    def back_home(rows):
        mine, sent = rows[:half_rows], swap_with_partner(rows[half_rows:])
        return jnp.where(half == 0, jnp.stack([mine, sent]), jnp.stack([sent, mine]))

    return (
        back_home(output),
        tokens_grad,
        own_query,
        own_key,
        own_value,
        own_out,
        own_up,
        own_down,
        *bias_grads,
        *vector_grads,
        rms_values,
    )


def solution(mesh):
    rows = P(None, BOTH, None)
    split, rows_split = P("dp", "mp"), P(("mp", "dp"), None)
    aligned = mesh.shape["dp"] == 8 and mesh.shape["mp"] == 4
    return jax.shard_map(
        body_fused if aligned else body_any,
        mesh=mesh,
        in_specs=(
            rows,
            rows,
            P(None, "dp"),
            split,
            split,
            split,
            rows_split,
            split,
            rows_split,
            P("mp"),
            P("mp"),
            P("mp"),
            *([P()] * 6),
        ),
        out_specs=(
            rows,
            rows,
            split,
            split,
            split,
            rows_split,
            split,
            rows_split,
            *([P(("mp", "dp"))] * 3),
            *([P(BOTH)] * 6),
            P(),
        ),
        check_vma=False,
    )
```

```python
import functools

import jax
import jax.numpy as jnp
from jax import lax
from jax.experimental import pallas as pl
from jax.experimental.pallas import tpu as pltpu
from jax.sharding import PartitionSpec as P

HD = 64
L = 1024
SEQ_MB = 2
MB = 2
GROUPS = 4
GH = 3
GC = GH * HD
PAD = 256

epsilon = 1e-05
masked_score = -1e30
exp2_scale = HD ** (-0.5) * 1.4426950408889634
score_scale = HD ** (-0.5)
BOTH = ("dp", "mp")
NT = (((1,), (1,)), ((), ()))


def product(left_side, right_side):
    return jnp.dot(left_side, right_side, preferred_element_type=jnp.float32)


def contract_rows(left_side, right_side):
    return lax.dot_general(
        left_side, right_side, (((0,), (0,)), ((), ())), preferred_element_type=jnp.float32
    )


def contract_cols(left_side, right_side):
    return lax.dot_general(left_side, right_side, NT, preferred_element_type=jnp.float32)


def layer_norm(values, norm_gain, norm_shift):
    center = values - jnp.mean(values, axis=-1, keepdims=True)
    spread = jnp.mean(center * center, axis=-1, keepdims=True)
    inverse = lax.rsqrt(spread + epsilon)
    scaled = center * inverse
    return (scaled * norm_gain + norm_shift, scaled, inverse)


def norm_back(upstream, scaled, inverse, norm_gain):
    gain_grad = jnp.sum(upstream * scaled, axis=0)
    shift_grad = jnp.sum(upstream, axis=0)
    through = upstream * norm_gain
    result = inverse * (
        through
        - jnp.mean(through, axis=-1, keepdims=True)
        - scaled * jnp.mean(through * scaled, axis=-1, keepdims=True)
    )
    return (result, gain_grad, shift_grad)


def head_keys(keys, bias, h, lane):
    kept = jnp.where((lane >= h * HD) & (lane < (h + 1) * HD), keys, jnp.zeros_like(keys))
    return jnp.where(lane == GC, bias, kept)


def attend_forward_kernel(bias_ref, qkv_ref, out_ref, lse_ref, turned):
    rows = qkv_ref.shape[1]
    chunk = 256
    lane = lax.broadcasted_iota(jnp.int32, (1, PAD), 1)
    keys = qkv_ref[0, :, PAD : 2 * PAD]
    values_t = qkv_ref[0, :, 2 * PAD :].T
    bias = bias_ref[...]
    for h in range(GH):
        own = head_keys(keys, bias, h, lane)
        own_values = values_t[h * HD : (h + 1) * HD, :]
        for at in range(0, rows, chunk):
            queries = qkv_ref[0, at : at + chunk, :PAD]
            scores = contract_cols(own, queries)
            top = jnp.max(scores, axis=0, keepdims=True) * exp2_scale
            raised = jnp.exp2(scores * exp2_scale - top)
            total = jnp.sum(raised, axis=0, keepdims=True)
            mixed = product(own_values, raised.astype(jnp.bfloat16))
            turned[h * HD : (h + 1) * HD, at : at + chunk] = mixed / total
            lse_ref[0, h : h + 1, at : at + chunk] = top + jnp.log2(total)
    turned[GC:, :] = jnp.zeros((PAD - GC, rows), jnp.float32)
    out_ref[0] = turned[...].T.astype(jnp.bfloat16)


def attend_forward(qkv, bias):
    rows = qkv.shape[1]
    return pl.pallas_call(
        attend_forward_kernel,
        grid=(GROUPS,),
        in_specs=[
            pl.BlockSpec((rows, 1), lambda g: (0, 0)),
            pl.BlockSpec((1, rows, 3 * PAD), lambda g: (g, 0, 0)),
        ],
        out_specs=[
            pl.BlockSpec((1, rows, PAD), lambda g: (g, 0, 0)),
            pl.BlockSpec((1, 8, rows), lambda g: (g, 0, 0)),
        ],
        out_shape=[
            jax.ShapeDtypeStruct((GROUPS, rows, PAD), jnp.bfloat16),
            jax.ShapeDtypeStruct((GROUPS, 8, rows), jnp.float32),
        ],
        scratch_shapes=[pltpu.VMEM((PAD, rows), jnp.float32)],
        cost_estimate=pl.CostEstimate(
            flops=45_000_000_000 // 3, bytes_accessed=10_000_000, transcendentals=12_000_000
        ),
    )(bias, qkv)


def attend_backward_kernel(
    bias_ref, qkv_ref, out_ref, lse_ref, grad_ref, joined_ref, sums_ref, probs, slopes, turned
):
    rows = qkv_ref.shape[1]
    chunk = 256
    lane = lax.broadcasted_iota(jnp.int32, (1, PAD), 1)
    keys = qkv_ref[0, :, PAD : 2 * PAD]
    keys_t = keys.T
    values = qkv_ref[0, :, 2 * PAD :]
    bias = bias_ref[...]
    crossed = (grad_ref[0].astype(jnp.float32) * out_ref[0].astype(jnp.float32)).T
    key_grad = jnp.zeros((rows, PAD), jnp.float32)
    value_grad = jnp.zeros((rows, PAD), jnp.float32)
    for h in range(GH):
        head = (lane >= h * HD) & (lane < (h + 1) * HD)
        own = head_keys(keys, bias, h, lane)
        own_values = jnp.where(head, values, jnp.zeros_like(values))
        delta = jnp.sum(crossed[h * HD : (h + 1) * HD, :], axis=0, keepdims=True)
        for at in range(0, rows, chunk):
            queries = qkv_ref[0, at : at + chunk, :PAD]
            grads = grad_ref[0, at : at + chunk, :]
            scores = contract_cols(own, queries)
            attn_probs = jnp.exp2(scores * exp2_scale - lse_ref[0, h : h + 1, at : at + chunk])
            prob_grad = contract_cols(own_values, grads)
            probs[:, at : at + chunk] = attn_probs.astype(jnp.bfloat16)
            slopes[:, at : at + chunk] = (
                attn_probs * (prob_grad - delta[:, at : at + chunk])
            ).astype(jnp.bfloat16)
        own_grads = jnp.where(head, grad_ref[0], jnp.zeros((), jnp.bfloat16))
        own_queries = jnp.where(head, qkv_ref[0, :, :PAD], jnp.zeros((), jnp.bfloat16))
        value_grad = value_grad + product(probs[...], own_grads)
        key_grad = key_grad + product(slopes[...], own_queries)
        turned[h * HD : (h + 1) * HD, :] = product(
            keys_t[h * HD : (h + 1) * HD, :], slopes[...]
        )
    turned[GC:, :] = jnp.zeros((PAD - GC, rows), jnp.float32)
    query_grad = turned[...].T * score_scale
    joined_ref[0, :, :PAD] = query_grad.astype(jnp.bfloat16)
    joined_ref[0, :, PAD : 2 * PAD] = (key_grad * score_scale).astype(jnp.bfloat16)
    joined_ref[0, :, 2 * PAD :] = value_grad.astype(jnp.bfloat16)
    sums_ref[0, 0:1, :] = jnp.sum(query_grad, axis=0, keepdims=True)
    sums_ref[0, 1:2, :] = jnp.sum(value_grad, axis=0, keepdims=True)


def attend_backward(qkv, bias, heads_out, lse, heads_grad):
    rows = qkv.shape[1]
    return pl.pallas_call(
        attend_backward_kernel,
        grid=(GROUPS,),
        in_specs=[
            pl.BlockSpec((rows, 1), lambda g: (0, 0)),
            pl.BlockSpec((1, rows, 3 * PAD), lambda g: (g, 0, 0)),
            pl.BlockSpec((1, rows, PAD), lambda g: (g, 0, 0)),
            pl.BlockSpec((1, 8, rows), lambda g: (g, 0, 0)),
            pl.BlockSpec((1, rows, PAD), lambda g: (g, 0, 0)),
        ],
        out_specs=[
            pl.BlockSpec((1, rows, 3 * PAD), lambda g: (g, 0, 0)),
            pl.BlockSpec((1, 8, PAD), lambda g: (g, 0, 0)),
        ],
        out_shape=[
            jax.ShapeDtypeStruct((GROUPS, rows, 3 * PAD), jnp.bfloat16),
            jax.ShapeDtypeStruct((GROUPS, 8, PAD), jnp.float32),
        ],
        scratch_shapes=[
            pltpu.VMEM((rows, rows), jnp.bfloat16),
            pltpu.VMEM((rows, rows), jnp.bfloat16),
            pltpu.VMEM((PAD, rows), jnp.float32),
        ],
        cost_estimate=pl.CostEstimate(
            flops=30_000_000_000, bytes_accessed=20_000_000, transcendentals=12_000_000
        ),
    )(bias, qkv, heads_out, lse, heads_grad)


def swap_with_partner(values):
    size = lax.axis_size("mp")
    return lax.ppermute(values, "mp", [(i, i ^ 1) for i in range(size)])


def pad_heads(values):
    return jnp.pad(values, [(0, 0)] * (values.ndim - 1) + [(0, PAD - values.shape[-1])])


MESH = pl.DeviceIdType.MESH


def positions():
    mp, dp = lax.axis_index("mp"), lax.axis_index("dp")
    return mp, lax.div(mp, 2), lax.rem(mp, 2), lax.div(dp, 2), lax.rem(dp, 2)


def at_place(x, c, z, y):
    return (2 * z + y, 2 * x + c)


def neighbours(nz):
    mp, x, c, z, y = positions()
    first = at_place(lax.rem(x + c, 2), c, z, lax.rem(y + 1 - c, 2))
    second = at_place(lax.rem(x + 1 - c, 2), c, z, lax.rem(y + c, 2))
    partner = at_place(x, 1 - c, z, y)
    along = [at_place(x, c, lax.rem(z + d, nz), y) for d in range(1, nz)]
    return first, second, partner, along


def meet(devices):
    barrier = pltpu.get_barrier_semaphore()
    for device in devices:
        pl.semaphore_signal(barrier, inc=1, device_id=device, device_id_type=MESH)
    pl.semaphore_wait(barrier, len(devices))


def regions(x, c, y):
    own = (x, y)
    first = (lax.rem(x + c, 2), lax.rem(y + 1 - c, 2))
    second = (lax.rem(x + 1 - c, 2), lax.rem(y + c, 2))
    third = (1 - x, 1 - y)
    return own, first, second, third


def gather_kernel(nz, parts, *refs):
    shards, fulls = refs[:parts], refs[parts : 2 * parts]
    own_sem, z_send, z_recv, send, recv = refs[2 * parts :]
    mp, x, c, z, y = positions()
    first, second, partner, along = neighbours(nz)
    meet([first, second, partner, *along])
    own, got1, got2, got3 = regions(x, c, y)
    other = regions(x, 1 - c, y)

    def remote(src, dst, s, r, device):
        return pltpu.make_async_remote_copy(
            src_ref=src, dst_ref=dst, send_sem=s, recv_sem=r, device_id=device, device_id_type=MESH
        )

    started = []
    locals_ = []
    spread = []
    for p in range(parts):
        keep = pltpu.make_async_copy(shards[p], fulls[p].at[x, c, z, y], own_sem.at[p])
        keep.start()
        locals_.append(keep)
        sends = [
            remote(shards[p], fulls[p].at[x, c, z, y], z_send.at[p, d], z_recv.at[p, d], along[d])
            for d in range(nz - 1)
        ]
        for copy in sends:
            copy.start()
        spread.append(sends)

    def block(p, core, place):
        return fulls[p].at[place[0], core, :, place[1]]

    def push(p, k, core, place, device):
        copy = remote(block(p, core, place), block(p, core, place), send.at[p, k], recv.at[p, k], device)
        copy.start()
        started.append(copy)
        return copy

    def arrived(p, k, core, place):
        here = block(p, core, place)
        remote(here, here, send.at[p, k], recv.at[p, k], first).wait_recv()

    for p in range(parts):
        locals_[p].wait()
        for copy in spread[p]:
            copy.wait_recv()
        push(p, 0, c, own, first)
        push(p, 1, c, own, second)
        push(p, 3, c, own, partner)
    for p in range(parts):
        arrived(p, 0, c, got1)
        push(p, 2, c, got1, second)
        push(p, 4, c, got1, partner)
    for p in range(parts):
        arrived(p, 1, c, got2)
        push(p, 5, c, got2, partner)
        arrived(p, 2, c, got3)
        push(p, 6, c, got3, partner)
    for p in range(parts):
        for k in range(4):
            arrived(p, 3 + k, 1 - c, other[k])
    for sends in spread:
        for copy in sends:
            copy.wait_send()
    for copy in started:
        copy.wait_send()


def gather_all(shards):
    n_dp = lax.axis_size("dp")
    nz, parts = n_dp // 2, len(shards)
    return pl.pallas_call(
        functools.partial(gather_kernel, nz, parts),
        in_specs=[pl.BlockSpec(memory_space=pltpu.VMEM)] * parts,
        out_specs=[pl.BlockSpec(memory_space=pl.ANY)] * parts,
        out_shape=[jax.ShapeDtypeStruct((2, 2, nz, 2, *s.shape), s.dtype) for s in shards],
        scratch_shapes=[
            pltpu.SemaphoreType.DMA((parts,)),
            pltpu.SemaphoreType.DMA((parts, nz - 1)),
            pltpu.SemaphoreType.DMA((parts, nz - 1)),
            pltpu.SemaphoreType.DMA((parts, 7)),
            pltpu.SemaphoreType.DMA((parts, 7)),
        ],
        compiler_params=pltpu.CompilerParams(collective_id=0, has_side_effects=True),
    )(*shards)


def scatter_kernel(nz, parts, side, *refs):
    partials, results = refs[:parts], refs[parts : 2 * parts]
    at = 2 * parts
    sums, heard1, heard2, heard3, heard4 = (
        refs[at + i * parts : at + (i + 1) * parts] for i in range(5)
    )
    own_sem, send, recv, z_send, z_recv = refs[at + 5 * parts :]
    mp, x, c, z, y = positions()
    first, second, partner, along = neighbours(nz)
    meet([first, second, partner, *along])
    own, got1, got2, got3 = regions(x, c, y)
    started = []

    def remote(src, dst, s, r, device):
        copy = pltpu.make_async_remote_copy(
            src_ref=src, dst_ref=dst, send_sem=s, recv_sem=r, device_id=device, device_id_type=MESH
        )
        copy.start()
        started.append(copy)
        return copy

    def add(p, place, more):
        for i in range(nz):
            here = sums[p].at[place[0], i, place[1]]
            here[...] = (here[...].astype(jnp.float32) + more[i].astype(jnp.float32)).astype(here.dtype)

    def cut(p, k, core):
        if p not in side:
            return partials[p].at[k, core]
        size = partials[p].shape[3] // 4
        return partials[p].at[:, :, :, pl.ds(pl.multiple_of((2 * k + core) * size, size), size)]

    kept, core_copies = [], []
    for p in range(parts):
        copies = []
        for k in range(2):
            keep = pltpu.make_async_copy(cut(p, k, c), sums[p].at[k], own_sem.at[p, k])
            keep.start()
            copies.append(keep)
        kept.append(copies)
        core_copies.append(
            [
                remote(cut(p, k, 1 - c), heard1[p].at[k], send.at[p, k], recv.at[p, k], partner)
                for k in range(2)
            ]
        )
    second_copies = []
    for p in range(parts):
        for copy in kept[p]:
            copy.wait()
        for copy in core_copies[p]:
            copy.wait_recv()
        copies = []
        for k, place in enumerate((got2, got3)):
            add(p, place, heard1[p].at[place[0], :, place[1]])
            copies.append(
                remote(
                    sums[p].at[place[0], :, place[1]],
                    heard2[p].at[k],
                    send.at[p, 2 + k],
                    recv.at[p, 2 + k],
                    second,
                )
            )
        second_copies.append(copies)
        for place in (got1, own):
            add(p, place, heard1[p].at[place[0], :, place[1]])
    first_copies = []
    for p in range(parts):
        second_copies[p][1].wait_recv()
        add(p, got1, heard2[p].at[1])
        first_copies.append(
            remote(sums[p].at[got1[0], :, got1[1]], heard3[p], send.at[p, 4], recv.at[p, 4], first)
        )
        second_copies[p][0].wait_recv()
        add(p, own, heard2[p].at[0])
    last_copies = []
    for p in range(parts):
        first_copies[p].wait_recv()
        add(p, own, heard3[p])
        last_copies.append(
            [
                remote(
                    sums[p].at[x, lax.rem(z + d + 1, nz), y],
                    heard4[p].at[d],
                    z_send.at[p, d],
                    z_recv.at[p, d],
                    along[d],
                )
                for d in range(nz - 1)
            ]
        )
    for p in range(parts):
        for copy in last_copies[p]:
            copy.wait_recv()
        total = sums[p][x, z, y].astype(jnp.float32)
        for d in range(nz - 1):
            total = total + heard4[p][d].astype(jnp.float32)
        results[p][...] = total
    for copy in started:
        copy.wait_send()


def scatter_sums(partials, side=()):
    nz, parts = lax.axis_size("dp") // 2, len(partials)
    tails = [
        (p.shape[2], p.shape[3] // 4) if i in side else p.shape[4:] for i, p in enumerate(partials)
    ]
    kinds = [p.dtype for p in partials]
    return pl.pallas_call(
        functools.partial(scatter_kernel, nz, parts, side),
        in_specs=[pl.BlockSpec(memory_space=pl.ANY)] * parts,
        out_specs=[pl.BlockSpec(memory_space=pltpu.VMEM)] * parts,
        out_shape=[jax.ShapeDtypeStruct(t, jnp.float32) for t in tails],
        scratch_shapes=[
            *[pltpu.VMEM((2, nz, 2, *t), k) for t, k in zip(tails, kinds)],
            *[pltpu.VMEM((2, nz, 2, *t), k) for t, k in zip(tails, kinds)],
            *[pltpu.VMEM((2, nz, *t), k) for t, k in zip(tails, kinds)],
            *[pltpu.VMEM((nz, *t), k) for t, k in zip(tails, kinds)],
            *[pltpu.VMEM((nz - 1, *t), k) for t, k in zip(tails, kinds)],
            pltpu.SemaphoreType.DMA((parts, 2)),
            pltpu.SemaphoreType.DMA((parts, 5)),
            pltpu.SemaphoreType.DMA((parts, 5)),
            pltpu.SemaphoreType.DMA((parts, nz - 1)),
            pltpu.SemaphoreType.DMA((parts, nz - 1)),
        ],
        compiler_params=pltpu.CompilerParams(
            collective_id=1, has_side_effects=True, vmem_limit_bytes=60 * 1024 * 1024
        ),
    )(*partials)


def in_place_order(blocks):
    return blocks.reshape(2, 2, blocks.shape[1] // 2, 2, *blocks.shape[2:])


def body_any(
    tokens,
    cotangent,
    lengths,
    w_query,
    w_key,
    w_value,
    w_out,
    w_up,
    w_down,
    b_query,
    b_value,
    b_up,
    b_out,
    b_down,
    norm1_gain,
    norm1_shift,
    norm2_gain,
    norm2_shift,
):
    half_rows = tokens.shape[1]
    width = tokens.shape[2]
    n_dp, n_mp = lax.axis_size("dp"), lax.axis_size("mp")
    unit_cols = w_up.shape[1]
    mp_index = lax.axis_index("mp")
    half = lax.rem(mp_index, 2)
    seq = lax.div(mp_index, 2)

    def own_of(pair):
        return jnp.where(half == 0, pair[0], pair[1])

    def other_of(pair):
        return jnp.where(half == 0, pair[1], pair[0])

    rows_in = jnp.concatenate([own_of(tokens), swap_with_partner(other_of(tokens))], axis=0)
    rows_cot = jnp.concatenate([own_of(cotangent), swap_with_partner(other_of(cotangent))], axis=0)
    length = lax.dynamic_slice(lengths, (half, seq), (1, 1))[0, 0]
    place = jnp.arange(half_rows, dtype=jnp.int32)
    place = jnp.concatenate([place + half * half_rows, place + (1 - half) * half_rows])
    valid_row = (place < length)[:, None]
    bias = jnp.where(valid_row, 0.0, masked_score).astype(jnp.bfloat16)
    valid_row = valid_row.astype(jnp.float32)

    biases = jnp.pad(jnp.concatenate([b_query, b_value, b_up]), (0, 896)).reshape(16, 128)
    qkv_shard = jnp.concatenate([w_query, w_key, w_value], axis=1)
    gathered = gather_all([qkv_shard, w_out, w_up, w_down, biases])
    full_qkv, full_out, full_up, full_down, full_bias = (
        g.reshape(n_mp, n_dp, *g.shape[4:]) for g in gathered
    )
    full_qkv = full_qkv.reshape(n_mp, width, 3, GC)
    w_joined = pad_heads(full_qkv).reshape(n_mp, width, 3 * PAD)
    full_out = full_out.reshape(n_mp, GC, width)
    out_pad = jnp.pad(full_out, ((0, 0), (0, PAD - GC), (0, 0))).reshape(n_mp * PAD, width)
    full_up = full_up.reshape(n_mp, width, unit_cols).transpose(1, 0, 2).reshape(width, n_mp * unit_cols)
    full_down = full_down.reshape(n_mp * unit_cols, width)
    full_bias = full_bias[:, 0].reshape(n_mp, -1)
    bias_q, bias_v, bias_up = full_bias[:, :GC], full_bias[:, GC:2*GC], full_bias[:, 2*GC:2*GC+unit_cols]
    mark = jnp.zeros((n_mp, PAD - GC), jnp.float32).at[:, 0].set(1.0)
    joined_bias = jnp.concatenate(
        [bias_q, mark, jnp.zeros((n_mp, PAD), jnp.float32), pad_heads(bias_v)], axis=1
    )

    qkv = lax.dot_general(
        jnp.broadcast_to(rows_in[None], (n_mp, *rows_in.shape)),
        w_joined,
        (((2,), (1,)), ((0,), (0,))),
        preferred_element_type=jnp.float32,
    )
    qkv = (qkv + joined_bias[:, None, :]).astype(jnp.bfloat16)
    heads_out, lse = attend_forward(qkv, bias)
    heads_flat = heads_out.transpose(1, 0, 2).reshape(2 * half_rows, n_mp * PAD)
    attention = product(heads_flat, out_pad) + b_out
    first_norm, first_scaled, first_inverse = layer_norm(
        rows_in.astype(jnp.float32) + attention, norm1_gain, norm1_shift
    )
    first_low = first_norm.astype(jnp.bfloat16)
    preact = product(first_low, full_up) + bias_up.reshape(-1)
    cumulative = 0.5 * (1.0 + lax.erf(preact * 0.7071067811865476))
    active = (preact * cumulative).astype(jnp.bfloat16)
    slope = cumulative + preact * (jnp.exp(-0.5 * preact * preact) * 0.3989422804014327)
    ffn_out = product(active, full_down) + b_down
    stream = first_norm + ffn_out
    final_norm, final_scaled, final_inverse = layer_norm(stream, norm2_gain, norm2_shift)
    output = final_norm.astype(jnp.bfloat16)
    squares = jnp.stack(
        [
            jnp.sum(valid_row * stream * stream),
            jnp.sum(valid_row * attention * attention),
            jnp.sum(valid_row * ffn_out * ffn_out),
            jnp.sum(valid_row),
        ]
    )

    stream_grad, gain2_grad, shift2_grad = norm_back(
        rows_cot.astype(jnp.float32), final_scaled, final_inverse, norm2_gain
    )
    down_bias_grad = jnp.sum(stream_grad, axis=0)
    ffn_grad_low = stream_grad.astype(jnp.bfloat16)
    active_grad = contract_cols(ffn_grad_low, full_down)
    down_wgrad = contract_rows(active, ffn_grad_low)
    preact_grad = active_grad * slope
    up_bias_grad = jnp.sum(preact_grad, axis=0)
    preact_low = preact_grad.astype(jnp.bfloat16)
    up_wgrad = contract_rows(first_low, preact_low)
    first_grad = stream_grad + contract_cols(preact_low, full_up)
    attn_grad, gain1_grad, shift1_grad = norm_back(
        first_grad, first_scaled, first_inverse, norm1_gain
    )
    out_bias_grad = jnp.sum(attn_grad, axis=0)
    attn_grad_low = attn_grad.astype(jnp.bfloat16)
    out_wgrad = contract_rows(heads_flat, attn_grad_low)
    heads_grad = contract_cols(attn_grad_low, out_pad).astype(jnp.bfloat16)
    heads_grad = heads_grad.reshape(2 * half_rows, n_mp, PAD).transpose(1, 0, 2)
    joined, sums = attend_backward(qkv, bias, heads_out, lse, heads_grad)
    joined_wgrad = lax.dot_general(
        jnp.broadcast_to(rows_in[None], (n_mp, *rows_in.shape)),
        joined,
        (((1,), (1,)), ((0,), (0,))),
        preferred_element_type=jnp.float32,
    )
    tokens_grad = attn_grad + jnp.sum(
        lax.dot_general(
            joined, w_joined, (((2,), (2,)), ((0,), (0,))), preferred_element_type=jnp.float32
        ),
        axis=0,
    )

    low = jnp.bfloat16
    joined_blocks = (
        joined_wgrad.astype(low)
        .reshape(n_mp, n_dp, width // n_dp, 3, PAD)[..., :GC]
        .reshape(n_mp, n_dp, width // n_dp, 3 * GC)
    )
    out_blocks = (
        out_wgrad.astype(low)
        .reshape(n_mp, PAD, width)[:, :GC]
        .reshape(n_mp, n_dp, GC // n_dp, width)
    )
    up_blocks = up_wgrad.astype(low).reshape(n_dp, width // n_dp, n_mp, unit_cols).transpose(2, 0, 1, 3)
    down_blocks = down_wgrad.astype(low).reshape(n_mp, n_dp, unit_cols // n_dp, width)

    def by_mp(vector):
        return vector.reshape(n_mp, n_dp, -1)

    def by_dp(vector):
        return vector.reshape(n_dp, n_mp, -1).transpose(1, 0, 2)

    vectors = [by_mp(sums[:, 0, :GC]), by_mp(sums[:, 1, :GC]), by_mp(up_bias_grad)]
    vectors += [
        by_dp(v)
        for v in (out_bias_grad, down_bias_grad, gain1_grad, shift1_grad, gain2_grad, shift2_grad)
    ]
    vectors.append(jnp.broadcast_to(squares, (n_mp, n_dp, 4)))
    ends = [v.shape[-1] for v in vectors]
    vectors = jnp.concatenate(vectors, axis=-1)
    vectors = jnp.pad(vectors, ((0, 0), (0, 0), (0, 1024 - vectors.shape[-1])))
    vectors = vectors.reshape(n_mp, n_dp, 8, 128)
    own_down, own_up, own_out, own_joined, own_vector = scatter_sums(
        [
            in_place_order(b)
            for b in (down_blocks, up_blocks, out_blocks, joined_blocks, vectors)
        ]
    )
    own_vector = own_vector.reshape(-1)
    own_vectors, start = [], 0
    for size in ends:
        own_vectors.append(own_vector[start : start + size])
        start += size
    totals = own_vectors.pop()
    rms_values = jnp.sqrt(totals[:3] / (totals[3] * width))

    def back_home(rows):
        mine, sent = rows[:half_rows], swap_with_partner(rows[half_rows:])
        return jnp.where(half == 0, jnp.stack([mine, sent]), jnp.stack([sent, mine]))

    return (
        back_home(output),
        back_home(tokens_grad),
        own_joined[:, :GC],
        own_joined[:, GC : 2 * GC],
        own_joined[:, 2 * GC :],
        own_out,
        own_up,
        own_down,
        *own_vectors,
        rms_values,
    )


PARTS = 4


def remote_copy(src, dst, s, r, device):
    return pltpu.make_async_remote_copy(
        src_ref=src, dst_ref=dst, send_sem=s, recv_sem=r, device_id=device, device_id_type=MESH
    )


def forward_kernel(
    nz,
    lengths,
    tokens,
    cotangent,
    shard_wq,
    shard_wk,
    shard_wv,
    shard_o,
    shard_u,
    shard_d,
    bias_shard,
    full_q,
    full_o,
    full_u,
    full_d,
    bias_full,
    rows_out,
    cot_out,
    w_out,
    qkv_out,
    heads_out,
    lse_out,
    shard_q,
    rows,
    cots,
    w_got,
    w_pad,
    qkv,
    values_t,
    turned,
    heads,
    own_sem,
    z_send,
    z_recv,
    relay_send,
    send,
    recv,
    swap_send,
    swap_recv,
    bias_send,
    bias_recv,
    out_sem,
):
    shards = (shard_q, shard_o, shard_u, shard_d)
    fulls = (full_q, full_o, full_u, full_d)
    half_rows = tokens.shape[1]
    length = 2 * half_rows
    mp, x, c, z, y = positions()
    half = c
    seq = x
    first, second, partner, along = neighbours(nz)
    across = at_place(1 - x, c, z, y)
    slanted = at_place(1 - x, 1 - c, z, y)
    own, got1, got2, got3 = regions(x, c, y)
    other = regions(x, 1 - c, y)
    for k, shard in enumerate((shard_wq, shard_wk, shard_wv)):
        shard_q[:, k * GC : (k + 1) * GC] = shard[...]
    meet([first, second, partner, slanted, *along])

    def block(p, core, place, d):
        return fulls[p].at[place[0], core, lax.rem(z + nz - d, nz), place[1]]

    places = (own, own, got1, own, got1, got2, got3)
    targets = (first, second, second, partner, partner, partner, partner)
    landing = (got1, got2, got3, *other)
    cores = (c, c, c, 1 - c, 1 - c, 1 - c, 1 - c)

    def outgoing(p, k, d):
        here = block(p, c, places[k], d)
        return remote_copy(here, here, send.at[p, k, d], recv.at[p, k, d], targets[k])

    def incoming(p, k, d):
        here = block(p, cores[k], landing[k], d)
        return remote_copy(here, here, send.at[p, k, d], recv.at[p, k, d], targets[k])

    at_low = 1 - lax.div(z + nz - 1, nz)
    near, far = 1 + 2 * at_low, 3 - 2 * at_low

    def z_copy(p, d):
        return remote_copy(
            shards[p], fulls[p].at[x, c, z, y], z_send.at[p, d - 1], z_recv.at[p, d - 1], along[d - 1]
        )

    def z_each(p, act):
        act(z_copy(p, 2))
        pl.when(z != nz - 1)(lambda: act(z_copy(p, 1)))
        pl.when(z != 0)(lambda: act(z_copy(p, 3)))

    def z_start(p):
        z_each(p, lambda copy: copy.start())

    def z_relay(p, low):
        here = block(p, c, own, 2)
        d = 1 if low else 3
        return remote_copy(here, here, relay_send.at[p], z_recv.at[p, d - 1], at_place(x, c, z + d - 2, y))

    def spread(p, d):
        if not (isinstance(d, int) and d == 0):
            here = block(p, c, own, d)
            remote_copy(here, here, z_send.at[p, d - 1], z_recv.at[p, d - 1], first).wait_recv()
        if isinstance(d, int) and d == 2:
            pl.when(z == 1)(lambda: z_relay(p, True).start())
            pl.when(z == 2)(lambda: z_relay(p, False).start())
        for k in (0, 1, 3):
            outgoing(p, k, d).start()

    def forward1(p):
        for d in range(nz):
            incoming(p, 0, d).wait_recv()
            outgoing(p, 2, d).start()
            outgoing(p, 4, d).start()

    def forward2(p):
        for d in range(nz):
            incoming(p, 1, d).wait_recv()
            outgoing(p, 5, d).start()

    def forward3(p):
        for d in range(nz):
            incoming(p, 2, d).wait_recv()
            outgoing(p, 6, d).start()

    def take(p, k):
        for d in range(nz):
            incoming(p, k, d).wait_recv()

    keep = [
        pltpu.make_async_copy(shards[p], fulls[p].at[x, c, z, y], own_sem.at[p]) for p in range(PARTS)
    ]
    keep_rows = pltpu.make_async_copy(tokens.at[half], rows.at[pl.ds(0, half_rows)], own_sem.at[PARTS])
    keep_cots = pltpu.make_async_copy(cotangent.at[half], cots.at[pl.ds(0, half_rows)], own_sem.at[PARTS + 2])
    swap_rows = remote_copy(
        tokens.at[1 - half], rows.at[pl.ds(half_rows, half_rows)], swap_send.at[0], swap_recv.at[0], partner
    )
    swap_cot = remote_copy(
        cotangent.at[1 - half], cots.at[pl.ds(half_rows, half_rows)], swap_send.at[1], swap_recv.at[1], partner
    )
    bias_copies = [
        remote_copy(bias_shard, bias_full.at[mp], bias_send.at[k], bias_recv.at[k], device)
        for k, device in enumerate((partner, across, slanted))
    ]
    z_start(0)
    keep[0].start()
    for copy in bias_copies:
        copy.start()
    swap_rows.start()
    keep_rows.start()
    for p in range(1, PARTS):
        keep[p].start()
    keep[0].wait()
    spread(0, 0)
    for p in range(1, PARTS):
        z_start(p)
    w_pad[...] = jnp.zeros_like(w_pad)
    turned[...] = jnp.zeros_like(turned)
    bias_full[mp] = bias_shard[...]
    for d in (2, near, far):
        spread(0, d)
    for copy in keep[1:]:
        copy.wait()
    forward1(0)
    for p in range(1, PARTS):
        spread(p, 0)
    forward2(0)
    swap_cot.start()
    keep_cots.start()
    keep_rows.wait()
    swap_rows.wait_recv()
    rows_copy = pltpu.make_async_copy(rows, rows_out, out_sem.at[2])
    rows_copy.start()
    cots_copy = pltpu.make_async_copy(cots, cot_out, out_sem.at[4])
    for copy in bias_copies:
        copy.wait_recv()

    hooks = {
        0: [lambda: [spread(1, d) for d in (2, near, far)]],
        1: [lambda: forward3(0)],
        2: [lambda: [spread(2, d) for d in (2, near)]],
        3: [lambda: spread(2, far), lambda: forward1(1)],
        4: [lambda: forward2(1), lambda: forward3(1)],
        5: [lambda: [spread(3, d) for d in (2, near)]],
        6: [lambda: spread(3, far)],
        7: [lambda: forward1(2)],
        8: [lambda: forward2(2)],
        10: [lambda: forward1(3)],
        11: [lambda: forward2(3)],
    }
    seq_length = lengths[half, seq]
    row = lax.broadcasted_iota(jnp.int32, (length, 1), 0)
    place = jnp.where(row < half_rows, row + half * half_rows, row - half * half_rows)
    bias = jnp.where(place < seq_length, 0.0, masked_score).astype(jnp.bfloat16)
    lane = lax.broadcasted_iota(jnp.int32, (1, PAD), 1)
    chunk = 256

    def heads_copy(gx, gc):
        columns = pl.ds(pl.multiple_of((2 * gx + gc) * PAD, PAD), PAD)
        return pltpu.make_async_copy(heads, heads_out.at[:, columns], out_sem.at[0])

    def qkv_copy(gx, gc):
        return pltpu.make_async_copy(qkv, qkv_out.at[2 * gx + gc], out_sem.at[1])

    def w_copy(gx, gc):
        return pltpu.make_async_copy(w_pad, w_out.at[2 * gx + gc], out_sem.at[3])

    def group_step(r, carry):
        gx, gc = lax.rem(x + lax.div(r, 2), 2), lax.rem(c + lax.rem(r, 2), 2)
        group = 2 * gx + gc

        @pl.when(r == 1)
        def _():
            for d in range(nz):
                incoming(0, 3, d).wait_recv()
            for d in range(nz):
                here = block(0, 1 - c, own, d)
                remote_copy(here, here, send.at[0, 5 - c, d], recv.at[0, 5 - c, d], first).wait_recv()

        @pl.when(r == 3)
        def _():
            for d in range(nz):
                here = block(0, 1 - c, own, d)
                remote_copy(here, here, send.at[0, 4 + c, d], recv.at[0, 4 + c, d], first).wait_recv()
            take(0, 6)

        load = pltpu.make_async_copy(full_q.at[gx, gc], w_got, own_sem.at[PARTS + 1])
        load.start()
        load.wait()

        @pl.when(r > 0)
        def _():
            qkv_copy(gx, gc).wait()
            w_copy(gx, gc).wait()

        w_flat = w_got[...].reshape(-1, 3 * GC)
        for k in range(3):
            w_pad[:, k * PAD : k * PAD + GC] = w_flat[:, k * GC : (k + 1) * GC]
        w_copy(gx, gc).start()
        joined_bias = bias_full[group, 0:1, :]
        for at in range(0, length, 512):
            qkv[at : at + 512, :] = (product(rows[at : at + 512, :], w_pad[...]) + joined_bias).astype(
                jnp.bfloat16
            )
        qkv_copy(gx, gc).start()
        values_t[...] = qkv[:, 2 * PAD :].T

        def head_step(h, carry):
            for k, todo in hooks.items():
                if todo:

                    @pl.when(r * GH + h == k)
                    def _():
                        for task in todo:
                            task()

            start = h * HD
            keys = qkv[:, PAD : 2 * PAD]
            kept = jnp.where((lane >= start) & (lane < start + HD), keys, jnp.zeros_like(keys))
            own_keys = jnp.where(lane == GC, bias, kept)
            own_values = values_t[pl.ds(pl.multiple_of(start, HD), HD), :]
            for at in range(0, length, chunk):
                scores = contract_cols(own_keys, qkv[at : at + chunk, :PAD])
                top = jnp.max(scores, axis=0, keepdims=True) * exp2_scale
                raised = jnp.exp2(scores * exp2_scale - top)
                total = jnp.sum(raised, axis=0, keepdims=True)
                mixed = product(own_values, raised.astype(jnp.bfloat16))
                turned[pl.ds(pl.multiple_of(start, HD), HD), at : at + chunk] = mixed / total
                lse_out[group, pl.ds(h, 1), at : at + chunk] = top + jnp.log2(total)
            return carry

        lax.fori_loop(0, GH, head_step, 0)

        @pl.when(r > 0)
        def _():
            heads_copy(gx, gc).wait()

        heads[...] = turned[...].T.astype(jnp.bfloat16)
        heads_copy(gx, gc).start()
        return carry

    lax.fori_loop(0, GROUPS, group_step, 0)
    keep_cots.wait()
    swap_cot.wait_recv()
    cots_copy.start()
    forward3(2)
    forward3(3)
    for p in range(1, PARTS):
        for k in range(3, 7):
            take(p, k)
    heads_copy(x, c).wait()
    qkv_copy(x, c).wait()
    w_copy(x, c).wait()
    rows_copy.wait()
    cots_copy.wait()
    swap_cot.wait_send()
    swap_rows.wait_send()
    for copy in bias_copies:
        copy.wait_send()
    for p in range(PARTS):
        z_each(p, lambda copy: copy.wait_send())
        pl.when(z == 1)(lambda: z_relay(p, True).wait_send())
        pl.when(z == 2)(lambda: z_relay(p, False).wait_send())
        for k in range(7):
            for d in range(nz):
                outgoing(p, k, d).wait_send()


def forward_attention(lengths, tokens, cotangent, shards, bias_shard):
    nz = lax.axis_size("dp") // 2
    half_rows, width = tokens.shape[1:]
    rows = 2 * half_rows
    low = jnp.bfloat16
    joined_shape = (shards[0].shape[0], 3 * GC)
    anywhere, vmem = pl.BlockSpec(memory_space=pl.ANY), pl.BlockSpec(memory_space=pltpu.VMEM)
    dma = pltpu.SemaphoreType.DMA
    return pl.pallas_call(
        functools.partial(forward_kernel, nz),
        in_specs=[pl.BlockSpec(memory_space=pltpu.SMEM), anywhere, anywhere, *[vmem] * 7],
        out_specs=[*[anywhere] * PARTS, vmem, *[anywhere] * 5, vmem],
        out_shape=[
            *[
                jax.ShapeDtypeStruct((2, 2, nz, 2, *shape), low)
                for shape in (joined_shape, *[s.shape for s in shards[3:]])
            ],
            jax.ShapeDtypeStruct((GROUPS, *bias_shard.shape), jnp.float32),
            jax.ShapeDtypeStruct((rows, width), low),
            jax.ShapeDtypeStruct((rows, width), low),
            jax.ShapeDtypeStruct((GROUPS, width, 3 * PAD), low),
            jax.ShapeDtypeStruct((GROUPS, rows, 3 * PAD), low),
            jax.ShapeDtypeStruct((rows, GROUPS * PAD), low),
            jax.ShapeDtypeStruct((GROUPS, 8, rows), jnp.float32),
        ],
        scratch_shapes=[
            pltpu.VMEM(joined_shape, low),
            pltpu.VMEM((rows, width), low),
            pltpu.VMEM((rows, width), low),
            pltpu.VMEM((nz, 2, *joined_shape), low),
            pltpu.VMEM((width, 3 * PAD), low),
            pltpu.VMEM((rows, 3 * PAD), low),
            pltpu.VMEM((PAD, rows), low),
            pltpu.VMEM((PAD, rows), jnp.float32),
            pltpu.VMEM((rows, PAD), low),
            dma((PARTS + 3,)),
            dma((PARTS, nz - 1)),
            dma((PARTS, nz - 1)),
            dma((PARTS,)),
            dma((PARTS, 7, nz)),
            dma((PARTS, 7, nz)),
            dma((2,)),
            dma((2,)),
            dma((3,)),
            dma((3,)),
            dma((5,)),
        ],
        compiler_params=pltpu.CompilerParams(
            collective_id=2, has_side_effects=True, vmem_limit_bytes=60 * 1024 * 1024
        ),
    )(lengths, tokens, cotangent, *shards, bias_shard)


def place_of(half, row, half_rows):
    return jnp.where(row < half_rows, row + half * half_rows, row - half * half_rows)


def dense_kernel(
    lengths,
    heads_ref,
    rows_ref,
    cot_ref,
    out_full,
    up_full,
    down_full,
    bias_ref,
    output_ref,
    first_ref,
    active_ref,
    ffn_low_ref,
    preact_low_ref,
    attn_ref,
    attn_low_ref,
    heads_grad_ref,
    sums_ref,
    slope,
    out_pad,
    up_w,
    down_w,
    load_sem,
):
    t = pl.program_id(0)
    mp = lax.axis_index("mp")
    half, seq = lax.rem(mp, 2), lax.div(mp, 2)
    low = jnp.bfloat16
    tile, width = rows_ref.shape
    units = up_w.shape[2]
    b_out, b_down, gain1, shift1, gain2, shift2 = (
        bias_ref[0, 2 + k : 3 + k, :] for k in range(6)
    )
    out_load = pltpu.make_async_copy(out_full, out_pad.at[:, pl.ds(0, GC), :], load_sem.at[2 * GROUPS])
    up_loads = [pltpu.make_async_copy(up_full.at[g], up_w.at[g], load_sem.at[g]) for g in range(GROUPS)]
    down_loads = [
        pltpu.make_async_copy(down_full.at[g], down_w.at[g], load_sem.at[GROUPS + g]) for g in range(GROUPS)
    ]

    @pl.when(t == 0)
    def _():
        out_load.start()
        for g in range(GROUPS):
            up_loads[g].start()
            down_loads[g].start()
        out_pad[:, GC:, :] = jnp.zeros((GROUPS, PAD - GC, width), low)
        sums_ref[...] = jnp.zeros_like(sums_ref)
        out_load.wait()

    out_w = out_pad[...].reshape(GROUPS * PAD, width)

    def count(k, values):
        sums_ref[k : k + 1, :] += jnp.sum(values, axis=0, keepdims=True)

    attention = product(heads_ref[...], out_w) + b_out
    first_norm, first_scaled, first_inverse = layer_norm(
        rows_ref[...].astype(jnp.float32) + attention, gain1, shift1
    )
    first_low = first_norm.astype(low)
    first_ref[...] = first_low

    @pl.when(t == 0)
    def _():
        for copy in (*up_loads, *down_loads):
            copy.wait()

    ffn_out = jnp.broadcast_to(b_down, (tile, width))
    for g in range(GROUPS):
        preact = product(first_low, up_w[g]) + bias_ref[g, 1:2, :]
        cumulative = 0.5 * (1.0 + lax.erf(preact * 0.7071067811865476))
        active = (preact * cumulative).astype(low)
        active_ref[:, g * units : (g + 1) * units] = active
        slope[:, g * units : (g + 1) * units] = cumulative + preact * (
            jnp.exp(-0.5 * preact * preact) * 0.3989422804014327
        )
        ffn_out = ffn_out + product(active, down_w[g])
    stream = first_norm + ffn_out
    row = lax.broadcasted_iota(jnp.int32, (tile, 1), 0) + t * tile
    valid = (place_of(half, row, pl.num_programs(0) * tile // 2) < lengths[half, seq]).astype(jnp.float32)
    count(6, valid * stream * stream)
    count(7, valid * attention * attention)
    count(8, valid * ffn_out * ffn_out)
    count(9, jnp.broadcast_to(valid, (tile, width)))
    final_norm, final_scaled, final_inverse = layer_norm(stream, gain2, shift2)
    output_ref[...] = final_norm.astype(low)

    def norm_step(k, upstream, scaled, inverse, gain):
        count(k, upstream * scaled)
        count(k + 1, upstream)
        through = upstream * gain
        return inverse * (
            through
            - jnp.mean(through, axis=-1, keepdims=True)
            - scaled * jnp.mean(through * scaled, axis=-1, keepdims=True)
        )

    stream_grad = norm_step(4, cot_ref[...].astype(jnp.float32), final_scaled, final_inverse, gain2)
    count(1, stream_grad)
    ffn_grad_low = stream_grad.astype(low)
    ffn_low_ref[...] = ffn_grad_low
    first_grad = stream_grad
    for g in range(GROUPS):
        preact_grad = contract_cols(ffn_grad_low, down_w[g]) * slope[:, g * units : (g + 1) * units]
        count(12 + g, preact_grad)
        preact_low = preact_grad.astype(low)
        preact_low_ref[:, g * units : (g + 1) * units] = preact_low
        first_grad = first_grad + contract_cols(preact_low, up_w[g])
    attn_grad = norm_step(2, first_grad, first_scaled, first_inverse, gain1)
    count(0, attn_grad)
    attn_ref[...] = attn_grad
    attn_grad_low = attn_grad.astype(low)
    attn_low_ref[...] = attn_grad_low
    heads_grad_ref[...] = contract_cols(attn_grad_low, out_w).astype(low)


def dense(lengths, heads, rows, cots, out_w, up_w, down_w, biases):
    count, width = rows.shape
    tile = 256
    units = up_w.shape[2]
    low = jnp.bfloat16

    def whole(shape):
        return pl.BlockSpec(shape, lambda t: (0,) * len(shape))

    def tiled(columns):
        return pl.BlockSpec((tile, columns), lambda t: (t, 0))

    outs = [
        (width, low),
        (width, low),
        (GROUPS * units, low),
        (width, low),
        (GROUPS * units, low),
        (width, jnp.float32),
        (width, low),
        (GROUPS * PAD, low),
    ]
    return pl.pallas_call(
        dense_kernel,
        grid=(count // tile,),
        in_specs=[
            pl.BlockSpec(memory_space=pltpu.SMEM),
            tiled(GROUPS * PAD),
            tiled(width),
            tiled(width),
            *[pl.BlockSpec(memory_space=pl.ANY)] * 3,
            whole(biases.shape),
        ],
        out_specs=[*[tiled(columns) for columns, _ in outs], whole((16, width))],
        out_shape=[
            *[jax.ShapeDtypeStruct((count, columns), kind) for columns, kind in outs],
            jax.ShapeDtypeStruct((16, width), jnp.float32),
        ],
        scratch_shapes=[
            pltpu.VMEM((tile, GROUPS * units), jnp.float32),
            pltpu.VMEM((GROUPS, PAD, width), low),
            pltpu.VMEM(up_w.shape, low),
            pltpu.VMEM(down_w.shape, low),
            pltpu.SemaphoreType.DMA((2 * GROUPS + 1,)),
        ],
        cost_estimate=pl.CostEstimate(
            flops=22_600_000_000, bytes_accessed=40_000_000, transcendentals=7_000_000
        ),
    )(lengths, heads, rows, cots, out_w, up_w, down_w, biases)


BIG = 4


def backward_kernel(
    nz,
    lengths,
    lse_ref,
    dense_sums,
    rows_in,
    w_joined,
    attn_grad,
    qkv,
    heads,
    heads_grad,
    active,
    ffn_low,
    first_low,
    preact_low,
    attn_low,
    normed,
    down_out,
    up_out,
    out_out,
    query_out,
    key_out,
    value_out,
    vectors_out,
    tokens_out,
    normed_out,
    *refs,
):
    parts, heard1, heard2, heard3, heard4 = (refs[BIG * i : BIG * (i + 1)] for i in range(5))
    (
        dense_total,
        head_total,
        dense_kept,
        head_kept,
        dense_heard,
        head_heard,
        acc,
        slots,
        right,
        left_t,
        joined,
        heads_in,
        grad_in,
        w_in,
        tokens,
        probs,
        slopes,
        turned,
        crossed,
        keys_t,
        key_acc,
        value_acc,
        send,
        recv,
        z_send,
        z_recv,
        v_send,
        v_recv,
        swap_sem,
        load_sem,
        slot_sem,
        heads_sem,
        grad_sem,
    ) = refs[5 * BIG :]
    low = jnp.bfloat16
    rows, width = tokens.shape
    half_rows = rows // 2
    chunk, span = 256, 384
    mp, x, c, z, y = positions()
    first, second, partner, along = neighbours(nz)
    own, got1, got2, got3 = regions(x, c, y)

    def group_of(r):
        return lax.rem(x + 1 + lax.rem(r, 2), 2), lax.rem(c + 1 + lax.div(r, 2), 2)

    def index_of(r):
        gx, gc = group_of(r)
        return 2 * gx + gc

    def columns(r, size):
        return pl.ds(pl.multiple_of(index_of(r) * size, size), size)

    def load(src, dst, k):
        return pltpu.make_async_copy(src, dst, load_sem.at[k])

    def slot_load(src, s):
        return pltpu.make_async_copy(src, slots.at[s], slot_sem.at[s])

    def active_load(r):
        return slot_load(active.at[:, columns(r, width)], lax.rem(r, 2))

    def preact_load(r):
        return slot_load(preact_low.at[:, columns(r, width)], lax.rem(r, 2))

    def qkv_load(r):
        return slot_load(qkv.at[index_of(r)], lax.rem(r, 2))

    def heads_load(r):
        s = lax.rem(r, 2)
        return pltpu.make_async_copy(heads.at[:, columns(r, PAD)], heads_in.at[s], heads_sem.at[s])

    def grad_load(r):
        s = lax.rem(r, 2)
        return pltpu.make_async_copy(heads_grad.at[:, columns(r, PAD)], grad_in.at[s], grad_sem.at[s])

    def w_load(r):
        return load(w_joined.at[index_of(r)], w_in, 3)

    ffn_load, attn_low_load = load(ffn_low, right, 0), load(attn_low, right, 0)
    first_load, rows_load = load(first_low, joined, 1), load(rows_in, joined, 1)
    tokens_load = load(attn_grad, tokens, 2)

    def core_copy(p, r):
        gx, gc = group_of(r)
        return remote_copy(parts[p].at[gx, gc], heard1[p].at[r], send.at[p, r], recv.at[p, r], partner)

    def second_copy(p, k):
        place = (got2, got3)[k]
        return remote_copy(
            parts[p].at[place[0], c, :, place[1]], heard2[p].at[k], send.at[p, 2 + k], recv.at[p, 2 + k], second
        )

    def first_copy(p):
        return remote_copy(
            parts[p].at[got1[0], c, :, got1[1]], heard3[p], send.at[p, 4], recv.at[p, 4], first
        )

    def z_copy(p, d):
        return remote_copy(
            parts[p].at[x, c, lax.rem(z + d + 1, nz), y],
            heard4[p].at[d],
            z_send.at[p, d],
            z_recv.at[p, d],
            along[d],
        )

    def add(p, place, more):
        for i in range(nz):
            here = parts[p].at[place[0], c, i, place[1]]
            here[...] = (here[...].astype(jnp.float32) + more[i].astype(jnp.float32)).astype(low)

    def take_second(p, k):
        second_copy(p, k).wait_recv()
        add(p, got1 if k else own, heard2[p].at[k])

    def pass_first(p):
        take_second(p, 1)
        first_copy(p).start()

    def take_first(p):
        first_copy(p).wait_recv()
        add(p, own, heard3[p])
        for d in range(nz - 1):
            z_copy(p, d).start()

    def take_z(p):
        total = parts[p][x, c, z, y].astype(jnp.float32)
        for d in range(nz - 1):
            z_copy(p, d).wait_recv()
            total = total + heard4[p][d].astype(jnp.float32)
        if p < BIG - 1:
            (down_out, up_out, out_out)[p][...] = total
        else:
            for k, result in enumerate((query_out, key_out, value_out)):
                result[...] = total[:, k * GC : (k + 1) * GC]

    kept, heard_sums = (dense_kept, head_kept), (dense_heard, head_heard)

    def sums_copy(v, k):
        device = (first, second)[k - 1] if 0 < k < 3 else along[k - 3] if k else partner
        return remote_copy(
            kept[v].at[min(k, 3)], heard_sums[v].at[k], v_send.at[v, k], v_recv.at[v, k], device
        )

    def sums_step(v, k):
        sums_copy(v, k).wait_recv()
        kept[v][k + 1] = kept[v][k] + heard_sums[v][k]
        for later in (k + 1,) if k < 2 else range(3, nz + 2):
            sums_copy(v, later).start()

    def sums_last(v):
        total = kept[v][3]
        for k in range(3, nz + 2):
            sums_copy(v, k).wait_recv()
            total = total + heard_sums[v][k]
        (dense_total, head_total)[v][...] = total

    def finish(p, r):
        gx, gc = group_of(r)
        deep, wide = parts[p].shape[4:]
        pieces = [(0, 0, wide)] if p < BIG - 1 else [(k * GC, k * PAD, GC) for k in range(3)]

        def put(more):
            for i in range(nz):
                for at, source, size in pieces:
                    value = acc[2 * deep * i : 2 * deep * (i + 1), source : source + size].reshape(2, deep, size)
                    if more is not None:
                        value = value + more[i, :, :, at : at + size].astype(jnp.float32)
                    parts[p][gx, gc, i, :, :, at : at + size] = value.astype(low)

        @pl.when(r < 2)
        def _():
            put(None)
            core_copy(p, r).start()

        @pl.when(r >= 2)
        def _():
            core_copy(p, r - 2).wait_recv()
            put(heard1[p].at[r - 2])

        @pl.when(r == 2)
        def _():
            second_copy(p, 1).start()
            pl.when(c == 0)(lambda: second_copy(p, 0).start())

        @pl.when(r == 3)
        def _():
            pl.when(c == 1)(lambda: second_copy(p, 0).start())

    ffn_load.start()
    active_load(0).start()
    heads_load(0).start()
    first_load.start()
    w_load(0).start()
    tokens_load.start()
    dense_kept[0] = dense_sums[...]
    meet([first, second, partner, *along])
    normed_swap = remote_copy(
        normed.at[pl.ds(half_rows, half_rows)], normed_out, swap_sem.at[2], swap_sem.at[3], partner
    )
    normed_swap.start()
    ffn_load.wait()

    def down_step(r, carry):
        active_load(r).wait()
        pl.when(r < 3)(lambda: active_load(r + 1).start())
        pl.when(r == 3)(lambda: preact_load(0).start())
        s = lax.rem(r, 2)
        for at in range(0, width, span):
            acc[at : at + span, :] = product(slots[s, :, at : at + span].T, right[...])
        finish(0, r)
        return carry

    lax.fori_loop(0, GROUPS, down_step, 0)
    sums_copy(0, 0).start()
    attn_low_load.start()
    first_load.wait()
    left_t[...] = joined[...].T
    rows_load.start()

    def up_step(r, carry):
        preact_load(r).wait()
        pl.when(r < 3)(lambda: preact_load(r + 1).start())
        pl.when(r == 3)(lambda: qkv_load(0).start())
        s = lax.rem(r, 2)
        for at in range(0, width, span):
            acc[at : at + span, :] = product(left_t[at : at + span, :], slots[s])
        finish(1, r)
        return carry

    lax.fori_loop(0, GROUPS, up_step, 0)
    sums_step(0, 0)
    attn_low_load.wait()

    def out_step(r, carry):
        heads_load(r).wait()
        heads_load(lax.rem(r + 1, GROUPS)).start()
        acc[:PAD, :] = product(heads_in[lax.rem(r, 2)].T, right[...])
        finish(2, r)
        return carry

    lax.fori_loop(0, GROUPS, out_step, 0)
    grad_load(0).start()
    rows_load.wait()
    left_t[...] = joined[...].T
    tokens_load.wait()

    hooks = {
        0: lambda: sums_step(0, 1),
        1: lambda: (pass_first(0), take_second(0, 0)),
        2: lambda: sums_step(0, 2),
        4: lambda: take_first(0),
        5: lambda: (pass_first(1), take_second(1, 0)),
        6: lambda: (pass_first(2), take_second(2, 0)),
        8: lambda: take_first(1),
        9: lambda: (take_first(2), sums_last(0)),
        10: lambda: take_z(0),
        11: lambda: pl.when(c == 1)(lambda: pass_first(3)),
    }
    row = lax.broadcasted_iota(jnp.int32, (rows, 1), 0)
    bias = jnp.where(place_of(c, row, half_rows) < lengths[c, x], 0.0, masked_score).astype(low)
    lane = lax.broadcasted_iota(jnp.int32, (1, PAD), 1)
    turned[...] = jnp.zeros_like(turned)

    def group_step(r, carry):
        s = lax.rem(r, 2)
        group = index_of(r)
        for copy in (qkv_load, heads_load, grad_load):
            copy(r).wait()

        @pl.when(r < 3)
        def _():
            for copy in (qkv_load, heads_load, grad_load):
                copy(r + 1).start()

        crossed[...] = (grad_in[s].astype(jnp.float32) * heads_in[s].astype(jnp.float32)).T
        keys_t[...] = slots[s, :, PAD : 2 * PAD].T
        key_acc[...] = jnp.zeros_like(key_acc)
        value_acc[...] = jnp.zeros_like(value_acc)

        def head_step(h, carry):
            for k, todo in hooks.items():
                pl.when(r * GH + h == k)(todo_of(todo))
            start = pl.multiple_of(h * HD, HD)
            head = (lane >= start) & (lane < start + HD)
            keys = slots[s, :, PAD : 2 * PAD]
            own_keys = jnp.where(lane == GC, bias, jnp.where(head, keys, jnp.zeros_like(keys)))
            own_values = jnp.where(head, slots[s, :, 2 * PAD :], jnp.zeros((), low))
            delta = jnp.sum(crossed[pl.ds(start, HD), :], axis=0, keepdims=True)
            for at in range(0, rows, chunk):
                scores = contract_cols(own_keys, slots[s, at : at + chunk, :PAD])
                attn_probs = jnp.exp2(scores * exp2_scale - lse_ref[group, pl.ds(h, 1), at : at + chunk])
                prob_grad = contract_cols(own_values, grad_in[s, at : at + chunk, :])
                probs[:, at : at + chunk] = attn_probs.astype(low)
                slopes[:, at : at + chunk] = (
                    attn_probs * (prob_grad - delta[:, at : at + chunk])
                ).astype(low)
            own_grads = jnp.where(head, grad_in[s], jnp.zeros((), low))
            own_queries = jnp.where(head, slots[s, :, :PAD], jnp.zeros((), low))
            value_acc[...] += product(probs[...], own_grads)
            key_acc[...] += product(slopes[...], own_queries)
            turned[pl.ds(start, HD), :] = product(keys_t[pl.ds(start, HD), :], slopes[...])
            return carry

        lax.fori_loop(0, GH, head_step, 0)
        query_grad = turned[...].T * score_scale
        joined[:, :PAD] = query_grad.astype(low)
        joined[:, PAD : 2 * PAD] = (key_acc[...] * score_scale).astype(low)
        joined[:, 2 * PAD :] = value_acc[...].astype(low)
        head_kept[0, pl.ds(group, 1), :] = jnp.sum(query_grad, axis=0, keepdims=True)
        head_kept[0, pl.ds(group + GROUPS, 1), :] = jnp.sum(value_acc[...], axis=0, keepdims=True)
        for at in range(0, width, span):
            acc[at : at + span, :] = product(left_t[at : at + span, :], joined[...])
        finish(3, r)
        w_load(r).wait()
        for at in range(0, rows, chunk):
            tokens[at : at + chunk, :] += contract_cols(joined[at : at + chunk, :], w_in[...])
        pl.when(r < 3)(lambda: w_load(r + 1).start())
        return carry

    lax.fori_loop(0, GROUPS, group_step, 0)
    sums_copy(1, 0).start()
    pl.when(c == 0)(lambda: pass_first(3))
    swap = remote_copy(
        tokens.at[pl.ds(half_rows, half_rows)], tokens_out.at[c], swap_sem.at[0], swap_sem.at[1], partner
    )
    keep = pltpu.make_async_copy(tokens.at[pl.ds(0, half_rows)], tokens_out.at[c], load_sem.at[4])
    swap.start()
    keep.start()

    def piece(values, index, count):
        size = values.shape[1] // count
        found = values[:, :size]
        for k in range(1, count):
            found = jnp.where(index == k, values[:, k * size : (k + 1) * size], found)
        return found

    dp = 2 * z + y
    vectors_out[...] = jnp.zeros_like(vectors_out)
    share = width // (8 * nz)
    vectors_out[0:6, :share] = piece(dense_total[0:6, :], dp * 4 + mp, 8 * nz)
    vectors_out[6:7, : width // (2 * nz)] = piece(dense_total[pl.ds(12 + mp, 1), :], dp, 2 * nz)
    for k in range(3):
        square = jnp.sum(dense_total[6 + k : 7 + k, :], axis=1, keepdims=True)
        vectors_out[12:13, k : k + 1] = jnp.sqrt(square / (dense_total[9:10, 0:1] * width))
    sums_step(1, 0)
    take_second(3, 0)
    sums_step(1, 1)
    take_z(1)
    take_first(3)
    sums_step(1, 2)
    take_z(2)
    take_z(3)
    sums_last(1)

    vectors_out[7:8, :share] = piece(head_total[pl.ds(mp, 1), :GC], dp, 2 * nz)
    vectors_out[8:9, :share] = piece(head_total[pl.ds(mp + GROUPS, 1), :GC], dp, 2 * nz)
    keep.wait()
    swap.wait()
    normed_swap.wait()
    for p in range(BIG):
        for r in range(2):
            core_copy(p, r).wait_send()
            second_copy(p, r).wait_send()
        first_copy(p).wait_send()
        for d in range(nz - 1):
            z_copy(p, d).wait_send()
    for v in range(2):
        for k in range(nz + 2):
            sums_copy(v, k).wait_send()


def todo_of(todo):
    def run():
        todo()

    return run


def backward(lengths, lse, dense_sums, *operands):
    rows_in, w_joined = operands[:2]
    nz = lax.axis_size("dp") // 2
    rows, width = rows_in.shape
    low, wide = jnp.bfloat16, jnp.float32
    deep = width // (2 * nz)
    tails = [(deep, width), (deep, width), (GC // (2 * nz), width), (deep, 3 * GC)]
    results = [*tails[:3], *[(deep, GC)] * 3]
    sums = [dense_sums.shape, (2 * GROUPS, PAD)]
    anywhere, vmem = pl.BlockSpec(memory_space=pl.ANY), pl.BlockSpec(memory_space=pltpu.VMEM)
    dma = pltpu.SemaphoreType.DMA
    return pl.pallas_call(
        functools.partial(backward_kernel, nz),
        in_specs=[pl.BlockSpec(memory_space=pltpu.SMEM), vmem, vmem, *[anywhere] * len(operands)],
        out_specs=[*[vmem] * 7, anywhere, anywhere],
        out_shape=[
            *[jax.ShapeDtypeStruct(shape, wide) for shape in (*results, (16, 128))],
            jax.ShapeDtypeStruct((MB, rows // 2, width), wide),
            jax.ShapeDtypeStruct((rows // 2, width), low),
        ],
        scratch_shapes=[
            *[pltpu.VMEM((2, 2, nz, 2, *t), low) for t in tails],
            *[pltpu.VMEM((2, nz, 2, *t), low) for t in tails],
            *[pltpu.VMEM((2, nz, *t), low) for t in tails],
            *[pltpu.VMEM((nz, *t), low) for t in tails],
            *[pltpu.VMEM((nz - 1, *t), low) for t in tails],
            *[pltpu.VMEM(shape, wide) for shape in sums],
            *[pltpu.VMEM((4, *shape), wide) for shape in sums],
            *[pltpu.VMEM((nz + 2, *shape), wide) for shape in sums],
            pltpu.VMEM((width, 3 * PAD), wide),
            pltpu.VMEM((2, rows, width), low),
            pltpu.VMEM((rows, width), low),
            pltpu.VMEM((width, rows), low),
            pltpu.VMEM((rows, 3 * PAD), low),
            pltpu.VMEM((2, rows, PAD), low),
            pltpu.VMEM((2, rows, PAD), low),
            pltpu.VMEM((width, 3 * PAD), low),
            pltpu.VMEM((rows, width), wide),
            pltpu.VMEM((rows, rows), low),
            pltpu.VMEM((rows, rows), low),
            pltpu.VMEM((PAD, rows), wide),
            pltpu.VMEM((PAD, rows), wide),
            pltpu.VMEM((PAD, rows), low),
            pltpu.VMEM((rows, PAD), wide),
            pltpu.VMEM((rows, PAD), wide),
            dma((BIG, 5)),
            dma((BIG, 5)),
            dma((BIG, nz - 1)),
            dma((BIG, nz - 1)),
            dma((2, nz + 2)),
            dma((2, nz + 2)),
            dma((4,)),
            dma((5,)),
            dma((2,)),
            dma((2,)),
            dma((2,)),
        ],
        compiler_params=pltpu.CompilerParams(
            collective_id=1, has_side_effects=True, vmem_limit_bytes=63 * 1024 * 1024
        ),
    )(lengths, lse, dense_sums, *operands)


def body_fused(
    tokens,
    cotangent,
    lengths,
    w_query,
    w_key,
    w_value,
    w_out,
    w_up,
    w_down,
    b_query,
    b_value,
    b_up,
    b_out,
    b_down,
    norm1_gain,
    norm1_shift,
    norm2_gain,
    norm2_shift,
):
    half_rows = tokens.shape[1]
    width = tokens.shape[2]
    n_dp, n_mp = lax.axis_size("dp"), lax.axis_size("mp")
    unit_cols = w_up.shape[1]
    mark = jnp.zeros((PAD - GC,), jnp.float32).at[0].set(1.0)
    bias_rows = jnp.concatenate(
        [
            b_query,
            mark,
            jnp.zeros((PAD,), jnp.float32),
            b_value,
            jnp.zeros((PAD - GC,), jnp.float32),
            b_up,
            b_out,
            b_down,
            norm1_gain,
            norm1_shift,
            norm2_gain,
            norm2_shift,
        ]
    ).reshape(8, width)
    gathered = forward_attention(
        lengths, tokens, cotangent, (w_query, w_key, w_value, w_out, w_up, w_down), bias_rows
    )
    full_out, full_up, full_down = (
        g.reshape(n_mp, n_dp * g.shape[4], g.shape[5]) for g in gathered[1:4]
    )
    full_bias, rows_in, rows_cot, w_joined, qkv, heads, lse = gathered[4:]
    (
        output,
        first_low,
        active,
        ffn_grad_low,
        preact_low,
        attn_grad,
        attn_grad_low,
        heads_grad,
        dense_sums,
    ) = dense(lengths, heads, rows_in, rows_cot, full_out, full_up, full_down, full_bias)
    *matrix_grads, vectors, tokens_grad, output_got = backward(
        lengths,
        lse,
        dense_sums,
        rows_in,
        w_joined,
        attn_grad,
        qkv,
        heads,
        heads_grad,
        active,
        ffn_grad_low,
        first_low,
        preact_low,
        attn_grad_low,
        output,
    )
    share = width // (n_dp * n_mp)
    sizes = [*[share] * 6, unit_cols // n_dp, share, share, 3]
    delivered = deliver(matrix_grads, vectors, output, output_got, tokens_grad, sizes)
    output, tokens_grad, own_down, own_up, own_out, own_query, own_key, own_value = delivered[:8]
    own_vectors = [v.reshape(-1) for v in delivered[8:]]
    return (
        output,
        tokens_grad,
        own_query,
        own_key,
        own_value,
        own_out,
        own_up,
        own_down,
        own_vectors[7],
        own_vectors[8],
        own_vectors[6],
        *own_vectors[:6],
        own_vectors[9],
    )


def deliver_kernel(mats, *refs):
    results, (vectors, normed, normed_got, tokens) = refs[:mats], refs[mats : mats + 4]
    outs = refs[mats + 4 :]
    normed_out, tokens_out = outs[:2]
    mat_outs, vec_outs = outs[2 : 2 + mats], outs[2 + mats : 12 + mats]
    normed_kept, tokens_kept, load_sem, store_sem = outs[12 + mats :]
    half = lax.rem(lax.axis_index("mp"), 2)
    half_rows = tokens.shape[1]
    moves = [
        (tokens.at[0], tokens_kept.at[0], tokens_out.at[0]),
        (tokens.at[1], tokens_kept.at[1], tokens_out.at[1]),
        (normed.at[pl.ds(0, half_rows)], normed_kept.at[0], normed_out.at[half]),
        (normed_got, normed_kept.at[1], normed_out.at[1 - half]),
    ]
    loads = [pltpu.make_async_copy(a, b, load_sem.at[k]) for k, (a, b, _) in enumerate(moves)]
    stores = [pltpu.make_async_copy(b, o, store_sem.at[k]) for k, (_, b, o) in enumerate(moves)]
    stores += [
        pltpu.make_async_copy(a, o, store_sem.at[len(moves) + k])
        for k, (a, o) in enumerate(zip(results, mat_outs))
    ]
    for copy in (*loads, *stores[len(moves) :]):
        copy.start()
    for k, out in enumerate(vec_outs[:9]):
        out[...] = vectors[k : k + 1, : out.shape[1]]
    vec_outs[9][...] = vectors[12:13, :3]
    for k, copy in enumerate(loads):
        copy.wait()
        stores[k].start()
    for copy in stores:
        copy.wait()


def deliver(results, vectors, normed, normed_got, tokens, sizes):
    mats = len(results)
    anywhere, vmem = pl.BlockSpec(memory_space=pl.ANY), pl.BlockSpec(memory_space=pltpu.VMEM)
    big = [jax.ShapeDtypeStruct((2, *normed_got.shape), normed.dtype), jax.ShapeDtypeStruct(tokens.shape, tokens.dtype)]
    rows = [jax.ShapeDtypeStruct((1, size), jnp.float32) for size in sizes]
    return pl.pallas_call(
        functools.partial(deliver_kernel, mats),
        grid=(1,),
        in_specs=[*[vmem] * (mats + 1), *[anywhere] * 3],
        out_specs=[
            *[anywhere] * (2 + mats),
            *[pl.BlockSpec((1, size), lambda i: (0, 0)) for size in sizes],
        ],
        out_shape=[*big, *[jax.ShapeDtypeStruct(r.shape, r.dtype) for r in results], *rows],
        scratch_shapes=[
            pltpu.VMEM(big[0].shape, big[0].dtype),
            pltpu.VMEM(big[1].shape, big[1].dtype),
            pltpu.SemaphoreType.DMA((4,)),
            pltpu.SemaphoreType.DMA((4 + mats,)),
        ],
    )(*results, vectors, normed, normed_got, tokens)


def solution(mesh):
    rows = P(None, BOTH, None)
    split, rows_split = P("dp", "mp"), P(("mp", "dp"), None)
    aligned = mesh.shape["dp"] == 8 and mesh.shape["mp"] == 4
    return jax.shard_map(
        body_fused if aligned else body_any,
        mesh=mesh,
        in_specs=(
            rows,
            rows,
            P(None, "dp"),
            split,
            split,
            split,
            rows_split,
            split,
            rows_split,
            P("mp"),
            P("mp"),
            P("mp"),
            *([P()] * 6),
        ),
        out_specs=(
            rows,
            rows,
            split,
            split,
            split,
            rows_split,
            split,
            rows_split,
            *([P(("mp", "dp"))] * 3),
            *([P(BOTH)] * 6),
            P(),
        ),
        check_vma=False,
    )
```

```python
import functools

import jax
import jax.numpy as jnp
from jax import lax
from jax.experimental import pallas as pl
from jax.experimental.pallas import tpu as pltpu
from jax.sharding import PartitionSpec as P

HD = 64
L = 1024
SEQ_MB = 2
MB = 2
GROUPS = 4
GH = 3
GC = GH * HD
PAD = 256

epsilon = 1e-05
masked_score = -1e30
exp2_scale = HD ** (-0.5) * 1.4426950408889634
score_scale = HD ** (-0.5)
BOTH = ("dp", "mp")
NT = (((1,), (1,)), ((), ()))


def product(left_side, right_side):
    return jnp.dot(left_side, right_side, preferred_element_type=jnp.float32)


def contract_rows(left_side, right_side):
    return lax.dot_general(
        left_side, right_side, (((0,), (0,)), ((), ())), preferred_element_type=jnp.float32
    )


def contract_cols(left_side, right_side):
    return lax.dot_general(left_side, right_side, NT, preferred_element_type=jnp.float32)


def layer_norm(values, norm_gain, norm_shift):
    center = values - jnp.mean(values, axis=-1, keepdims=True)
    spread = jnp.mean(center * center, axis=-1, keepdims=True)
    inverse = lax.rsqrt(spread + epsilon)
    scaled = center * inverse
    return (scaled * norm_gain + norm_shift, scaled, inverse)


def norm_back(upstream, scaled, inverse, norm_gain):
    gain_grad = jnp.sum(upstream * scaled, axis=0)
    shift_grad = jnp.sum(upstream, axis=0)
    through = upstream * norm_gain
    result = inverse * (
        through
        - jnp.mean(through, axis=-1, keepdims=True)
        - scaled * jnp.mean(through * scaled, axis=-1, keepdims=True)
    )
    return (result, gain_grad, shift_grad)


def head_keys(keys, bias, h, lane):
    kept = jnp.where((lane >= h * HD) & (lane < (h + 1) * HD), keys, jnp.zeros_like(keys))
    return jnp.where(lane == GC, bias, kept)


def attend_forward_kernel(bias_ref, qkv_ref, out_ref, lse_ref, turned):
    rows = qkv_ref.shape[1]
    chunk = 256
    lane = lax.broadcasted_iota(jnp.int32, (1, PAD), 1)
    keys = qkv_ref[0, :, PAD : 2 * PAD]
    values_t = qkv_ref[0, :, 2 * PAD :].T
    bias = bias_ref[...]
    for h in range(GH):
        own = head_keys(keys, bias, h, lane)
        own_values = values_t[h * HD : (h + 1) * HD, :]
        for at in range(0, rows, chunk):
            queries = qkv_ref[0, at : at + chunk, :PAD]
            scores = contract_cols(own, queries)
            top = jnp.max(scores, axis=0, keepdims=True) * exp2_scale
            raised = jnp.exp2(scores * exp2_scale - top)
            total = jnp.sum(raised, axis=0, keepdims=True)
            mixed = product(own_values, raised.astype(jnp.bfloat16))
            turned[h * HD : (h + 1) * HD, at : at + chunk] = mixed / total
            lse_ref[0, h : h + 1, at : at + chunk] = top + jnp.log2(total)
    turned[GC:, :] = jnp.zeros((PAD - GC, rows), jnp.float32)
    out_ref[0] = turned[...].T.astype(jnp.bfloat16)


def attend_forward(qkv, bias):
    rows = qkv.shape[1]
    return pl.pallas_call(
        attend_forward_kernel,
        grid=(GROUPS,),
        in_specs=[
            pl.BlockSpec((rows, 1), lambda g: (0, 0)),
            pl.BlockSpec((1, rows, 3 * PAD), lambda g: (g, 0, 0)),
        ],
        out_specs=[
            pl.BlockSpec((1, rows, PAD), lambda g: (g, 0, 0)),
            pl.BlockSpec((1, 8, rows), lambda g: (g, 0, 0)),
        ],
        out_shape=[
            jax.ShapeDtypeStruct((GROUPS, rows, PAD), jnp.bfloat16),
            jax.ShapeDtypeStruct((GROUPS, 8, rows), jnp.float32),
        ],
        scratch_shapes=[pltpu.VMEM((PAD, rows), jnp.float32)],
        cost_estimate=pl.CostEstimate(
            flops=45_000_000_000 // 3, bytes_accessed=10_000_000, transcendentals=12_000_000
        ),
    )(bias, qkv)


def attend_backward_kernel(
    bias_ref, qkv_ref, out_ref, lse_ref, grad_ref, joined_ref, sums_ref, probs, slopes, turned
):
    rows = qkv_ref.shape[1]
    chunk = 256
    lane = lax.broadcasted_iota(jnp.int32, (1, PAD), 1)
    keys = qkv_ref[0, :, PAD : 2 * PAD]
    keys_t = keys.T
    values = qkv_ref[0, :, 2 * PAD :]
    bias = bias_ref[...]
    crossed = (grad_ref[0].astype(jnp.float32) * out_ref[0].astype(jnp.float32)).T
    key_grad = jnp.zeros((rows, PAD), jnp.float32)
    value_grad = jnp.zeros((rows, PAD), jnp.float32)
    for h in range(GH):
        head = (lane >= h * HD) & (lane < (h + 1) * HD)
        own = head_keys(keys, bias, h, lane)
        own_values = jnp.where(head, values, jnp.zeros_like(values))
        delta = jnp.sum(crossed[h * HD : (h + 1) * HD, :], axis=0, keepdims=True)
        for at in range(0, rows, chunk):
            queries = qkv_ref[0, at : at + chunk, :PAD]
            grads = grad_ref[0, at : at + chunk, :]
            scores = contract_cols(own, queries)
            attn_probs = jnp.exp2(scores * exp2_scale - lse_ref[0, h : h + 1, at : at + chunk])
            prob_grad = contract_cols(own_values, grads)
            probs[:, at : at + chunk] = attn_probs.astype(jnp.bfloat16)
            slopes[:, at : at + chunk] = (
                attn_probs * (prob_grad - delta[:, at : at + chunk])
            ).astype(jnp.bfloat16)
        own_grads = jnp.where(head, grad_ref[0], jnp.zeros((), jnp.bfloat16))
        own_queries = jnp.where(head, qkv_ref[0, :, :PAD], jnp.zeros((), jnp.bfloat16))
        value_grad = value_grad + product(probs[...], own_grads)
        key_grad = key_grad + product(slopes[...], own_queries)
        turned[h * HD : (h + 1) * HD, :] = product(
            keys_t[h * HD : (h + 1) * HD, :], slopes[...]
        )
    turned[GC:, :] = jnp.zeros((PAD - GC, rows), jnp.float32)
    query_grad = turned[...].T * score_scale
    joined_ref[0, :, :PAD] = query_grad.astype(jnp.bfloat16)
    joined_ref[0, :, PAD : 2 * PAD] = (key_grad * score_scale).astype(jnp.bfloat16)
    joined_ref[0, :, 2 * PAD :] = value_grad.astype(jnp.bfloat16)
    sums_ref[0, 0:1, :] = jnp.sum(query_grad, axis=0, keepdims=True)
    sums_ref[0, 1:2, :] = jnp.sum(value_grad, axis=0, keepdims=True)


def attend_backward(qkv, bias, heads_out, lse, heads_grad):
    rows = qkv.shape[1]
    return pl.pallas_call(
        attend_backward_kernel,
        grid=(GROUPS,),
        in_specs=[
            pl.BlockSpec((rows, 1), lambda g: (0, 0)),
            pl.BlockSpec((1, rows, 3 * PAD), lambda g: (g, 0, 0)),
            pl.BlockSpec((1, rows, PAD), lambda g: (g, 0, 0)),
            pl.BlockSpec((1, 8, rows), lambda g: (g, 0, 0)),
            pl.BlockSpec((1, rows, PAD), lambda g: (g, 0, 0)),
        ],
        out_specs=[
            pl.BlockSpec((1, rows, 3 * PAD), lambda g: (g, 0, 0)),
            pl.BlockSpec((1, 8, PAD), lambda g: (g, 0, 0)),
        ],
        out_shape=[
            jax.ShapeDtypeStruct((GROUPS, rows, 3 * PAD), jnp.bfloat16),
            jax.ShapeDtypeStruct((GROUPS, 8, PAD), jnp.float32),
        ],
        scratch_shapes=[
            pltpu.VMEM((rows, rows), jnp.bfloat16),
            pltpu.VMEM((rows, rows), jnp.bfloat16),
            pltpu.VMEM((PAD, rows), jnp.float32),
        ],
        cost_estimate=pl.CostEstimate(
            flops=30_000_000_000, bytes_accessed=20_000_000, transcendentals=12_000_000
        ),
    )(bias, qkv, heads_out, lse, heads_grad)


def swap_with_partner(values):
    size = lax.axis_size("mp")
    return lax.ppermute(values, "mp", [(i, i ^ 1) for i in range(size)])


def pad_heads(values):
    return jnp.pad(values, [(0, 0)] * (values.ndim - 1) + [(0, PAD - values.shape[-1])])


MESH = pl.DeviceIdType.MESH


def positions():
    mp, dp = lax.axis_index("mp"), lax.axis_index("dp")
    return mp, lax.div(mp, 2), lax.rem(mp, 2), lax.div(dp, 2), lax.rem(dp, 2)


def at_place(x, c, z, y):
    return (2 * z + y, 2 * x + c)


def neighbours(nz):
    mp, x, c, z, y = positions()
    first = at_place(lax.rem(x + c, 2), c, z, lax.rem(y + 1 - c, 2))
    second = at_place(lax.rem(x + 1 - c, 2), c, z, lax.rem(y + c, 2))
    partner = at_place(x, 1 - c, z, y)
    along = [at_place(x, c, lax.rem(z + d, nz), y) for d in range(1, nz)]
    return first, second, partner, along


def meet(devices):
    barrier = pltpu.get_barrier_semaphore()
    for device in devices:
        pl.semaphore_signal(barrier, inc=1, device_id=device, device_id_type=MESH)
    pl.semaphore_wait(barrier, len(devices))


def regions(x, c, y):
    own = (x, y)
    first = (lax.rem(x + c, 2), lax.rem(y + 1 - c, 2))
    second = (lax.rem(x + 1 - c, 2), lax.rem(y + c, 2))
    third = (1 - x, 1 - y)
    return own, first, second, third


def gather_kernel(nz, parts, *refs):
    shards, fulls = refs[:parts], refs[parts : 2 * parts]
    own_sem, z_send, z_recv, send, recv = refs[2 * parts :]
    mp, x, c, z, y = positions()
    first, second, partner, along = neighbours(nz)
    meet([first, second, partner, *along])
    own, got1, got2, got3 = regions(x, c, y)
    other = regions(x, 1 - c, y)

    def remote(src, dst, s, r, device):
        return pltpu.make_async_remote_copy(
            src_ref=src, dst_ref=dst, send_sem=s, recv_sem=r, device_id=device, device_id_type=MESH
        )

    started = []
    locals_ = []
    spread = []
    for p in range(parts):
        keep = pltpu.make_async_copy(shards[p], fulls[p].at[x, c, z, y], own_sem.at[p])
        keep.start()
        locals_.append(keep)
        sends = [
            remote(shards[p], fulls[p].at[x, c, z, y], z_send.at[p, d], z_recv.at[p, d], along[d])
            for d in range(nz - 1)
        ]
        for copy in sends:
            copy.start()
        spread.append(sends)

    def block(p, core, place):
        return fulls[p].at[place[0], core, :, place[1]]

    def push(p, k, core, place, device):
        copy = remote(block(p, core, place), block(p, core, place), send.at[p, k], recv.at[p, k], device)
        copy.start()
        started.append(copy)
        return copy

    def arrived(p, k, core, place):
        here = block(p, core, place)
        remote(here, here, send.at[p, k], recv.at[p, k], first).wait_recv()

    for p in range(parts):
        locals_[p].wait()
        for copy in spread[p]:
            copy.wait_recv()
        push(p, 0, c, own, first)
        push(p, 1, c, own, second)
        push(p, 3, c, own, partner)
    for p in range(parts):
        arrived(p, 0, c, got1)
        push(p, 2, c, got1, second)
        push(p, 4, c, got1, partner)
    for p in range(parts):
        arrived(p, 1, c, got2)
        push(p, 5, c, got2, partner)
        arrived(p, 2, c, got3)
        push(p, 6, c, got3, partner)
    for p in range(parts):
        for k in range(4):
            arrived(p, 3 + k, 1 - c, other[k])
    for sends in spread:
        for copy in sends:
            copy.wait_send()
    for copy in started:
        copy.wait_send()


def gather_all(shards):
    n_dp = lax.axis_size("dp")
    nz, parts = n_dp // 2, len(shards)
    return pl.pallas_call(
        functools.partial(gather_kernel, nz, parts),
        in_specs=[pl.BlockSpec(memory_space=pltpu.VMEM)] * parts,
        out_specs=[pl.BlockSpec(memory_space=pl.ANY)] * parts,
        out_shape=[jax.ShapeDtypeStruct((2, 2, nz, 2, *s.shape), s.dtype) for s in shards],
        scratch_shapes=[
            pltpu.SemaphoreType.DMA((parts,)),
            pltpu.SemaphoreType.DMA((parts, nz - 1)),
            pltpu.SemaphoreType.DMA((parts, nz - 1)),
            pltpu.SemaphoreType.DMA((parts, 7)),
            pltpu.SemaphoreType.DMA((parts, 7)),
        ],
        compiler_params=pltpu.CompilerParams(collective_id=0, has_side_effects=True),
    )(*shards)


def scatter_kernel(nz, parts, side, *refs):
    partials, results = refs[:parts], refs[parts : 2 * parts]
    at = 2 * parts
    sums, heard1, heard2, heard3, heard4 = (
        refs[at + i * parts : at + (i + 1) * parts] for i in range(5)
    )
    own_sem, send, recv, z_send, z_recv = refs[at + 5 * parts :]
    mp, x, c, z, y = positions()
    first, second, partner, along = neighbours(nz)
    meet([first, second, partner, *along])
    own, got1, got2, got3 = regions(x, c, y)
    started = []

    def remote(src, dst, s, r, device):
        copy = pltpu.make_async_remote_copy(
            src_ref=src, dst_ref=dst, send_sem=s, recv_sem=r, device_id=device, device_id_type=MESH
        )
        copy.start()
        started.append(copy)
        return copy

    def add(p, place, more):
        for i in range(nz):
            here = sums[p].at[place[0], i, place[1]]
            here[...] = (here[...].astype(jnp.float32) + more[i].astype(jnp.float32)).astype(here.dtype)

    def cut(p, k, core):
        if p not in side:
            return partials[p].at[k, core]
        size = partials[p].shape[3] // 4
        return partials[p].at[:, :, :, pl.ds(pl.multiple_of((2 * k + core) * size, size), size)]

    kept, core_copies = [], []
    for p in range(parts):
        copies = []
        for k in range(2):
            keep = pltpu.make_async_copy(cut(p, k, c), sums[p].at[k], own_sem.at[p, k])
            keep.start()
            copies.append(keep)
        kept.append(copies)
        core_copies.append(
            [
                remote(cut(p, k, 1 - c), heard1[p].at[k], send.at[p, k], recv.at[p, k], partner)
                for k in range(2)
            ]
        )
    second_copies = []
    for p in range(parts):
        for copy in kept[p]:
            copy.wait()
        for copy in core_copies[p]:
            copy.wait_recv()
        copies = []
        for k, place in enumerate((got2, got3)):
            add(p, place, heard1[p].at[place[0], :, place[1]])
            copies.append(
                remote(
                    sums[p].at[place[0], :, place[1]],
                    heard2[p].at[k],
                    send.at[p, 2 + k],
                    recv.at[p, 2 + k],
                    second,
                )
            )
        second_copies.append(copies)
        for place in (got1, own):
            add(p, place, heard1[p].at[place[0], :, place[1]])
    first_copies = []
    for p in range(parts):
        second_copies[p][1].wait_recv()
        add(p, got1, heard2[p].at[1])
        first_copies.append(
            remote(sums[p].at[got1[0], :, got1[1]], heard3[p], send.at[p, 4], recv.at[p, 4], first)
        )
        second_copies[p][0].wait_recv()
        add(p, own, heard2[p].at[0])
    last_copies = []
    for p in range(parts):
        first_copies[p].wait_recv()
        add(p, own, heard3[p])
        last_copies.append(
            [
                remote(
                    sums[p].at[x, lax.rem(z + d + 1, nz), y],
                    heard4[p].at[d],
                    z_send.at[p, d],
                    z_recv.at[p, d],
                    along[d],
                )
                for d in range(nz - 1)
            ]
        )
    for p in range(parts):
        for copy in last_copies[p]:
            copy.wait_recv()
        total = sums[p][x, z, y].astype(jnp.float32)
        for d in range(nz - 1):
            total = total + heard4[p][d].astype(jnp.float32)
        results[p][...] = total
    for copy in started:
        copy.wait_send()


def scatter_sums(partials, side=()):
    nz, parts = lax.axis_size("dp") // 2, len(partials)
    tails = [
        (p.shape[2], p.shape[3] // 4) if i in side else p.shape[4:] for i, p in enumerate(partials)
    ]
    kinds = [p.dtype for p in partials]
    return pl.pallas_call(
        functools.partial(scatter_kernel, nz, parts, side),
        in_specs=[pl.BlockSpec(memory_space=pl.ANY)] * parts,
        out_specs=[pl.BlockSpec(memory_space=pltpu.VMEM)] * parts,
        out_shape=[jax.ShapeDtypeStruct(t, jnp.float32) for t in tails],
        scratch_shapes=[
            *[pltpu.VMEM((2, nz, 2, *t), k) for t, k in zip(tails, kinds)],
            *[pltpu.VMEM((2, nz, 2, *t), k) for t, k in zip(tails, kinds)],
            *[pltpu.VMEM((2, nz, *t), k) for t, k in zip(tails, kinds)],
            *[pltpu.VMEM((nz, *t), k) for t, k in zip(tails, kinds)],
            *[pltpu.VMEM((nz - 1, *t), k) for t, k in zip(tails, kinds)],
            pltpu.SemaphoreType.DMA((parts, 2)),
            pltpu.SemaphoreType.DMA((parts, 5)),
            pltpu.SemaphoreType.DMA((parts, 5)),
            pltpu.SemaphoreType.DMA((parts, nz - 1)),
            pltpu.SemaphoreType.DMA((parts, nz - 1)),
        ],
        compiler_params=pltpu.CompilerParams(
            collective_id=1, has_side_effects=True, vmem_limit_bytes=60 * 1024 * 1024
        ),
    )(*partials)


def in_place_order(blocks):
    return blocks.reshape(2, 2, blocks.shape[1] // 2, 2, *blocks.shape[2:])


def body_any(
    tokens,
    cotangent,
    lengths,
    w_query,
    w_key,
    w_value,
    w_out,
    w_up,
    w_down,
    b_query,
    b_value,
    b_up,
    b_out,
    b_down,
    norm1_gain,
    norm1_shift,
    norm2_gain,
    norm2_shift,
):
    half_rows = tokens.shape[1]
    width = tokens.shape[2]
    n_dp, n_mp = lax.axis_size("dp"), lax.axis_size("mp")
    unit_cols = w_up.shape[1]
    mp_index = lax.axis_index("mp")
    half = lax.rem(mp_index, 2)
    seq = lax.div(mp_index, 2)

    def own_of(pair):
        return jnp.where(half == 0, pair[0], pair[1])

    def other_of(pair):
        return jnp.where(half == 0, pair[1], pair[0])

    rows_in = jnp.concatenate([own_of(tokens), swap_with_partner(other_of(tokens))], axis=0)
    rows_cot = jnp.concatenate([own_of(cotangent), swap_with_partner(other_of(cotangent))], axis=0)
    length = lax.dynamic_slice(lengths, (half, seq), (1, 1))[0, 0]
    place = jnp.arange(half_rows, dtype=jnp.int32)
    place = jnp.concatenate([place + half * half_rows, place + (1 - half) * half_rows])
    valid_row = (place < length)[:, None]
    bias = jnp.where(valid_row, 0.0, masked_score).astype(jnp.bfloat16)
    valid_row = valid_row.astype(jnp.float32)

    biases = jnp.pad(jnp.concatenate([b_query, b_value, b_up]), (0, 896)).reshape(16, 128)
    qkv_shard = jnp.concatenate([w_query, w_key, w_value], axis=1)
    gathered = gather_all([qkv_shard, w_out, w_up, w_down, biases])
    full_qkv, full_out, full_up, full_down, full_bias = (
        g.reshape(n_mp, n_dp, *g.shape[4:]) for g in gathered
    )
    full_qkv = full_qkv.reshape(n_mp, width, 3, GC)
    w_joined = pad_heads(full_qkv).reshape(n_mp, width, 3 * PAD)
    full_out = full_out.reshape(n_mp, GC, width)
    out_pad = jnp.pad(full_out, ((0, 0), (0, PAD - GC), (0, 0))).reshape(n_mp * PAD, width)
    full_up = full_up.reshape(n_mp, width, unit_cols).transpose(1, 0, 2).reshape(width, n_mp * unit_cols)
    full_down = full_down.reshape(n_mp * unit_cols, width)
    full_bias = full_bias[:, 0].reshape(n_mp, -1)
    bias_q, bias_v, bias_up = full_bias[:, :GC], full_bias[:, GC:2*GC], full_bias[:, 2*GC:2*GC+unit_cols]
    mark = jnp.zeros((n_mp, PAD - GC), jnp.float32).at[:, 0].set(1.0)
    joined_bias = jnp.concatenate(
        [bias_q, mark, jnp.zeros((n_mp, PAD), jnp.float32), pad_heads(bias_v)], axis=1
    )

    qkv = lax.dot_general(
        jnp.broadcast_to(rows_in[None], (n_mp, *rows_in.shape)),
        w_joined,
        (((2,), (1,)), ((0,), (0,))),
        preferred_element_type=jnp.float32,
    )
    qkv = (qkv + joined_bias[:, None, :]).astype(jnp.bfloat16)
    heads_out, lse = attend_forward(qkv, bias)
    heads_flat = heads_out.transpose(1, 0, 2).reshape(2 * half_rows, n_mp * PAD)
    attention = product(heads_flat, out_pad) + b_out
    first_norm, first_scaled, first_inverse = layer_norm(
        rows_in.astype(jnp.float32) + attention, norm1_gain, norm1_shift
    )
    first_low = first_norm.astype(jnp.bfloat16)
    preact = product(first_low, full_up) + bias_up.reshape(-1)
    cumulative = 0.5 * (1.0 + lax.erf(preact * 0.7071067811865476))
    active = (preact * cumulative).astype(jnp.bfloat16)
    slope = cumulative + preact * (jnp.exp(-0.5 * preact * preact) * 0.3989422804014327)
    ffn_out = product(active, full_down) + b_down
    stream = first_norm + ffn_out
    final_norm, final_scaled, final_inverse = layer_norm(stream, norm2_gain, norm2_shift)
    output = final_norm.astype(jnp.bfloat16)
    squares = jnp.stack(
        [
            jnp.sum(valid_row * stream * stream),
            jnp.sum(valid_row * attention * attention),
            jnp.sum(valid_row * ffn_out * ffn_out),
            jnp.sum(valid_row),
        ]
    )

    stream_grad, gain2_grad, shift2_grad = norm_back(
        rows_cot.astype(jnp.float32), final_scaled, final_inverse, norm2_gain
    )
    down_bias_grad = jnp.sum(stream_grad, axis=0)
    ffn_grad_low = stream_grad.astype(jnp.bfloat16)
    active_grad = contract_cols(ffn_grad_low, full_down)
    down_wgrad = contract_rows(active, ffn_grad_low)
    preact_grad = active_grad * slope
    up_bias_grad = jnp.sum(preact_grad, axis=0)
    preact_low = preact_grad.astype(jnp.bfloat16)
    up_wgrad = contract_rows(first_low, preact_low)
    first_grad = stream_grad + contract_cols(preact_low, full_up)
    attn_grad, gain1_grad, shift1_grad = norm_back(
        first_grad, first_scaled, first_inverse, norm1_gain
    )
    out_bias_grad = jnp.sum(attn_grad, axis=0)
    attn_grad_low = attn_grad.astype(jnp.bfloat16)
    out_wgrad = contract_rows(heads_flat, attn_grad_low)
    heads_grad = contract_cols(attn_grad_low, out_pad).astype(jnp.bfloat16)
    heads_grad = heads_grad.reshape(2 * half_rows, n_mp, PAD).transpose(1, 0, 2)
    joined, sums = attend_backward(qkv, bias, heads_out, lse, heads_grad)
    joined_wgrad = lax.dot_general(
        jnp.broadcast_to(rows_in[None], (n_mp, *rows_in.shape)),
        joined,
        (((1,), (1,)), ((0,), (0,))),
        preferred_element_type=jnp.float32,
    )
    tokens_grad = attn_grad + jnp.sum(
        lax.dot_general(
            joined, w_joined, (((2,), (2,)), ((0,), (0,))), preferred_element_type=jnp.float32
        ),
        axis=0,
    )

    low = jnp.bfloat16
    joined_blocks = (
        joined_wgrad.astype(low)
        .reshape(n_mp, n_dp, width // n_dp, 3, PAD)[..., :GC]
        .reshape(n_mp, n_dp, width // n_dp, 3 * GC)
    )
    out_blocks = (
        out_wgrad.astype(low)
        .reshape(n_mp, PAD, width)[:, :GC]
        .reshape(n_mp, n_dp, GC // n_dp, width)
    )
    up_blocks = up_wgrad.astype(low).reshape(n_dp, width // n_dp, n_mp, unit_cols).transpose(2, 0, 1, 3)
    down_blocks = down_wgrad.astype(low).reshape(n_mp, n_dp, unit_cols // n_dp, width)

    def by_mp(vector):
        return vector.reshape(n_mp, n_dp, -1)

    def by_dp(vector):
        return vector.reshape(n_dp, n_mp, -1).transpose(1, 0, 2)

    vectors = [by_mp(sums[:, 0, :GC]), by_mp(sums[:, 1, :GC]), by_mp(up_bias_grad)]
    vectors += [
        by_dp(v)
        for v in (out_bias_grad, down_bias_grad, gain1_grad, shift1_grad, gain2_grad, shift2_grad)
    ]
    vectors.append(jnp.broadcast_to(squares, (n_mp, n_dp, 4)))
    ends = [v.shape[-1] for v in vectors]
    vectors = jnp.concatenate(vectors, axis=-1)
    vectors = jnp.pad(vectors, ((0, 0), (0, 0), (0, 1024 - vectors.shape[-1])))
    vectors = vectors.reshape(n_mp, n_dp, 8, 128)
    own_down, own_up, own_out, own_joined, own_vector = scatter_sums(
        [
            in_place_order(b)
            for b in (down_blocks, up_blocks, out_blocks, joined_blocks, vectors)
        ]
    )
    own_vector = own_vector.reshape(-1)
    own_vectors, start = [], 0
    for size in ends:
        own_vectors.append(own_vector[start : start + size])
        start += size
    totals = own_vectors.pop()
    rms_values = jnp.sqrt(totals[:3] / (totals[3] * width))

    def back_home(rows):
        mine, sent = rows[:half_rows], swap_with_partner(rows[half_rows:])
        return jnp.where(half == 0, jnp.stack([mine, sent]), jnp.stack([sent, mine]))

    return (
        back_home(output),
        back_home(tokens_grad),
        own_joined[:, :GC],
        own_joined[:, GC : 2 * GC],
        own_joined[:, 2 * GC :],
        own_out,
        own_up,
        own_down,
        *own_vectors,
        rms_values,
    )


PARTS = 4


def remote_copy(src, dst, s, r, device):
    return pltpu.make_async_remote_copy(
        src_ref=src, dst_ref=dst, send_sem=s, recv_sem=r, device_id=device, device_id_type=MESH
    )


def forward_kernel(
    nz,
    lengths,
    tokens,
    cotangent,
    shard_wq,
    shard_wk,
    shard_wv,
    shard_o,
    shard_u,
    shard_d,
    bias_shard,
    full_q,
    full_o,
    full_u,
    full_d,
    bias_full,
    rows_out,
    cot_out,
    w_out,
    qkv_out,
    heads_out,
    lse_out,
    shard_q,
    rows,
    cots,
    w_got,
    w_pad,
    qkv,
    values_t,
    turned,
    heads,
    own_sem,
    z_send,
    z_recv,
    relay_send,
    send,
    recv,
    swap_send,
    swap_recv,
    bias_send,
    bias_recv,
    out_sem,
):
    shards = (shard_q, shard_o, shard_u, shard_d)
    fulls = (full_q, full_o, full_u, full_d)
    half_rows = tokens.shape[1]
    length = 2 * half_rows
    mp, x, c, z, y = positions()
    half = c
    seq = x
    first, second, partner, along = neighbours(nz)
    across = at_place(1 - x, c, z, y)
    slanted = at_place(1 - x, 1 - c, z, y)
    own, got1, got2, got3 = regions(x, c, y)
    other = regions(x, 1 - c, y)
    for k, shard in enumerate((shard_wq, shard_wk, shard_wv)):
        shard_q[:, k * GC : (k + 1) * GC] = shard[...]
    meet([first, second, partner, slanted, *along])

    def block(p, core, place, d):
        return fulls[p].at[place[0], core, lax.rem(z + nz - d, nz), place[1]]

    places = (own, own, got1, own, got1, got2, got3)
    targets = (first, second, second, partner, partner, partner, partner)
    landing = (got1, got2, got3, *other)
    cores = (c, c, c, 1 - c, 1 - c, 1 - c, 1 - c)

    def outgoing(p, k, d):
        here = block(p, c, places[k], d)
        return remote_copy(here, here, send.at[p, k, d], recv.at[p, k, d], targets[k])

    def incoming(p, k, d):
        here = block(p, cores[k], landing[k], d)
        return remote_copy(here, here, send.at[p, k, d], recv.at[p, k, d], targets[k])

    at_low = 1 - lax.div(z + nz - 1, nz)
    near, far = 1 + 2 * at_low, 3 - 2 * at_low

    def z_copy(p, d):
        return remote_copy(
            shards[p], fulls[p].at[x, c, z, y], z_send.at[p, d - 1], z_recv.at[p, d - 1], along[d - 1]
        )

    def z_each(p, act):
        act(z_copy(p, 2))
        pl.when(z != nz - 1)(lambda: act(z_copy(p, 1)))
        pl.when(z != 0)(lambda: act(z_copy(p, 3)))

    def z_start(p):
        z_each(p, lambda copy: copy.start())

    def z_relay(p, low):
        here = block(p, c, own, 2)
        d = 1 if low else 3
        return remote_copy(here, here, relay_send.at[p], z_recv.at[p, d - 1], at_place(x, c, z + d - 2, y))

    def spread(p, d):
        if not (isinstance(d, int) and d == 0):
            here = block(p, c, own, d)
            remote_copy(here, here, z_send.at[p, d - 1], z_recv.at[p, d - 1], first).wait_recv()
        if isinstance(d, int) and d == 2:
            pl.when(z == 1)(lambda: z_relay(p, True).start())
            pl.when(z == 2)(lambda: z_relay(p, False).start())
        for k in (0, 1, 3):
            outgoing(p, k, d).start()

    def forward1(p):
        for d in range(nz):
            incoming(p, 0, d).wait_recv()
            outgoing(p, 2, d).start()
            outgoing(p, 4, d).start()

    def forward2(p):
        for d in range(nz):
            incoming(p, 1, d).wait_recv()
            outgoing(p, 5, d).start()

    def forward3(p):
        for d in range(nz):
            incoming(p, 2, d).wait_recv()
            outgoing(p, 6, d).start()

    def take(p, k):
        for d in range(nz):
            incoming(p, k, d).wait_recv()

    keep = [
        pltpu.make_async_copy(shards[p], fulls[p].at[x, c, z, y], own_sem.at[p]) for p in range(PARTS)
    ]
    keep_rows = pltpu.make_async_copy(tokens.at[half], rows.at[pl.ds(0, half_rows)], own_sem.at[PARTS])
    keep_cots = pltpu.make_async_copy(cotangent.at[half], cots.at[pl.ds(0, half_rows)], own_sem.at[PARTS + 2])
    swap_rows = remote_copy(
        tokens.at[1 - half], rows.at[pl.ds(half_rows, half_rows)], swap_send.at[0], swap_recv.at[0], partner
    )
    swap_cot = remote_copy(
        cotangent.at[1 - half], cots.at[pl.ds(half_rows, half_rows)], swap_send.at[1], swap_recv.at[1], partner
    )
    bias_copies = [
        remote_copy(bias_shard, bias_full.at[mp], bias_send.at[k], bias_recv.at[k], device)
        for k, device in enumerate((partner, across, slanted))
    ]
    z_start(0)
    keep[0].start()
    for copy in bias_copies:
        copy.start()
    swap_rows.start()
    keep_rows.start()
    for p in range(1, PARTS):
        keep[p].start()
    keep[0].wait()
    spread(0, 0)
    for p in range(1, PARTS):
        z_start(p)
    w_pad[...] = jnp.zeros_like(w_pad)
    turned[...] = jnp.zeros_like(turned)
    bias_full[mp] = bias_shard[...]
    for d in (2, near, far):
        spread(0, d)
    for copy in keep[1:]:
        copy.wait()
    forward1(0)
    for p in range(1, PARTS):
        spread(p, 0)
    forward2(0)
    swap_cot.start()
    keep_cots.start()
    keep_rows.wait()
    swap_rows.wait_recv()
    rows_copy = pltpu.make_async_copy(rows, rows_out, out_sem.at[2])
    rows_copy.start()
    cots_copy = pltpu.make_async_copy(cots, cot_out, out_sem.at[4])
    for copy in bias_copies:
        copy.wait_recv()

    hooks = {
        0: [lambda: [spread(1, d) for d in (2, near, far)]],
        1: [lambda: forward3(0)],
        2: [lambda: [spread(2, d) for d in (2, near)]],
        3: [lambda: spread(2, far), lambda: forward1(1)],
        4: [lambda: forward2(1), lambda: forward3(1)],
        5: [lambda: [spread(3, d) for d in (2, near)]],
        6: [lambda: spread(3, far)],
        7: [lambda: forward1(2)],
        8: [lambda: forward2(2)],
        10: [lambda: forward1(3)],
        11: [lambda: forward2(3)],
    }
    seq_length = lengths[half, seq]
    row = lax.broadcasted_iota(jnp.int32, (length, 1), 0)
    place = jnp.where(row < half_rows, row + half * half_rows, row - half * half_rows)
    bias = jnp.where(place < seq_length, 0.0, masked_score).astype(jnp.bfloat16)
    lane = lax.broadcasted_iota(jnp.int32, (1, PAD), 1)
    chunk = 256

    def heads_copy(gx, gc):
        columns = pl.ds(pl.multiple_of((2 * gx + gc) * PAD, PAD), PAD)
        return pltpu.make_async_copy(heads, heads_out.at[:, columns], out_sem.at[0])

    def qkv_copy(gx, gc):
        return pltpu.make_async_copy(qkv, qkv_out.at[2 * gx + gc], out_sem.at[1])

    def w_copy(gx, gc):
        return pltpu.make_async_copy(w_pad, w_out.at[2 * gx + gc], out_sem.at[3])

    def group_step(r, carry):
        gx, gc = lax.rem(x + lax.div(r, 2), 2), lax.rem(c + lax.rem(r, 2), 2)
        group = 2 * gx + gc

        @pl.when(r == 1)
        def _():
            for d in range(nz):
                incoming(0, 3, d).wait_recv()
            for d in range(nz):
                here = block(0, 1 - c, own, d)
                remote_copy(here, here, send.at[0, 5 - c, d], recv.at[0, 5 - c, d], first).wait_recv()

        @pl.when(r == 3)
        def _():
            for d in range(nz):
                here = block(0, 1 - c, own, d)
                remote_copy(here, here, send.at[0, 4 + c, d], recv.at[0, 4 + c, d], first).wait_recv()
            take(0, 6)

        load = pltpu.make_async_copy(full_q.at[gx, gc], w_got, own_sem.at[PARTS + 1])
        load.start()
        load.wait()

        @pl.when(r > 0)
        def _():
            qkv_copy(gx, gc).wait()
            w_copy(gx, gc).wait()

        w_flat = w_got[...].reshape(-1, 3 * GC)
        for k in range(3):
            w_pad[:, k * PAD : k * PAD + GC] = w_flat[:, k * GC : (k + 1) * GC]
        w_copy(gx, gc).start()
        joined_bias = bias_full[group, 0:1, :]
        for at in range(0, length, 512):
            qkv[at : at + 512, :] = (product(rows[at : at + 512, :], w_pad[...]) + joined_bias).astype(
                jnp.bfloat16
            )
        qkv_copy(gx, gc).start()
        values_t[...] = qkv[:, 2 * PAD :].T

        def head_step(h, carry):
            for k, todo in hooks.items():
                if todo:

                    @pl.when(r * GH + h == k)
                    def _():
                        for task in todo:
                            task()

            start = h * HD
            keys = qkv[:, PAD : 2 * PAD]
            kept = jnp.where((lane >= start) & (lane < start + HD), keys, jnp.zeros_like(keys))
            own_keys = jnp.where(lane == GC, bias, kept)
            own_values = values_t[pl.ds(pl.multiple_of(start, HD), HD), :]
            for at in range(0, length, chunk):
                scores = contract_cols(own_keys, qkv[at : at + chunk, :PAD])
                top = jnp.max(scores, axis=0, keepdims=True) * exp2_scale
                raised = jnp.exp2(scores * exp2_scale - top)
                total = jnp.sum(raised, axis=0, keepdims=True)
                mixed = product(own_values, raised.astype(jnp.bfloat16))
                turned[pl.ds(pl.multiple_of(start, HD), HD), at : at + chunk] = mixed / total
                lse_out[group, pl.ds(h, 1), at : at + chunk] = top + jnp.log2(total)
            return carry

        lax.fori_loop(0, GH, head_step, 0)

        @pl.when(r > 0)
        def _():
            heads_copy(gx, gc).wait()

        heads[...] = turned[...].T.astype(jnp.bfloat16)
        heads_copy(gx, gc).start()
        return carry

    lax.fori_loop(0, GROUPS, group_step, 0)
    keep_cots.wait()
    swap_cot.wait_recv()
    cots_copy.start()
    forward3(2)
    forward3(3)
    for p in range(1, PARTS):
        for k in range(3, 7):
            take(p, k)
    heads_copy(x, c).wait()
    qkv_copy(x, c).wait()
    w_copy(x, c).wait()
    rows_copy.wait()
    cots_copy.wait()
    swap_cot.wait_send()
    swap_rows.wait_send()
    for copy in bias_copies:
        copy.wait_send()
    for p in range(PARTS):
        z_each(p, lambda copy: copy.wait_send())
        pl.when(z == 1)(lambda: z_relay(p, True).wait_send())
        pl.when(z == 2)(lambda: z_relay(p, False).wait_send())
        for k in range(7):
            for d in range(nz):
                outgoing(p, k, d).wait_send()


def forward_attention(lengths, tokens, cotangent, shards, bias_shard):
    nz = lax.axis_size("dp") // 2
    half_rows, width = tokens.shape[1:]
    rows = 2 * half_rows
    low = jnp.bfloat16
    joined_shape = (shards[0].shape[0], 3 * GC)
    anywhere, vmem = pl.BlockSpec(memory_space=pl.ANY), pl.BlockSpec(memory_space=pltpu.VMEM)
    dma = pltpu.SemaphoreType.DMA
    return pl.pallas_call(
        functools.partial(forward_kernel, nz),
        in_specs=[pl.BlockSpec(memory_space=pltpu.SMEM), anywhere, anywhere, *[vmem] * 7],
        out_specs=[*[anywhere] * PARTS, vmem, *[anywhere] * 5, vmem],
        out_shape=[
            *[
                jax.ShapeDtypeStruct((2, 2, nz, 2, *shape), low)
                for shape in (joined_shape, *[s.shape for s in shards[3:]])
            ],
            jax.ShapeDtypeStruct((GROUPS, *bias_shard.shape), jnp.float32),
            jax.ShapeDtypeStruct((rows, width), low),
            jax.ShapeDtypeStruct((rows, width), low),
            jax.ShapeDtypeStruct((GROUPS, width, 3 * PAD), low),
            jax.ShapeDtypeStruct((GROUPS, rows, 3 * PAD), low),
            jax.ShapeDtypeStruct((rows, GROUPS * PAD), low),
            jax.ShapeDtypeStruct((GROUPS, 8, rows), jnp.float32),
        ],
        scratch_shapes=[
            pltpu.VMEM(joined_shape, low),
            pltpu.VMEM((rows, width), low),
            pltpu.VMEM((rows, width), low),
            pltpu.VMEM((nz, 2, *joined_shape), low),
            pltpu.VMEM((width, 3 * PAD), low),
            pltpu.VMEM((rows, 3 * PAD), low),
            pltpu.VMEM((PAD, rows), low),
            pltpu.VMEM((PAD, rows), jnp.float32),
            pltpu.VMEM((rows, PAD), low),
            dma((PARTS + 3,)),
            dma((PARTS, nz - 1)),
            dma((PARTS, nz - 1)),
            dma((PARTS,)),
            dma((PARTS, 7, nz)),
            dma((PARTS, 7, nz)),
            dma((2,)),
            dma((2,)),
            dma((3,)),
            dma((3,)),
            dma((5,)),
        ],
        compiler_params=pltpu.CompilerParams(
            collective_id=2, has_side_effects=True, vmem_limit_bytes=60 * 1024 * 1024
        ),
    )(lengths, tokens, cotangent, *shards, bias_shard)


def place_of(half, row, half_rows):
    return jnp.where(row < half_rows, row + half * half_rows, row - half * half_rows)


def dense_kernel(
    lengths,
    heads_ref,
    rows_ref,
    cot_ref,
    out_full,
    up_full,
    down_full,
    bias_ref,
    output_ref,
    first_ref,
    active_ref,
    ffn_low_ref,
    preact_low_ref,
    attn_ref,
    attn_low_ref,
    heads_grad_ref,
    sums_ref,
    slope,
    out_pad,
    up_w,
    down_w,
    load_sem,
):
    t = pl.program_id(0)
    mp = lax.axis_index("mp")
    half, seq = lax.rem(mp, 2), lax.div(mp, 2)
    low = jnp.bfloat16
    tile, width = rows_ref.shape
    units = up_w.shape[2]
    b_out, b_down, gain1, shift1, gain2, shift2 = (
        bias_ref[0, 2 + k : 3 + k, :] for k in range(6)
    )
    out_load = pltpu.make_async_copy(out_full, out_pad.at[:, pl.ds(0, GC), :], load_sem.at[2 * GROUPS])
    up_loads = [pltpu.make_async_copy(up_full.at[g], up_w.at[g], load_sem.at[g]) for g in range(GROUPS)]
    down_loads = [
        pltpu.make_async_copy(down_full.at[g], down_w.at[g], load_sem.at[GROUPS + g]) for g in range(GROUPS)
    ]

    @pl.when(t == 0)
    def _():
        out_load.start()
        for g in range(GROUPS):
            up_loads[g].start()
            down_loads[g].start()
        out_pad[:, GC:, :] = jnp.zeros((GROUPS, PAD - GC, width), low)
        sums_ref[...] = jnp.zeros_like(sums_ref)
        out_load.wait()

    out_w = out_pad[...].reshape(GROUPS * PAD, width)

    def count(k, values):
        sums_ref[k : k + 1, :] += jnp.sum(values, axis=0, keepdims=True)

    attention = product(heads_ref[...], out_w) + b_out
    first_norm, first_scaled, first_inverse = layer_norm(
        rows_ref[...].astype(jnp.float32) + attention, gain1, shift1
    )
    first_low = first_norm.astype(low)
    first_ref[...] = first_low

    @pl.when(t == 0)
    def _():
        for copy in (*up_loads, *down_loads):
            copy.wait()

    ffn_out = jnp.broadcast_to(b_down, (tile, width))
    for g in range(GROUPS):
        preact = product(first_low, up_w[g]) + bias_ref[g, 1:2, :]
        cumulative = 0.5 * (1.0 + lax.erf(preact * 0.7071067811865476))
        active = (preact * cumulative).astype(low)
        active_ref[:, g * units : (g + 1) * units] = active
        slope[:, g * units : (g + 1) * units] = cumulative + preact * (
            jnp.exp(-0.5 * preact * preact) * 0.3989422804014327
        )
        ffn_out = ffn_out + product(active, down_w[g])
    stream = first_norm + ffn_out
    row = lax.broadcasted_iota(jnp.int32, (tile, 1), 0) + t * tile
    valid = (place_of(half, row, pl.num_programs(0) * tile // 2) < lengths[half, seq]).astype(jnp.float32)
    count(6, valid * stream * stream)
    count(7, valid * attention * attention)
    count(8, valid * ffn_out * ffn_out)
    count(9, jnp.broadcast_to(valid, (tile, width)))
    final_norm, final_scaled, final_inverse = layer_norm(stream, gain2, shift2)
    output_ref[...] = final_norm.astype(low)

    def norm_step(k, upstream, scaled, inverse, gain):
        count(k, upstream * scaled)
        count(k + 1, upstream)
        through = upstream * gain
        return inverse * (
            through
            - jnp.mean(through, axis=-1, keepdims=True)
            - scaled * jnp.mean(through * scaled, axis=-1, keepdims=True)
        )

    stream_grad = norm_step(4, cot_ref[...].astype(jnp.float32), final_scaled, final_inverse, gain2)
    count(1, stream_grad)
    ffn_grad_low = stream_grad.astype(low)
    ffn_low_ref[...] = ffn_grad_low
    first_grad = stream_grad
    for g in range(GROUPS):
        preact_grad = contract_cols(ffn_grad_low, down_w[g]) * slope[:, g * units : (g + 1) * units]
        count(12 + g, preact_grad)
        preact_low = preact_grad.astype(low)
        preact_low_ref[:, g * units : (g + 1) * units] = preact_low
        first_grad = first_grad + contract_cols(preact_low, up_w[g])
    attn_grad = norm_step(2, first_grad, first_scaled, first_inverse, gain1)
    count(0, attn_grad)
    attn_ref[...] = attn_grad
    attn_grad_low = attn_grad.astype(low)
    attn_low_ref[...] = attn_grad_low
    heads_grad_ref[...] = contract_cols(attn_grad_low, out_w).astype(low)


def dense(lengths, heads, rows, cots, out_w, up_w, down_w, biases):
    count, width = rows.shape
    tile = 256
    units = up_w.shape[2]
    low = jnp.bfloat16

    def whole(shape):
        return pl.BlockSpec(shape, lambda t: (0,) * len(shape))

    def tiled(columns):
        return pl.BlockSpec((tile, columns), lambda t: (t, 0))

    outs = [
        (width, low),
        (width, low),
        (GROUPS * units, low),
        (width, low),
        (GROUPS * units, low),
        (width, jnp.float32),
        (width, low),
        (GROUPS * PAD, low),
    ]
    return pl.pallas_call(
        dense_kernel,
        grid=(count // tile,),
        in_specs=[
            pl.BlockSpec(memory_space=pltpu.SMEM),
            tiled(GROUPS * PAD),
            tiled(width),
            tiled(width),
            *[pl.BlockSpec(memory_space=pl.ANY)] * 3,
            whole(biases.shape),
        ],
        out_specs=[*[tiled(columns) for columns, _ in outs], whole((16, width))],
        out_shape=[
            *[jax.ShapeDtypeStruct((count, columns), kind) for columns, kind in outs],
            jax.ShapeDtypeStruct((16, width), jnp.float32),
        ],
        scratch_shapes=[
            pltpu.VMEM((tile, GROUPS * units), jnp.float32),
            pltpu.VMEM((GROUPS, PAD, width), low),
            pltpu.VMEM(up_w.shape, low),
            pltpu.VMEM(down_w.shape, low),
            pltpu.SemaphoreType.DMA((2 * GROUPS + 1,)),
        ],
        cost_estimate=pl.CostEstimate(
            flops=22_600_000_000, bytes_accessed=40_000_000, transcendentals=7_000_000
        ),
    )(lengths, heads, rows, cots, out_w, up_w, down_w, biases)


GRAIN = 64
BIG = 4


def backward_kernel(
    nz,
    lengths,
    lse_ref,
    dense_sums,
    rows_in,
    w_joined,
    attn_grad,
    qkv,
    heads,
    heads_grad,
    active,
    ffn_low,
    first_low,
    preact_low,
    attn_low,
    normed,
    down_out,
    up_out,
    out_out,
    query_out,
    key_out,
    value_out,
    vectors_out,
    tokens_out,
    normed_out,
    joined_kept,
    *refs,
):
    parts, heard1, heard2, heard3, heard4 = (refs[BIG * i : BIG * (i + 1)] for i in range(5))
    (
        dense_total,
        bias_sums,
        dense_kept,
        dense_heard,
        acc,
        slots,
        right,
        left_t,
        joined,
        heads_in,
        grad_in,
        w_in,
        tokens,
        probs,
        slopes,
        turned,
        crossed,
        keys_t,
        key_acc,
        value_acc,
        send,
        recv,
        z_send,
        z_recv,
        v_send,
        v_recv,
        swap_sem,
        load_sem,
        slot_sem,
        heads_sem,
        grad_sem,
    ) = refs[5 * BIG :]
    low = jnp.bfloat16
    rows, width = tokens.shape
    half_rows = rows // 2
    chunk, span = 256, 384
    bias_share = GC // (2 * nz)
    mp, x, c, z, y = positions()
    first, second, partner, along = neighbours(nz)
    own, got1, got2, got3 = regions(x, c, y)

    def group_of(r):
        return lax.rem(x + 1 + lax.rem(r, 2), 2), lax.rem(c + 1 + lax.div(r, 2), 2)

    def index_of(r):
        gx, gc = group_of(r)
        return 2 * gx + gc

    def columns(r, size):
        return pl.ds(pl.multiple_of(index_of(r) * size, size), size)

    def load(src, dst, k):
        return pltpu.make_async_copy(src, dst, load_sem.at[k])

    def slot_load(src, s):
        return pltpu.make_async_copy(src, slots.at[s], slot_sem.at[s])

    def active_load(r):
        return slot_load(active.at[:, columns(r, width)], lax.rem(r, 2))

    def preact_load(r):
        return slot_load(preact_low.at[:, columns(r, width)], lax.rem(r, 2))

    def qkv_load(r):
        return slot_load(qkv.at[index_of(r)], lax.rem(r, 2))

    def heads_load(r):
        s = lax.rem(r, 2)
        return pltpu.make_async_copy(heads.at[:, columns(r, PAD)], heads_in.at[s], heads_sem.at[s])

    def grad_load(r):
        s = lax.rem(r, 2)
        return pltpu.make_async_copy(heads_grad.at[:, columns(r, PAD)], grad_in.at[s], grad_sem.at[s])

    w_other = right.at[pl.ds(0, width)]

    def w_load(r, other=False):
        return load(w_joined.at[index_of(r)], w_other if other else w_in, 6 if other else 3)

    def keep_joined(r):
        return load(joined, joined_kept.at[r], 5)

    def back_load(r):
        return slot_load(joined_kept.at[r], lax.rem(r, 2))

    ffn_load, attn_low_load = load(ffn_low, right, 0), load(attn_low, right, 0)
    first_load, rows_load = load(first_low, joined, 1), load(rows_in, joined, 1)
    tokens_load = load(attn_grad, tokens, 2)

    def core_copy(p, r):
        gx, gc = group_of(r)
        return remote_copy(parts[p].at[gx, gc], heard1[p].at[r], send.at[p, r], recv.at[p, r], partner)

    def second_copy(p, k):
        place = (got2, got3)[k]
        return remote_copy(
            parts[p].at[place[0], c, :, place[1]], heard2[p].at[k], send.at[p, 2 + k], recv.at[p, 2 + k], second
        )

    def first_copy(p):
        return remote_copy(
            parts[p].at[got1[0], c, :, got1[1]], heard3[p], send.at[p, 4], recv.at[p, 4], first
        )

    def z_copy(p, d):
        return remote_copy(
            parts[p].at[x, c, lax.rem(z + d + 1, nz), y],
            heard4[p].at[d],
            z_send.at[p, d],
            z_recv.at[p, d],
            along[d],
        )

    def add(p, place, more):
        for i in range(nz):
            here = parts[p].at[place[0], c, i, place[1]]
            here[...] = (here[...].astype(jnp.float32) + more[i].astype(jnp.float32)).astype(low)

    def take_second(p, k):
        second_copy(p, k).wait_recv()
        add(p, got1 if k else own, heard2[p].at[k])

    def pass_first(p):
        take_second(p, 1)
        first_copy(p).start()

    def take_first(p):
        first_copy(p).wait_recv()
        add(p, own, heard3[p])
        for d in range(nz - 1):
            z_copy(p, d).start()

    def take_z(p):
        total = parts[p][x, c, z, y].astype(jnp.float32)
        for d in range(nz - 1):
            z_copy(p, d).wait_recv()
            total = total + heard4[p][d].astype(jnp.float32)
        if p < BIG - 1:
            (down_out, up_out, out_out)[p][...] = total
        else:
            for k, result in enumerate((query_out, key_out, value_out)):
                result[...] = total[:, k * GC : (k + 1) * GC]
            vectors_out[7:9, :bias_share] = total[0:2, 3 * GC : 3 * GC + bias_share]

    def sums_copy(k):
        device = (first, second)[k - 1] if 0 < k < 3 else along[k - 3] if k else partner
        return remote_copy(dense_kept.at[min(k, 3)], dense_heard.at[k], v_send.at[k], v_recv.at[k], device)

    def sums_step(k):
        sums_copy(k).wait_recv()
        dense_kept[k + 1] = dense_kept[k] + dense_heard[k]
        for later in (k + 1,) if k < 2 else range(3, nz + 2):
            sums_copy(later).start()

    def sums_last():
        total = dense_kept[3]
        for k in range(3, nz + 2):
            sums_copy(k).wait_recv()
            total = total + dense_heard[k]
        dense_total[...] = total

    def finish(p, r):
        gx, gc = group_of(r)
        deep, wide = parts[p].shape[4:]
        pieces = [(0, 0, wide)] if p < BIG - 1 else [(k * GC, k * PAD, GC) for k in range(3)]

        def put(more):
            for i in range(nz):
                for at, source, size in pieces:
                    value = acc[2 * deep * i : 2 * deep * (i + 1), source : source + size].reshape(2, deep, size)
                    if more is not None:
                        value = value + more[i, :, :, at : at + size].astype(jnp.float32)
                    parts[p][gx, gc, i, :, :, at : at + size] = value.astype(low)
            if p < BIG - 1:
                return
            beside = slice(3 * GC, 3 * GC + bias_share)
            for i in range(nz):
                for j in range(2):
                    at = (2 * i + j) * bias_share
                    value = bias_sums[:, at : at + bias_share]
                    if more is not None:
                        value = value + more[i, j, :16, beside].astype(jnp.float32)
                    parts[p][gx, gc, i, j, :16, beside] = value.astype(low)

        @pl.when(r < 2)
        def _():
            put(None)
            core_copy(p, r).start()

        @pl.when(r >= 2)
        def _():
            core_copy(p, r - 2).wait_recv()
            put(heard1[p].at[r - 2])

        @pl.when(r == 2)
        def _():
            second_copy(p, 1).start()
            pl.when(c == 0)(lambda: second_copy(p, 0).start())

        @pl.when(r == 3)
        def _():
            pl.when(c == 1)(lambda: second_copy(p, 0).start())

    ffn_load.start()
    active_load(0).start()
    heads_load(0).start()
    first_load.start()
    w_load(3).start()
    tokens_load.start()
    dense_kept[0] = dense_sums[...]
    bias_sums[...] = jnp.zeros_like(bias_sums)
    for gx in range(2):
        for gc in range(2):
            parts[3][gx, gc, :, :, :, 3 * GC :] = jnp.zeros((nz, 2, width // (2 * nz), GRAIN), low)
    meet([first, second, partner, *along])
    normed_swap = remote_copy(
        normed.at[pl.ds(half_rows, half_rows)], normed_out, swap_sem.at[2], swap_sem.at[3], partner
    )
    normed_swap.start()
    ffn_load.wait()

    def down_step(r, carry):
        active_load(r).wait()
        pl.when(r < 3)(lambda: active_load(r + 1).start())
        pl.when(r == 3)(lambda: preact_load(0).start())
        s = lax.rem(r, 2)
        for at in range(0, width, span):
            acc[at : at + span, :] = product(slots[s, :, at : at + span].T, right[...])
        finish(0, r)
        return carry

    lax.fori_loop(0, GROUPS, down_step, 0)
    sums_copy(0).start()
    attn_low_load.start()
    first_load.wait()
    left_t[...] = joined[...].T
    rows_load.start()

    def up_step(r, carry):
        preact_load(r).wait()
        pl.when(r < 3)(lambda: preact_load(r + 1).start())
        pl.when(r == 3)(lambda: qkv_load(0).start())
        s = lax.rem(r, 2)
        for at in range(0, width, span):
            acc[at : at + span, :] = product(left_t[at : at + span, :], slots[s])
        finish(1, r)
        return carry

    lax.fori_loop(0, GROUPS, up_step, 0)
    sums_step(0)
    attn_low_load.wait()

    def out_step(r, carry):
        heads_load(r).wait()
        heads_load(lax.rem(r + 1, GROUPS)).start()
        acc[:PAD, :] = product(heads_in[lax.rem(r, 2)].T, right[...])
        finish(2, r)
        return carry

    lax.fori_loop(0, GROUPS, out_step, 0)
    grad_load(0).start()
    w_load(0, True).start()
    rows_load.wait()
    left_t[...] = joined[...].T
    tokens_load.wait()

    hooks = {
        0: lambda: sums_step(1),
        1: lambda: (pass_first(0), take_second(0, 0)),
        2: lambda: sums_step(2),
        4: lambda: take_first(0),
        5: lambda: (pass_first(1), take_second(1, 0)),
        6: lambda: (pass_first(2), take_second(2, 0)),
        8: lambda: take_first(1),
        9: lambda: (take_first(2), sums_last()),
        10: lambda: take_z(0),
        11: lambda: pl.when(c == 1)(lambda: pass_first(3)),
    }
    row = lax.broadcasted_iota(jnp.int32, (rows, 1), 0)
    bias = jnp.where(place_of(c, row, half_rows) < lengths[c, x], 0.0, masked_score).astype(low)
    lane = lax.broadcasted_iota(jnp.int32, (1, PAD), 1)
    turned[...] = jnp.zeros_like(turned)

    def group_step(r, carry):
        s = lax.rem(r, 2)
        group = index_of(r)
        for copy in (qkv_load, heads_load, grad_load):
            copy(r).wait()

        @pl.when(r < 3)
        def _():
            for copy in (qkv_load, heads_load, grad_load):
                copy(r + 1).start()

        pl.when(r == 3)(lambda: back_load(0).start())
        crossed[...] = (grad_in[s].astype(jnp.float32) * heads_in[s].astype(jnp.float32)).T
        keys_t[...] = slots[s, :, PAD : 2 * PAD].T
        key_acc[...] = jnp.zeros_like(key_acc)
        value_acc[...] = jnp.zeros_like(value_acc)

        def head_step(h, carry):
            for k, todo in hooks.items():
                pl.when(r * GH + h == k)(todo_of(todo))
            start = pl.multiple_of(h * HD, HD)
            head = (lane >= start) & (lane < start + HD)
            keys = slots[s, :, PAD : 2 * PAD]
            own_keys = jnp.where(lane == GC, bias, jnp.where(head, keys, jnp.zeros_like(keys)))
            own_values = jnp.where(head, slots[s, :, 2 * PAD :], jnp.zeros((), low))
            delta = jnp.sum(crossed[pl.ds(start, HD), :], axis=0, keepdims=True)
            for at in range(0, rows, chunk):
                scores = contract_cols(own_keys, slots[s, at : at + chunk, :PAD])
                attn_probs = jnp.exp2(scores * exp2_scale - lse_ref[group, pl.ds(h, 1), at : at + chunk])
                prob_grad = contract_cols(own_values, grad_in[s, at : at + chunk, :])
                probs[:, at : at + chunk] = attn_probs.astype(low)
                slopes[:, at : at + chunk] = (
                    attn_probs * (prob_grad - delta[:, at : at + chunk])
                ).astype(low)
            own_grads = jnp.where(head, grad_in[s], jnp.zeros((), low))
            own_queries = jnp.where(head, slots[s, :, :PAD], jnp.zeros((), low))
            value_acc[...] += product(probs[...], own_grads)
            key_acc[...] += product(slopes[...], own_queries)
            turned[pl.ds(start, HD), :] = product(keys_t[pl.ds(start, HD), :], slopes[...])
            return carry

        lax.fori_loop(0, GH, head_step, 0)
        query_grad = turned[...].T * score_scale
        pl.when(r > 0)(lambda: keep_joined(r - 1).wait())
        joined[:, :PAD] = query_grad.astype(low)
        joined[:, PAD : 2 * PAD] = (key_acc[...] * score_scale).astype(low)
        joined[:, 2 * PAD :] = value_acc[...].astype(low)
        bias_sums[0:1, :] = jnp.sum(query_grad, axis=0, keepdims=True)
        bias_sums[1:2, :] = jnp.sum(value_acc[...], axis=0, keepdims=True)
        for at in range(0, width, span):
            acc[at : at + span, :] = product(left_t[at : at + span, :], joined[...])
        finish(3, r)
        pl.when(r < 3)(lambda: keep_joined(r).start())
        return carry

    lax.fori_loop(0, GROUPS, group_step, 0)
    pl.when(c == 0)(lambda: pass_first(3))

    def add_tokens(kept_group, weights):
        for at in range(0, rows, chunk):
            tokens[at : at + chunk, :] += contract_cols(kept_group[at : at + chunk, :], weights[...])

    back_load(1).start()
    w_load(3).wait()
    add_tokens(joined, w_in)
    w_load(1).start()
    w_load(0, True).wait()
    back_load(0).wait()
    add_tokens(slots.at[0], w_other)
    w_load(2, True).start()
    back_load(2).start()
    take_second(3, 0)
    w_load(1).wait()
    back_load(1).wait()
    add_tokens(slots.at[1], w_in)
    take_first(3)
    w_load(2, True).wait()
    back_load(2).wait()
    add_tokens(slots.at[0], w_other)
    swap = remote_copy(
        tokens.at[pl.ds(half_rows, half_rows)], tokens_out.at[c], swap_sem.at[0], swap_sem.at[1], partner
    )
    keep = pltpu.make_async_copy(tokens.at[pl.ds(0, half_rows)], tokens_out.at[c], load_sem.at[4])
    swap.start()
    keep.start()

    def piece(values, index, count):
        size = values.shape[1] // count
        found = values[:, :size]
        for k in range(1, count):
            found = jnp.where(index == k, values[:, k * size : (k + 1) * size], found)
        return found

    dp = 2 * z + y
    vectors_out[...] = jnp.zeros_like(vectors_out)
    share = width // (8 * nz)
    vectors_out[0:6, :share] = piece(dense_total[0:6, :], dp * 4 + mp, 8 * nz)
    vectors_out[6:7, : width // (2 * nz)] = piece(dense_total[pl.ds(12 + mp, 1), :], dp, 2 * nz)
    for k in range(3):
        square = jnp.sum(dense_total[6 + k : 7 + k, :], axis=1, keepdims=True)
        vectors_out[12:13, k : k + 1] = jnp.sqrt(square / (dense_total[9:10, 0:1] * width))
    take_z(1)
    take_z(2)
    take_z(3)

    keep.wait()
    swap.wait()
    normed_swap.wait()
    for p in range(BIG):
        for r in range(2):
            core_copy(p, r).wait_send()
            second_copy(p, r).wait_send()
        first_copy(p).wait_send()
        for d in range(nz - 1):
            z_copy(p, d).wait_send()
    for k in range(nz + 2):
        sums_copy(k).wait_send()


def todo_of(todo):
    def run():
        todo()

    return run


def backward(lengths, lse, dense_sums, *operands):
    rows_in, w_joined = operands[:2]
    nz = lax.axis_size("dp") // 2
    rows, width = rows_in.shape
    low, wide = jnp.bfloat16, jnp.float32
    deep = width // (2 * nz)
    tails = [(deep, width), (deep, width), (GC // (2 * nz), width), (deep, 3 * GC + GRAIN)]
    results = [*tails[:3], *[(deep, GC)] * 3]
    sums = dense_sums.shape
    anywhere, vmem = pl.BlockSpec(memory_space=pl.ANY), pl.BlockSpec(memory_space=pltpu.VMEM)
    dma = pltpu.SemaphoreType.DMA
    return pl.pallas_call(
        functools.partial(backward_kernel, nz),
        in_specs=[pl.BlockSpec(memory_space=pltpu.SMEM), vmem, vmem, *[anywhere] * len(operands)],
        out_specs=[*[vmem] * 7, *[anywhere] * 3],
        out_shape=[
            *[jax.ShapeDtypeStruct(shape, wide) for shape in (*results, (16, 128))],
            jax.ShapeDtypeStruct((MB, rows // 2, width), wide),
            jax.ShapeDtypeStruct((rows // 2, width), low),
            jax.ShapeDtypeStruct((GROUPS, rows, 3 * PAD), low),
        ],
        scratch_shapes=[
            *[pltpu.VMEM((2, 2, nz, 2, *t), low) for t in tails],
            *[pltpu.VMEM((2, nz, 2, *t), low) for t in tails],
            *[pltpu.VMEM((2, nz, *t), low) for t in tails],
            *[pltpu.VMEM((nz, *t), low) for t in tails],
            *[pltpu.VMEM((nz - 1, *t), low) for t in tails],
            pltpu.VMEM(sums, wide),
            pltpu.VMEM((16, PAD), wide),
            pltpu.VMEM((4, *sums), wide),
            pltpu.VMEM((nz + 2, *sums), wide),
            pltpu.VMEM((width, 3 * PAD), wide),
            pltpu.VMEM((2, rows, width), low),
            pltpu.VMEM((rows, width), low),
            pltpu.VMEM((width, rows), low),
            pltpu.VMEM((rows, 3 * PAD), low),
            pltpu.VMEM((2, rows, PAD), low),
            pltpu.VMEM((2, rows, PAD), low),
            pltpu.VMEM((width, 3 * PAD), low),
            pltpu.VMEM((rows, width), wide),
            pltpu.VMEM((rows, rows), low),
            pltpu.VMEM((rows, rows), low),
            pltpu.VMEM((PAD, rows), wide),
            pltpu.VMEM((PAD, rows), wide),
            pltpu.VMEM((PAD, rows), low),
            pltpu.VMEM((rows, PAD), wide),
            pltpu.VMEM((rows, PAD), wide),
            dma((BIG, 5)),
            dma((BIG, 5)),
            dma((BIG, nz - 1)),
            dma((BIG, nz - 1)),
            dma((nz + 2,)),
            dma((nz + 2,)),
            dma((4,)),
            dma((7,)),
            dma((2,)),
            dma((2,)),
            dma((2,)),
        ],
        compiler_params=pltpu.CompilerParams(
            collective_id=1, has_side_effects=True, vmem_limit_bytes=63 * 1024 * 1024
        ),
    )(lengths, lse, dense_sums, *operands)


def body_fused(
    tokens,
    cotangent,
    lengths,
    w_query,
    w_key,
    w_value,
    w_out,
    w_up,
    w_down,
    b_query,
    b_value,
    b_up,
    b_out,
    b_down,
    norm1_gain,
    norm1_shift,
    norm2_gain,
    norm2_shift,
):
    half_rows = tokens.shape[1]
    width = tokens.shape[2]
    n_dp, n_mp = lax.axis_size("dp"), lax.axis_size("mp")
    unit_cols = w_up.shape[1]
    mark = jnp.zeros((PAD - GC,), jnp.float32).at[0].set(1.0)
    bias_rows = jnp.concatenate(
        [
            b_query,
            mark,
            jnp.zeros((PAD,), jnp.float32),
            b_value,
            jnp.zeros((PAD - GC,), jnp.float32),
            b_up,
            b_out,
            b_down,
            norm1_gain,
            norm1_shift,
            norm2_gain,
            norm2_shift,
        ]
    ).reshape(8, width)
    gathered = forward_attention(
        lengths, tokens, cotangent, (w_query, w_key, w_value, w_out, w_up, w_down), bias_rows
    )
    full_out, full_up, full_down = (
        g.reshape(n_mp, n_dp * g.shape[4], g.shape[5]) for g in gathered[1:4]
    )
    full_bias, rows_in, rows_cot, w_joined, qkv, heads, lse = gathered[4:]
    (
        output,
        first_low,
        active,
        ffn_grad_low,
        preact_low,
        attn_grad,
        attn_grad_low,
        heads_grad,
        dense_sums,
    ) = dense(lengths, heads, rows_in, rows_cot, full_out, full_up, full_down, full_bias)
    *matrix_grads, vectors, tokens_grad, output_got, _ = backward(
        lengths,
        lse,
        dense_sums,
        rows_in,
        w_joined,
        attn_grad,
        qkv,
        heads,
        heads_grad,
        active,
        ffn_grad_low,
        first_low,
        preact_low,
        attn_grad_low,
        output,
    )
    share = width // (n_dp * n_mp)
    sizes = [*[share] * 6, unit_cols // n_dp, share, share, 3]
    delivered = deliver(matrix_grads, vectors, output, output_got, tokens_grad, sizes)
    output, tokens_grad, own_down, own_up, own_out, own_query, own_key, own_value = delivered[:8]
    own_vectors = [v.reshape(-1) for v in delivered[8:]]
    return (
        output,
        tokens_grad,
        own_query,
        own_key,
        own_value,
        own_out,
        own_up,
        own_down,
        own_vectors[7],
        own_vectors[8],
        own_vectors[6],
        *own_vectors[:6],
        own_vectors[9],
    )


def deliver_kernel(mats, *refs):
    results, (vectors, normed, normed_got, tokens) = refs[:mats], refs[mats : mats + 4]
    outs = refs[mats + 4 :]
    normed_out, tokens_out = outs[:2]
    mat_outs, vec_outs = outs[2 : 2 + mats], outs[2 + mats : 12 + mats]
    normed_kept, tokens_kept, load_sem, store_sem = outs[12 + mats :]
    half = lax.rem(lax.axis_index("mp"), 2)
    half_rows = tokens.shape[1]
    moves = [
        (tokens.at[0], tokens_kept.at[0], tokens_out.at[0]),
        (tokens.at[1], tokens_kept.at[1], tokens_out.at[1]),
        (normed.at[pl.ds(0, half_rows)], normed_kept.at[0], normed_out.at[half]),
        (normed_got, normed_kept.at[1], normed_out.at[1 - half]),
    ]
    loads = [pltpu.make_async_copy(a, b, load_sem.at[k]) for k, (a, b, _) in enumerate(moves)]
    stores = [pltpu.make_async_copy(b, o, store_sem.at[k]) for k, (_, b, o) in enumerate(moves)]
    stores += [
        pltpu.make_async_copy(a, o, store_sem.at[len(moves) + k])
        for k, (a, o) in enumerate(zip(results, mat_outs))
    ]
    for copy in (*loads, *stores[len(moves) :]):
        copy.start()
    for k, out in enumerate(vec_outs[:9]):
        out[...] = vectors[k : k + 1, : out.shape[1]]
    vec_outs[9][...] = vectors[12:13, :3]
    for k, copy in enumerate(loads):
        copy.wait()
        stores[k].start()
    for copy in stores:
        copy.wait()


def deliver(results, vectors, normed, normed_got, tokens, sizes):
    mats = len(results)
    anywhere, vmem = pl.BlockSpec(memory_space=pl.ANY), pl.BlockSpec(memory_space=pltpu.VMEM)
    big = [jax.ShapeDtypeStruct((2, *normed_got.shape), normed.dtype), jax.ShapeDtypeStruct(tokens.shape, tokens.dtype)]
    rows = [jax.ShapeDtypeStruct((1, size), jnp.float32) for size in sizes]
    return pl.pallas_call(
        functools.partial(deliver_kernel, mats),
        grid=(1,),
        in_specs=[*[vmem] * (mats + 1), *[anywhere] * 3],
        out_specs=[
            *[anywhere] * (2 + mats),
            *[pl.BlockSpec((1, size), lambda i: (0, 0)) for size in sizes],
        ],
        out_shape=[*big, *[jax.ShapeDtypeStruct(r.shape, r.dtype) for r in results], *rows],
        scratch_shapes=[
            pltpu.VMEM(big[0].shape, big[0].dtype),
            pltpu.VMEM(big[1].shape, big[1].dtype),
            pltpu.SemaphoreType.DMA((4,)),
            pltpu.SemaphoreType.DMA((4 + mats,)),
        ],
    )(*results, vectors, normed, normed_got, tokens)


def solution(mesh):
    rows = P(None, BOTH, None)
    split, rows_split = P("dp", "mp"), P(("mp", "dp"), None)
    aligned = mesh.shape["dp"] == 8 and mesh.shape["mp"] == 4
    return jax.shard_map(
        body_fused if aligned else body_any,
        mesh=mesh,
        in_specs=(
            rows,
            rows,
            P(None, "dp"),
            split,
            split,
            split,
            rows_split,
            split,
            rows_split,
            P("mp"),
            P("mp"),
            P("mp"),
            *([P()] * 6),
        ),
        out_specs=(
            rows,
            rows,
            split,
            split,
            split,
            rows_split,
            split,
            rows_split,
            *([P(("mp", "dp"))] * 3),
            *([P(BOTH)] * 6),
            P(),
        ),
        check_vma=False,
    )
```

```python
import functools

import jax
import jax.numpy as jnp
from jax import lax
from jax.experimental import pallas as pl
from jax.experimental.pallas import tpu as pltpu
from jax.sharding import PartitionSpec as P

HD = 64
L = 1024
SEQ_MB = 2
MB = 2
GROUPS = 4
GH = 3
GC = GH * HD
PAD = 256

epsilon = 1e-05
masked_score = -1e30
exp2_scale = HD ** (-0.5) * 1.4426950408889634
score_scale = HD ** (-0.5)
BOTH = ("dp", "mp")
NT = (((1,), (1,)), ((), ()))


def product(left_side, right_side):
    return jnp.dot(left_side, right_side, preferred_element_type=jnp.float32)


def contract_rows(left_side, right_side):
    return lax.dot_general(
        left_side, right_side, (((0,), (0,)), ((), ())), preferred_element_type=jnp.float32
    )


def contract_cols(left_side, right_side):
    return lax.dot_general(left_side, right_side, NT, preferred_element_type=jnp.float32)


def layer_norm(values, norm_gain, norm_shift):
    center = values - jnp.mean(values, axis=-1, keepdims=True)
    spread = jnp.mean(center * center, axis=-1, keepdims=True)
    inverse = lax.rsqrt(spread + epsilon)
    scaled = center * inverse
    return (scaled * norm_gain + norm_shift, scaled, inverse)


def norm_back(upstream, scaled, inverse, norm_gain):
    gain_grad = jnp.sum(upstream * scaled, axis=0)
    shift_grad = jnp.sum(upstream, axis=0)
    through = upstream * norm_gain
    result = inverse * (
        through
        - jnp.mean(through, axis=-1, keepdims=True)
        - scaled * jnp.mean(through * scaled, axis=-1, keepdims=True)
    )
    return (result, gain_grad, shift_grad)


def head_keys(keys, bias, h, lane):
    kept = jnp.where((lane >= h * HD) & (lane < (h + 1) * HD), keys, jnp.zeros_like(keys))
    return jnp.where(lane == GC, bias, kept)


def attend_forward_kernel(bias_ref, qkv_ref, out_ref, lse_ref, turned):
    rows = qkv_ref.shape[1]
    chunk = 256
    lane = lax.broadcasted_iota(jnp.int32, (1, PAD), 1)
    keys = qkv_ref[0, :, PAD : 2 * PAD]
    values_t = qkv_ref[0, :, 2 * PAD :].T
    bias = bias_ref[...]
    for h in range(GH):
        own = head_keys(keys, bias, h, lane)
        own_values = values_t[h * HD : (h + 1) * HD, :]
        for at in range(0, rows, chunk):
            queries = qkv_ref[0, at : at + chunk, :PAD]
            scores = contract_cols(own, queries)
            top = jnp.max(scores, axis=0, keepdims=True) * exp2_scale
            raised = jnp.exp2(scores * exp2_scale - top)
            total = jnp.sum(raised, axis=0, keepdims=True)
            mixed = product(own_values, raised.astype(jnp.bfloat16))
            turned[h * HD : (h + 1) * HD, at : at + chunk] = mixed / total
            lse_ref[0, h : h + 1, at : at + chunk] = top + jnp.log2(total)
    turned[GC:, :] = jnp.zeros((PAD - GC, rows), jnp.float32)
    out_ref[0] = turned[...].T.astype(jnp.bfloat16)


def attend_forward(qkv, bias):
    rows = qkv.shape[1]
    return pl.pallas_call(
        attend_forward_kernel,
        grid=(GROUPS,),
        in_specs=[
            pl.BlockSpec((rows, 1), lambda g: (0, 0)),
            pl.BlockSpec((1, rows, 3 * PAD), lambda g: (g, 0, 0)),
        ],
        out_specs=[
            pl.BlockSpec((1, rows, PAD), lambda g: (g, 0, 0)),
            pl.BlockSpec((1, 8, rows), lambda g: (g, 0, 0)),
        ],
        out_shape=[
            jax.ShapeDtypeStruct((GROUPS, rows, PAD), jnp.bfloat16),
            jax.ShapeDtypeStruct((GROUPS, 8, rows), jnp.float32),
        ],
        scratch_shapes=[pltpu.VMEM((PAD, rows), jnp.float32)],
        cost_estimate=pl.CostEstimate(
            flops=45_000_000_000 // 3, bytes_accessed=10_000_000, transcendentals=12_000_000
        ),
    )(bias, qkv)


def attend_backward_kernel(
    bias_ref, qkv_ref, out_ref, lse_ref, grad_ref, joined_ref, sums_ref, probs, slopes, turned
):
    rows = qkv_ref.shape[1]
    chunk = 256
    lane = lax.broadcasted_iota(jnp.int32, (1, PAD), 1)
    keys = qkv_ref[0, :, PAD : 2 * PAD]
    keys_t = keys.T
    values = qkv_ref[0, :, 2 * PAD :]
    bias = bias_ref[...]
    crossed = (grad_ref[0].astype(jnp.float32) * out_ref[0].astype(jnp.float32)).T
    key_grad = jnp.zeros((rows, PAD), jnp.float32)
    value_grad = jnp.zeros((rows, PAD), jnp.float32)
    for h in range(GH):
        head = (lane >= h * HD) & (lane < (h + 1) * HD)
        own = head_keys(keys, bias, h, lane)
        own_values = jnp.where(head, values, jnp.zeros_like(values))
        delta = jnp.sum(crossed[h * HD : (h + 1) * HD, :], axis=0, keepdims=True)
        for at in range(0, rows, chunk):
            queries = qkv_ref[0, at : at + chunk, :PAD]
            grads = grad_ref[0, at : at + chunk, :]
            scores = contract_cols(own, queries)
            attn_probs = jnp.exp2(scores * exp2_scale - lse_ref[0, h : h + 1, at : at + chunk])
            prob_grad = contract_cols(own_values, grads)
            probs[:, at : at + chunk] = attn_probs.astype(jnp.bfloat16)
            slopes[:, at : at + chunk] = (
                attn_probs * (prob_grad - delta[:, at : at + chunk])
            ).astype(jnp.bfloat16)
        own_grads = jnp.where(head, grad_ref[0], jnp.zeros((), jnp.bfloat16))
        own_queries = jnp.where(head, qkv_ref[0, :, :PAD], jnp.zeros((), jnp.bfloat16))
        value_grad = value_grad + product(probs[...], own_grads)
        key_grad = key_grad + product(slopes[...], own_queries)
        turned[h * HD : (h + 1) * HD, :] = product(
            keys_t[h * HD : (h + 1) * HD, :], slopes[...]
        )
    turned[GC:, :] = jnp.zeros((PAD - GC, rows), jnp.float32)
    query_grad = turned[...].T * score_scale
    joined_ref[0, :, :PAD] = query_grad.astype(jnp.bfloat16)
    joined_ref[0, :, PAD : 2 * PAD] = (key_grad * score_scale).astype(jnp.bfloat16)
    joined_ref[0, :, 2 * PAD :] = value_grad.astype(jnp.bfloat16)
    sums_ref[0, 0:1, :] = jnp.sum(query_grad, axis=0, keepdims=True)
    sums_ref[0, 1:2, :] = jnp.sum(value_grad, axis=0, keepdims=True)


def attend_backward(qkv, bias, heads_out, lse, heads_grad):
    rows = qkv.shape[1]
    return pl.pallas_call(
        attend_backward_kernel,
        grid=(GROUPS,),
        in_specs=[
            pl.BlockSpec((rows, 1), lambda g: (0, 0)),
            pl.BlockSpec((1, rows, 3 * PAD), lambda g: (g, 0, 0)),
            pl.BlockSpec((1, rows, PAD), lambda g: (g, 0, 0)),
            pl.BlockSpec((1, 8, rows), lambda g: (g, 0, 0)),
            pl.BlockSpec((1, rows, PAD), lambda g: (g, 0, 0)),
        ],
        out_specs=[
            pl.BlockSpec((1, rows, 3 * PAD), lambda g: (g, 0, 0)),
            pl.BlockSpec((1, 8, PAD), lambda g: (g, 0, 0)),
        ],
        out_shape=[
            jax.ShapeDtypeStruct((GROUPS, rows, 3 * PAD), jnp.bfloat16),
            jax.ShapeDtypeStruct((GROUPS, 8, PAD), jnp.float32),
        ],
        scratch_shapes=[
            pltpu.VMEM((rows, rows), jnp.bfloat16),
            pltpu.VMEM((rows, rows), jnp.bfloat16),
            pltpu.VMEM((PAD, rows), jnp.float32),
        ],
        cost_estimate=pl.CostEstimate(
            flops=30_000_000_000, bytes_accessed=20_000_000, transcendentals=12_000_000
        ),
    )(bias, qkv, heads_out, lse, heads_grad)


def swap_with_partner(values):
    size = lax.axis_size("mp")
    return lax.ppermute(values, "mp", [(i, i ^ 1) for i in range(size)])


def pad_heads(values):
    return jnp.pad(values, [(0, 0)] * (values.ndim - 1) + [(0, PAD - values.shape[-1])])


MESH = pl.DeviceIdType.MESH


def positions():
    mp, dp = lax.axis_index("mp"), lax.axis_index("dp")
    return mp, lax.div(mp, 2), lax.rem(mp, 2), lax.div(dp, 2), lax.rem(dp, 2)


def at_place(x, c, z, y):
    return (2 * z + y, 2 * x + c)


def neighbours(nz):
    mp, x, c, z, y = positions()
    first = at_place(lax.rem(x + c, 2), c, z, lax.rem(y + 1 - c, 2))
    second = at_place(lax.rem(x + 1 - c, 2), c, z, lax.rem(y + c, 2))
    partner = at_place(x, 1 - c, z, y)
    along = [at_place(x, c, lax.rem(z + d, nz), y) for d in range(1, nz)]
    return first, second, partner, along


def meet(devices):
    barrier = pltpu.get_barrier_semaphore()
    for device in devices:
        pl.semaphore_signal(barrier, inc=1, device_id=device, device_id_type=MESH)
    pl.semaphore_wait(barrier, len(devices))


def regions(x, c, y):
    own = (x, y)
    first = (lax.rem(x + c, 2), lax.rem(y + 1 - c, 2))
    second = (lax.rem(x + 1 - c, 2), lax.rem(y + c, 2))
    third = (1 - x, 1 - y)
    return own, first, second, third


def gather_kernel(nz, parts, *refs):
    shards, fulls = refs[:parts], refs[parts : 2 * parts]
    own_sem, z_send, z_recv, send, recv = refs[2 * parts :]
    mp, x, c, z, y = positions()
    first, second, partner, along = neighbours(nz)
    meet([first, second, partner, *along])
    own, got1, got2, got3 = regions(x, c, y)
    other = regions(x, 1 - c, y)

    def remote(src, dst, s, r, device):
        return pltpu.make_async_remote_copy(
            src_ref=src, dst_ref=dst, send_sem=s, recv_sem=r, device_id=device, device_id_type=MESH
        )

    started = []
    locals_ = []
    spread = []
    for p in range(parts):
        keep = pltpu.make_async_copy(shards[p], fulls[p].at[x, c, z, y], own_sem.at[p])
        keep.start()
        locals_.append(keep)
        sends = [
            remote(shards[p], fulls[p].at[x, c, z, y], z_send.at[p, d], z_recv.at[p, d], along[d])
            for d in range(nz - 1)
        ]
        for copy in sends:
            copy.start()
        spread.append(sends)

    def block(p, core, place):
        return fulls[p].at[place[0], core, :, place[1]]

    def push(p, k, core, place, device):
        copy = remote(block(p, core, place), block(p, core, place), send.at[p, k], recv.at[p, k], device)
        copy.start()
        started.append(copy)
        return copy

    def arrived(p, k, core, place):
        here = block(p, core, place)
        remote(here, here, send.at[p, k], recv.at[p, k], first).wait_recv()

    for p in range(parts):
        locals_[p].wait()
        for copy in spread[p]:
            copy.wait_recv()
        push(p, 0, c, own, first)
        push(p, 1, c, own, second)
        push(p, 3, c, own, partner)
    for p in range(parts):
        arrived(p, 0, c, got1)
        push(p, 2, c, got1, second)
        push(p, 4, c, got1, partner)
    for p in range(parts):
        arrived(p, 1, c, got2)
        push(p, 5, c, got2, partner)
        arrived(p, 2, c, got3)
        push(p, 6, c, got3, partner)
    for p in range(parts):
        for k in range(4):
            arrived(p, 3 + k, 1 - c, other[k])
    for sends in spread:
        for copy in sends:
            copy.wait_send()
    for copy in started:
        copy.wait_send()


def gather_all(shards):
    n_dp = lax.axis_size("dp")
    nz, parts = n_dp // 2, len(shards)
    return pl.pallas_call(
        functools.partial(gather_kernel, nz, parts),
        in_specs=[pl.BlockSpec(memory_space=pltpu.VMEM)] * parts,
        out_specs=[pl.BlockSpec(memory_space=pl.ANY)] * parts,
        out_shape=[jax.ShapeDtypeStruct((2, 2, nz, 2, *s.shape), s.dtype) for s in shards],
        scratch_shapes=[
            pltpu.SemaphoreType.DMA((parts,)),
            pltpu.SemaphoreType.DMA((parts, nz - 1)),
            pltpu.SemaphoreType.DMA((parts, nz - 1)),
            pltpu.SemaphoreType.DMA((parts, 7)),
            pltpu.SemaphoreType.DMA((parts, 7)),
        ],
        compiler_params=pltpu.CompilerParams(collective_id=0, has_side_effects=True),
    )(*shards)


def scatter_kernel(nz, parts, side, *refs):
    partials, results = refs[:parts], refs[parts : 2 * parts]
    at = 2 * parts
    sums, heard1, heard2, heard3, heard4 = (
        refs[at + i * parts : at + (i + 1) * parts] for i in range(5)
    )
    own_sem, send, recv, z_send, z_recv = refs[at + 5 * parts :]
    mp, x, c, z, y = positions()
    first, second, partner, along = neighbours(nz)
    meet([first, second, partner, *along])
    own, got1, got2, got3 = regions(x, c, y)
    started = []

    def remote(src, dst, s, r, device):
        copy = pltpu.make_async_remote_copy(
            src_ref=src, dst_ref=dst, send_sem=s, recv_sem=r, device_id=device, device_id_type=MESH
        )
        copy.start()
        started.append(copy)
        return copy

    def add(p, place, more):
        for i in range(nz):
            here = sums[p].at[place[0], i, place[1]]
            here[...] = (here[...].astype(jnp.float32) + more[i].astype(jnp.float32)).astype(here.dtype)

    def cut(p, k, core):
        if p not in side:
            return partials[p].at[k, core]
        size = partials[p].shape[3] // 4
        return partials[p].at[:, :, :, pl.ds(pl.multiple_of((2 * k + core) * size, size), size)]

    kept, core_copies = [], []
    for p in range(parts):
        copies = []
        for k in range(2):
            keep = pltpu.make_async_copy(cut(p, k, c), sums[p].at[k], own_sem.at[p, k])
            keep.start()
            copies.append(keep)
        kept.append(copies)
        core_copies.append(
            [
                remote(cut(p, k, 1 - c), heard1[p].at[k], send.at[p, k], recv.at[p, k], partner)
                for k in range(2)
            ]
        )
    second_copies = []
    for p in range(parts):
        for copy in kept[p]:
            copy.wait()
        for copy in core_copies[p]:
            copy.wait_recv()
        copies = []
        for k, place in enumerate((got2, got3)):
            add(p, place, heard1[p].at[place[0], :, place[1]])
            copies.append(
                remote(
                    sums[p].at[place[0], :, place[1]],
                    heard2[p].at[k],
                    send.at[p, 2 + k],
                    recv.at[p, 2 + k],
                    second,
                )
            )
        second_copies.append(copies)
        for place in (got1, own):
            add(p, place, heard1[p].at[place[0], :, place[1]])
    first_copies = []
    for p in range(parts):
        second_copies[p][1].wait_recv()
        add(p, got1, heard2[p].at[1])
        first_copies.append(
            remote(sums[p].at[got1[0], :, got1[1]], heard3[p], send.at[p, 4], recv.at[p, 4], first)
        )
        second_copies[p][0].wait_recv()
        add(p, own, heard2[p].at[0])
    last_copies = []
    for p in range(parts):
        first_copies[p].wait_recv()
        add(p, own, heard3[p])
        last_copies.append(
            [
                remote(
                    sums[p].at[x, lax.rem(z + d + 1, nz), y],
                    heard4[p].at[d],
                    z_send.at[p, d],
                    z_recv.at[p, d],
                    along[d],
                )
                for d in range(nz - 1)
            ]
        )
    for p in range(parts):
        for copy in last_copies[p]:
            copy.wait_recv()
        total = sums[p][x, z, y].astype(jnp.float32)
        for d in range(nz - 1):
            total = total + heard4[p][d].astype(jnp.float32)
        results[p][...] = total
    for copy in started:
        copy.wait_send()


def scatter_sums(partials, side=()):
    nz, parts = lax.axis_size("dp") // 2, len(partials)
    tails = [
        (p.shape[2], p.shape[3] // 4) if i in side else p.shape[4:] for i, p in enumerate(partials)
    ]
    kinds = [p.dtype for p in partials]
    return pl.pallas_call(
        functools.partial(scatter_kernel, nz, parts, side),
        in_specs=[pl.BlockSpec(memory_space=pl.ANY)] * parts,
        out_specs=[pl.BlockSpec(memory_space=pltpu.VMEM)] * parts,
        out_shape=[jax.ShapeDtypeStruct(t, jnp.float32) for t in tails],
        scratch_shapes=[
            *[pltpu.VMEM((2, nz, 2, *t), k) for t, k in zip(tails, kinds)],
            *[pltpu.VMEM((2, nz, 2, *t), k) for t, k in zip(tails, kinds)],
            *[pltpu.VMEM((2, nz, *t), k) for t, k in zip(tails, kinds)],
            *[pltpu.VMEM((nz, *t), k) for t, k in zip(tails, kinds)],
            *[pltpu.VMEM((nz - 1, *t), k) for t, k in zip(tails, kinds)],
            pltpu.SemaphoreType.DMA((parts, 2)),
            pltpu.SemaphoreType.DMA((parts, 5)),
            pltpu.SemaphoreType.DMA((parts, 5)),
            pltpu.SemaphoreType.DMA((parts, nz - 1)),
            pltpu.SemaphoreType.DMA((parts, nz - 1)),
        ],
        compiler_params=pltpu.CompilerParams(
            collective_id=1, has_side_effects=True, vmem_limit_bytes=60 * 1024 * 1024
        ),
    )(*partials)


def in_place_order(blocks):
    return blocks.reshape(2, 2, blocks.shape[1] // 2, 2, *blocks.shape[2:])


def body_any(
    tokens,
    cotangent,
    lengths,
    w_query,
    w_key,
    w_value,
    w_out,
    w_up,
    w_down,
    b_query,
    b_value,
    b_up,
    b_out,
    b_down,
    norm1_gain,
    norm1_shift,
    norm2_gain,
    norm2_shift,
):
    half_rows = tokens.shape[1]
    width = tokens.shape[2]
    n_dp, n_mp = lax.axis_size("dp"), lax.axis_size("mp")
    unit_cols = w_up.shape[1]
    mp_index = lax.axis_index("mp")
    half = lax.rem(mp_index, 2)
    seq = lax.div(mp_index, 2)

    def own_of(pair):
        return jnp.where(half == 0, pair[0], pair[1])

    def other_of(pair):
        return jnp.where(half == 0, pair[1], pair[0])

    rows_in = jnp.concatenate([own_of(tokens), swap_with_partner(other_of(tokens))], axis=0)
    rows_cot = jnp.concatenate([own_of(cotangent), swap_with_partner(other_of(cotangent))], axis=0)
    length = lax.dynamic_slice(lengths, (half, seq), (1, 1))[0, 0]
    place = jnp.arange(half_rows, dtype=jnp.int32)
    place = jnp.concatenate([place + half * half_rows, place + (1 - half) * half_rows])
    valid_row = (place < length)[:, None]
    bias = jnp.where(valid_row, 0.0, masked_score).astype(jnp.bfloat16)
    valid_row = valid_row.astype(jnp.float32)

    biases = jnp.pad(jnp.concatenate([b_query, b_value, b_up]), (0, 896)).reshape(16, 128)
    qkv_shard = jnp.concatenate([w_query, w_key, w_value], axis=1)
    gathered = gather_all([qkv_shard, w_out, w_up, w_down, biases])
    full_qkv, full_out, full_up, full_down, full_bias = (
        g.reshape(n_mp, n_dp, *g.shape[4:]) for g in gathered
    )
    full_qkv = full_qkv.reshape(n_mp, width, 3, GC)
    w_joined = pad_heads(full_qkv).reshape(n_mp, width, 3 * PAD)
    full_out = full_out.reshape(n_mp, GC, width)
    out_pad = jnp.pad(full_out, ((0, 0), (0, PAD - GC), (0, 0))).reshape(n_mp * PAD, width)
    full_up = full_up.reshape(n_mp, width, unit_cols).transpose(1, 0, 2).reshape(width, n_mp * unit_cols)
    full_down = full_down.reshape(n_mp * unit_cols, width)
    full_bias = full_bias[:, 0].reshape(n_mp, -1)
    bias_q, bias_v, bias_up = full_bias[:, :GC], full_bias[:, GC:2*GC], full_bias[:, 2*GC:2*GC+unit_cols]
    mark = jnp.zeros((n_mp, PAD - GC), jnp.float32).at[:, 0].set(1.0)
    joined_bias = jnp.concatenate(
        [bias_q, mark, jnp.zeros((n_mp, PAD), jnp.float32), pad_heads(bias_v)], axis=1
    )

    qkv = lax.dot_general(
        jnp.broadcast_to(rows_in[None], (n_mp, *rows_in.shape)),
        w_joined,
        (((2,), (1,)), ((0,), (0,))),
        preferred_element_type=jnp.float32,
    )
    qkv = (qkv + joined_bias[:, None, :]).astype(jnp.bfloat16)
    heads_out, lse = attend_forward(qkv, bias)
    heads_flat = heads_out.transpose(1, 0, 2).reshape(2 * half_rows, n_mp * PAD)
    attention = product(heads_flat, out_pad) + b_out
    first_norm, first_scaled, first_inverse = layer_norm(
        rows_in.astype(jnp.float32) + attention, norm1_gain, norm1_shift
    )
    first_low = first_norm.astype(jnp.bfloat16)
    preact = product(first_low, full_up) + bias_up.reshape(-1)
    cumulative = 0.5 * (1.0 + lax.erf(preact * 0.7071067811865476))
    active = (preact * cumulative).astype(jnp.bfloat16)
    slope = cumulative + preact * (jnp.exp(-0.5 * preact * preact) * 0.3989422804014327)
    ffn_out = product(active, full_down) + b_down
    stream = first_norm + ffn_out
    final_norm, final_scaled, final_inverse = layer_norm(stream, norm2_gain, norm2_shift)
    output = final_norm.astype(jnp.bfloat16)
    squares = jnp.stack(
        [
            jnp.sum(valid_row * stream * stream),
            jnp.sum(valid_row * attention * attention),
            jnp.sum(valid_row * ffn_out * ffn_out),
            jnp.sum(valid_row),
        ]
    )

    stream_grad, gain2_grad, shift2_grad = norm_back(
        rows_cot.astype(jnp.float32), final_scaled, final_inverse, norm2_gain
    )
    down_bias_grad = jnp.sum(stream_grad, axis=0)
    ffn_grad_low = stream_grad.astype(jnp.bfloat16)
    active_grad = contract_cols(ffn_grad_low, full_down)
    down_wgrad = contract_rows(active, ffn_grad_low)
    preact_grad = active_grad * slope
    up_bias_grad = jnp.sum(preact_grad, axis=0)
    preact_low = preact_grad.astype(jnp.bfloat16)
    up_wgrad = contract_rows(first_low, preact_low)
    first_grad = stream_grad + contract_cols(preact_low, full_up)
    attn_grad, gain1_grad, shift1_grad = norm_back(
        first_grad, first_scaled, first_inverse, norm1_gain
    )
    out_bias_grad = jnp.sum(attn_grad, axis=0)
    attn_grad_low = attn_grad.astype(jnp.bfloat16)
    out_wgrad = contract_rows(heads_flat, attn_grad_low)
    heads_grad = contract_cols(attn_grad_low, out_pad).astype(jnp.bfloat16)
    heads_grad = heads_grad.reshape(2 * half_rows, n_mp, PAD).transpose(1, 0, 2)
    joined, sums = attend_backward(qkv, bias, heads_out, lse, heads_grad)
    joined_wgrad = lax.dot_general(
        jnp.broadcast_to(rows_in[None], (n_mp, *rows_in.shape)),
        joined,
        (((1,), (1,)), ((0,), (0,))),
        preferred_element_type=jnp.float32,
    )
    tokens_grad = attn_grad + jnp.sum(
        lax.dot_general(
            joined, w_joined, (((2,), (2,)), ((0,), (0,))), preferred_element_type=jnp.float32
        ),
        axis=0,
    )

    low = jnp.bfloat16
    joined_blocks = (
        joined_wgrad.astype(low)
        .reshape(n_mp, n_dp, width // n_dp, 3, PAD)[..., :GC]
        .reshape(n_mp, n_dp, width // n_dp, 3 * GC)
    )
    out_blocks = (
        out_wgrad.astype(low)
        .reshape(n_mp, PAD, width)[:, :GC]
        .reshape(n_mp, n_dp, GC // n_dp, width)
    )
    up_blocks = up_wgrad.astype(low).reshape(n_dp, width // n_dp, n_mp, unit_cols).transpose(2, 0, 1, 3)
    down_blocks = down_wgrad.astype(low).reshape(n_mp, n_dp, unit_cols // n_dp, width)

    def by_mp(vector):
        return vector.reshape(n_mp, n_dp, -1)

    def by_dp(vector):
        return vector.reshape(n_dp, n_mp, -1).transpose(1, 0, 2)

    vectors = [by_mp(sums[:, 0, :GC]), by_mp(sums[:, 1, :GC]), by_mp(up_bias_grad)]
    vectors += [
        by_dp(v)
        for v in (out_bias_grad, down_bias_grad, gain1_grad, shift1_grad, gain2_grad, shift2_grad)
    ]
    vectors.append(jnp.broadcast_to(squares, (n_mp, n_dp, 4)))
    ends = [v.shape[-1] for v in vectors]
    vectors = jnp.concatenate(vectors, axis=-1)
    vectors = jnp.pad(vectors, ((0, 0), (0, 0), (0, 1024 - vectors.shape[-1])))
    vectors = vectors.reshape(n_mp, n_dp, 8, 128)
    own_down, own_up, own_out, own_joined, own_vector = scatter_sums(
        [
            in_place_order(b)
            for b in (down_blocks, up_blocks, out_blocks, joined_blocks, vectors)
        ]
    )
    own_vector = own_vector.reshape(-1)
    own_vectors, start = [], 0
    for size in ends:
        own_vectors.append(own_vector[start : start + size])
        start += size
    totals = own_vectors.pop()
    rms_values = jnp.sqrt(totals[:3] / (totals[3] * width))

    def back_home(rows):
        mine, sent = rows[:half_rows], swap_with_partner(rows[half_rows:])
        return jnp.where(half == 0, jnp.stack([mine, sent]), jnp.stack([sent, mine]))

    return (
        back_home(output),
        back_home(tokens_grad),
        own_joined[:, :GC],
        own_joined[:, GC : 2 * GC],
        own_joined[:, 2 * GC :],
        own_out,
        own_up,
        own_down,
        *own_vectors,
        rms_values,
    )


PARTS = 4


def remote_copy(src, dst, s, r, device):
    return pltpu.make_async_remote_copy(
        src_ref=src, dst_ref=dst, send_sem=s, recv_sem=r, device_id=device, device_id_type=MESH
    )


def forward_kernel(
    nz,
    lengths,
    tokens,
    cotangent,
    shard_wq,
    shard_wk,
    shard_wv,
    shard_o,
    shard_u,
    shard_d,
    bias_shard,
    full_q,
    full_o,
    full_u,
    full_d,
    bias_full,
    rows_out,
    cot_out,
    w_out,
    qkv_out,
    heads_out,
    lse_out,
    shard_q,
    rows,
    cots,
    w_got,
    w_pad,
    qkv,
    values_t,
    turned,
    heads,
    own_sem,
    z_send,
    z_recv,
    relay_send,
    send,
    recv,
    swap_send,
    swap_recv,
    bias_send,
    bias_recv,
    out_sem,
):
    shards = (shard_q, shard_o, shard_u, shard_d)
    fulls = (full_q, full_o, full_u, full_d)
    half_rows = tokens.shape[1]
    length = 2 * half_rows
    mp, x, c, z, y = positions()
    half = c
    seq = x
    first, second, partner, along = neighbours(nz)
    across = at_place(1 - x, c, z, y)
    slanted = at_place(1 - x, 1 - c, z, y)
    own, got1, got2, got3 = regions(x, c, y)
    other = regions(x, 1 - c, y)
    for k, shard in enumerate((shard_wq, shard_wk, shard_wv)):
        shard_q[:, k * GC : (k + 1) * GC] = shard[...]
    meet([first, second, partner, slanted, *along])

    def block(p, core, place, d):
        return fulls[p].at[place[0], core, lax.rem(z + nz - d, nz), place[1]]

    places = (own, own, got1, own, got1, got2, got3)
    targets = (first, second, second, partner, partner, partner, partner)
    landing = (got1, got2, got3, *other)
    cores = (c, c, c, 1 - c, 1 - c, 1 - c, 1 - c)

    def outgoing(p, k, d):
        here = block(p, c, places[k], d)
        return remote_copy(here, here, send.at[p, k, d], recv.at[p, k, d], targets[k])

    def incoming(p, k, d):
        here = block(p, cores[k], landing[k], d)
        return remote_copy(here, here, send.at[p, k, d], recv.at[p, k, d], targets[k])

    at_low = 1 - lax.div(z + nz - 1, nz)
    near, far = 1 + 2 * at_low, 3 - 2 * at_low

    def z_copy(p, d):
        return remote_copy(
            shards[p], fulls[p].at[x, c, z, y], z_send.at[p, d - 1], z_recv.at[p, d - 1], along[d - 1]
        )

    def z_each(p, act):
        act(z_copy(p, 2))
        pl.when(z != nz - 1)(lambda: act(z_copy(p, 1)))
        pl.when(z != 0)(lambda: act(z_copy(p, 3)))

    def z_start(p):
        z_each(p, lambda copy: copy.start())

    def z_relay(p, low):
        here = block(p, c, own, 2)
        d = 1 if low else 3
        return remote_copy(here, here, relay_send.at[p], z_recv.at[p, d - 1], at_place(x, c, z + d - 2, y))

    def spread(p, d):
        if not (isinstance(d, int) and d == 0):
            here = block(p, c, own, d)
            remote_copy(here, here, z_send.at[p, d - 1], z_recv.at[p, d - 1], first).wait_recv()
        if isinstance(d, int) and d == 2:
            pl.when(z == 1)(lambda: z_relay(p, True).start())
            pl.when(z == 2)(lambda: z_relay(p, False).start())
        for k in (0, 1, 3):
            outgoing(p, k, d).start()

    def forward1(p):
        for d in range(nz):
            incoming(p, 0, d).wait_recv()
            outgoing(p, 2, d).start()
            outgoing(p, 4, d).start()

    def forward2(p):
        for d in range(nz):
            incoming(p, 1, d).wait_recv()
            outgoing(p, 5, d).start()

    def forward3(p):
        for d in range(nz):
            incoming(p, 2, d).wait_recv()
            outgoing(p, 6, d).start()

    def take(p, k):
        for d in range(nz):
            incoming(p, k, d).wait_recv()

    keep = [
        pltpu.make_async_copy(shards[p], fulls[p].at[x, c, z, y], own_sem.at[p]) for p in range(PARTS)
    ]
    keep_rows = pltpu.make_async_copy(tokens.at[half], rows.at[pl.ds(0, half_rows)], own_sem.at[PARTS])
    keep_cots = pltpu.make_async_copy(cotangent.at[half], cots.at[pl.ds(0, half_rows)], own_sem.at[PARTS + 2])
    swap_rows = remote_copy(
        tokens.at[1 - half], rows.at[pl.ds(half_rows, half_rows)], swap_send.at[0], swap_recv.at[0], partner
    )
    swap_cot = remote_copy(
        cotangent.at[1 - half], cots.at[pl.ds(half_rows, half_rows)], swap_send.at[1], swap_recv.at[1], partner
    )
    bias_copies = [
        remote_copy(bias_shard, bias_full.at[mp], bias_send.at[k], bias_recv.at[k], device)
        for k, device in enumerate((partner, across, slanted))
    ]
    z_start(0)
    keep[0].start()
    for copy in bias_copies:
        copy.start()
    swap_rows.start()
    keep_rows.start()
    for p in range(1, PARTS):
        keep[p].start()
    keep[0].wait()
    spread(0, 0)
    for p in range(1, PARTS):
        z_start(p)
    w_pad[...] = jnp.zeros_like(w_pad)
    turned[...] = jnp.zeros_like(turned)
    bias_full[mp] = bias_shard[...]
    for d in (2, near, far):
        spread(0, d)
    for copy in keep[1:]:
        copy.wait()
    forward1(0)
    for p in range(1, PARTS):
        spread(p, 0)
    forward2(0)
    swap_cot.start()
    keep_cots.start()
    keep_rows.wait()
    swap_rows.wait_recv()
    rows_copy = pltpu.make_async_copy(rows, rows_out, out_sem.at[2])
    rows_copy.start()
    cots_copy = pltpu.make_async_copy(cots, cot_out, out_sem.at[4])
    for copy in bias_copies:
        copy.wait_recv()

    hooks = {
        0: [lambda: [spread(1, d) for d in (2, near, far)]],
        1: [lambda: forward3(0)],
        2: [lambda: [spread(2, d) for d in (2, near)]],
        3: [lambda: spread(2, far), lambda: forward1(1)],
        4: [lambda: forward2(1), lambda: forward3(1)],
        5: [lambda: [spread(3, d) for d in (2, near)]],
        6: [lambda: spread(3, far)],
        7: [lambda: forward1(2)],
        8: [lambda: forward2(2)],
        10: [lambda: forward1(3)],
        11: [lambda: forward2(3)],
    }
    seq_length = lengths[half, seq]
    row = lax.broadcasted_iota(jnp.int32, (length, 1), 0)
    place = jnp.where(row < half_rows, row + half * half_rows, row - half * half_rows)
    bias = jnp.where(place < seq_length, 0.0, masked_score).astype(jnp.bfloat16)
    lane = lax.broadcasted_iota(jnp.int32, (1, PAD), 1)
    chunk = 256

    def heads_copy(gx, gc):
        columns = pl.ds(pl.multiple_of((2 * gx + gc) * PAD, PAD), PAD)
        return pltpu.make_async_copy(heads, heads_out.at[:, columns], out_sem.at[0])

    def qkv_copy(gx, gc):
        return pltpu.make_async_copy(qkv, qkv_out.at[2 * gx + gc], out_sem.at[1])

    def w_copy(gx, gc):
        return pltpu.make_async_copy(w_pad, w_out.at[2 * gx + gc], out_sem.at[3])

    def group_step(r, carry):
        gx, gc = lax.rem(x + lax.div(r, 2), 2), lax.rem(c + lax.rem(r, 2), 2)
        group = 2 * gx + gc

        @pl.when(r == 1)
        def _():
            for d in range(nz):
                incoming(0, 3, d).wait_recv()
            for d in range(nz):
                here = block(0, 1 - c, own, d)
                remote_copy(here, here, send.at[0, 5 - c, d], recv.at[0, 5 - c, d], first).wait_recv()

        @pl.when(r == 3)
        def _():
            for d in range(nz):
                here = block(0, 1 - c, own, d)
                remote_copy(here, here, send.at[0, 4 + c, d], recv.at[0, 4 + c, d], first).wait_recv()
            take(0, 6)

        load = pltpu.make_async_copy(full_q.at[gx, gc], w_got, own_sem.at[PARTS + 1])
        load.start()
        load.wait()

        @pl.when(r > 0)
        def _():
            qkv_copy(gx, gc).wait()
            w_copy(gx, gc).wait()

        w_flat = w_got[...].reshape(-1, 3 * GC)
        for k in range(3):
            w_pad[:, k * PAD : k * PAD + GC] = w_flat[:, k * GC : (k + 1) * GC]
        w_copy(gx, gc).start()
        joined_bias = bias_full[group, 0:1, :]
        for at in range(0, length, 512):
            qkv[at : at + 512, :] = (product(rows[at : at + 512, :], w_pad[...]) + joined_bias).astype(
                jnp.bfloat16
            )
        qkv_copy(gx, gc).start()
        values_t[...] = qkv[:, 2 * PAD :].T

        def head_step(h, carry):
            for k, todo in hooks.items():
                if todo:

                    @pl.when(r * GH + h == k)
                    def _():
                        for task in todo:
                            task()

            start = h * HD
            keys = qkv[:, PAD : 2 * PAD]
            kept = jnp.where((lane >= start) & (lane < start + HD), keys, jnp.zeros_like(keys))
            own_keys = jnp.where(lane == GC, bias, kept)
            own_values = values_t[pl.ds(pl.multiple_of(start, HD), HD), :]
            for at in range(0, length, chunk):
                scores = contract_cols(own_keys, qkv[at : at + chunk, :PAD])
                top = jnp.max(scores, axis=0, keepdims=True) * exp2_scale
                raised = jnp.exp2(scores * exp2_scale - top)
                total = jnp.sum(raised, axis=0, keepdims=True)
                mixed = product(own_values, raised.astype(jnp.bfloat16))
                turned[pl.ds(pl.multiple_of(start, HD), HD), at : at + chunk] = mixed / total
                lse_out[group, pl.ds(h, 1), at : at + chunk] = top + jnp.log2(total)
            return carry

        lax.fori_loop(0, GH, head_step, 0)

        @pl.when(r > 0)
        def _():
            heads_copy(gx, gc).wait()

        heads[...] = turned[...].T.astype(jnp.bfloat16)
        heads_copy(gx, gc).start()
        return carry

    lax.fori_loop(0, GROUPS, group_step, 0)
    keep_cots.wait()
    swap_cot.wait_recv()
    cots_copy.start()
    forward3(2)
    forward3(3)
    for p in range(1, PARTS):
        for k in range(3, 7):
            take(p, k)
    heads_copy(x, c).wait()
    qkv_copy(x, c).wait()
    w_copy(x, c).wait()
    rows_copy.wait()
    cots_copy.wait()
    swap_cot.wait_send()
    swap_rows.wait_send()
    for copy in bias_copies:
        copy.wait_send()
    for p in range(PARTS):
        z_each(p, lambda copy: copy.wait_send())
        pl.when(z == 1)(lambda: z_relay(p, True).wait_send())
        pl.when(z == 2)(lambda: z_relay(p, False).wait_send())
        for k in range(7):
            for d in range(nz):
                outgoing(p, k, d).wait_send()


def forward_attention(lengths, tokens, cotangent, shards, bias_shard):
    nz = lax.axis_size("dp") // 2
    half_rows, width = tokens.shape[1:]
    rows = 2 * half_rows
    low = jnp.bfloat16
    joined_shape = (shards[0].shape[0], 3 * GC)
    anywhere, vmem = pl.BlockSpec(memory_space=pl.ANY), pl.BlockSpec(memory_space=pltpu.VMEM)
    dma = pltpu.SemaphoreType.DMA
    return pl.pallas_call(
        functools.partial(forward_kernel, nz),
        in_specs=[pl.BlockSpec(memory_space=pltpu.SMEM), anywhere, anywhere, *[vmem] * 7],
        out_specs=[*[anywhere] * PARTS, vmem, *[anywhere] * 5, vmem],
        out_shape=[
            *[
                jax.ShapeDtypeStruct((2, 2, nz, 2, *shape), low)
                for shape in (joined_shape, *[s.shape for s in shards[3:]])
            ],
            jax.ShapeDtypeStruct((GROUPS, *bias_shard.shape), jnp.float32),
            jax.ShapeDtypeStruct((rows, width), low),
            jax.ShapeDtypeStruct((rows, width), low),
            jax.ShapeDtypeStruct((GROUPS, width, 3 * PAD), low),
            jax.ShapeDtypeStruct((GROUPS, rows, 3 * PAD), low),
            jax.ShapeDtypeStruct((rows, GROUPS * PAD), low),
            jax.ShapeDtypeStruct((GROUPS, 8, rows), jnp.float32),
        ],
        scratch_shapes=[
            pltpu.VMEM(joined_shape, low),
            pltpu.VMEM((rows, width), low),
            pltpu.VMEM((rows, width), low),
            pltpu.VMEM((nz, 2, *joined_shape), low),
            pltpu.VMEM((width, 3 * PAD), low),
            pltpu.VMEM((rows, 3 * PAD), low),
            pltpu.VMEM((PAD, rows), low),
            pltpu.VMEM((PAD, rows), jnp.float32),
            pltpu.VMEM((rows, PAD), low),
            dma((PARTS + 3,)),
            dma((PARTS, nz - 1)),
            dma((PARTS, nz - 1)),
            dma((PARTS,)),
            dma((PARTS, 7, nz)),
            dma((PARTS, 7, nz)),
            dma((2,)),
            dma((2,)),
            dma((3,)),
            dma((3,)),
            dma((5,)),
        ],
        compiler_params=pltpu.CompilerParams(
            collective_id=2, has_side_effects=True, vmem_limit_bytes=60 * 1024 * 1024
        ),
    )(lengths, tokens, cotangent, *shards, bias_shard)


def place_of(half, row, half_rows):
    return jnp.where(row < half_rows, row + half * half_rows, row - half * half_rows)


def dense_kernel(
    lengths,
    heads_ref,
    rows_ref,
    cot_ref,
    out_full,
    up_full,
    down_full,
    bias_ref,
    output_ref,
    first_ref,
    active_ref,
    ffn_low_ref,
    preact_low_ref,
    attn_ref,
    attn_low_ref,
    heads_grad_ref,
    sums_ref,
    slope,
    out_pad,
    up_w,
    down_w,
    load_sem,
):
    t = pl.program_id(0)
    mp = lax.axis_index("mp")
    half, seq = lax.rem(mp, 2), lax.div(mp, 2)
    low = jnp.bfloat16
    tile, width = rows_ref.shape
    units = up_w.shape[2]
    b_out, b_down, gain1, shift1, gain2, shift2 = (
        bias_ref[0, 2 + k : 3 + k, :] for k in range(6)
    )
    out_load = pltpu.make_async_copy(out_full, out_pad.at[:, pl.ds(0, GC), :], load_sem.at[2 * GROUPS])
    up_loads = [pltpu.make_async_copy(up_full.at[g], up_w.at[g], load_sem.at[g]) for g in range(GROUPS)]
    down_loads = [
        pltpu.make_async_copy(down_full.at[g], down_w.at[g], load_sem.at[GROUPS + g]) for g in range(GROUPS)
    ]

    @pl.when(t == 0)
    def _():
        out_load.start()
        for g in range(GROUPS):
            up_loads[g].start()
            down_loads[g].start()
        out_pad[:, GC:, :] = jnp.zeros((GROUPS, PAD - GC, width), low)
        sums_ref[...] = jnp.zeros_like(sums_ref)
        out_load.wait()

    out_w = out_pad[...].reshape(GROUPS * PAD, width)

    def count(k, values):
        sums_ref[k : k + 1, :] += jnp.sum(values, axis=0, keepdims=True)

    attention = product(heads_ref[...], out_w) + b_out
    first_norm, first_scaled, first_inverse = layer_norm(
        rows_ref[...].astype(jnp.float32) + attention, gain1, shift1
    )
    first_low = first_norm.astype(low)
    first_ref[...] = first_low

    @pl.when(t == 0)
    def _():
        for copy in (*up_loads, *down_loads):
            copy.wait()

    ffn_out = jnp.broadcast_to(b_down, (tile, width))
    for g in range(GROUPS):
        preact = product(first_low, up_w[g]) + bias_ref[g, 1:2, :]
        cumulative = 0.5 * (1.0 + lax.erf(preact * 0.7071067811865476))
        active = (preact * cumulative).astype(low)
        active_ref[:, g * units : (g + 1) * units] = active
        slope[:, g * units : (g + 1) * units] = cumulative + preact * (
            jnp.exp(-0.5 * preact * preact) * 0.3989422804014327
        )
        ffn_out = ffn_out + product(active, down_w[g])
    stream = first_norm + ffn_out
    row = lax.broadcasted_iota(jnp.int32, (tile, 1), 0) + t * tile
    valid = (place_of(half, row, pl.num_programs(0) * tile // 2) < lengths[half, seq]).astype(jnp.float32)
    count(6, valid * stream * stream)
    count(7, valid * attention * attention)
    count(8, valid * ffn_out * ffn_out)
    count(9, jnp.broadcast_to(valid, (tile, width)))
    final_norm, final_scaled, final_inverse = layer_norm(stream, gain2, shift2)
    output_ref[...] = final_norm.astype(low)

    def norm_step(k, upstream, scaled, inverse, gain):
        count(k, upstream * scaled)
        count(k + 1, upstream)
        through = upstream * gain
        return inverse * (
            through
            - jnp.mean(through, axis=-1, keepdims=True)
            - scaled * jnp.mean(through * scaled, axis=-1, keepdims=True)
        )

    stream_grad = norm_step(4, cot_ref[...].astype(jnp.float32), final_scaled, final_inverse, gain2)
    count(1, stream_grad)
    ffn_grad_low = stream_grad.astype(low)
    ffn_low_ref[...] = ffn_grad_low
    first_grad = stream_grad
    for g in range(GROUPS):
        preact_grad = contract_cols(ffn_grad_low, down_w[g]) * slope[:, g * units : (g + 1) * units]
        count(12 + g, preact_grad)
        preact_low = preact_grad.astype(low)
        preact_low_ref[:, g * units : (g + 1) * units] = preact_low
        first_grad = first_grad + contract_cols(preact_low, up_w[g])
    attn_grad = norm_step(2, first_grad, first_scaled, first_inverse, gain1)
    count(0, attn_grad)
    attn_ref[...] = attn_grad
    attn_grad_low = attn_grad.astype(low)
    attn_low_ref[...] = attn_grad_low
    heads_grad_ref[...] = contract_cols(attn_grad_low, out_w).astype(low)


def dense(lengths, heads, rows, cots, out_w, up_w, down_w, biases):
    count, width = rows.shape
    tile = 256
    units = up_w.shape[2]
    low = jnp.bfloat16

    def whole(shape):
        return pl.BlockSpec(shape, lambda t: (0,) * len(shape))

    def tiled(columns):
        return pl.BlockSpec((tile, columns), lambda t: (t, 0))

    outs = [
        (width, low),
        (width, low),
        (GROUPS * units, low),
        (width, low),
        (GROUPS * units, low),
        (width, jnp.float32),
        (width, low),
        (GROUPS * PAD, low),
    ]
    return pl.pallas_call(
        dense_kernel,
        grid=(count // tile,),
        in_specs=[
            pl.BlockSpec(memory_space=pltpu.SMEM),
            tiled(GROUPS * PAD),
            tiled(width),
            tiled(width),
            *[pl.BlockSpec(memory_space=pl.ANY)] * 3,
            whole(biases.shape),
        ],
        out_specs=[*[tiled(columns) for columns, _ in outs], whole((16, width))],
        out_shape=[
            *[jax.ShapeDtypeStruct((count, columns), kind) for columns, kind in outs],
            jax.ShapeDtypeStruct((16, width), jnp.float32),
        ],
        scratch_shapes=[
            pltpu.VMEM((tile, GROUPS * units), jnp.float32),
            pltpu.VMEM((GROUPS, PAD, width), low),
            pltpu.VMEM(up_w.shape, low),
            pltpu.VMEM(down_w.shape, low),
            pltpu.SemaphoreType.DMA((2 * GROUPS + 1,)),
        ],
        cost_estimate=pl.CostEstimate(
            flops=22_600_000_000, bytes_accessed=40_000_000, transcendentals=7_000_000
        ),
    )(lengths, heads, rows, cots, out_w, up_w, down_w, biases)


GRAIN = 64
BIG = 4


def backward_kernel(
    nz,
    lengths,
    lse_ref,
    dense_sums,
    rows_in,
    w_joined,
    attn_grad,
    qkv,
    heads,
    heads_grad,
    active,
    ffn_low,
    first_low,
    preact_low,
    attn_low,
    normed,
    down_out,
    up_out,
    out_out,
    query_out,
    key_out,
    value_out,
    vectors_out,
    tokens_out,
    normed_out,
    joined_kept,
    *refs,
):
    parts, heard1, heard2, heard3, heard4 = (refs[BIG * i : BIG * (i + 1)] for i in range(5))
    (
        dense_total,
        bias_sums,
        dense_kept,
        dense_heard,
        acc,
        slots,
        right,
        left_t,
        joined,
        heads_in,
        grad_in,
        w_in,
        tokens,
        probs,
        slopes,
        turned,
        crossed,
        keys_t,
        key_acc,
        value_acc,
        send,
        recv,
        z_send,
        z_recv,
        v_send,
        v_recv,
        swap_sem,
        load_sem,
        slot_sem,
        heads_sem,
        grad_sem,
    ) = refs[5 * BIG :]
    low = jnp.bfloat16
    rows, width = tokens.shape
    half_rows = rows // 2
    chunk, span = 256, 384
    bias_share = GC // (2 * nz)
    mp, x, c, z, y = positions()
    first, second, partner, along = neighbours(nz)
    own, got1, got2, got3 = regions(x, c, y)

    def group_of(r):
        return lax.rem(x + 1 + lax.rem(r, 2), 2), lax.rem(c + 1 + lax.div(r, 2), 2)

    def index_of(r):
        gx, gc = group_of(r)
        return 2 * gx + gc

    def columns(r, size):
        return pl.ds(pl.multiple_of(index_of(r) * size, size), size)

    def load(src, dst, k):
        return pltpu.make_async_copy(src, dst, load_sem.at[k])

    def slot_load(src, s):
        return pltpu.make_async_copy(src, slots.at[s], slot_sem.at[s])

    def active_load(r):
        return slot_load(active.at[:, columns(r, width)], lax.rem(r, 2))

    def preact_load(r):
        return slot_load(preact_low.at[:, columns(r, width)], lax.rem(r, 2))

    def qkv_load(r):
        return slot_load(qkv.at[index_of(r)], lax.rem(r, 2))

    def heads_load(r):
        s = lax.rem(r, 2)
        return pltpu.make_async_copy(heads.at[:, columns(r, PAD)], heads_in.at[s], heads_sem.at[s])

    def grad_load(r):
        s = lax.rem(r, 2)
        return pltpu.make_async_copy(heads_grad.at[:, columns(r, PAD)], grad_in.at[s], grad_sem.at[s])

    w_other = right.at[pl.ds(0, width)]

    def w_load(r, other=False):
        return load(w_joined.at[index_of(r)], w_other if other else w_in, 6 if other else 3)

    def keep_joined(r):
        return load(joined, joined_kept.at[r], 5)

    def back_load(r):
        return slot_load(joined_kept.at[r], lax.rem(r, 2))

    ffn_load, attn_low_load = load(ffn_low, right, 0), load(attn_low, right, 0)
    first_load, rows_load = load(first_low, joined, 1), load(rows_in, joined, 1)
    tokens_load = load(attn_grad, tokens, 2)

    def core_copy(p, r):
        gx, gc = group_of(r)
        return remote_copy(parts[p].at[gx, gc], heard1[p].at[r], send.at[p, r], recv.at[p, r], partner)

    def second_copy(p, k):
        place = (got2, got3)[k]
        return remote_copy(
            parts[p].at[place[0], c, :, place[1]], heard2[p].at[k], send.at[p, 2 + k], recv.at[p, 2 + k], second
        )

    def first_copy(p):
        return remote_copy(
            parts[p].at[got1[0], c, :, got1[1]], heard3[p], send.at[p, 4], recv.at[p, 4], first
        )

    def z_copy(p, d):
        return remote_copy(
            parts[p].at[x, c, lax.rem(z + d + 1, nz), y],
            heard4[p].at[d],
            z_send.at[p, d],
            z_recv.at[p, d],
            along[d],
        )

    def add(p, place, more):
        for i in range(nz):
            here = parts[p].at[place[0], c, i, place[1]]
            here[...] = (here[...].astype(jnp.float32) + more[i].astype(jnp.float32)).astype(low)

    def take_second(p, k):
        second_copy(p, k).wait_recv()
        add(p, got1 if k else own, heard2[p].at[k])

    def pass_first(p):
        take_second(p, 1)
        first_copy(p).start()

    def take_first(p):
        first_copy(p).wait_recv()
        add(p, own, heard3[p])
        for d in range(nz - 1):
            z_copy(p, d).start()

    def take_z(p):
        total = parts[p][x, c, z, y].astype(jnp.float32)
        for d in range(nz - 1):
            z_copy(p, d).wait_recv()
            total = total + heard4[p][d].astype(jnp.float32)
        if p < BIG - 1:
            (down_out, up_out, out_out)[p][...] = total
        else:
            for k, result in enumerate((query_out, key_out, value_out)):
                result[...] = total[:, k * GC : (k + 1) * GC]
            vectors_out[7:9, :bias_share] = total[0:2, 3 * GC : 3 * GC + bias_share]

    def sums_copy(k):
        device = (first, second)[k - 1] if 0 < k < 3 else along[k - 3] if k else partner
        return remote_copy(dense_kept.at[min(k, 3)], dense_heard.at[k], v_send.at[k], v_recv.at[k], device)

    def sums_step(k):
        sums_copy(k).wait_recv()
        dense_kept[k + 1] = dense_kept[k] + dense_heard[k]
        for later in (k + 1,) if k < 2 else range(3, nz + 2):
            sums_copy(later).start()

    def sums_last():
        total = dense_kept[3]
        for k in range(3, nz + 2):
            sums_copy(k).wait_recv()
            total = total + dense_heard[k]
        dense_total[...] = total

    def finish(p, r):
        gx, gc = group_of(r)
        deep, wide = parts[p].shape[4:]
        pieces = [(0, 0, wide)] if p < BIG - 1 else [(k * GC, k * PAD, GC) for k in range(3)]

        def put(more):
            for i in range(nz):
                for at, source, size in pieces:
                    value = acc[2 * deep * i : 2 * deep * (i + 1), source : source + size].reshape(2, deep, size)
                    if more is not None:
                        value = value + more[i, :, :, at : at + size].astype(jnp.float32)
                    parts[p][gx, gc, i, :, :, at : at + size] = value.astype(low)
            if p < BIG - 1:
                return
            beside = slice(3 * GC, 3 * GC + bias_share)
            for i in range(nz):
                for j in range(2):
                    at = (2 * i + j) * bias_share
                    value = bias_sums[:, at : at + bias_share]
                    if more is not None:
                        value = value + more[i, j, :16, beside].astype(jnp.float32)
                    parts[p][gx, gc, i, j, :16, beside] = value.astype(low)

        @pl.when(r < 2)
        def _():
            put(None)
            core_copy(p, r).start()

        @pl.when(r >= 2)
        def _():
            core_copy(p, r - 2).wait_recv()
            put(heard1[p].at[r - 2])

        @pl.when(r == 2)
        def _():
            second_copy(p, 1).start()
            pl.when(c == 0)(lambda: second_copy(p, 0).start())

        @pl.when(r == 3)
        def _():
            pl.when(c == 1)(lambda: second_copy(p, 0).start())

    ffn_load.start()
    active_load(0).start()
    heads_load(0).start()
    first_load.start()
    w_load(3).start()
    tokens_load.start()
    dense_kept[0] = dense_sums[...]
    bias_sums[...] = jnp.zeros_like(bias_sums)
    for gx in range(2):
        for gc in range(2):
            parts[3][gx, gc, :, :, :, 3 * GC :] = jnp.zeros((nz, 2, width // (2 * nz), GRAIN), low)
    meet([first, second, partner, *along])
    normed_swap = remote_copy(
        normed.at[pl.ds(half_rows, half_rows)], normed_out, swap_sem.at[2], swap_sem.at[3], partner
    )
    normed_swap.start()
    ffn_load.wait()

    def down_step(r, carry):
        active_load(r).wait()
        pl.when(r < 3)(lambda: active_load(r + 1).start())
        pl.when(r == 3)(lambda: preact_load(0).start())
        s = lax.rem(r, 2)
        for at in range(0, width, span):
            acc[at : at + span, :] = product(slots[s, :, at : at + span].T, right[...])
        finish(0, r)
        return carry

    lax.fori_loop(0, GROUPS, down_step, 0)
    sums_copy(0).start()
    attn_low_load.start()
    first_load.wait()
    left_t[...] = joined[...].T
    rows_load.start()

    def up_step(r, carry):
        preact_load(r).wait()
        pl.when(r < 3)(lambda: preact_load(r + 1).start())
        pl.when(r == 3)(lambda: qkv_load(0).start())
        s = lax.rem(r, 2)
        for at in range(0, width, span):
            acc[at : at + span, :] = product(left_t[at : at + span, :], slots[s])
        finish(1, r)
        return carry

    lax.fori_loop(0, GROUPS, up_step, 0)
    sums_step(0)
    attn_low_load.wait()

    def out_step(r, carry):
        heads_load(r).wait()
        heads_load(lax.rem(r + 1, GROUPS)).start()
        acc[:PAD, :] = product(heads_in[lax.rem(r, 2)].T, right[...])
        finish(2, r)
        return carry

    lax.fori_loop(0, GROUPS, out_step, 0)
    grad_load(0).start()
    w_load(0, True).start()
    rows_load.wait()
    left_t[...] = joined[...].T
    tokens_load.wait()

    hooks = {
        1: lambda: (pass_first(0), take_second(0, 0)),
        2: lambda: sums_step(1),
        4: lambda: take_first(0),
        6: lambda: (pass_first(1), take_second(1, 0)),
        7: lambda: (pass_first(2), take_second(2, 0)),
        8: lambda: sums_step(2),
        9: lambda: take_first(1),
        10: lambda: take_first(2),
        11: lambda: (take_z(0), sums_last(), pl.when(c == 1)(lambda: pass_first(3))),
    }
    row = lax.broadcasted_iota(jnp.int32, (rows, 1), 0)
    bias = jnp.where(place_of(c, row, half_rows) < lengths[c, x], 0.0, masked_score).astype(low)
    lane = lax.broadcasted_iota(jnp.int32, (1, PAD), 1)
    turned[...] = jnp.zeros_like(turned)

    def group_step(r, carry):
        s = lax.rem(r, 2)
        group = index_of(r)
        for copy in (qkv_load, heads_load, grad_load):
            copy(r).wait()

        @pl.when(r < 3)
        def _():
            for copy in (qkv_load, heads_load, grad_load):
                copy(r + 1).start()

        pl.when(r == 3)(lambda: back_load(0).start())
        crossed[...] = (grad_in[s].astype(jnp.float32) * heads_in[s].astype(jnp.float32)).T
        keys_t[...] = slots[s, :, PAD : 2 * PAD].T
        key_acc[...] = jnp.zeros_like(key_acc)
        value_acc[...] = jnp.zeros_like(value_acc)

        def head_step(h, carry):
            for k, todo in hooks.items():
                pl.when(r * GH + h == k)(todo_of(todo))
            start = pl.multiple_of(h * HD, HD)
            head = (lane >= start) & (lane < start + HD)
            keys = slots[s, :, PAD : 2 * PAD]
            own_keys = jnp.where(lane == GC, bias, jnp.where(head, keys, jnp.zeros_like(keys)))
            own_values = jnp.where(head, slots[s, :, 2 * PAD :], jnp.zeros((), low))
            delta = jnp.sum(crossed[pl.ds(start, HD), :], axis=0, keepdims=True)
            for at in range(0, rows, chunk):
                scores = contract_cols(own_keys, slots[s, at : at + chunk, :PAD])
                attn_probs = jnp.exp2(scores * exp2_scale - lse_ref[group, pl.ds(h, 1), at : at + chunk])
                prob_grad = contract_cols(own_values, grad_in[s, at : at + chunk, :])
                probs[:, at : at + chunk] = attn_probs.astype(low)
                slopes[:, at : at + chunk] = (
                    attn_probs * (prob_grad - delta[:, at : at + chunk])
                ).astype(low)
            own_grads = jnp.where(head, grad_in[s], jnp.zeros((), low))
            own_queries = jnp.where(head, slots[s, :, :PAD], jnp.zeros((), low))
            value_acc[...] += product(probs[...], own_grads)
            key_acc[...] += product(slopes[...], own_queries)
            turned[pl.ds(start, HD), :] = product(keys_t[pl.ds(start, HD), :], slopes[...])
            return carry

        lax.fori_loop(0, GH, head_step, 0)
        query_grad = turned[...].T * score_scale
        pl.when(r > 0)(lambda: keep_joined(r - 1).wait())
        joined[:, :PAD] = query_grad.astype(low)
        joined[:, PAD : 2 * PAD] = (key_acc[...] * score_scale).astype(low)
        joined[:, 2 * PAD :] = value_acc[...].astype(low)
        bias_sums[0:1, :] = jnp.sum(query_grad, axis=0, keepdims=True)
        bias_sums[1:2, :] = jnp.sum(value_acc[...], axis=0, keepdims=True)
        for at in range(0, width, span):
            acc[at : at + span, :] = product(left_t[at : at + span, :], joined[...])
        finish(3, r)
        pl.when(r < 3)(lambda: keep_joined(r).start())
        return carry

    lax.fori_loop(0, GROUPS, group_step, 0)
    pl.when(c == 0)(lambda: pass_first(3))

    def add_tokens(kept_group, weights):
        for at in range(0, rows, chunk):
            tokens[at : at + chunk, :] += contract_cols(kept_group[at : at + chunk, :], weights[...])

    back_load(1).start()
    w_load(3).wait()
    add_tokens(joined, w_in)
    w_load(1).start()
    w_load(0, True).wait()
    back_load(0).wait()
    add_tokens(slots.at[0], w_other)
    w_load(2, True).start()
    back_load(2).start()
    take_second(3, 0)
    w_load(1).wait()
    back_load(1).wait()
    add_tokens(slots.at[1], w_in)
    take_first(3)
    w_load(2, True).wait()
    back_load(2).wait()
    add_tokens(slots.at[0], w_other)
    swap = remote_copy(
        tokens.at[pl.ds(half_rows, half_rows)], tokens_out.at[c], swap_sem.at[0], swap_sem.at[1], partner
    )
    keep = pltpu.make_async_copy(tokens.at[pl.ds(0, half_rows)], tokens_out.at[c], load_sem.at[4])
    swap.start()
    keep.start()

    def piece(values, index, count):
        size = values.shape[1] // count
        found = values[:, :size]
        for k in range(1, count):
            found = jnp.where(index == k, values[:, k * size : (k + 1) * size], found)
        return found

    dp = 2 * z + y
    vectors_out[...] = jnp.zeros_like(vectors_out)
    share = width // (8 * nz)
    vectors_out[0:6, :share] = piece(dense_total[0:6, :], dp * 4 + mp, 8 * nz)
    vectors_out[6:7, : width // (2 * nz)] = piece(dense_total[pl.ds(12 + mp, 1), :], dp, 2 * nz)
    for k in range(3):
        square = jnp.sum(dense_total[6 + k : 7 + k, :], axis=1, keepdims=True)
        vectors_out[12:13, k : k + 1] = jnp.sqrt(square / (dense_total[9:10, 0:1] * width))
    take_z(1)
    take_z(2)
    take_z(3)

    keep.wait()
    swap.wait()
    normed_swap.wait()
    for p in range(BIG):
        for r in range(2):
            core_copy(p, r).wait_send()
            second_copy(p, r).wait_send()
        first_copy(p).wait_send()
        for d in range(nz - 1):
            z_copy(p, d).wait_send()
    for k in range(nz + 2):
        sums_copy(k).wait_send()


def todo_of(todo):
    def run():
        todo()

    return run


def backward(lengths, lse, dense_sums, *operands):
    rows_in, w_joined = operands[:2]
    nz = lax.axis_size("dp") // 2
    rows, width = rows_in.shape
    low, wide = jnp.bfloat16, jnp.float32
    deep = width // (2 * nz)
    tails = [(deep, width), (deep, width), (GC // (2 * nz), width), (deep, 3 * GC + GRAIN)]
    results = [*tails[:3], *[(deep, GC)] * 3]
    sums = dense_sums.shape
    anywhere, vmem = pl.BlockSpec(memory_space=pl.ANY), pl.BlockSpec(memory_space=pltpu.VMEM)
    dma = pltpu.SemaphoreType.DMA
    return pl.pallas_call(
        functools.partial(backward_kernel, nz),
        in_specs=[pl.BlockSpec(memory_space=pltpu.SMEM), vmem, vmem, *[anywhere] * len(operands)],
        out_specs=[*[vmem] * 7, *[anywhere] * 3],
        out_shape=[
            *[jax.ShapeDtypeStruct(shape, wide) for shape in (*results, (16, 128))],
            jax.ShapeDtypeStruct((MB, rows // 2, width), wide),
            jax.ShapeDtypeStruct((rows // 2, width), low),
            jax.ShapeDtypeStruct((GROUPS, rows, 3 * PAD), low),
        ],
        scratch_shapes=[
            *[pltpu.VMEM((2, 2, nz, 2, *t), low) for t in tails],
            *[pltpu.VMEM((2, nz, 2, *t), low) for t in tails],
            *[pltpu.VMEM((2, nz, *t), low) for t in tails],
            *[pltpu.VMEM((nz, *t), low) for t in tails],
            *[pltpu.VMEM((nz - 1, *t), low) for t in tails],
            pltpu.VMEM(sums, wide),
            pltpu.VMEM((16, PAD), wide),
            pltpu.VMEM((4, *sums), wide),
            pltpu.VMEM((nz + 2, *sums), wide),
            pltpu.VMEM((width, 3 * PAD), wide),
            pltpu.VMEM((2, rows, width), low),
            pltpu.VMEM((rows, width), low),
            pltpu.VMEM((width, rows), low),
            pltpu.VMEM((rows, 3 * PAD), low),
            pltpu.VMEM((2, rows, PAD), low),
            pltpu.VMEM((2, rows, PAD), low),
            pltpu.VMEM((width, 3 * PAD), low),
            pltpu.VMEM((rows, width), wide),
            pltpu.VMEM((rows, rows), low),
            pltpu.VMEM((rows, rows), low),
            pltpu.VMEM((PAD, rows), wide),
            pltpu.VMEM((PAD, rows), wide),
            pltpu.VMEM((PAD, rows), low),
            pltpu.VMEM((rows, PAD), wide),
            pltpu.VMEM((rows, PAD), wide),
            dma((BIG, 5)),
            dma((BIG, 5)),
            dma((BIG, nz - 1)),
            dma((BIG, nz - 1)),
            dma((nz + 2,)),
            dma((nz + 2,)),
            dma((4,)),
            dma((7,)),
            dma((2,)),
            dma((2,)),
            dma((2,)),
        ],
        compiler_params=pltpu.CompilerParams(
            collective_id=1, has_side_effects=True, vmem_limit_bytes=63 * 1024 * 1024
        ),
    )(lengths, lse, dense_sums, *operands)


def body_fused(
    tokens,
    cotangent,
    lengths,
    w_query,
    w_key,
    w_value,
    w_out,
    w_up,
    w_down,
    b_query,
    b_value,
    b_up,
    b_out,
    b_down,
    norm1_gain,
    norm1_shift,
    norm2_gain,
    norm2_shift,
):
    half_rows = tokens.shape[1]
    width = tokens.shape[2]
    n_dp, n_mp = lax.axis_size("dp"), lax.axis_size("mp")
    unit_cols = w_up.shape[1]
    mark = jnp.zeros((PAD - GC,), jnp.float32).at[0].set(1.0)
    bias_rows = jnp.concatenate(
        [
            b_query,
            mark,
            jnp.zeros((PAD,), jnp.float32),
            b_value,
            jnp.zeros((PAD - GC,), jnp.float32),
            b_up,
            b_out,
            b_down,
            norm1_gain,
            norm1_shift,
            norm2_gain,
            norm2_shift,
        ]
    ).reshape(8, width)
    gathered = forward_attention(
        lengths, tokens, cotangent, (w_query, w_key, w_value, w_out, w_up, w_down), bias_rows
    )
    full_out, full_up, full_down = (
        g.reshape(n_mp, n_dp * g.shape[4], g.shape[5]) for g in gathered[1:4]
    )
    full_bias, rows_in, rows_cot, w_joined, qkv, heads, lse = gathered[4:]
    (
        output,
        first_low,
        active,
        ffn_grad_low,
        preact_low,
        attn_grad,
        attn_grad_low,
        heads_grad,
        dense_sums,
    ) = dense(lengths, heads, rows_in, rows_cot, full_out, full_up, full_down, full_bias)
    *matrix_grads, vectors, tokens_grad, output_got, _ = backward(
        lengths,
        lse,
        dense_sums,
        rows_in,
        w_joined,
        attn_grad,
        qkv,
        heads,
        heads_grad,
        active,
        ffn_grad_low,
        first_low,
        preact_low,
        attn_grad_low,
        output,
    )
    share = width // (n_dp * n_mp)
    sizes = [*[share] * 6, unit_cols // n_dp, share, share, 3]
    delivered = deliver(matrix_grads, vectors, output, output_got, tokens_grad, sizes)
    output, tokens_grad, own_down, own_up, own_out, own_query, own_key, own_value = delivered[:8]
    own_vectors = [v.reshape(-1) for v in delivered[8:]]
    return (
        output,
        tokens_grad,
        own_query,
        own_key,
        own_value,
        own_out,
        own_up,
        own_down,
        own_vectors[7],
        own_vectors[8],
        own_vectors[6],
        *own_vectors[:6],
        own_vectors[9],
    )


def deliver_kernel(mats, *refs):
    results, (vectors, normed, normed_got, tokens) = refs[:mats], refs[mats : mats + 4]
    outs = refs[mats + 4 :]
    normed_out, tokens_out = outs[:2]
    mat_outs, vec_outs = outs[2 : 2 + mats], outs[2 + mats : 12 + mats]
    normed_kept, tokens_kept, load_sem, store_sem = outs[12 + mats :]
    half = lax.rem(lax.axis_index("mp"), 2)
    half_rows = tokens.shape[1]
    moves = [
        (tokens.at[0], tokens_kept.at[0], tokens_out.at[0]),
        (tokens.at[1], tokens_kept.at[1], tokens_out.at[1]),
        (normed.at[pl.ds(0, half_rows)], normed_kept.at[0], normed_out.at[half]),
        (normed_got, normed_kept.at[1], normed_out.at[1 - half]),
    ]
    loads = [pltpu.make_async_copy(a, b, load_sem.at[k]) for k, (a, b, _) in enumerate(moves)]
    stores = [pltpu.make_async_copy(b, o, store_sem.at[k]) for k, (_, b, o) in enumerate(moves)]
    stores += [
        pltpu.make_async_copy(a, o, store_sem.at[len(moves) + k])
        for k, (a, o) in enumerate(zip(results, mat_outs))
    ]
    for copy in (*loads, *stores[len(moves) :]):
        copy.start()
    for k, out in enumerate(vec_outs[:9]):
        out[...] = vectors[k : k + 1, : out.shape[1]]
    vec_outs[9][...] = vectors[12:13, :3]
    for k, copy in enumerate(loads):
        copy.wait()
        stores[k].start()
    for copy in stores:
        copy.wait()


def deliver(results, vectors, normed, normed_got, tokens, sizes):
    mats = len(results)
    anywhere, vmem = pl.BlockSpec(memory_space=pl.ANY), pl.BlockSpec(memory_space=pltpu.VMEM)
    big = [jax.ShapeDtypeStruct((2, *normed_got.shape), normed.dtype), jax.ShapeDtypeStruct(tokens.shape, tokens.dtype)]
    rows = [jax.ShapeDtypeStruct((1, size), jnp.float32) for size in sizes]
    return pl.pallas_call(
        functools.partial(deliver_kernel, mats),
        grid=(1,),
        in_specs=[*[vmem] * (mats + 1), *[anywhere] * 3],
        out_specs=[
            *[anywhere] * (2 + mats),
            *[pl.BlockSpec((1, size), lambda i: (0, 0)) for size in sizes],
        ],
        out_shape=[*big, *[jax.ShapeDtypeStruct(r.shape, r.dtype) for r in results], *rows],
        scratch_shapes=[
            pltpu.VMEM(big[0].shape, big[0].dtype),
            pltpu.VMEM(big[1].shape, big[1].dtype),
            pltpu.SemaphoreType.DMA((4,)),
            pltpu.SemaphoreType.DMA((4 + mats,)),
        ],
    )(*results, vectors, normed, normed_got, tokens)


def solution(mesh):
    rows = P(None, BOTH, None)
    split, rows_split = P("dp", "mp"), P(("mp", "dp"), None)
    aligned = mesh.shape["dp"] == 8 and mesh.shape["mp"] == 4
    return jax.shard_map(
        body_fused if aligned else body_any,
        mesh=mesh,
        in_specs=(
            rows,
            rows,
            P(None, "dp"),
            split,
            split,
            split,
            rows_split,
            split,
            rows_split,
            P("mp"),
            P("mp"),
            P("mp"),
            *([P()] * 6),
        ),
        out_specs=(
            rows,
            rows,
            split,
            split,
            split,
            rows_split,
            split,
            rows_split,
            *([P(("mp", "dp"))] * 3),
            *([P(BOTH)] * 6),
            P(),
        ),
        check_vma=False,
    )
```
